32 devices in a mesh: ep: 4 (over x, core), rep: 8 (over z, y).
Axes of the slice: x: 2, y: 2, z: 4, core: 2. Of those that a mesh axis runs over, the one named last changes fastest.
Arguments:
- tokens: float32 [4, 2048, 1024], P('ep', 'rep'), may hold values from -6 to 6
- segments: int32 [4, 2048], P('ep', 'rep'), may hold values from 0 to 2, never falling along the last dimension, each value on 1 to 1536 neighbouring positions
- routes: int32 [4, 2048, 8], P('ep', 'rep'), may hold values from 0 to 31, all different within a row
- attn_gain: float32 [1024], replicated, may hold values from 0.5 to 1.5
- w_query: bfloat16 [1024, 1024], P(('ep', 'rep')), may hold values from -0.75 to 0.75
- w_key: bfloat16 [1024, 512], P(('ep', 'rep')), may hold values from -0.75 to 0.75
- w_value: bfloat16 [1024, 512], P(('ep', 'rep')), may hold values from -0.1875 to 0.1875
- w_out: bfloat16 [1024, 1024], P(('ep', 'rep')), may hold values from -3 to 3
- mlp_gain: float32 [1024], replicated, may hold values from 0.5 to 1.5
- w_router: bfloat16 [1024, 32], P(('ep', 'rep')), may hold values from -0.09375 to 0.09375
- w_gate_up: bfloat16 [32, 1024, 1024], P('ep'), may hold values from -0.1875 to 0.1875
- w_down: bfloat16 [32, 512, 1024], P('ep'), may hold values from -3 to 3
- cotangent: float32 [4, 2048, 1024], P('ep', 'rep'), may hold values from -6 to 6
Outputs:
- output: float32 [4, 2048, 1024], P('ep', 'rep')
- grad_tokens: float32 [4, 2048, 1024], P('ep', 'rep')
- grad_attn_gain: float32 [1024], P(('ep', 'rep'))
- grad_w_query: float32 [1024, 1024], P(('ep', 'rep'))
- grad_w_key: float32 [1024, 512], P(('ep', 'rep'))
- grad_w_value: float32 [1024, 512], P(('ep', 'rep'))
- grad_w_out: float32 [1024, 1024], P(('ep', 'rep'))
- grad_mlp_gain: float32 [1024], P(('ep', 'rep'))
- grad_w_router: float32 [1024, 32], P(('ep', 'rep'))
- grad_w_gate_up: float32 [32, 1024, 1024], P('ep', 'rep')
- grad_w_down: float32 [32, 512, 1024], P('ep', None, 'rep')
The draws below stay inside these ranges and needn't reach their ends.
Inputs may be any that keep to these rules, and one draw needn't show every extreme that they name: `segments`: segment numbers never fall along a pack; each of the 3 documents of a pack has 1 to 1536 tokens, one of them exactly 1536. `routes`: each token names 8 different experts.
All inputs are finite; a program needn't handle non-finite values.
Results may differ from the reference program's by a relative error of at most 0.015.
The reference program's roundings to bfloat16 on the way count: a program that leaves them out, or rounds other values in their place, can miss the bound.
Values may be sent and summed in bfloat16 or wider, within the bound.
A program may use at most 256 MiB of HBM per device.

```python
import math
import jax
import jax.numpy as jnp
import numpy as np
from jax import lax

D = 1024
HEADS = 16
KV_HEADS = 8
HEAD_DIM = 64
FE = 512
E = 32
TOPK = 8
PACK = 2048
DOC_MOST = 1536
SEGS = 3
CAP = 80
N_EP = 4
N_REP = 8


def shard_levels(rng, extent, pieces, low, high):
    level = 1.0
    for dim, parts in pieces:
        draws = jax.random.uniform(jax.random.fold_in(jax.random.fold_in(rng, 6), dim), (parts,), jnp.float32, low / len(pieces), high / len(pieces))
        level = level * jnp.repeat(jnp.exp(draws), extent[dim] // parts).reshape((-1,) + (1,) * (len(extent) - 1 - dim))
    return level


def different_ones(stream_key, rows, count, top, lift):
    sequence = jax.random.permutation(jax.random.fold_in(stream_key, 1), count)
    boost = sequence
    for power in range(3):
        boost = boost * boost // count
    boost = boost * lift // count
    lots = jax.random.randint(jax.random.fold_in(stream_key, 2), (rows, count), 0, 4096) + boost
    holders = jax.random.permutation(jax.random.fold_in(stream_key, 3), rows)[jnp.arange(count) % rows]
    lots = jnp.where(jnp.arange(rows)[:, None] == holders[None, :], 1 << 14, lots)
    priority = lots * count + jnp.arange(count)
    return lax.top_k(priority.astype(jnp.int32), top)[1].astype(jnp.int32)


def split_up(amount, total, most, lean):
    portions = [(1 << 20) // math.isqrt(standing ** lean) + 1 for standing in range(2, amount + 1)]
    spare, holding = total - most - (amount - 1), [1] * (amount - 1)
    while spare > 0:
        candidates = [i for i in range(amount - 1) if holding[i] < most]
        pool, left = sum([portions[i] for i in candidates]), spare
        for i in candidates:
            more = min(most - holding[i], max(1, left * portions[i] // pool), spare)
            holding[i] = holding[i] + more
            spare = spare - more
    return np.array([most] + holding)


def ragged(stream_key, number_of, total, reach, lean):
    if number_of == 2:
        one = jax.random.randint(stream_key, (), max(1, total - reach), min(reach, total - 1) + 1)
        return jnp.stack([one, total - one])
    tallies = jnp.asarray(split_up(number_of, total, reach, lean), jnp.int32)
    twos = (number_of - 1) // 2
    source_of, sink = tallies[1:1 + 2 * twos:2], tallies[2:2 + 2 * twos:2]
    slack = jnp.minimum(source_of - 1, reach - sink)
    shifted = jax.random.randint(jax.random.fold_in(stream_key, 1), (twos,), 0, 1 << 20) % (slack + 1)
    tallies = tallies.at[1:1 + 2 * twos:2].set(source_of - shifted).at[2:2 + 2 * twos:2].set(sink + shifted)
    return tallies[jax.random.permutation(jax.random.fold_in(stream_key, 2), number_of)]


def normal_values(rng, extent, width, bound, cuts=(), kind=jnp.bfloat16):
    entries = width * jax.random.normal(rng, extent, jnp.float32)
    if cuts:
        entries = entries * shard_levels(rng, extent, cuts, -0.22, 0.18)
    return jnp.clip(entries, -bound, bound).astype(kind)


def setup_inputs(seed: int = 0) -> dict:
    key_of = jax.random.split(jax.random.key(seed), 14)
    tokens = normal_values(key_of[0], (N_EP, PACK, D), 1.0, 6.0, ((0, 4), (1, 8)), jnp.float32)
    segments = jax.vmap(lambda own: jnp.searchsorted(jnp.cumsum(ragged(own, SEGS, PACK, DOC_MOST, 1)), jnp.arange(PACK), side="right"))(jax.random.split(key_of[1], N_EP)).reshape((N_EP, PACK)).astype(jnp.int32)
    routes = different_ones(key_of[2], N_EP * PACK, E, TOPK, 2048).reshape((N_EP, PACK, TOPK))
    attn_gain = jnp.clip(1.0 + 0.1 * jax.random.normal(key_of[3], (D,), jnp.float32), 0.5, 1.5)
    w_query = normal_values(key_of[4], (D, HEADS * HEAD_DIM), 0.125, 0.75, ((0, 32),))
    w_key = normal_values(key_of[5], (D, KV_HEADS * HEAD_DIM), 0.125, 0.75, ((0, 32),))
    w_value = normal_values(key_of[6], (D, KV_HEADS * HEAD_DIM), D ** -0.5, 0.1875, ((0, 32),))
    w_out = normal_values(key_of[7], (HEADS * HEAD_DIM, D), 0.5, 3.0, ((0, 32),))
    mlp_gain = jnp.clip(1.0 + 0.1 * jax.random.normal(key_of[8], (D,), jnp.float32), 0.5, 1.5)
    w_router = normal_values(key_of[9], (D, E), 0.015625, 0.09375, ((0, 32),))
    w_gate_up = normal_values(key_of[10], (E, D, 2 * FE), D ** -0.5, 0.1875, ((0, 4),))
    w_down = normal_values(key_of[11], (E, FE, D), 0.5, 3.0, ((0, 4),))
    cotangent = normal_values(key_of[12], (N_EP, PACK, D), 1.0, 6.0, ((0, 4), (1, 8)), jnp.float32)
    return {"tokens": tokens, "segments": segments, "routes": routes, "attn_gain": attn_gain, "w_query": w_query, "w_key": w_key, "w_value": w_value, "w_out": w_out, "mlp_gain": mlp_gain, "w_router": w_router, "w_gate_up": w_gate_up, "w_down": w_down, "cotangent": cotangent}


epsilon = 1e-06
score_scale = 0.015625
branch_scale = 0.22
far_below = -1e+30

@jax.custom_vjp
def low(v):
    return lax.optimization_barrier(v.astype(jnp.bfloat16)).astype(jnp.float32)

@jax.custom_vjp
def low_back(v):
    return v

def low_keep(v):
    return (low(v), None)

def low_pass(kept, grad):
    return (grad,)

def back_keep(v):
    return (v, None)

def back_low(kept, grad):
    return (low(grad),)
low.defvjp(low_keep, low_pass)
low_back.defvjp(back_keep, back_low)

def highest(form, left, right):
    return jnp.einsum(form, left, right, precision=lax.Precision.HIGHEST)

def rms_norm(values, gain):
    factor = lax.rsqrt(lax.optimization_barrier(jnp.mean(values * values, -1, keepdims=True)) + epsilon)
    return values * factor * gain

def rotate(values, cosine, sine_table):
    half_dim = values.shape[-1] // 2
    lower = values[..., :half_dim]
    upper = values[..., half_dim:]
    return jnp.concatenate([lower * cosine - upper * sine_table, upper * cosine + lower * sine_table], -1)

def attend_pack(pack_tokens, pack_ids, attn_gain, w_query, w_key, w_value, w_out):
    length = pack_tokens.shape[0]
    normed = low(rms_norm(pack_tokens, attn_gain))
    query_rows = low_back(highest('td,df->tf', normed, w_query)).reshape(length, HEADS, HEAD_DIM)
    key_rows = low_back(highest('td,df->tf', normed, w_key)).reshape(length, KV_HEADS, HEAD_DIM)
    value_rows = low(low_back(highest('td,df->tf', normed, w_value))).reshape(length, KV_HEADS, HEAD_DIM)
    doc_start = lax.optimization_barrier(jnp.sum((pack_ids[None, :] < pack_ids[:, None]).astype(jnp.int32), 1))
    places = jnp.arange(length, dtype=jnp.int32)
    position = (places - doc_start).astype(jnp.float32)
    half_dim = HEAD_DIM // 2
    angles = position[:, None] * jnp.exp(jnp.arange(half_dim, dtype=jnp.float32) * (-math.log(10000.0) / half_dim))[None, :]
    cosine = jnp.cos(angles)[:, None, :]
    sine_table = jnp.sin(angles)[:, None, :]
    query_rows = low(rotate(query_rows, cosine, sine_table))
    key_rows = low(rotate(key_rows, cosine, sine_table))
    group_size = HEADS // KV_HEADS
    keys_all = jnp.repeat(key_rows, group_size, axis=1)
    values_all = jnp.repeat(value_rows, group_size, axis=1)
    block_rows = min(512, length)

    def one_block(start):
        query_block = lax.dynamic_slice_in_dim(query_rows, start, block_rows, 0)
        id_block = lax.dynamic_slice_in_dim(pack_ids, start, block_rows, 0)
        place_block = start + jnp.arange(block_rows, dtype=jnp.int32)
        scores = low_back(highest('qhd,khd->hqk', query_block, keys_all)) * score_scale
        allowed = (id_block[:, None] == pack_ids[None, :]) & (places[None, :] <= place_block[:, None])
        scores = jnp.where(allowed[None], scores, far_below)
        attn_prob = low(jax.nn.softmax(scores, -1))
        return highest('hqk,khd->qhd', attn_prob, values_all)
    starts = jnp.arange(length // block_rows, dtype=jnp.int32) * block_rows
    mixed_rows = lax.map(jax.checkpoint(one_block), starts).reshape(length, HEADS * HEAD_DIM)
    mixed_rows = low(low_back(mixed_rows))
    return pack_tokens + branch_scale * low_back(highest('tf,fd->td', mixed_rows, w_out))

def mix_experts(hidden, mlp_gain, w_router, w_gate_up, w_down, routes):
    devices, rows_dev, model_width = hidden.shape
    normed = low(rms_norm(hidden, mlp_gain))
    logits = highest('vtd,de->vte', normed, w_router)
    numbers = jnp.arange(E, dtype=jnp.int32)
    pick_table = (routes[..., None] == numbers).astype(jnp.int32)
    chosen = lax.optimization_barrier(jnp.sum(pick_table.astype(jnp.float32) * logits[:, :, None, :], -1))
    gate_probs = jax.nn.softmax(chosen, -1)
    onehot = lax.optimization_barrier(jnp.sum(pick_table, 2))
    before = jnp.cumsum(onehot, 1) - onehot
    slot_rank = lax.optimization_barrier(jnp.sum(pick_table * before[:, :, None, :], -1))
    kept_mask = slot_rank < CAP
    slot_index = jnp.where(kept_mask, routes * CAP + slot_rank, E * CAP)
    copies = jnp.broadcast_to(normed[:, :, None, :], (devices, rows_dev, TOPK, model_width))

    def fill_slots(index_dev, copies_dev):
        empty = jnp.zeros((E * CAP, model_width), jnp.float32)
        return empty.at[index_dev.reshape(-1)].add(copies_dev.reshape(-1, model_width), mode='drop')
    buffers = low_back(jax.vmap(fill_slots)(slot_index, copies))
    buffers = buffers.reshape(devices, E, CAP, model_width).transpose(1, 0, 2, 3).reshape(E, devices * CAP, model_width)

    def expert(operands):
        rows_in, gate_up, down = operands
        gate_up_out = low_back(highest('rd,df->rf', rows_in, gate_up))
        gate_part = gate_up_out[:, :FE]
        up_part = gate_up_out[:, FE:]
        active = low(jax.nn.silu(gate_part) * up_part)
        return low(low_back(highest('rf,fd->rd', active, down)))
    outputs = lax.map(jax.checkpoint(expert), (buffers, w_gate_up, w_down))
    outputs = outputs.reshape(E, devices, CAP, model_width).transpose(1, 0, 2, 3).reshape(devices, E * CAP, model_width)
    safe_index = jnp.minimum(slot_index, E * CAP - 1)

    def take_rows(out_dev, index_dev):
        return out_dev[index_dev]
    picked = jax.vmap(take_rows)(outputs, safe_index)
    weights_kept = gate_probs * kept_mask.astype(jnp.float32)
    return hidden + branch_scale * lax.optimization_barrier(jnp.sum(weights_kept[..., None] * picked, 2))

def forward(tokens, attn_gain, w_query, w_key, w_value, w_out, mlp_gain, w_router, w_gate_up, w_down, segments, routes):

    def one_pack(operands):
        return attend_pack(operands[0], operands[1], attn_gain, w_query, w_key, w_value, w_out)
    hidden = lax.map(jax.checkpoint(one_pack), (tokens, segments))
    packs, length, model_width = hidden.shape
    devices = packs * N_REP
    rows_dev = length // N_REP
    result = mix_experts(hidden.reshape(devices, rows_dev, model_width), mlp_gain, w_router, w_gate_up, w_down, routes.reshape(devices, rows_dev, TOPK))
    return result.reshape(packs, length, model_width)

def reference(tokens, segments, routes, attn_gain, w_query, w_key, w_value, w_out, mlp_gain, w_router, w_gate_up, w_down, cotangent):

    def wrapped(tok_in, gain_one, query_w, key_w, value_w, out_w, gain_two, router_w, gate_up_w, down_w):
        return forward(tok_in, gain_one, query_w, key_w, value_w, out_w, gain_two, router_w, gate_up_w, down_w, segments, routes)
    result, pullback = jax.vjp(wrapped, tokens.astype(jnp.float32), attn_gain.astype(jnp.float32), w_query.astype(jnp.float32), w_key.astype(jnp.float32), w_value.astype(jnp.float32), w_out.astype(jnp.float32), mlp_gain.astype(jnp.float32), w_router.astype(jnp.float32), w_gate_up.astype(jnp.float32), w_down.astype(jnp.float32))
    grads = pullback(cotangent.astype(jnp.float32))
    return (result, grads[0], grads[1], grads[2], grads[3], grads[4], grads[5], grads[6], grads[7], grads[8], grads[9])
```

```python
import functools
import math

import jax
import jax.numpy as jnp
from jax import lax
from jax.experimental import pallas as pl
from jax.experimental.pallas import tpu as pltpu
from jax.sharding import PartitionSpec as P

HEADS = 16
KV_HEADS = 8
HEAD_DIM = 64
CAP = 80
BLOCK = 256

epsilon = 1e-06
score_scale = 0.015625
branch_scale = 0.22
far_below = -1e30

NT = (((1,), (1,)), ((), ()))
TN = (((0,), (0,)), ((), ()))


def product(left, right):
    return jnp.dot(left, right, preferred_element_type=jnp.float32)


def dot_nt(left, right):
    return lax.dot_general(left, right, NT, preferred_element_type=jnp.float32)


def dot_tn(left, right):
    return lax.dot_general(left, right, TN, preferred_element_type=jnp.float32)


def rms_norm(values, gain):
    factor = lax.rsqrt(jnp.mean(values * values, -1, keepdims=True) + epsilon)
    return (values * factor * gain, factor)


def norm_back(grad_normed, values, factor, gain):
    scaled = grad_normed * gain
    gain_part = jnp.sum(grad_normed * values * factor, 0)
    inner_sum = jnp.mean(scaled * values, -1, keepdims=True)
    return (factor * scaled - values * (factor * factor * factor) * inner_sum, gain_part)


def swap_halves(values):
    count, width = values.shape
    half_dim = HEAD_DIM // 2
    lane = lax.broadcasted_iota(jnp.int32, values.shape, 1)
    return jnp.where(
        lane % HEAD_DIM < half_dim,
        jnp.roll(values, -half_dim, 1),
        jnp.roll(values, half_dim, 1),
    )


def attend_forward_kernel(
    low_ref, rows_ref, start_ref, mixed_ref, out_ref, total_ref, key_s, value_s, *, heads
):
    step = pl.program_id(0)
    width = heads * HEAD_DIM

    @pl.when(step == 0)
    def _():
        key_s[...] = rows_ref[:, width : width + HEAD_DIM]
        value_s[...] = rows_ref[:, width + HEAD_DIM : width + 2 * HEAD_DIM]

    block_rows = rows_ref[pl.ds(pl.multiple_of(step * BLOCK, BLOCK), BLOCK), :]
    queries = [
        block_rows[:, h * HEAD_DIM : (h + 1) * HEAD_DIM] * jnp.bfloat16(score_scale)
        for h in range(heads)
    ]
    starts = start_ref[0]
    at = step * BLOCK + lax.broadcasted_iota(jnp.int32, (1, BLOCK), 1)

    def one(j, carry):
        rows = pl.ds(pl.multiple_of(j * BLOCK, BLOCK), BLOCK)
        key_block = key_s[rows, :]
        value_block = value_s[rows, :]
        place = j * BLOCK + lax.broadcasted_iota(jnp.int32, (BLOCK, BLOCK), 0)
        allowed = (place >= starts) & (place <= at)
        result = []
        for h in range(heads):
            peak, total, mixed = carry[h]
            scores = jnp.where(allowed, dot_nt(key_block, queries[h]), far_below)
            new_peak = jnp.maximum(peak, jnp.max(scores, 0, keepdims=True))
            fade = jnp.exp(peak - new_peak)
            raised = jnp.exp(scores - new_peak)
            total = fade * total + jnp.sum(raised, 0, keepdims=True)
            mixed = fade * mixed + dot_tn(value_block, raised.astype(jnp.bfloat16))
            result.append((new_peak, total, mixed))
        return tuple(result)

    first = tuple(
        (
            jnp.full((1, BLOCK), far_below, jnp.float32),
            jnp.zeros((1, BLOCK), jnp.float32),
            jnp.zeros((HEAD_DIM, BLOCK), jnp.float32),
        )
        for _ in range(heads)
    )
    done = lax.fori_loop(low_ref[step], step + 1, one, first)
    for h in range(heads):
        peak, total, mixed = done[h]
        mixed = mixed / total
        out_ref[h * HEAD_DIM : (h + 1) * HEAD_DIM, :] = mixed
        total_ref[0, h : h + 1, :] = peak + jnp.log(total)
        mixed_ref[:, h * HEAD_DIM : (h + 1) * HEAD_DIM] = mixed.T.astype(jnp.bfloat16)


def attend_forward(rows, starts, lows, heads):
    length, width = rows.shape
    blocks = length // BLOCK
    whole = lambda i, low: (0, 0)
    return pl.pallas_call(
        functools.partial(attend_forward_kernel, heads=heads),
        out_shape=(
            jax.ShapeDtypeStruct((length, heads * HEAD_DIM), jnp.bfloat16),
            jax.ShapeDtypeStruct((heads * HEAD_DIM, length), jnp.float32),
            jax.ShapeDtypeStruct((blocks, heads, BLOCK), jnp.float32),
        ),
        grid_spec=pltpu.PrefetchScalarGridSpec(
            num_scalar_prefetch=1,
            grid=(blocks,),
            in_specs=[
                pl.BlockSpec((length, width), whole),
                pl.BlockSpec((1, 1, BLOCK), lambda i, low: (i, 0, 0)),
            ],
            out_specs=[
                pl.BlockSpec((BLOCK, heads * HEAD_DIM), lambda i, low: (i, 0)),
                pl.BlockSpec((heads * HEAD_DIM, BLOCK), lambda i, low: (0, i)),
                pl.BlockSpec((1, heads, BLOCK), lambda i, low: (i, 0, 0)),
            ],
            scratch_shapes=[
                pltpu.VMEM((length, HEAD_DIM), jnp.bfloat16),
                pltpu.VMEM((length, HEAD_DIM), jnp.bfloat16),
            ],
        ),
        name="attend_forward",
    )(lows, rows, starts)


def attend_backward_kernel(
    low_ref,
    rows_ref,
    grad_ref,
    out_ref,
    total_ref,
    start_ref,
    grad_query_ref,
    grad_key_ref,
    grad_value_ref,
    key_s,
    value_s,
    *,
    heads,
):
    step = pl.program_id(0)
    width = heads * HEAD_DIM

    @pl.when(step == 0)
    def _():
        key_s[...] = rows_ref[:, width : width + HEAD_DIM]
        value_s[...] = rows_ref[:, width + HEAD_DIM : width + 2 * HEAD_DIM]
        grad_key_ref[...] = jnp.zeros_like(grad_key_ref)
        grad_value_ref[...] = jnp.zeros_like(grad_value_ref)

    own = pl.ds(pl.multiple_of(step * BLOCK, BLOCK), BLOCK)
    block_rows = rows_ref[own, :]
    grads_all = grad_ref[...]
    starts = start_ref[0]
    at = step * BLOCK + lax.broadcasted_iota(jnp.int32, (1, BLOCK), 1)
    queries, scaled, grads, inners, totals = [], [], [], [], []
    for h in range(heads):
        span = slice(h * HEAD_DIM, (h + 1) * HEAD_DIM)
        queries.append(block_rows[:, span])
        scaled.append(block_rows[:, span] * jnp.bfloat16(score_scale))
        grads.append(grads_all[:, span])
        turned = grads_all[:, span].astype(jnp.float32).T
        inners.append(jnp.sum(turned * out_ref[span, :], 0, keepdims=True))
        totals.append(total_ref[0, h : h + 1, :])

    def one(j, carry):
        rows = pl.ds(pl.multiple_of(j * BLOCK, BLOCK), BLOCK)
        key_block = key_s[rows, :]
        value_block = value_s[rows, :]
        place = j * BLOCK + lax.broadcasted_iota(jnp.int32, (BLOCK, BLOCK), 0)
        allowed = (place >= starts) & (place <= at)
        result = []
        key_sum = grad_key_ref[rows, :]
        value_sum = grad_value_ref[rows, :]
        for h in range(heads):
            scores = jnp.where(allowed, dot_nt(key_block, scaled[h]), far_below)
            prob = jnp.exp(scores - totals[h])
            grad_prob = dot_nt(value_block, grads[h])
            grad_scores = (prob * (grad_prob - inners[h]) * score_scale).astype(jnp.bfloat16)
            value_sum = value_sum + product(prob.astype(jnp.bfloat16), grads[h])
            key_sum = key_sum + product(grad_scores, queries[h])
            result.append(carry[h] + dot_tn(grad_scores, key_block))
        grad_key_ref[rows, :] = key_sum
        grad_value_ref[rows, :] = value_sum
        return tuple(result)

    first = tuple(jnp.zeros((BLOCK, HEAD_DIM), jnp.float32) for _ in range(heads))
    done = lax.fori_loop(low_ref[step], step + 1, one, first)
    for h in range(heads):
        grad_query_ref[:, h * HEAD_DIM : (h + 1) * HEAD_DIM] = done[h]


def attend_backward(rows, grads, outs, totals, starts, lows, heads):
    length, width = rows.shape
    blocks = length // BLOCK
    whole = lambda i, low: (0, 0)
    return pl.pallas_call(
        functools.partial(attend_backward_kernel, heads=heads),
        out_shape=(
            jax.ShapeDtypeStruct((length, heads * HEAD_DIM), jnp.float32),
            jax.ShapeDtypeStruct((length, HEAD_DIM), jnp.float32),
            jax.ShapeDtypeStruct((length, HEAD_DIM), jnp.float32),
        ),
        grid_spec=pltpu.PrefetchScalarGridSpec(
            num_scalar_prefetch=1,
            grid=(blocks,),
            in_specs=[
                pl.BlockSpec((length, width), whole),
                pl.BlockSpec((BLOCK, heads * HEAD_DIM), lambda i, low: (i, 0)),
                pl.BlockSpec((heads * HEAD_DIM, BLOCK), lambda i, low: (0, i)),
                pl.BlockSpec((1, heads, BLOCK), lambda i, low: (i, 0, 0)),
                pl.BlockSpec((1, 1, BLOCK), lambda i, low: (i, 0, 0)),
            ],
            out_specs=[
                pl.BlockSpec((BLOCK, heads * HEAD_DIM), lambda i, low: (i, 0)),
                pl.BlockSpec((length, HEAD_DIM), whole),
                pl.BlockSpec((length, HEAD_DIM), whole),
            ],
            scratch_shapes=[
                pltpu.VMEM((length, HEAD_DIM), jnp.bfloat16),
                pltpu.VMEM((length, HEAD_DIM), jnp.bfloat16),
            ],
        ),
        name="attend_backward",
    )(lows, rows, grads, outs, totals, starts)


def experts_kernel(
    rows_ref,
    cot_ref,
    rank_ref,
    prob_ref,
    gate_up_ref,
    down_ref,
    out_ref,
    grad_ref,
    inner_ref,
    grad_gate_up_ref,
    grad_down_ref,
    picks_s,
    out_s,
    grad_s,
    *,
    sources,
    rows_dev,
    count,
):
    step = pl.program_id(0)
    slots = pl.ds(pl.multiple_of(step * CAP, 16), CAP)
    numbers = lax.broadcasted_iota(jnp.int32, (CAP, rows_dev), 0).astype(jnp.float32)
    rows_in, cots, weights, picks = [], [], [], []
    for s in range(sources):
        rank = rank_ref[s, pl.ds(step, 1), :]
        pick = jnp.where(rank == numbers, 1.0, 0.0)
        weights.append(jnp.sum(pick * prob_ref[s, pl.ds(step, 1), :], 1, keepdims=True))
        pick_b = pick.astype(jnp.bfloat16)
        picks.append(pick)
        picks_s[s, slots, :] = pick_b
        own = slice(s * rows_dev, (s + 1) * rows_dev)
        rows_in.append(product(pick_b, rows_ref[own, :]).astype(jnp.bfloat16))
        cots.append(product(pick_b, cot_ref[own, :]))
    arrived = jnp.concatenate(rows_in, 0)
    weight = jnp.concatenate(weights, 0)
    grad_mix = branch_scale * jnp.concatenate(cots, 0)
    gate_up = gate_up_ref[0]
    down = down_ref[0]
    hidden_units = down.shape[0]
    both = product(arrived, gate_up)
    gate_part = both[:, :hidden_units]
    up_part = both[:, hidden_units:]
    sigmoid_gate = jax.nn.sigmoid(gate_part)
    active = (gate_part * sigmoid_gate * up_part).astype(jnp.bfloat16)
    produced = product(active, down).astype(jnp.bfloat16).astype(jnp.float32)
    inner = jnp.sum(grad_mix * produced, 1, keepdims=True)
    sent_out = (weight * produced).astype(jnp.bfloat16)
    grad_out = (weight * grad_mix).astype(jnp.bfloat16)
    grad_active = dot_nt(grad_out, down)
    grad_down_ref[0] = dot_tn(active, grad_out).astype(grad_down_ref.dtype)
    grad_gate = grad_active * up_part * sigmoid_gate * (1.0 + gate_part * (1.0 - sigmoid_gate))
    grad_up = grad_active * gate_part * sigmoid_gate
    grad_both = jnp.concatenate([grad_gate, grad_up], 1).astype(jnp.bfloat16)
    grad_gate_up_ref[0] = dot_tn(arrived, grad_both).astype(grad_gate_up_ref.dtype)
    grad_in = dot_nt(grad_both, gate_up).astype(jnp.bfloat16)
    for s in range(sources):
        part = slice(s * CAP, (s + 1) * CAP)
        out_s[s, slots, :] = sent_out[part]
        grad_s[s, slots, :] = grad_in[part]
        inner_ref[s, pl.ds(step, 1), :] = jnp.sum(picks[s] * inner[part], 0, keepdims=True)

    @pl.when(step == count - 1)
    def _():
        for s in range(sources):
            own = slice(s * rows_dev, (s + 1) * rows_dev)
            table = picks_s[s]
            out_ref[own, :] = dot_tn(table, out_s[s]).astype(jnp.bfloat16)
            grad_ref[own, :] = dot_tn(table, grad_s[s]).astype(jnp.bfloat16)


def experts(rows, cots, ranks, probs, w_gate_up, w_down):
    sources, count, rows_dev = ranks.shape
    total, model_width = rows.shape
    hidden_units = w_down.shape[1]
    flat = lambda i: (0, 0)
    cube = lambda i: (0, 0, 0)
    once = pl.Buffered(1)
    return pl.pallas_call(
        functools.partial(experts_kernel, sources=sources, rows_dev=rows_dev, count=count),
        out_shape=(
            jax.ShapeDtypeStruct((total, model_width), jnp.bfloat16),
            jax.ShapeDtypeStruct((total, model_width), jnp.bfloat16),
            jax.ShapeDtypeStruct((sources, count, rows_dev), jnp.float32),
            jax.ShapeDtypeStruct(w_gate_up.shape, jnp.bfloat16),
            jax.ShapeDtypeStruct(w_down.shape, jnp.bfloat16),
        ),
        grid=(count,),
        in_specs=[
            pl.BlockSpec((total, model_width), flat, pipeline_mode=once),
            pl.BlockSpec((total, model_width), flat, pipeline_mode=once),
            pl.BlockSpec((sources, count, rows_dev), cube, pipeline_mode=once),
            pl.BlockSpec((sources, count, rows_dev), cube, pipeline_mode=once),
            pl.BlockSpec((1, model_width, 2 * hidden_units), lambda i: (i, 0, 0)),
            pl.BlockSpec((1, hidden_units, model_width), lambda i: (i, 0, 0)),
        ],
        out_specs=[
            pl.BlockSpec((total, model_width), flat),
            pl.BlockSpec((total, model_width), flat),
            pl.BlockSpec((sources, count, rows_dev), cube),
            pl.BlockSpec((1, model_width, 2 * hidden_units), lambda i: (i, 0, 0)),
            pl.BlockSpec((1, hidden_units, model_width), lambda i: (i, 0, 0)),
        ],
        scratch_shapes=[
            pltpu.VMEM((sources, count * CAP, rows_dev), jnp.bfloat16),
            pltpu.VMEM((sources, count * CAP, model_width), jnp.bfloat16),
            pltpu.VMEM((sources, count * CAP, model_width), jnp.bfloat16),
        ],
        compiler_params=pltpu.CompilerParams(vmem_limit_bytes=64 * 1000 * 1000),
        name="experts",
    )(rows, cots, ranks, probs, w_gate_up, w_down)


def on_device(
    tokens,
    segments,
    routes,
    attn_gain,
    w_query,
    w_key,
    w_value,
    w_out,
    mlp_gain,
    w_router,
    w_gate_up,
    w_down,
    cotangent,
    *,
    n_ep,
    n_rep,
):
    inputs = tokens[0]
    own_routes = routes[0]
    grad_output = cotangent[0]
    rows_dev, model_width = inputs.shape
    everyone = ("ep", "rep")
    heads = HEADS // n_rep
    head_width = heads * HEAD_DIM
    shared = max(1, n_rep // KV_HEADS)
    query_width = w_query.shape[1]
    key_width = w_key.shape[1]
    experts_all = w_router.shape[1]
    half_dim = HEAD_DIM // 2

    pack_ids = lax.all_gather(segments[0], "rep", axis=0, tiled=True)
    length = pack_ids.shape[0]
    blocks = length // BLOCK
    offset = lax.axis_index("rep") * rows_dev
    doc_start = jnp.sum((pack_ids[None, :] < pack_ids[:, None]).astype(jnp.int32), 1)
    position = (jnp.arange(length, dtype=jnp.int32) - doc_start).astype(jnp.float32)
    angles = (
        position[:, None]
        * jnp.exp(jnp.arange(half_dim, dtype=jnp.float32) * (-math.log(10000.0) / half_dim))[
            None, :
        ]
    )
    cosine = jnp.cos(angles)
    sine = jnp.sin(angles)
    cosine = jnp.concatenate([cosine, cosine], 1)
    sine = jnp.concatenate([-sine, sine], 1)
    own_cosine = lax.dynamic_slice_in_dim(cosine, offset, rows_dev, 0)
    own_sine = lax.dynamic_slice_in_dim(sine, offset, rows_dev, 0)
    starts = doc_start.reshape(blocks, 1, BLOCK)
    lows = doc_start[::BLOCK] // BLOCK

    joined = jnp.concatenate([w_query, w_key, w_value, w_out, w_router], 1)
    full = lax.all_gather(joined, everyone, axis=0, tiled=True)
    rotated_width = query_width + key_width
    input_width = rotated_width + key_width
    full_in = full[:, :input_width]
    full_out = full[:, input_width : input_width + model_width]
    full_router = full[:, input_width + model_width :]

    normed, factor_one = rms_norm(inputs, attn_gain)
    normed_b = normed.astype(jnp.bfloat16)
    mixed_in = product(normed_b, full_in)
    turn = mixed_in[:, :rotated_width]
    times = rotated_width // HEAD_DIM
    turned = turn * jnp.tile(own_cosine, (1, times)) + swap_halves(turn) * jnp.tile(
        own_sine, (1, times)
    )
    turned_b = turned.astype(jnp.bfloat16)
    value_b = mixed_in[:, rotated_width:].astype(jnp.bfloat16)
    query_part = turned_b[:, :query_width].reshape(rows_dev, n_rep, head_width)
    key_part = turned_b[:, query_width:].reshape(rows_dev, KV_HEADS, HEAD_DIM)
    value_part = value_b.reshape(rows_dev, KV_HEADS, HEAD_DIM)
    if shared > 1:
        key_part = jnp.repeat(key_part, shared, 1)
        value_part = jnp.repeat(value_part, shared, 1)
    sending = jnp.concatenate([query_part, key_part, value_part], 2).transpose(1, 0, 2)
    head_rows = lax.all_to_all(sending, "rep", split_axis=0, concat_axis=0, tiled=True)
    head_rows = head_rows.reshape(length, head_width + 2 * HEAD_DIM)
    mixed, mixed_out, totals = attend_forward(head_rows, starts, lows, heads)
    mixed_rows = lax.all_to_all(
        mixed.reshape(n_rep, rows_dev, head_width), "rep", split_axis=0, concat_axis=0, tiled=True
    )
    mixed_rows = mixed_rows.transpose(1, 0, 2).reshape(rows_dev, query_width)
    hidden = inputs + branch_scale * product(mixed_rows, full_out)

    normed_two, factor_two = rms_norm(hidden, mlp_gain)
    normed_two_b = normed_two.astype(jnp.bfloat16)
    router_f = full_router.astype(jnp.float32)
    logits = product(normed_two_b, full_router)
    numbers = jnp.arange(experts_all, dtype=jnp.int32)
    onehot = jnp.sum((own_routes[:, :, None] == numbers).astype(jnp.float32), 1)
    chosen = onehot > 0.5
    peak = jnp.max(jnp.where(chosen, logits, far_below), 1, keepdims=True)
    raised = jnp.where(chosen, jnp.exp(jnp.minimum(logits - peak, 0.0)), 0.0)
    probs = raised / jnp.sum(raised, 1, keepdims=True)
    before = (
        lax.broadcasted_iota(jnp.int32, (rows_dev, rows_dev), 0)
        > lax.broadcasted_iota(jnp.int32, (rows_dev, rows_dev), 1)
    ).astype(jnp.bfloat16)
    rank = product(before, onehot.astype(jnp.bfloat16))
    kept = chosen & (rank < CAP)
    rank_sent = jnp.where(kept, rank, -1.0).T
    probs_sent = probs.T
    ranks = lax.all_to_all(
        rank_sent.reshape(n_ep, -1, rows_dev), "ep", split_axis=0, concat_axis=0, tiled=True
    )
    prob_all = lax.all_to_all(
        probs_sent.reshape(n_ep, -1, rows_dev), "ep", split_axis=0, concat_axis=0, tiled=True
    )
    expert_rows = lax.all_gather(normed_two_b, "ep", axis=0, tiled=True)
    expert_cots = lax.all_gather(grad_output.astype(jnp.bfloat16), "ep", axis=0, tiled=True)
    out_sum, grad_sum, inner, grad_gate_up, grad_down = experts(
        expert_rows, expert_cots, ranks, prob_all, w_gate_up, w_down
    )
    expert_up = lax.psum_scatter(grad_gate_up, "rep", scatter_dimension=1, tiled=True)
    expert_down = lax.psum_scatter(grad_down, "rep", scatter_dimension=2, tiled=True)
    out_back = lax.all_to_all(
        out_sum.reshape(n_ep, rows_dev, model_width), "ep", split_axis=0, concat_axis=0, tiled=True
    )
    grad_back = lax.all_to_all(
        grad_sum.reshape(n_ep, rows_dev, model_width), "ep", split_axis=0, concat_axis=0, tiled=True
    )
    inner_back = lax.all_to_all(inner, "ep", split_axis=0, concat_axis=0, tiled=True)
    output = hidden + branch_scale * jnp.sum(out_back.astype(jnp.float32), 0)
    grad_probs = inner_back.reshape(experts_all, rows_dev).T
    grad_logits = probs * (grad_probs - jnp.sum(grad_probs * probs, -1, keepdims=True))
    normed_two_f = normed_two_b.astype(jnp.float32)
    grad_router = jnp.dot(normed_two_f.T, grad_logits, precision=lax.Precision.HIGHEST)
    grad_normed_two = jnp.sum(grad_back.astype(jnp.float32), 0) + jnp.dot(
        grad_logits, router_f.T, precision=lax.Precision.HIGHEST
    )
    grad_hidden_norm, grad_mlp_gain = norm_back(grad_normed_two, hidden, factor_two, mlp_gain)
    grad_hidden = grad_output + grad_hidden_norm
    grad_attn = (branch_scale * grad_hidden).astype(jnp.bfloat16)
    grad_out_w = dot_tn(mixed_rows, grad_attn)
    grad_mixed = dot_nt(grad_attn, full_out).astype(jnp.bfloat16)
    grad_heads = lax.all_to_all(
        grad_mixed.reshape(rows_dev, n_rep, head_width).transpose(1, 0, 2),
        "rep",
        split_axis=0,
        concat_axis=0,
        tiled=True,
    ).reshape(length, head_width)
    grad_query, grad_key, grad_value = attend_backward(
        head_rows, grad_heads, mixed_out, totals, starts, lows, heads
    )
    turn_back = jnp.concatenate([grad_query, grad_key], 1)
    turn_back = turn_back * jnp.tile(cosine, (1, heads + 1)) - swap_halves(turn_back) * jnp.tile(
        sine, (1, heads + 1)
    )
    returning = jnp.concatenate([turn_back, grad_value], 1).astype(jnp.bfloat16)
    returned = lax.all_to_all(
        returning.reshape(n_rep, rows_dev, head_width + 2 * HEAD_DIM),
        "rep",
        split_axis=0,
        concat_axis=0,
        tiled=True,
    ).transpose(1, 0, 2)
    grad_query_rows = returned[:, :, :head_width].reshape(rows_dev, query_width)
    key_back = returned[:, :, head_width : head_width + HEAD_DIM]
    value_back = returned[:, :, head_width + HEAD_DIM :]
    if shared > 1:
        key_back = jnp.sum(
            key_back.reshape(rows_dev, KV_HEADS, shared, HEAD_DIM).astype(jnp.float32), 2
        ).astype(jnp.bfloat16)
        value_back = jnp.sum(
            value_back.reshape(rows_dev, KV_HEADS, shared, HEAD_DIM).astype(jnp.float32), 2
        ).astype(jnp.bfloat16)
    grad_in_rows = jnp.concatenate(
        [
            grad_query_rows,
            key_back.reshape(rows_dev, key_width),
            value_back.reshape(rows_dev, key_width),
        ],
        1,
    )
    grad_w_in = dot_tn(normed_b, grad_in_rows)
    grad_normed = dot_nt(grad_in_rows, full_in)
    grad_inputs_norm, grad_attn_gain = norm_back(grad_normed, inputs, factor_one, attn_gain)
    grad_inputs = grad_hidden + grad_inputs_norm
    weight_grads = jnp.concatenate([grad_w_in, grad_out_w, grad_router], 1).astype(jnp.bfloat16)
    summed = lax.psum_scatter(weight_grads, everyone, scatter_dimension=0, tiled=True)
    summed = summed.astype(jnp.float32)
    gains = lax.psum_scatter(
        jnp.stack([grad_attn_gain, grad_mlp_gain], 1), everyone, scatter_dimension=0, tiled=True
    )
    return (
        output[None],
        grad_inputs[None],
        gains[:, 0],
        summed[:, :query_width],
        summed[:, query_width:rotated_width],
        summed[:, rotated_width:input_width],
        summed[:, input_width : input_width + model_width],
        gains[:, 1],
        summed[:, input_width + model_width :],
        expert_up.astype(jnp.float32),
        expert_down.astype(jnp.float32),
    )


def solution(mesh):
    placed = (
        P("ep", "rep", None),
        P("ep", "rep"),
        P("ep", "rep", None),
        P(),
        P(("ep", "rep"), None),
        P(("ep", "rep"), None),
        P(("ep", "rep"), None),
        P(("ep", "rep"), None),
        P(),
        P(("ep", "rep"), None),
        P("ep", None, None),
        P("ep", None, None),
        P("ep", "rep", None),
    )
    return jax.shard_map(
        functools.partial(on_device, n_ep=mesh.shape["ep"], n_rep=mesh.shape["rep"]),
        mesh=mesh,
        in_specs=placed,
        out_specs=(
            P("ep", "rep", None),
            P("ep", "rep", None),
            P(("ep", "rep")),
            P(("ep", "rep"), None),
            P(("ep", "rep"), None),
            P(("ep", "rep"), None),
            P(("ep", "rep"), None),
            P(("ep", "rep")),
            P(("ep", "rep"), None),
            P("ep", "rep", None),
            P("ep", None, "rep"),
        ),
        check_vma=False,
    )
```

```python
import functools
import math

import jax
import jax.numpy as jnp
from jax import lax
from jax.experimental import pallas as pl
from jax.experimental.pallas import tpu as pltpu
from jax.sharding import PartitionSpec as P

HEADS = 16
KV_HEADS = 8
HEAD_DIM = 64
CAP = 80
BLOCK = 256

epsilon = 1e-06
score_scale = 0.015625
branch_scale = 0.22
far_below = -1e30

NT = (((1,), (1,)), ((), ()))
TN = (((0,), (0,)), ((), ()))


def product(left, right):
    return jnp.dot(left, right, preferred_element_type=jnp.float32)


def dot_nt(left, right):
    return lax.dot_general(left, right, NT, preferred_element_type=jnp.float32)


def dot_tn(left, right):
    return lax.dot_general(left, right, TN, preferred_element_type=jnp.float32)


def rms_norm(values, gain):
    factor = lax.rsqrt(jnp.mean(values * values, -1, keepdims=True) + epsilon)
    return (values * factor * gain, factor)


def norm_back(grad_normed, values, factor, gain):
    scaled = grad_normed * gain
    gain_part = jnp.sum(grad_normed * values * factor, 0)
    inner_sum = jnp.mean(scaled * values, -1, keepdims=True)
    return (factor * scaled - values * (factor * factor * factor) * inner_sum, gain_part)


def swap_halves(values):
    count, width = values.shape
    half_dim = HEAD_DIM // 2
    lane = lax.broadcasted_iota(jnp.int32, values.shape, 1)
    return jnp.where(
        lane % HEAD_DIM < half_dim,
        jnp.roll(values, -half_dim, 1),
        jnp.roll(values, half_dim, 1),
    )


def attend_forward_kernel(
    low_ref, rows_ref, start_ref, mixed_ref, out_ref, total_ref, key_s, value_s, *, heads
):
    step = pl.program_id(0)
    width = heads * HEAD_DIM

    @pl.when(step == 0)
    def _():
        key_s[...] = rows_ref[:, width : width + HEAD_DIM]
        value_s[...] = rows_ref[:, width + HEAD_DIM : width + 2 * HEAD_DIM]

    block_rows = rows_ref[pl.ds(pl.multiple_of(step * BLOCK, BLOCK), BLOCK), :]
    queries = [
        block_rows[:, h * HEAD_DIM : (h + 1) * HEAD_DIM] * jnp.bfloat16(score_scale)
        for h in range(heads)
    ]
    starts = start_ref[0]
    at = step * BLOCK + lax.broadcasted_iota(jnp.int32, (1, BLOCK), 1)

    def one(j, carry):
        rows = pl.ds(pl.multiple_of(j * BLOCK, BLOCK), BLOCK)
        key_block = key_s[rows, :]
        value_block = value_s[rows, :]
        place = j * BLOCK + lax.broadcasted_iota(jnp.int32, (BLOCK, BLOCK), 0)
        allowed = (place >= starts) & (place <= at)
        result = []
        for h in range(heads):
            peak, total, mixed = carry[h]
            scores = jnp.where(allowed, dot_nt(key_block, queries[h]), far_below)
            new_peak = jnp.maximum(peak, jnp.max(scores, 0, keepdims=True))
            fade = jnp.exp(peak - new_peak)
            raised = jnp.exp(scores - new_peak)
            total = fade * total + jnp.sum(raised, 0, keepdims=True)
            mixed = fade * mixed + dot_tn(value_block, raised.astype(jnp.bfloat16))
            result.append((new_peak, total, mixed))
        return tuple(result)

    first = tuple(
        (
            jnp.full((1, BLOCK), far_below, jnp.float32),
            jnp.zeros((1, BLOCK), jnp.float32),
            jnp.zeros((HEAD_DIM, BLOCK), jnp.float32),
        )
        for _ in range(heads)
    )
    done = lax.fori_loop(low_ref[step], step + 1, one, first)
    for h in range(heads):
        peak, total, mixed = done[h]
        mixed = mixed / total
        out_ref[h * HEAD_DIM : (h + 1) * HEAD_DIM, :] = mixed
        total_ref[0, h : h + 1, :] = peak + jnp.log(total)
        mixed_ref[:, h * HEAD_DIM : (h + 1) * HEAD_DIM] = mixed.T.astype(jnp.bfloat16)


def attend_forward(rows, starts, lows, heads):
    length, width = rows.shape
    blocks = length // BLOCK
    whole = lambda i, low: (0, 0)
    return pl.pallas_call(
        functools.partial(attend_forward_kernel, heads=heads),
        out_shape=(
            jax.ShapeDtypeStruct((length, heads * HEAD_DIM), jnp.bfloat16),
            jax.ShapeDtypeStruct((heads * HEAD_DIM, length), jnp.float32),
            jax.ShapeDtypeStruct((blocks, heads, BLOCK), jnp.float32),
        ),
        grid_spec=pltpu.PrefetchScalarGridSpec(
            num_scalar_prefetch=1,
            grid=(blocks,),
            in_specs=[
                pl.BlockSpec((length, width), whole),
                pl.BlockSpec((1, 1, BLOCK), lambda i, low: (i, 0, 0)),
            ],
            out_specs=[
                pl.BlockSpec((BLOCK, heads * HEAD_DIM), lambda i, low: (i, 0)),
                pl.BlockSpec((heads * HEAD_DIM, BLOCK), lambda i, low: (0, i)),
                pl.BlockSpec((1, heads, BLOCK), lambda i, low: (i, 0, 0)),
            ],
            scratch_shapes=[
                pltpu.VMEM((length, HEAD_DIM), jnp.bfloat16),
                pltpu.VMEM((length, HEAD_DIM), jnp.bfloat16),
            ],
        ),
        name="attend_forward",
    )(lows, rows, starts)


def attend_backward_kernel(
    low_ref,
    rows_ref,
    grad_ref,
    out_ref,
    total_ref,
    start_ref,
    grad_query_ref,
    grad_key_ref,
    grad_value_ref,
    key_s,
    value_s,
    *,
    heads,
):
    step = pl.program_id(0)
    width = heads * HEAD_DIM

    @pl.when(step == 0)
    def _():
        key_s[...] = rows_ref[:, width : width + HEAD_DIM]
        value_s[...] = rows_ref[:, width + HEAD_DIM : width + 2 * HEAD_DIM]
        grad_key_ref[...] = jnp.zeros_like(grad_key_ref)
        grad_value_ref[...] = jnp.zeros_like(grad_value_ref)

    own = pl.ds(pl.multiple_of(step * BLOCK, BLOCK), BLOCK)
    block_rows = rows_ref[own, :]
    grads_all = grad_ref[...]
    starts = start_ref[0]
    at = step * BLOCK + lax.broadcasted_iota(jnp.int32, (1, BLOCK), 1)
    queries, scaled, grads, inners, totals = [], [], [], [], []
    for h in range(heads):
        span = slice(h * HEAD_DIM, (h + 1) * HEAD_DIM)
        queries.append(block_rows[:, span])
        scaled.append(block_rows[:, span] * jnp.bfloat16(score_scale))
        grads.append(grads_all[:, span])
        turned = grads_all[:, span].astype(jnp.float32).T
        inners.append(jnp.sum(turned * out_ref[span, :], 0, keepdims=True))
        totals.append(total_ref[0, h : h + 1, :])

    def one(j, carry):
        rows = pl.ds(pl.multiple_of(j * BLOCK, BLOCK), BLOCK)
        key_block = key_s[rows, :]
        value_block = value_s[rows, :]
        place = j * BLOCK + lax.broadcasted_iota(jnp.int32, (BLOCK, BLOCK), 0)
        allowed = (place >= starts) & (place <= at)
        result = []
        key_sum = grad_key_ref[rows, :]
        value_sum = grad_value_ref[rows, :]
        for h in range(heads):
            scores = jnp.where(allowed, dot_nt(key_block, scaled[h]), far_below)
            prob = jnp.exp(scores - totals[h])
            grad_prob = dot_nt(value_block, grads[h])
            grad_scores = (prob * (grad_prob - inners[h]) * score_scale).astype(jnp.bfloat16)
            value_sum = value_sum + product(prob.astype(jnp.bfloat16), grads[h])
            key_sum = key_sum + product(grad_scores, queries[h])
            result.append(carry[h] + dot_tn(grad_scores, key_block))
        grad_key_ref[rows, :] = key_sum
        grad_value_ref[rows, :] = value_sum
        return tuple(result)

    first = tuple(jnp.zeros((BLOCK, HEAD_DIM), jnp.float32) for _ in range(heads))
    done = lax.fori_loop(low_ref[step], step + 1, one, first)
    for h in range(heads):
        grad_query_ref[:, h * HEAD_DIM : (h + 1) * HEAD_DIM] = done[h]


def attend_backward(rows, grads, outs, totals, starts, lows, heads):
    length, width = rows.shape
    blocks = length // BLOCK
    whole = lambda i, low: (0, 0)
    return pl.pallas_call(
        functools.partial(attend_backward_kernel, heads=heads),
        out_shape=(
            jax.ShapeDtypeStruct((length, heads * HEAD_DIM), jnp.float32),
            jax.ShapeDtypeStruct((length, HEAD_DIM), jnp.float32),
            jax.ShapeDtypeStruct((length, HEAD_DIM), jnp.float32),
        ),
        grid_spec=pltpu.PrefetchScalarGridSpec(
            num_scalar_prefetch=1,
            grid=(blocks,),
            in_specs=[
                pl.BlockSpec((length, width), whole),
                pl.BlockSpec((BLOCK, heads * HEAD_DIM), lambda i, low: (i, 0)),
                pl.BlockSpec((heads * HEAD_DIM, BLOCK), lambda i, low: (0, i)),
                pl.BlockSpec((1, heads, BLOCK), lambda i, low: (i, 0, 0)),
                pl.BlockSpec((1, 1, BLOCK), lambda i, low: (i, 0, 0)),
            ],
            out_specs=[
                pl.BlockSpec((BLOCK, heads * HEAD_DIM), lambda i, low: (i, 0)),
                pl.BlockSpec((length, HEAD_DIM), whole),
                pl.BlockSpec((length, HEAD_DIM), whole),
            ],
            scratch_shapes=[
                pltpu.VMEM((length, HEAD_DIM), jnp.bfloat16),
                pltpu.VMEM((length, HEAD_DIM), jnp.bfloat16),
            ],
        ),
        name="attend_backward",
    )(lows, rows, grads, outs, totals, starts)


def experts_kernel(
    rows_ref,
    cot_ref,
    rank_ref,
    prob_ref,
    gate_up_ref,
    down_ref,
    out_ref,
    grad_ref,
    inner_ref,
    grad_w_ref,
    picks_s,
    out_s,
    grad_s,
    *,
    sources,
    rows_dev,
    count,
    copies,
):
    step = pl.program_id(0)
    slots = pl.ds(pl.multiple_of(step * CAP, 16), CAP)
    numbers = lax.broadcasted_iota(jnp.int32, (CAP, rows_dev), 0).astype(jnp.float32)
    rows_in, cots, weights, picks = [], [], [], []
    for s in range(sources):
        rank = rank_ref[s, pl.ds(step, 1), :]
        pick = jnp.where(rank == numbers, 1.0, 0.0)
        weights.append(jnp.sum(pick * prob_ref[s, pl.ds(step, 1), :], 1, keepdims=True))
        pick_b = pick.astype(jnp.bfloat16)
        picks.append(pick)
        picks_s[s, slots, :] = pick_b
        own = slice(s * rows_dev, (s + 1) * rows_dev)
        rows_in.append(product(pick_b, rows_ref[own, :]).astype(jnp.bfloat16))
        cots.append(product(pick_b, cot_ref[own, :]))
    arrived = jnp.concatenate(rows_in, 0)
    weight = jnp.concatenate(weights, 0)
    grad_mix = branch_scale * jnp.concatenate(cots, 0)
    gate_up = gate_up_ref[0]
    down = down_ref[0]
    hidden_units = down.shape[0]
    both = product(arrived, gate_up)
    gate_part = both[:, :hidden_units]
    up_part = both[:, hidden_units:]
    sigmoid_gate = jax.nn.sigmoid(gate_part)
    active = (gate_part * sigmoid_gate * up_part).astype(jnp.bfloat16)
    produced = product(active, down).astype(jnp.bfloat16).astype(jnp.float32)
    inner = jnp.sum(grad_mix * produced, 1, keepdims=True)
    sent_out = (weight * produced).astype(jnp.bfloat16)
    grad_out = (weight * grad_mix).astype(jnp.bfloat16)
    grad_active = dot_nt(grad_out, down)
    grad_down = dot_tn(active, grad_out).astype(grad_w_ref.dtype)
    share = grad_down.shape[1] // copies
    tall = hidden_units // copies
    for r in range(copies):
        for k in range(copies):
            grad_w_ref[0, r, 0, share : share + tall, k * share : (k + 1) * share] = grad_down[
                k * tall : (k + 1) * tall, r * share : (r + 1) * share
            ]
    grad_gate = grad_active * up_part * sigmoid_gate * (1.0 + gate_part * (1.0 - sigmoid_gate))
    grad_up = grad_active * gate_part * sigmoid_gate
    grad_both = jnp.concatenate([grad_gate, grad_up], 1).astype(jnp.bfloat16)
    grad_gate_up = dot_tn(arrived, grad_both).astype(grad_w_ref.dtype)
    for r in range(copies):
        grad_w_ref[0, r, 0, :share, :] = grad_gate_up[r * share : (r + 1) * share]
    grad_in = dot_nt(grad_both, gate_up).astype(jnp.bfloat16)
    for s in range(sources):
        part = slice(s * CAP, (s + 1) * CAP)
        out_s[s, slots, :] = sent_out[part]
        grad_s[s, slots, :] = grad_in[part]
        inner_ref[s, pl.ds(step, 1), :] = jnp.sum(picks[s] * inner[part], 0, keepdims=True)

    @pl.when(step == count - 1)
    def _():
        for s in range(sources):
            own = slice(s * rows_dev, (s + 1) * rows_dev)
            table = picks_s[s]
            out_ref[own, :] = dot_tn(table, out_s[s]).astype(jnp.bfloat16)
            grad_ref[own, :] = dot_tn(table, grad_s[s]).astype(jnp.bfloat16)


def experts(rows, cots, ranks, probs, w_gate_up, w_down, copies, chunks):
    sources, count, rows_dev = ranks.shape
    total, model_width = rows.shape
    hidden_units = w_down.shape[1]
    per = count // chunks
    tall = model_width // copies + hidden_units // copies
    flat = lambda i: (0, 0)
    cube = lambda i: (0, 0, 0)
    once = pl.Buffered(1)
    return pl.pallas_call(
        functools.partial(
            experts_kernel, sources=sources, rows_dev=rows_dev, count=count, copies=copies
        ),
        out_shape=(
            jax.ShapeDtypeStruct((total, model_width), jnp.bfloat16),
            jax.ShapeDtypeStruct((total, model_width), jnp.bfloat16),
            jax.ShapeDtypeStruct((sources, count, rows_dev), jnp.float32),
            jax.ShapeDtypeStruct((chunks, copies, per, tall, model_width), jnp.bfloat16),
        ),
        grid=(count,),
        in_specs=[
            pl.BlockSpec((total, model_width), flat, pipeline_mode=once),
            pl.BlockSpec((total, model_width), flat, pipeline_mode=once),
            pl.BlockSpec((sources, count, rows_dev), cube, pipeline_mode=once),
            pl.BlockSpec((sources, count, rows_dev), cube, pipeline_mode=once),
            pl.BlockSpec((1, model_width, 2 * hidden_units), lambda i: (i, 0, 0)),
            pl.BlockSpec((1, hidden_units, model_width), lambda i: (i, 0, 0)),
        ],
        out_specs=[
            pl.BlockSpec((total, model_width), flat),
            pl.BlockSpec((total, model_width), flat),
            pl.BlockSpec((sources, count, rows_dev), cube),
            pl.BlockSpec(
                (1, copies, 1, tall, model_width), lambda i: (i // per, 0, i % per, 0, 0)
            ),
        ],
        scratch_shapes=[
            pltpu.VMEM((sources, count * CAP, rows_dev), jnp.bfloat16),
            pltpu.VMEM((sources, count * CAP, model_width), jnp.bfloat16),
            pltpu.VMEM((sources, count * CAP, model_width), jnp.bfloat16),
        ],
        compiler_params=pltpu.CompilerParams(vmem_limit_bytes=64 * 1000 * 1000),
        name="experts",
    )(rows, cots, ranks, probs, w_gate_up, w_down)


def bits_of(size):
    return max(size.bit_length() - 1, 0)


def halving(block, labels, order, last=jnp.bfloat16):
    labels = list(labels)
    for number, (axis, bit) in enumerate(order):
        dim = labels.index((axis, bit))
        mine = (lax.axis_index(axis) >> bit) & 1
        sent = lax.dynamic_index_in_dim(block, 1 - mine, dim, keepdims=False)
        kept = lax.dynamic_index_in_dim(block, mine, dim, keepdims=False)
        size = lax.axis_size(axis)
        came = lax.ppermute(sent, axis, [(i, i ^ (1 << bit)) for i in range(size)])
        total = kept.astype(jnp.float32) + came.astype(jnp.float32)
        block = total.astype(last if number == len(order) - 1 else jnp.bfloat16)
        labels.pop(dim)
    return block


def on_device(
    tokens,
    segments,
    routes,
    attn_gain,
    w_query,
    w_key,
    w_value,
    w_out,
    mlp_gain,
    w_router,
    w_gate_up,
    w_down,
    cotangent,
    *,
    n_ep,
    n_rep,
):
    inputs = tokens[0]
    own_routes = routes[0]
    grad_output = cotangent[0]
    rows_dev, model_width = inputs.shape
    everyone = ("ep", "rep")
    heads = HEADS // n_rep
    head_width = heads * HEAD_DIM
    shared = max(1, n_rep // KV_HEADS)
    query_width = w_query.shape[1]
    key_width = w_key.shape[1]
    experts_all = w_router.shape[1]
    half_dim = HEAD_DIM // 2

    pack_ids = lax.all_gather(segments[0], "rep", axis=0, tiled=True)
    length = pack_ids.shape[0]
    blocks = length // BLOCK
    offset = lax.axis_index("rep") * rows_dev
    doc_start = jnp.sum((pack_ids[None, :] < pack_ids[:, None]).astype(jnp.int32), 1)
    position = (jnp.arange(length, dtype=jnp.int32) - doc_start).astype(jnp.float32)
    angles = (
        position[:, None]
        * jnp.exp(jnp.arange(half_dim, dtype=jnp.float32) * (-math.log(10000.0) / half_dim))[
            None, :
        ]
    )
    cosine = jnp.cos(angles)
    sine = jnp.sin(angles)
    cosine = jnp.concatenate([cosine, cosine], 1)
    sine = jnp.concatenate([-sine, sine], 1)
    own_cosine = lax.dynamic_slice_in_dim(cosine, offset, rows_dev, 0)
    own_sine = lax.dynamic_slice_in_dim(sine, offset, rows_dev, 0)
    starts = doc_start.reshape(blocks, 1, BLOCK)
    lows = doc_start[::BLOCK] // BLOCK

    joined = jnp.concatenate([w_query, w_key, w_value, w_out, w_router], 1)
    full = lax.all_gather(joined, everyone, axis=0, tiled=True)
    rotated_width = query_width + key_width
    input_width = rotated_width + key_width
    full_in = full[:, :input_width]
    full_out = full[:, input_width : input_width + model_width]
    full_router = full[:, input_width + model_width :]

    normed, factor_one = rms_norm(inputs, attn_gain)
    normed_b = normed.astype(jnp.bfloat16)
    mixed_in = product(normed_b, full_in)
    turn = mixed_in[:, :rotated_width]
    times = rotated_width // HEAD_DIM
    turned = turn * jnp.tile(own_cosine, (1, times)) + swap_halves(turn) * jnp.tile(
        own_sine, (1, times)
    )
    turned_b = turned.astype(jnp.bfloat16)
    value_b = mixed_in[:, rotated_width:].astype(jnp.bfloat16)
    query_part = turned_b[:, :query_width].reshape(rows_dev, n_rep, head_width)
    key_part = turned_b[:, query_width:].reshape(rows_dev, KV_HEADS, HEAD_DIM)
    value_part = value_b.reshape(rows_dev, KV_HEADS, HEAD_DIM)
    if shared > 1:
        key_part = jnp.repeat(key_part, shared, 1)
        value_part = jnp.repeat(value_part, shared, 1)
    sending = jnp.concatenate([query_part, key_part, value_part], 2).transpose(1, 0, 2)
    head_rows = lax.all_to_all(sending, "rep", split_axis=0, concat_axis=0, tiled=True)
    head_rows = head_rows.reshape(length, head_width + 2 * HEAD_DIM)
    mixed, mixed_out, totals = attend_forward(head_rows, starts, lows, heads)
    mixed_rows = lax.all_to_all(
        mixed.reshape(n_rep, rows_dev, head_width), "rep", split_axis=0, concat_axis=0, tiled=True
    )
    mixed_rows = mixed_rows.transpose(1, 0, 2).reshape(rows_dev, query_width)
    hidden = inputs + branch_scale * product(mixed_rows, full_out)

    normed_two, factor_two = rms_norm(hidden, mlp_gain)
    normed_two_b = normed_two.astype(jnp.bfloat16)
    router_f = full_router.astype(jnp.float32)
    logits = product(normed_two_b, full_router)
    numbers = jnp.arange(experts_all, dtype=jnp.int32)
    onehot = jnp.sum((own_routes[:, :, None] == numbers).astype(jnp.float32), 1)
    chosen = onehot > 0.5
    peak = jnp.max(jnp.where(chosen, logits, far_below), 1, keepdims=True)
    raised = jnp.where(chosen, jnp.exp(jnp.minimum(logits - peak, 0.0)), 0.0)
    probs = raised / jnp.sum(raised, 1, keepdims=True)
    before = (
        lax.broadcasted_iota(jnp.int32, (rows_dev, rows_dev), 0)
        > lax.broadcasted_iota(jnp.int32, (rows_dev, rows_dev), 1)
    ).astype(jnp.bfloat16)
    rank = product(before, onehot.astype(jnp.bfloat16))
    kept = chosen & (rank < CAP)
    rank_sent = jnp.where(kept, rank, -1.0).T
    probs_sent = probs.T
    both_sent = jnp.concatenate(
        [rank_sent.reshape(n_ep, -1, rows_dev), probs_sent.reshape(n_ep, -1, rows_dev)], 1
    )
    both_all = lax.all_to_all(both_sent, "ep", split_axis=0, concat_axis=0, tiled=True)
    ranks = both_all[:, : experts_all // n_ep]
    prob_all = both_all[:, experts_all // n_ep :]
    expert_rows = lax.all_gather(normed_two_b, "ep", axis=0, tiled=True)
    expert_cots = lax.all_gather(grad_output.astype(jnp.bfloat16), "ep", axis=0, tiled=True)
    chunks = 4
    out_sum, grad_sum, inner, grad_experts = experts(
        expert_rows, expert_cots, ranks, prob_all, w_gate_up, w_down, n_rep, chunks
    )
    rep_bits = [("rep", b) for b in reversed(range(bits_of(n_rep)))]
    ep_bits = [("ep", b) for b in reversed(range(bits_of(n_ep)))]
    near_first = rep_bits[::-1]
    far_first = near_first[-2:-1] + near_first[:-2] + near_first[-1:]
    share = model_width // n_rep
    tall = w_down.shape[1] // n_rep
    pieces = []
    for c in range(chunks):
        block = grad_experts[c].reshape(
            (2,) * len(rep_bits) + grad_experts.shape[2:]
        )
        order = far_first if c == chunks - 1 else near_first
        pieces.append(halving(block, rep_bits, order, jnp.float32))
    grad_experts = jnp.concatenate(pieces, 0)
    expert_up = grad_experts[:, :share, :]
    expert_down = (
        grad_experts[:, share:, :]
        .reshape(-1, tall, n_rep, share)
        .transpose(0, 2, 1, 3)
        .reshape(-1, tall * n_rep, share)
    )
    out_back = lax.all_to_all(
        out_sum.reshape(n_ep, rows_dev, model_width), "ep", split_axis=0, concat_axis=0, tiled=True
    )
    grad_back = lax.all_to_all(
        grad_sum.reshape(n_ep, rows_dev, model_width), "ep", split_axis=0, concat_axis=0, tiled=True
    )
    inner_back = lax.all_to_all(inner, "ep", split_axis=0, concat_axis=0, tiled=True)
    output = hidden + branch_scale * jnp.sum(out_back.astype(jnp.float32), 0)
    grad_probs = inner_back.reshape(experts_all, rows_dev).T
    grad_logits = probs * (grad_probs - jnp.sum(grad_probs * probs, -1, keepdims=True))
    normed_two_f = normed_two_b.astype(jnp.float32)
    grad_router = jnp.dot(normed_two_f.T, grad_logits, precision=lax.Precision.HIGHEST)
    grad_normed_two = jnp.sum(grad_back.astype(jnp.float32), 0) + jnp.dot(
        grad_logits, router_f.T, precision=lax.Precision.HIGHEST
    )
    grad_hidden_norm, grad_mlp_gain = norm_back(grad_normed_two, hidden, factor_two, mlp_gain)
    grad_hidden = grad_output + grad_hidden_norm
    grad_attn = (branch_scale * grad_hidden).astype(jnp.bfloat16)
    grad_out_w = dot_tn(mixed_rows, grad_attn)
    grad_mixed = dot_nt(grad_attn, full_out).astype(jnp.bfloat16)
    grad_heads = lax.all_to_all(
        grad_mixed.reshape(rows_dev, n_rep, head_width).transpose(1, 0, 2),
        "rep",
        split_axis=0,
        concat_axis=0,
        tiled=True,
    ).reshape(length, head_width)
    grad_query, grad_key, grad_value = attend_backward(
        head_rows, grad_heads, mixed_out, totals, starts, lows, heads
    )
    turn_back = jnp.concatenate([grad_query, grad_key], 1)
    turn_back = turn_back * jnp.tile(cosine, (1, heads + 1)) - swap_halves(turn_back) * jnp.tile(
        sine, (1, heads + 1)
    )
    returning = jnp.concatenate([turn_back, grad_value], 1).astype(jnp.bfloat16)
    returned = lax.all_to_all(
        returning.reshape(n_rep, rows_dev, head_width + 2 * HEAD_DIM),
        "rep",
        split_axis=0,
        concat_axis=0,
        tiled=True,
    ).transpose(1, 0, 2)
    grad_query_rows = returned[:, :, :head_width].reshape(rows_dev, query_width)
    key_back = returned[:, :, head_width : head_width + HEAD_DIM]
    value_back = returned[:, :, head_width + HEAD_DIM :]
    if shared > 1:
        key_back = jnp.sum(
            key_back.reshape(rows_dev, KV_HEADS, shared, HEAD_DIM).astype(jnp.float32), 2
        ).astype(jnp.bfloat16)
        value_back = jnp.sum(
            value_back.reshape(rows_dev, KV_HEADS, shared, HEAD_DIM).astype(jnp.float32), 2
        ).astype(jnp.bfloat16)
    grad_in_rows = jnp.concatenate(
        [
            grad_query_rows,
            key_back.reshape(rows_dev, key_width),
            value_back.reshape(rows_dev, key_width),
        ],
        1,
    )
    grad_w_query = dot_tn(normed_b, grad_in_rows[:, :query_width])
    grad_w_rest = dot_tn(normed_b, grad_in_rows[:, query_width:])
    grad_normed = dot_nt(grad_in_rows, full_in)
    grad_inputs_norm, grad_attn_gain = norm_back(grad_normed, inputs, factor_one, attn_gain)
    grad_inputs = grad_hidden + grad_inputs_norm
    shape = (2,) * (len(ep_bits) + len(rep_bits)) + (-1,)
    near = ep_bits[::-1] + near_first
    other = ep_bits[::-1][:1] + near_first + ep_bits[::-1][1:]
    first = jnp.concatenate([grad_out_w, grad_router], 1).astype(jnp.bfloat16)
    first = halving(
        first.reshape(shape + first.shape[1:]), ep_bits + rep_bits, near, jnp.float32
    )
    query_grad = grad_w_query.astype(jnp.bfloat16)
    query_grad = halving(
        query_grad.reshape(shape + query_grad.shape[1:]), ep_bits + rep_bits, near, jnp.float32
    )
    rest_grad = grad_w_rest.astype(jnp.bfloat16)
    rest_grad = halving(
        rest_grad.reshape(shape + rest_grad.shape[1:]), ep_bits + rep_bits, other, jnp.float32
    )
    everything = n_ep * n_rep
    gains = jnp.concatenate(
        [grad_attn_gain.reshape(everything, -1), grad_mlp_gain.reshape(everything, -1)], 1
    )
    gains = jnp.sum(
        lax.all_to_all(gains, everyone, split_axis=0, concat_axis=0, tiled=True), 0
    )
    part = model_width // everything
    return (
        output[None],
        grad_inputs[None],
        gains[:part],
        query_grad,
        rest_grad[:, :key_width],
        rest_grad[:, key_width:],
        first[:, :model_width],
        gains[part:],
        first[:, model_width:],
        expert_up,
        expert_down,
    )


def solution(mesh):
    placed = (
        P("ep", "rep", None),
        P("ep", "rep"),
        P("ep", "rep", None),
        P(),
        P(("ep", "rep"), None),
        P(("ep", "rep"), None),
        P(("ep", "rep"), None),
        P(("ep", "rep"), None),
        P(),
        P(("ep", "rep"), None),
        P("ep", None, None),
        P("ep", None, None),
        P("ep", "rep", None),
    )
    return jax.shard_map(
        functools.partial(on_device, n_ep=mesh.shape["ep"], n_rep=mesh.shape["rep"]),
        mesh=mesh,
        in_specs=placed,
        out_specs=(
            P("ep", "rep", None),
            P("ep", "rep", None),
            P(("ep", "rep")),
            P(("ep", "rep"), None),
            P(("ep", "rep"), None),
            P(("ep", "rep"), None),
            P(("ep", "rep"), None),
            P(("ep", "rep")),
            P(("ep", "rep"), None),
            P("ep", "rep", None),
            P("ep", None, "rep"),
        ),
        check_vma=False,
    )
```

```python
import functools
import math

import jax
import jax.numpy as jnp
from jax import lax
from jax.experimental import pallas as pl
from jax.experimental.pallas import tpu as pltpu
from jax.sharding import PartitionSpec as P

HEADS = 16
KV_HEADS = 8
HEAD_DIM = 64
CAP = 80
BLOCK = 256

epsilon = 1e-06
score_scale = 0.015625
branch_scale = 0.22
far_below = -1e30

NT = (((1,), (1,)), ((), ()))
TN = (((0,), (0,)), ((), ()))


def product(left, right):
    return jnp.dot(left, right, preferred_element_type=jnp.float32)


def dot_nt(left, right):
    return lax.dot_general(left, right, NT, preferred_element_type=jnp.float32)


def dot_tn(left, right):
    return lax.dot_general(left, right, TN, preferred_element_type=jnp.float32)


def rms_norm(values, gain):
    factor = lax.rsqrt(jnp.mean(values * values, -1, keepdims=True) + epsilon)
    return (values * factor * gain, factor)


def norm_back(grad_normed, values, factor, gain):
    scaled = grad_normed * gain
    gain_part = jnp.sum(grad_normed * values * factor, 0)
    inner_sum = jnp.mean(scaled * values, -1, keepdims=True)
    return (factor * scaled - values * (factor * factor * factor) * inner_sum, gain_part)


def swap_halves(values):
    count, width = values.shape
    half_dim = HEAD_DIM // 2
    lane = lax.broadcasted_iota(jnp.int32, values.shape, 1)
    return jnp.where(
        lane % HEAD_DIM < half_dim,
        jnp.roll(values, -half_dim, 1),
        jnp.roll(values, half_dim, 1),
    )


def attend_forward_kernel(
    low_ref, rows_ref, start_ref, mixed_ref, out_ref, total_ref, key_s, value_s, *, heads
):
    step = pl.program_id(0)
    width = heads * HEAD_DIM

    @pl.when(step == 0)
    def _():
        key_s[...] = rows_ref[:, width : width + HEAD_DIM]
        value_s[...] = rows_ref[:, width + HEAD_DIM : width + 2 * HEAD_DIM]

    block_rows = rows_ref[pl.ds(pl.multiple_of(step * BLOCK, BLOCK), BLOCK), :]
    queries = [
        block_rows[:, h * HEAD_DIM : (h + 1) * HEAD_DIM] * jnp.bfloat16(score_scale)
        for h in range(heads)
    ]
    starts = start_ref[0]
    at = step * BLOCK + lax.broadcasted_iota(jnp.int32, (1, BLOCK), 1)

    def one(j, carry):
        rows = pl.ds(pl.multiple_of(j * BLOCK, BLOCK), BLOCK)
        key_block = key_s[rows, :]
        value_block = value_s[rows, :]
        place = j * BLOCK + lax.broadcasted_iota(jnp.int32, (BLOCK, BLOCK), 0)
        allowed = (place >= starts) & (place <= at)
        result = []
        for h in range(heads):
            peak, total, mixed = carry[h]
            scores = jnp.where(allowed, dot_nt(key_block, queries[h]), far_below)
            new_peak = jnp.maximum(peak, jnp.max(scores, 0, keepdims=True))
            fade = jnp.exp(peak - new_peak)
            raised = jnp.exp(scores - new_peak)
            total = fade * total + jnp.sum(raised, 0, keepdims=True)
            mixed = fade * mixed + dot_tn(value_block, raised.astype(jnp.bfloat16))
            result.append((new_peak, total, mixed))
        return tuple(result)

    first = tuple(
        (
            jnp.full((1, BLOCK), far_below, jnp.float32),
            jnp.zeros((1, BLOCK), jnp.float32),
            jnp.zeros((HEAD_DIM, BLOCK), jnp.float32),
        )
        for _ in range(heads)
    )
    done = lax.fori_loop(low_ref[step], step + 1, one, first)
    for h in range(heads):
        peak, total, mixed = done[h]
        mixed = mixed / total
        out_ref[h * HEAD_DIM : (h + 1) * HEAD_DIM, :] = mixed
        total_ref[0, h : h + 1, :] = peak + jnp.log(total)
        mixed_ref[:, h * HEAD_DIM : (h + 1) * HEAD_DIM] = mixed.T.astype(jnp.bfloat16)


def attend_forward(rows, starts, lows, heads):
    length, width = rows.shape
    blocks = length // BLOCK
    whole = lambda i, low: (0, 0)
    return pl.pallas_call(
        functools.partial(attend_forward_kernel, heads=heads),
        out_shape=(
            jax.ShapeDtypeStruct((length, heads * HEAD_DIM), jnp.bfloat16),
            jax.ShapeDtypeStruct((heads * HEAD_DIM, length), jnp.float32),
            jax.ShapeDtypeStruct((blocks, heads, BLOCK), jnp.float32),
        ),
        grid_spec=pltpu.PrefetchScalarGridSpec(
            num_scalar_prefetch=1,
            grid=(blocks,),
            in_specs=[
                pl.BlockSpec((length, width), whole),
                pl.BlockSpec((1, 1, BLOCK), lambda i, low: (i, 0, 0)),
            ],
            out_specs=[
                pl.BlockSpec((BLOCK, heads * HEAD_DIM), lambda i, low: (i, 0)),
                pl.BlockSpec((heads * HEAD_DIM, BLOCK), lambda i, low: (0, i)),
                pl.BlockSpec((1, heads, BLOCK), lambda i, low: (i, 0, 0)),
            ],
            scratch_shapes=[
                pltpu.VMEM((length, HEAD_DIM), jnp.bfloat16),
                pltpu.VMEM((length, HEAD_DIM), jnp.bfloat16),
            ],
        ),
        name="attend_forward",
    )(lows, rows, starts)


def attend_backward_kernel(
    low_ref,
    rows_ref,
    grad_ref,
    out_ref,
    total_ref,
    start_ref,
    grad_query_ref,
    grad_key_ref,
    grad_value_ref,
    key_s,
    value_s,
    *,
    heads,
):
    step = pl.program_id(0)
    width = heads * HEAD_DIM

    @pl.when(step == 0)
    def _():
        key_s[...] = rows_ref[:, width : width + HEAD_DIM]
        value_s[...] = rows_ref[:, width + HEAD_DIM : width + 2 * HEAD_DIM]
        grad_key_ref[...] = jnp.zeros_like(grad_key_ref)
        grad_value_ref[...] = jnp.zeros_like(grad_value_ref)

    own = pl.ds(pl.multiple_of(step * BLOCK, BLOCK), BLOCK)
    block_rows = rows_ref[own, :]
    grads_all = grad_ref[...]
    starts = start_ref[0]
    at = step * BLOCK + lax.broadcasted_iota(jnp.int32, (1, BLOCK), 1)
    queries, scaled, grads, inners, totals = [], [], [], [], []
    for h in range(heads):
        span = slice(h * HEAD_DIM, (h + 1) * HEAD_DIM)
        queries.append(block_rows[:, span])
        scaled.append(block_rows[:, span] * jnp.bfloat16(score_scale))
        grads.append(grads_all[:, span])
        turned = grads_all[:, span].astype(jnp.float32).T
        inners.append(jnp.sum(turned * out_ref[span, :], 0, keepdims=True))
        totals.append(total_ref[0, h : h + 1, :])

    def one(j, carry):
        rows = pl.ds(pl.multiple_of(j * BLOCK, BLOCK), BLOCK)
        key_block = key_s[rows, :]
        value_block = value_s[rows, :]
        place = j * BLOCK + lax.broadcasted_iota(jnp.int32, (BLOCK, BLOCK), 0)
        allowed = (place >= starts) & (place <= at)
        result = []
        key_sum = grad_key_ref[rows, :]
        value_sum = grad_value_ref[rows, :]
        for h in range(heads):
            scores = jnp.where(allowed, dot_nt(key_block, scaled[h]), far_below)
            prob = jnp.exp(scores - totals[h])
            grad_prob = dot_nt(value_block, grads[h])
            grad_scores = (prob * (grad_prob - inners[h]) * score_scale).astype(jnp.bfloat16)
            value_sum = value_sum + product(prob.astype(jnp.bfloat16), grads[h])
            key_sum = key_sum + product(grad_scores, queries[h])
            result.append(carry[h] + dot_tn(grad_scores, key_block))
        grad_key_ref[rows, :] = key_sum
        grad_value_ref[rows, :] = value_sum
        return tuple(result)

    first = tuple(jnp.zeros((BLOCK, HEAD_DIM), jnp.float32) for _ in range(heads))
    done = lax.fori_loop(low_ref[step], step + 1, one, first)
    for h in range(heads):
        grad_query_ref[:, h * HEAD_DIM : (h + 1) * HEAD_DIM] = done[h]


def attend_backward(rows, grads, outs, totals, starts, lows, heads):
    length, width = rows.shape
    blocks = length // BLOCK
    whole = lambda i, low: (0, 0)
    return pl.pallas_call(
        functools.partial(attend_backward_kernel, heads=heads),
        out_shape=(
            jax.ShapeDtypeStruct((length, heads * HEAD_DIM), jnp.float32),
            jax.ShapeDtypeStruct((length, HEAD_DIM), jnp.float32),
            jax.ShapeDtypeStruct((length, HEAD_DIM), jnp.float32),
        ),
        grid_spec=pltpu.PrefetchScalarGridSpec(
            num_scalar_prefetch=1,
            grid=(blocks,),
            in_specs=[
                pl.BlockSpec((length, width), whole),
                pl.BlockSpec((BLOCK, heads * HEAD_DIM), lambda i, low: (i, 0)),
                pl.BlockSpec((heads * HEAD_DIM, BLOCK), lambda i, low: (0, i)),
                pl.BlockSpec((1, heads, BLOCK), lambda i, low: (i, 0, 0)),
                pl.BlockSpec((1, 1, BLOCK), lambda i, low: (i, 0, 0)),
            ],
            out_specs=[
                pl.BlockSpec((BLOCK, heads * HEAD_DIM), lambda i, low: (i, 0)),
                pl.BlockSpec((length, HEAD_DIM), whole),
                pl.BlockSpec((length, HEAD_DIM), whole),
            ],
            scratch_shapes=[
                pltpu.VMEM((length, HEAD_DIM), jnp.bfloat16),
                pltpu.VMEM((length, HEAD_DIM), jnp.bfloat16),
            ],
        ),
        name="attend_backward",
    )(lows, rows, grads, outs, totals, starts)


def experts_kernel(
    place_ref,
    rows_ref,
    cot_ref,
    rank_ref,
    prob_ref,
    gate_up_ref,
    down_ref,
    out_ref,
    grad_ref,
    inner_ref,
    keep_ref,
    *others,
    sources,
    rows_dev,
    count,
    copies,
    per,
    orders,
):
    send_refs = others[:-3]
    picks_s, out_s, grad_s = others[-3:]
    step = pl.program_id(0)
    slots = pl.ds(pl.multiple_of(step * CAP, 16), CAP)
    numbers = lax.broadcasted_iota(jnp.int32, (CAP, rows_dev), 0).astype(jnp.float32)
    rows_in, cots, weights, picks = [], [], [], []
    for s in range(sources):
        rank = rank_ref[s, pl.ds(step, 1), :]
        pick = jnp.where(rank == numbers, 1.0, 0.0)
        weights.append(jnp.sum(pick * prob_ref[s, pl.ds(step, 1), :], 1, keepdims=True))
        pick_b = pick.astype(jnp.bfloat16)
        picks.append(pick)
        picks_s[s, slots, :] = pick_b
        own = slice(s * rows_dev, (s + 1) * rows_dev)
        rows_in.append(product(pick_b, rows_ref[own, :]).astype(jnp.bfloat16))
        cots.append(product(pick_b, cot_ref[own, :]))
    arrived = jnp.concatenate(rows_in, 0)
    weight = jnp.concatenate(weights, 0)
    grad_mix = branch_scale * jnp.concatenate(cots, 0)
    gate_up = gate_up_ref[0]
    down = down_ref[0]
    hidden_units = down.shape[0]
    both = product(arrived, gate_up)
    gate_part = both[:, :hidden_units]
    up_part = both[:, hidden_units:]
    sigmoid_gate = jax.nn.sigmoid(gate_part)
    active = (gate_part * sigmoid_gate * up_part).astype(jnp.bfloat16)
    produced = product(active, down).astype(jnp.bfloat16).astype(jnp.float32)
    inner = jnp.sum(grad_mix * produced, 1, keepdims=True)
    sent_out = (weight * produced).astype(jnp.bfloat16)
    grad_out = (weight * grad_mix).astype(jnp.bfloat16)
    grad_active = dot_nt(grad_out, down)
    grad_down = dot_tn(active, grad_out).astype(keep_ref.dtype)
    grad_gate = grad_active * up_part * sigmoid_gate * (1.0 + gate_part * (1.0 - sigmoid_gate))
    grad_up = grad_active * gate_part * sigmoid_gate
    grad_both = jnp.concatenate([grad_gate, grad_up], 1).astype(jnp.bfloat16)
    grad_gate_up = dot_tn(arrived, grad_both).astype(keep_ref.dtype)
    share = grad_down.shape[1] // copies
    tall = hidden_units // copies

    def put(order, mine, send_ref):
        bit, *later = order
        for r in range(copies):
            spot = 0
            for b in later:
                spot = 2 * spot + ((r >> b) & 1)
            ref = keep_ref.at[0] if (r >> bit) & 1 == mine else send_ref
            ref[spot, 0, :share, :] = grad_gate_up[r * share : (r + 1) * share]
            for k in range(copies):
                ref[spot, 0, share : share + tall, k * share : (k + 1) * share] = grad_down[
                    k * tall : (k + 1) * tall, r * share : (r + 1) * share
                ]

    place = place_ref[0]
    for c, send_ref in enumerate(send_refs):
        for mine in range(2):

            @pl.when((step // per == c) & ((place >> orders[c][0]) & 1 == mine))
            def _(order=orders[c], mine=mine, send_ref=send_ref):
                put(order, mine, send_ref)

    grad_in = dot_nt(grad_both, gate_up).astype(jnp.bfloat16)
    for s in range(sources):
        part = slice(s * CAP, (s + 1) * CAP)
        out_s[s, slots, :] = sent_out[part]
        grad_s[s, slots, :] = grad_in[part]
        inner_ref[s, pl.ds(step, 1), :] = jnp.sum(picks[s] * inner[part], 0, keepdims=True)

    @pl.when(step == count - 1)
    def _():
        for s in range(sources):
            own = slice(s * rows_dev, (s + 1) * rows_dev)
            table = picks_s[s]
            out_ref[own, :] = dot_tn(table, out_s[s]).astype(jnp.bfloat16)
            grad_ref[own, :] = dot_tn(table, grad_s[s]).astype(jnp.bfloat16)


def experts(place, rows, cots, ranks, probs, w_gate_up, w_down, copies, orders):
    sources, count, rows_dev = ranks.shape
    total, model_width = rows.shape
    hidden_units = w_down.shape[1]
    chunks = len(orders)
    per = count // chunks
    tall = model_width // copies + hidden_units // copies
    flat = lambda i: (0, 0)
    cube = lambda i: (0, 0, 0)
    part = lambda i: (i // per, 0, i % per, 0, 0)
    once = pl.Buffered(1)
    return pl.pallas_call(
        functools.partial(
            experts_kernel,
            sources=sources,
            rows_dev=rows_dev,
            count=count,
            copies=copies,
            per=per,
            orders=orders,
        ),
        out_shape=(
            jax.ShapeDtypeStruct((total, model_width), jnp.bfloat16),
            jax.ShapeDtypeStruct((total, model_width), jnp.bfloat16),
            jax.ShapeDtypeStruct((sources, count, rows_dev), jnp.float32),
            jax.ShapeDtypeStruct((chunks, copies // 2, per, tall, model_width), jnp.bfloat16),
        )
        + (jax.ShapeDtypeStruct((copies // 2, per, tall, model_width), jnp.bfloat16),) * chunks,
        grid=(count,),
        in_specs=[
            pl.BlockSpec(memory_space=pltpu.SMEM),
            pl.BlockSpec((total, model_width), flat, pipeline_mode=once),
            pl.BlockSpec((total, model_width), flat, pipeline_mode=once),
            pl.BlockSpec((sources, count, rows_dev), cube, pipeline_mode=once),
            pl.BlockSpec((sources, count, rows_dev), cube, pipeline_mode=once),
            pl.BlockSpec((1, model_width, 2 * hidden_units), lambda i: (i, 0, 0)),
            pl.BlockSpec((1, hidden_units, model_width), lambda i: (i, 0, 0)),
        ],
        out_specs=[
            pl.BlockSpec((total, model_width), flat, pipeline_mode=once),
            pl.BlockSpec((total, model_width), flat, pipeline_mode=once),
            pl.BlockSpec((sources, count, rows_dev), cube, pipeline_mode=once),
            pl.BlockSpec((1, copies // 2, 1, tall, model_width), part),
        ]
        + [
            pl.BlockSpec(
                (copies // 2, 1, tall, model_width),
                lambda i, c=c: (0, jnp.clip(i - c * per, 0, per - 1), 0, 0),
            )
            for c in range(chunks)
        ],
        scratch_shapes=[
            pltpu.VMEM((sources, count * CAP, rows_dev), jnp.bfloat16),
            pltpu.VMEM((sources, count * CAP, model_width), jnp.bfloat16),
            pltpu.VMEM((sources, count * CAP, model_width), jnp.bfloat16),
        ],
        compiler_params=pltpu.CompilerParams(vmem_limit_bytes=67 * 1000 * 1000),
        name="experts",
    )(place, rows, cots, ranks, probs, w_gate_up, w_down)


def bits_of(size):
    return max(size.bit_length() - 1, 0)


def take(block, dim, index):
    if not isinstance(block, tuple):
        return lax.dynamic_index_in_dim(block, index, dim, keepdims=False)
    stack, chunk = block
    starts = [jnp.int32(0)] * stack.ndim
    starts[0] = jnp.int32(chunk)
    starts[dim + 1] = index.astype(jnp.int32)
    sizes = list(stack.shape)
    sizes[0] = sizes[dim + 1] = 1
    sliced = lax.dynamic_slice(stack, starts, sizes)
    return sliced.reshape(stack.shape[1 : dim + 1] + stack.shape[dim + 2 :])


def split(total, labels, axis, bit):
    dim = labels.index((axis, bit))
    mine = (lax.axis_index(axis) >> bit) & 1
    sent = total(lambda block: take(block, dim, 1 - mine))
    kept = total(lambda block: take(block, dim, mine))
    return (sent, kept, labels[:dim] + labels[dim + 1 :])


def swap(sent, axis, bit):
    size = lax.axis_size(axis)
    return lax.ppermute(sent, axis, [(i, i ^ (1 << bit)) for i in range(size)])


def after(value, *others):
    return lax.optimization_barrier((value, *others))[0]


class Halving:
    def __init__(self, order, labels, block=None, halves=None):
        self.order = list(order)
        if halves is None:
            axis, bit = self.order[0]
            self.sent, self.kept, self.labels = split(
                lambda slicer: slicer(block), list(labels), axis, bit
            )
        else:
            self.sent, self.kept = halves
            self.labels = [label for label in labels if label != self.order[0]]

    def send(self, *others):
        if others:
            self.sent = after(self.sent, *others)
        self.came = swap(self.sent, *self.order[0])
        return self

    def add(self):
        self.order = self.order[1:]
        kept, came = self.kept, self.came

        def total(slicer):
            return slicer(kept).astype(jnp.float32) + slicer(came).astype(jnp.float32)

        if self.order:
            axis, bit = self.order[0]
            self.sent, self.kept, self.labels = split(
                lambda slicer: total(slicer).astype(jnp.bfloat16), self.labels, axis, bit
            )
        else:
            self.result = total(lambda block: block)
        return self

    def rest(self):
        while self.order:
            self.send().add()
        return self.result


def on_device(
    tokens,
    segments,
    routes,
    attn_gain,
    w_query,
    w_key,
    w_value,
    w_out,
    mlp_gain,
    w_router,
    w_gate_up,
    w_down,
    cotangent,
    *,
    n_ep,
    n_rep,
):
    inputs = tokens[0]
    own_routes = routes[0]
    grad_output = cotangent[0]
    rows_dev, model_width = inputs.shape
    everyone = ("ep", "rep")
    heads = HEADS // n_rep
    head_width = heads * HEAD_DIM
    shared = max(1, n_rep // KV_HEADS)
    query_width = w_query.shape[1]
    key_width = w_key.shape[1]
    experts_all = w_router.shape[1]
    half_dim = HEAD_DIM // 2

    pack_ids = lax.all_gather(segments[0], "rep", axis=0, tiled=True)
    length = pack_ids.shape[0]
    blocks = length // BLOCK
    offset = lax.axis_index("rep") * rows_dev
    doc_start = jnp.sum((pack_ids[None, :] < pack_ids[:, None]).astype(jnp.int32), 1)
    position = (jnp.arange(length, dtype=jnp.int32) - doc_start).astype(jnp.float32)
    angles = (
        position[:, None]
        * jnp.exp(jnp.arange(half_dim, dtype=jnp.float32) * (-math.log(10000.0) / half_dim))[
            None, :
        ]
    )
    cosine = jnp.cos(angles)
    sine = jnp.sin(angles)
    cosine = jnp.concatenate([cosine, cosine], 1)
    sine = jnp.concatenate([-sine, sine], 1)
    own_cosine = lax.dynamic_slice_in_dim(cosine, offset, rows_dev, 0)
    own_sine = lax.dynamic_slice_in_dim(sine, offset, rows_dev, 0)
    starts = doc_start.reshape(blocks, 1, BLOCK)
    lows = doc_start[::BLOCK] // BLOCK

    joined = jnp.concatenate([w_query, w_key, w_value, w_out, w_router], 1)
    full = lax.all_gather(joined, everyone, axis=0, tiled=True)
    rotated_width = query_width + key_width
    input_width = rotated_width + key_width
    full_in = full[:, :input_width]
    full_out = full[:, input_width : input_width + model_width]
    full_router = full[:, input_width + model_width :]

    normed, factor_one = rms_norm(inputs, attn_gain)
    normed_b = normed.astype(jnp.bfloat16)
    mixed_in = product(normed_b, full_in)
    turn = mixed_in[:, :rotated_width]
    times = rotated_width // HEAD_DIM
    turned = turn * jnp.tile(own_cosine, (1, times)) + swap_halves(turn) * jnp.tile(
        own_sine, (1, times)
    )
    turned_b = turned.astype(jnp.bfloat16)
    value_b = mixed_in[:, rotated_width:].astype(jnp.bfloat16)
    query_part = turned_b[:, :query_width].reshape(rows_dev, n_rep, head_width)
    key_part = turned_b[:, query_width:].reshape(rows_dev, KV_HEADS, HEAD_DIM)
    value_part = value_b.reshape(rows_dev, KV_HEADS, HEAD_DIM)
    if shared > 1:
        key_part = jnp.repeat(key_part, shared, 1)
        value_part = jnp.repeat(value_part, shared, 1)
    sending = jnp.concatenate([query_part, key_part, value_part], 2).transpose(1, 0, 2)
    head_rows = lax.all_to_all(sending, "rep", split_axis=0, concat_axis=0, tiled=True)
    head_rows = head_rows.reshape(length, head_width + 2 * HEAD_DIM)
    mixed, mixed_out, totals = attend_forward(head_rows, starts, lows, heads)
    mixed_rows = lax.all_to_all(
        mixed.reshape(n_rep, rows_dev, head_width), "rep", split_axis=0, concat_axis=0, tiled=True
    )
    mixed_rows = mixed_rows.transpose(1, 0, 2).reshape(rows_dev, query_width)
    hidden = inputs + branch_scale * product(mixed_rows, full_out)

    normed_two, factor_two = rms_norm(hidden, mlp_gain)
    normed_two_b = normed_two.astype(jnp.bfloat16)
    router_f = full_router.astype(jnp.float32)
    logits = product(normed_two_b, full_router)
    numbers = jnp.arange(experts_all, dtype=jnp.int32)
    onehot = jnp.sum((own_routes[:, :, None] == numbers).astype(jnp.float32), 1)
    chosen = onehot > 0.5
    peak = jnp.max(jnp.where(chosen, logits, far_below), 1, keepdims=True)
    raised = jnp.where(chosen, jnp.exp(jnp.minimum(logits - peak, 0.0)), 0.0)
    probs = raised / jnp.sum(raised, 1, keepdims=True)
    before = (
        lax.broadcasted_iota(jnp.int32, (rows_dev, rows_dev), 0)
        > lax.broadcasted_iota(jnp.int32, (rows_dev, rows_dev), 1)
    ).astype(jnp.bfloat16)
    rank = product(before, onehot.astype(jnp.bfloat16))
    kept = chosen & (rank < CAP)
    rank_sent = jnp.where(kept, rank, -1.0).T
    probs_sent = probs.T
    both_sent = jnp.concatenate(
        [rank_sent.reshape(n_ep, -1, rows_dev), probs_sent.reshape(n_ep, -1, rows_dev)], 1
    )
    both_all = lax.all_to_all(both_sent, "ep", split_axis=0, concat_axis=0, tiled=True)
    ranks = both_all[:, : experts_all // n_ep]
    prob_all = both_all[:, experts_all // n_ep :]
    expert_rows = lax.all_gather(normed_two_b, "ep", axis=0, tiled=True)
    expert_cots = lax.all_gather(grad_output.astype(jnp.bfloat16), "ep", axis=0, tiled=True)
    chunks = 4
    rep_bits = [("rep", b) for b in reversed(range(bits_of(n_rep)))]
    ep_bits = [("ep", b) for b in reversed(range(bits_of(n_ep)))]
    near_first = rep_bits[::-1]
    far_bit = len(rep_bits) - 2
    far_first = [("rep", far_bit)] + near_first[:far_bit] + near_first[-1:]
    chunk_orders = [near_first] * (chunks - 1) + [far_first]
    out_sum, grad_sum, inner, grad_keep, *grad_send = experts(
        lax.axis_index("rep").astype(jnp.int32).reshape(1),
        expert_rows,
        expert_cots,
        ranks,
        prob_all,
        w_gate_up,
        w_down,
        n_rep,
        [tuple(b for _, b in order) for order in chunk_orders],
    )
    share = model_width // n_rep
    tall = w_down.shape[1] // n_rep
    lanes = []
    shape = (2,) * (len(rep_bits) - 1) + grad_keep.shape[2:]
    grad_keep = grad_keep.reshape((chunks,) + shape)
    for c in range(chunks):
        lanes.append(
            Halving(
                chunk_orders[c],
                chunk_orders[c],
                halves=(grad_send[c].reshape(shape), (grad_keep, c)),
            )
        )
    lanes[0].send()
    lanes[3].send()
    out_back = lax.all_to_all(
        out_sum.reshape(n_ep, rows_dev, model_width), "ep", split_axis=0, concat_axis=0, tiled=True
    )
    grad_back = lax.all_to_all(
        grad_sum.reshape(n_ep, rows_dev, model_width), "ep", split_axis=0, concat_axis=0, tiled=True
    )
    inner_back = lax.all_to_all(inner, "ep", split_axis=0, concat_axis=0, tiled=True)
    output = hidden + branch_scale * jnp.sum(out_back.astype(jnp.float32), 0)
    grad_probs = inner_back.reshape(experts_all, rows_dev).T
    grad_logits = probs * (grad_probs - jnp.sum(grad_probs * probs, -1, keepdims=True))
    normed_two_f = normed_two_b.astype(jnp.float32)
    grad_router = jnp.dot(normed_two_f.T, grad_logits, precision=lax.Precision.HIGHEST)
    grad_normed_two = jnp.sum(grad_back.astype(jnp.float32), 0) + jnp.dot(
        grad_logits, router_f.T, precision=lax.Precision.HIGHEST
    )
    grad_hidden_norm, grad_mlp_gain = norm_back(grad_normed_two, hidden, factor_two, mlp_gain)
    grad_hidden = grad_output + grad_hidden_norm
    grad_attn = (branch_scale * grad_hidden).astype(jnp.bfloat16)
    grad_out_w = dot_tn(mixed_rows, grad_attn)
    grad_mixed = dot_nt(grad_attn, full_out).astype(jnp.bfloat16)
    first = jnp.concatenate([grad_out_w, grad_router], 1).astype(jnp.bfloat16)
    weight_bits = ep_bits + rep_bits
    weight_shape = (2,) * len(weight_bits) + (-1,)

    def weight_lane(grad):
        return Halving(
            ep_bits[::-1] + near_first,
            weight_bits,
            block=grad.reshape(weight_shape + grad.shape[1:]),
        )

    first = weight_lane(first)
    for _ in ep_bits[1:]:
        first.send().add()
    first.send()
    grad_heads = lax.all_to_all(
        grad_mixed.reshape(rows_dev, n_rep, head_width).transpose(1, 0, 2),
        "rep",
        split_axis=0,
        concat_axis=0,
        tiled=True,
    ).reshape(length, head_width)
    lanes[0].add().send()
    lanes[1].send(lanes[0].sent)
    lanes[3].add().send()
    grad_heads = after(grad_heads, lanes[0].sent, lanes[1].sent, lanes[3].sent)
    grad_query, grad_key, grad_value = attend_backward(
        head_rows, grad_heads, mixed_out, totals, starts, lows, heads
    )
    turn_back = jnp.concatenate([grad_query, grad_key], 1)
    turn_back = turn_back * jnp.tile(cosine, (1, heads + 1)) - swap_halves(turn_back) * jnp.tile(
        sine, (1, heads + 1)
    )
    returning = jnp.concatenate([turn_back, grad_value], 1).astype(jnp.bfloat16)
    returned = lax.all_to_all(
        returning.reshape(n_rep, rows_dev, head_width + 2 * HEAD_DIM),
        "rep",
        split_axis=0,
        concat_axis=0,
        tiled=True,
    ).transpose(1, 0, 2)
    grad_query_rows = returned[:, :, :head_width].reshape(rows_dev, query_width)
    key_back = returned[:, :, head_width : head_width + HEAD_DIM]
    value_back = returned[:, :, head_width + HEAD_DIM :]
    if shared > 1:
        key_back = jnp.sum(
            key_back.reshape(rows_dev, KV_HEADS, shared, HEAD_DIM).astype(jnp.float32), 2
        ).astype(jnp.bfloat16)
        value_back = jnp.sum(
            value_back.reshape(rows_dev, KV_HEADS, shared, HEAD_DIM).astype(jnp.float32), 2
        ).astype(jnp.bfloat16)
    grad_in_rows = jnp.concatenate(
        [
            grad_query_rows,
            key_back.reshape(rows_dev, key_width),
            value_back.reshape(rows_dev, key_width),
        ],
        1,
    )
    grad_w_query = dot_tn(normed_b, grad_in_rows[:, :query_width])
    grad_w_rest = dot_tn(normed_b, grad_in_rows[:, query_width:])
    grad_normed = dot_nt(grad_in_rows, full_in)
    grad_inputs_norm, grad_attn_gain = norm_back(grad_normed, inputs, factor_one, attn_gain)
    grad_inputs = grad_hidden + grad_inputs_norm
    query_lane = weight_lane(grad_w_query.astype(jnp.bfloat16))
    rest_lane = weight_lane(grad_w_rest.astype(jnp.bfloat16))
    for lane in (query_lane, rest_lane):
        for _ in ep_bits:
            lane.send().add()
    first.add()
    joint = Halving(
        near_first,
        rep_bits,
        halves=tuple(
            jnp.concatenate([query, rest, own], -1)
            for query, rest, own in zip(
                (query_lane.sent, query_lane.kept),
                (rest_lane.sent, rest_lane.kept),
                (first.sent, first.kept),
            )
        ),
    )
    weights = joint.rest()
    lanes[0].add().send()
    lanes[1].add().send()
    lanes[2].send(lanes[1].sent)
    grad_experts = jnp.concatenate([lane.add().rest() for lane in lanes], 0)
    expert_up = grad_experts[:, :share, :]
    expert_down = (
        grad_experts[:, share:, :]
        .reshape(-1, tall, n_rep, share)
        .transpose(0, 2, 1, 3)
        .reshape(-1, tall * n_rep, share)
    )
    everything = n_ep * n_rep
    gains = jnp.concatenate(
        [grad_attn_gain.reshape(everything, -1), grad_mlp_gain.reshape(everything, -1)], 1
    )
    gains = jnp.sum(
        lax.all_to_all(gains, everyone, split_axis=0, concat_axis=0, tiled=True), 0
    )
    part = model_width // everything
    return (
        output[None],
        grad_inputs[None],
        gains[:part],
        weights[:, :query_width],
        weights[:, query_width:rotated_width],
        weights[:, rotated_width:input_width],
        weights[:, input_width : input_width + model_width],
        gains[part:],
        weights[:, input_width + model_width :],
        expert_up,
        expert_down,
    )


def solution(mesh):
    placed = (
        P("ep", "rep", None),
        P("ep", "rep"),
        P("ep", "rep", None),
        P(),
        P(("ep", "rep"), None),
        P(("ep", "rep"), None),
        P(("ep", "rep"), None),
        P(("ep", "rep"), None),
        P(),
        P(("ep", "rep"), None),
        P("ep", None, None),
        P("ep", None, None),
        P("ep", "rep", None),
    )
    return jax.shard_map(
        functools.partial(on_device, n_ep=mesh.shape["ep"], n_rep=mesh.shape["rep"]),
        mesh=mesh,
        in_specs=placed,
        out_specs=(
            P("ep", "rep", None),
            P("ep", "rep", None),
            P(("ep", "rep")),
            P(("ep", "rep"), None),
            P(("ep", "rep"), None),
            P(("ep", "rep"), None),
            P(("ep", "rep"), None),
            P(("ep", "rep")),
            P(("ep", "rep"), None),
            P("ep", "rep", None),
            P("ep", None, "rep"),
        ),
        check_vma=False,
    )
```

```python
import functools
import math

import jax
import jax.numpy as jnp
from jax import lax
from jax.experimental import pallas as pl
from jax.experimental.pallas import tpu as pltpu
from jax.sharding import PartitionSpec as P

HEADS = 16
KV_HEADS = 8
HEAD_DIM = 64
CAP = 80
BLOCK = 256

epsilon = 1e-06
score_scale = 0.015625
branch_scale = 0.22
far_below = -1e30

NT = (((1,), (1,)), ((), ()))
TN = (((0,), (0,)), ((), ()))


def product(left, right):
    return jnp.dot(left, right, preferred_element_type=jnp.float32)


def dot_nt(left, right):
    return lax.dot_general(left, right, NT, preferred_element_type=jnp.float32)


def dot_tn(left, right):
    return lax.dot_general(left, right, TN, preferred_element_type=jnp.float32)


def rms_norm(values, gain):
    factor = lax.rsqrt(jnp.mean(values * values, -1, keepdims=True) + epsilon)
    return (values * factor * gain, factor)


def norm_back(grad_normed, values, factor, gain):
    scaled = grad_normed * gain
    gain_part = jnp.sum(grad_normed * values * factor, 0)
    inner_sum = jnp.mean(scaled * values, -1, keepdims=True)
    return (factor * scaled - values * (factor * factor * factor) * inner_sum, gain_part)


def swap_halves(values):
    count, width = values.shape
    half_dim = HEAD_DIM // 2
    lane = lax.broadcasted_iota(jnp.int32, values.shape, 1)
    return jnp.where(
        lane % HEAD_DIM < half_dim,
        jnp.roll(values, -half_dim, 1),
        jnp.roll(values, half_dim, 1),
    )


def attend_forward_kernel(
    low_ref, rows_ref, start_ref, mixed_ref, out_ref, total_ref, key_s, value_s, *, heads
):
    step = pl.program_id(0)
    width = heads * HEAD_DIM

    @pl.when(step == 0)
    def _():
        key_s[...] = rows_ref[:, width : width + HEAD_DIM]
        value_s[...] = rows_ref[:, width + HEAD_DIM : width + 2 * HEAD_DIM]

    block_rows = rows_ref[pl.ds(pl.multiple_of(step * BLOCK, BLOCK), BLOCK), :]
    queries = [
        block_rows[:, h * HEAD_DIM : (h + 1) * HEAD_DIM] * jnp.bfloat16(score_scale)
        for h in range(heads)
    ]
    starts = start_ref[0]
    at = step * BLOCK + lax.broadcasted_iota(jnp.int32, (1, BLOCK), 1)

    def one(j, carry):
        rows = pl.ds(pl.multiple_of(j * BLOCK, BLOCK), BLOCK)
        key_block = key_s[rows, :]
        value_block = value_s[rows, :]
        place = j * BLOCK + lax.broadcasted_iota(jnp.int32, (BLOCK, BLOCK), 0)
        allowed = (place >= starts) & (place <= at)
        result = []
        for h in range(heads):
            peak, total, mixed = carry[h]
            scores = jnp.where(allowed, dot_nt(key_block, queries[h]), far_below)
            new_peak = jnp.maximum(peak, jnp.max(scores, 0, keepdims=True))
            fade = jnp.exp(peak - new_peak)
            raised = jnp.exp(scores - new_peak)
            total = fade * total + jnp.sum(raised, 0, keepdims=True)
            mixed = fade * mixed + dot_tn(value_block, raised.astype(jnp.bfloat16))
            result.append((new_peak, total, mixed))
        return tuple(result)

    first = tuple(
        (
            jnp.full((1, BLOCK), far_below, jnp.float32),
            jnp.zeros((1, BLOCK), jnp.float32),
            jnp.zeros((HEAD_DIM, BLOCK), jnp.float32),
        )
        for _ in range(heads)
    )
    done = lax.fori_loop(low_ref[step], step + 1, one, first)
    for h in range(heads):
        peak, total, mixed = done[h]
        mixed = mixed / total
        out_ref[h * HEAD_DIM : (h + 1) * HEAD_DIM, :] = mixed
        total_ref[0, h : h + 1, :] = peak + jnp.log(total)
        mixed_ref[:, h * HEAD_DIM : (h + 1) * HEAD_DIM] = mixed.T.astype(jnp.bfloat16)


def attend_forward(rows, starts, lows, heads):
    length, width = rows.shape
    blocks = length // BLOCK
    whole = lambda i, low: (0, 0)
    return pl.pallas_call(
        functools.partial(attend_forward_kernel, heads=heads),
        out_shape=(
            jax.ShapeDtypeStruct((length, heads * HEAD_DIM), jnp.bfloat16),
            jax.ShapeDtypeStruct((heads * HEAD_DIM, length), jnp.float32),
            jax.ShapeDtypeStruct((blocks, heads, BLOCK), jnp.float32),
        ),
        grid_spec=pltpu.PrefetchScalarGridSpec(
            num_scalar_prefetch=1,
            grid=(blocks,),
            in_specs=[
                pl.BlockSpec((length, width), whole),
                pl.BlockSpec((1, 1, BLOCK), lambda i, low: (i, 0, 0)),
            ],
            out_specs=[
                pl.BlockSpec((BLOCK, heads * HEAD_DIM), lambda i, low: (i, 0)),
                pl.BlockSpec((heads * HEAD_DIM, BLOCK), lambda i, low: (0, i)),
                pl.BlockSpec((1, heads, BLOCK), lambda i, low: (i, 0, 0)),
            ],
            scratch_shapes=[
                pltpu.VMEM((length, HEAD_DIM), jnp.bfloat16),
                pltpu.VMEM((length, HEAD_DIM), jnp.bfloat16),
            ],
        ),
        name="attend_forward",
    )(lows, rows, starts)


def attend_backward_kernel(
    low_ref,
    rows_ref,
    grad_ref,
    out_ref,
    total_ref,
    start_ref,
    grad_query_ref,
    grad_key_ref,
    grad_value_ref,
    key_s,
    value_s,
    *,
    heads,
):
    step = pl.program_id(0)
    width = heads * HEAD_DIM

    @pl.when(step == 0)
    def _():
        key_s[...] = rows_ref[:, width : width + HEAD_DIM]
        value_s[...] = rows_ref[:, width + HEAD_DIM : width + 2 * HEAD_DIM]
        grad_key_ref[...] = jnp.zeros_like(grad_key_ref)
        grad_value_ref[...] = jnp.zeros_like(grad_value_ref)

    own = pl.ds(pl.multiple_of(step * BLOCK, BLOCK), BLOCK)
    block_rows = rows_ref[own, :]
    grads_all = grad_ref[...]
    starts = start_ref[0]
    at = step * BLOCK + lax.broadcasted_iota(jnp.int32, (1, BLOCK), 1)
    queries, scaled, grads, inners, totals = [], [], [], [], []
    for h in range(heads):
        span = slice(h * HEAD_DIM, (h + 1) * HEAD_DIM)
        queries.append(block_rows[:, span])
        scaled.append(block_rows[:, span] * jnp.bfloat16(score_scale))
        grads.append(grads_all[:, span])
        turned = grads_all[:, span].astype(jnp.float32).T
        inners.append(jnp.sum(turned * out_ref[span, :], 0, keepdims=True))
        totals.append(total_ref[0, h : h + 1, :])

    def one(j, carry):
        rows = pl.ds(pl.multiple_of(j * BLOCK, BLOCK), BLOCK)
        key_block = key_s[rows, :]
        value_block = value_s[rows, :]
        place = j * BLOCK + lax.broadcasted_iota(jnp.int32, (BLOCK, BLOCK), 0)
        allowed = (place >= starts) & (place <= at)
        result = []
        key_sum = grad_key_ref[rows, :]
        value_sum = grad_value_ref[rows, :]
        for h in range(heads):
            scores = jnp.where(allowed, dot_nt(key_block, scaled[h]), far_below)
            prob = jnp.exp(scores - totals[h])
            grad_prob = dot_nt(value_block, grads[h])
            grad_scores = (prob * (grad_prob - inners[h]) * score_scale).astype(jnp.bfloat16)
            value_sum = value_sum + product(prob.astype(jnp.bfloat16), grads[h])
            key_sum = key_sum + product(grad_scores, queries[h])
            result.append(carry[h] + dot_tn(grad_scores, key_block))
        grad_key_ref[rows, :] = key_sum
        grad_value_ref[rows, :] = value_sum
        return tuple(result)

    first = tuple(jnp.zeros((BLOCK, HEAD_DIM), jnp.float32) for _ in range(heads))
    done = lax.fori_loop(low_ref[step], step + 1, one, first)
    for h in range(heads):
        grad_query_ref[:, h * HEAD_DIM : (h + 1) * HEAD_DIM] = done[h]


def attend_backward(rows, grads, outs, totals, starts, lows, heads):
    length, width = rows.shape
    blocks = length // BLOCK
    whole = lambda i, low: (0, 0)
    return pl.pallas_call(
        functools.partial(attend_backward_kernel, heads=heads),
        out_shape=(
            jax.ShapeDtypeStruct((length, heads * HEAD_DIM), jnp.float32),
            jax.ShapeDtypeStruct((length, HEAD_DIM), jnp.float32),
            jax.ShapeDtypeStruct((length, HEAD_DIM), jnp.float32),
        ),
        grid_spec=pltpu.PrefetchScalarGridSpec(
            num_scalar_prefetch=1,
            grid=(blocks,),
            in_specs=[
                pl.BlockSpec((length, width), whole),
                pl.BlockSpec((BLOCK, heads * HEAD_DIM), lambda i, low: (i, 0)),
                pl.BlockSpec((heads * HEAD_DIM, BLOCK), lambda i, low: (0, i)),
                pl.BlockSpec((1, heads, BLOCK), lambda i, low: (i, 0, 0)),
                pl.BlockSpec((1, 1, BLOCK), lambda i, low: (i, 0, 0)),
            ],
            out_specs=[
                pl.BlockSpec((BLOCK, heads * HEAD_DIM), lambda i, low: (i, 0)),
                pl.BlockSpec((length, HEAD_DIM), whole),
                pl.BlockSpec((length, HEAD_DIM), whole),
            ],
            scratch_shapes=[
                pltpu.VMEM((length, HEAD_DIM), jnp.bfloat16),
                pltpu.VMEM((length, HEAD_DIM), jnp.bfloat16),
            ],
        ),
        name="attend_backward",
    )(lows, rows, grads, outs, totals, starts)


def experts_kernel(
    place_ref,
    rows_ref,
    cot_ref,
    rank_ref,
    prob_ref,
    gate_up_ref,
    down_ref,
    out_ref,
    grad_ref,
    inner_ref,
    keep_ref,
    *others,
    sources,
    rows_dev,
    count,
    copies,
    groups,
):
    send_refs = others[:-3]
    picks_s, out_s, grad_s = others[-3:]
    step = pl.program_id(0)
    slots = pl.ds(pl.multiple_of(step * CAP, 16), CAP)
    numbers = lax.broadcasted_iota(jnp.int32, (CAP, rows_dev), 0).astype(jnp.float32)
    rows_in, cots, weights, picks = [], [], [], []
    for s in range(sources):
        rank = rank_ref[s, pl.ds(step, 1), :]
        pick = jnp.where(rank == numbers, 1.0, 0.0)
        weights.append(jnp.sum(pick * prob_ref[s, pl.ds(step, 1), :], 1, keepdims=True))
        pick_b = pick.astype(jnp.bfloat16)
        picks.append(pick)
        picks_s[s, slots, :] = pick_b
        own = slice(s * rows_dev, (s + 1) * rows_dev)
        rows_in.append(product(pick_b, rows_ref[own, :]).astype(jnp.bfloat16))
        cots.append(product(pick_b, cot_ref[own, :]))
    arrived = jnp.concatenate(rows_in, 0)
    weight = jnp.concatenate(weights, 0)
    grad_mix = branch_scale * jnp.concatenate(cots, 0)
    gate_up = gate_up_ref[0]
    down = down_ref[0]
    hidden_units = down.shape[0]
    both = product(arrived, gate_up)
    gate_part = both[:, :hidden_units]
    up_part = both[:, hidden_units:]
    sigmoid_gate = jax.nn.sigmoid(gate_part)
    active = (gate_part * sigmoid_gate * up_part).astype(jnp.bfloat16)
    produced = product(active, down).astype(jnp.bfloat16).astype(jnp.float32)
    inner = jnp.sum(grad_mix * produced, 1, keepdims=True)
    sent_out = (weight * produced).astype(jnp.bfloat16)
    grad_out = (weight * grad_mix).astype(jnp.bfloat16)
    grad_active = dot_nt(grad_out, down)
    grad_down = dot_tn(active, grad_out).astype(keep_ref.dtype)
    grad_gate = grad_active * up_part * sigmoid_gate * (1.0 + gate_part * (1.0 - sigmoid_gate))
    grad_up = grad_active * gate_part * sigmoid_gate
    grad_both = jnp.concatenate([grad_gate, grad_up], 1).astype(jnp.bfloat16)
    grad_gate_up = dot_tn(arrived, grad_both).astype(keep_ref.dtype)
    share = grad_down.shape[1] // copies
    tall = hidden_units // copies

    def put(order, mine, send_ref):
        bit, *later = order
        for r in range(copies):
            spot = 0
            for b in later:
                spot = 2 * spot + ((r >> b) & 1)
            ref = keep_ref if (r >> bit) & 1 == mine else send_ref
            ref[0, spot, :share, :] = grad_gate_up[r * share : (r + 1) * share]
            for k in range(copies):
                ref[0, spot, share : share + tall, k * share : (k + 1) * share] = grad_down[
                    k * tall : (k + 1) * tall, r * share : (r + 1) * share
                ]

    place = place_ref[0]
    for (begin, size, order), send_ref in zip(groups, send_refs):
        for mine in range(2):

            @pl.when(
                (step >= begin)
                & (step < begin + size)
                & ((place >> order[0]) & 1 == mine)
            )
            def _(order=order, mine=mine, send_ref=send_ref):
                put(order, mine, send_ref)

    grad_in = dot_nt(grad_both, gate_up).astype(jnp.bfloat16)
    for s in range(sources):
        part = slice(s * CAP, (s + 1) * CAP)
        out_s[s, slots, :] = sent_out[part]
        grad_s[s, slots, :] = grad_in[part]
        inner_ref[s, pl.ds(step, 1), :] = jnp.sum(picks[s] * inner[part], 0, keepdims=True)

    @pl.when(step == count - 1)
    def _():
        for s in range(sources):
            own = slice(s * rows_dev, (s + 1) * rows_dev)
            table = picks_s[s]
            out_ref[own, :] = dot_tn(table, out_s[s]).astype(jnp.bfloat16)
            grad_ref[own, :] = dot_tn(table, grad_s[s]).astype(jnp.bfloat16)


def experts(place, rows, cots, ranks, probs, w_gate_up, w_down, copies, groups):
    sources, count, rows_dev = ranks.shape
    total, model_width = rows.shape
    hidden_units = w_down.shape[1]
    tall = model_width // copies + hidden_units // copies
    flat = lambda i: (0, 0)
    cube = lambda i: (0, 0, 0)
    once = pl.Buffered(1)
    return pl.pallas_call(
        functools.partial(
            experts_kernel,
            sources=sources,
            rows_dev=rows_dev,
            count=count,
            copies=copies,
            groups=groups,
        ),
        out_shape=(
            jax.ShapeDtypeStruct((total, model_width), jnp.bfloat16),
            jax.ShapeDtypeStruct((total, model_width), jnp.bfloat16),
            jax.ShapeDtypeStruct((sources, count, rows_dev), jnp.float32),
            jax.ShapeDtypeStruct((count, copies // 2, tall, model_width), jnp.bfloat16),
        )
        + tuple(
            jax.ShapeDtypeStruct((size, copies // 2, tall, model_width), jnp.bfloat16)
            for _, size, _ in groups
        ),
        grid=(count,),
        in_specs=[
            pl.BlockSpec(memory_space=pltpu.SMEM),
            pl.BlockSpec((total, model_width), flat, pipeline_mode=once),
            pl.BlockSpec((total, model_width), flat, pipeline_mode=once),
            pl.BlockSpec((sources, count, rows_dev), cube, pipeline_mode=once),
            pl.BlockSpec((sources, count, rows_dev), cube, pipeline_mode=once),
            pl.BlockSpec((1, model_width, 2 * hidden_units), lambda i: (i, 0, 0)),
            pl.BlockSpec((1, hidden_units, model_width), lambda i: (i, 0, 0)),
        ],
        out_specs=[
            pl.BlockSpec((total, model_width), flat, pipeline_mode=once),
            pl.BlockSpec((total, model_width), flat, pipeline_mode=once),
            pl.BlockSpec((sources, count, rows_dev), cube, pipeline_mode=once),
            pl.BlockSpec((1, copies // 2, tall, model_width), lambda i: (i, 0, 0, 0)),
        ]
        + [
            pl.BlockSpec(
                (1, copies // 2, tall, model_width),
                lambda i, begin=begin, size=size: (jnp.clip(i - begin, 0, size - 1), 0, 0, 0),
            )
            for begin, size, _ in groups
        ],
        scratch_shapes=[
            pltpu.VMEM((sources, count * CAP, rows_dev), jnp.bfloat16),
            pltpu.VMEM((sources, count * CAP, model_width), jnp.bfloat16),
            pltpu.VMEM((sources, count * CAP, model_width), jnp.bfloat16),
        ],
        compiler_params=pltpu.CompilerParams(vmem_limit_bytes=67 * 1000 * 1000),
        name="experts",
    )(place, rows, cots, ranks, probs, w_gate_up, w_down)


def bits_of(size):
    return max(size.bit_length() - 1, 0)


def swap(sent, axis, bit):
    size = lax.axis_size(axis)
    return lax.ppermute(sent, axis, [(i, i ^ (1 << bit)) for i in range(size)])


def side(axis, bit):
    index = lax.axis_index(axis)
    mine = (index // (1 << bit)) % 2
    return (mine, index + (1 - 2 * mine) * (1 << bit))


def pick(dim, index):
    return (slice(None),) * dim + (index,)


def digits(number, count):
    return tuple((number // (1 << (count - 1 - k))) % 2 for k in range(count))


def reduce_kernel(*refs, groups, labels, weight_order, share):
    n_groups = len(groups)
    keep_ref, *refs = refs
    came_refs, refs = (refs[:n_groups], refs[n_groups:])
    weight_ref, gain_ref, up_ref, down_ref, weight_out, gain_out, *refs = refs
    steps = len(groups[0][2]) - 1
    sends, keeps, gets = ([], [], [])
    for _ in range(steps):
        sends.append(refs[0])
        keeps.append(refs[1])
        gets.append(refs[2])
        refs = refs[3:]
    bits = len(labels)
    lanes = []
    for first, out in ((weight_ref, weight_out), (gain_ref, gain_out)):
        lanes.append((first, refs[: bits - 1], refs[bits - 1 : 2 * bits - 1], out))
        refs = refs[2 * bits - 1 :]
    load_keep, load_came, load_sem, unit_send, unit_get, lane_send, lane_get = refs
    count, spots, tall, width = keep_ref.shape
    rows = 32 if tall % 32 == 0 else tall
    blocks = tall // rows

    barrier = pltpu.get_barrier_semaphore()
    for axis, bit in weight_order:
        pl.semaphore_signal(
            barrier,
            inc=1,
            device_id={axis: side(axis, bit)[1]},
            device_id_type=pl.DeviceIdType.MESH,
        )
    pl.semaphore_wait(barrier, bits)

    lane_labels = [list(labels)]
    for label in weight_order:
        lane_labels.append([other for other in lane_labels[-1] if other != label])

    def lane_copy(number, k):
        first, sums, got, _ = lanes[number]
        source = first if k == 0 else sums[k - 1]
        axis, bit = weight_order[k]
        mine, partner = side(axis, bit)
        dim = lane_labels[k].index((axis, bit))
        return pltpu.make_async_remote_copy(
            src_ref=source.at[pick(dim, 1 - mine)],
            dst_ref=got[k],
            send_sem=lane_send.at[number, k],
            recv_sem=lane_get.at[number, k],
            device_id={axis: partner},
            device_id_type=pl.DeviceIdType.MESH,
        )

    def lane_start(k):
        for number in range(2):
            lane_copy(number, k).start()

    def lane_add(k):
        axis, bit = weight_order[k]
        mine, _ = side(axis, bit)
        dim = lane_labels[k].index((axis, bit))
        left = bits - 1 - k
        for number, (first, sums, got, out) in enumerate(lanes):
            source = first if k == 0 else sums[k - 1]
            lane_copy(number, k).wait_recv()

            def one(at):
                here = at[:dim] + (mine,) + at[dim:]
                return source[here].astype(jnp.float32) + got[k][at].astype(jnp.float32)

            if left == 0:
                out[...] = one(())
            else:
                target = sums[k]

                def body(i, carry):
                    at = digits(i, left)
                    target[at] = one(at).astype(target.dtype)
                    return carry

                lax.fori_loop(0, 1 << left, body, 0)

    lane_start(0)

    units = []
    for place in range(max(size for _, size, _ in groups)):
        for g, (begin, size, order) in enumerate(groups):
            if place < size:
                units.append((begin + place, g, place, order))

    def loads(n):
        unit, g, place, _ = units[n]
        slot = n % 2
        return (
            pltpu.make_async_copy(keep_ref.at[unit], load_keep.at[slot], load_sem.at[slot, 0]),
            pltpu.make_async_copy(
                came_refs[g].at[place], load_came.at[slot], load_sem.at[slot, 1]
            ),
        )

    def unit_copy(unit, order, k):
        axis, bit = order[k + 1]
        return pltpu.make_async_remote_copy(
            src_ref=sends[k].at[unit],
            dst_ref=gets[k].at[unit],
            send_sem=unit_send.at[unit, k],
            recv_sem=unit_get.at[unit, k],
            device_id={axis: side(axis, bit)[1]},
            device_id_type=pl.DeviceIdType.MESH,
        )

    def unit_add(unit, order, k, left, right):
        mine, _ = side(*order[k + 1])
        half = spots >> (k + 1)

        def fill(target, which):
            def body(i, carry):
                piece = i // blocks
                own = pl.ds(pl.multiple_of((i % blocks) * rows, rows), rows)
                total = left[which * half + piece, own, :].astype(jnp.float32) + right[
                    which * half + piece, own, :
                ].astype(jnp.float32)
                target[unit, piece, own, :] = total.astype(jnp.bfloat16)
                return carry

            lax.fori_loop(0, half * blocks, body, 0)

        fill(sends[k], 1 - mine)
        unit_copy(unit, order, k).start()
        fill(keeps[k], mine)

    def begin_unit(n):
        unit, _, _, order = units[n]
        for copy in loads(n):
            copy.wait()
        unit_add(unit, order, 0, load_keep.at[n % 2], load_came.at[n % 2])
        if n + 2 < len(units):
            for copy in loads(n + 2):
                copy.start()

    def next_unit(n, k):
        unit, _, _, order = units[n]
        unit_copy(unit, order, k - 1).wait_recv()
        unit_add(unit, order, k, keeps[k - 1].at[unit], gets[k - 1].at[unit])

    def end_unit(n):
        unit, _, _, order = units[n]
        unit_copy(unit, order, steps - 1).wait_recv()
        total = keeps[-1][unit, 0].astype(jnp.float32) + gets[-1][unit, 0].astype(jnp.float32)
        up_ref[unit] = total[:share]
        pieces = width // share
        rest = tall - share
        for p in range(pieces):
            down_ref[unit, p * rest : (p + 1) * rest, :] = total[
                share:, p * share : (p + 1) * share
            ]

    for n in range(min(2, len(units))):
        for copy in loads(n):
            copy.start()
    work = [functools.partial(begin_unit, n) for n in range(len(units))]
    for k in range(1, steps):
        work += [functools.partial(next_unit, n, k) for n in range(len(units))]
    work += [functools.partial(end_unit, n) for n in range(len(units))]
    marks = [len(units) + (len(work) - len(units)) * k // bits for k in range(bits)]
    for number, job in enumerate(work):
        for k, mark in enumerate(marks[:-1]):
            if number == mark:
                lane_add(k)
                lane_start(k + 1)
        job()
    lane_add(bits - 1)
    for unit, _, _, order in units:
        for k in range(steps):
            unit_copy(unit, order, k).wait_send()
    for k in range(bits):
        for number in range(2):
            lane_copy(number, k).wait_send()


def reduce_rest(keep, came, weights, gains, groups, labels, weight_order, share):
    count, spots, tall, width = keep.shape
    bits = len(labels)
    steps = len(groups[0][2]) - 1
    anywhere = pl.BlockSpec(memory_space=pl.ANY)
    vmem = pl.BlockSpec(memory_space=pltpu.VMEM)
    scratch = []
    for k in range(steps):
        scratch += [pltpu.VMEM((count, spots >> (k + 1), tall, width), jnp.bfloat16)] * 3
    for lane in (weights, gains):
        tail = lane.shape[bits:]
        shapes = [pltpu.VMEM((2,) * (bits - 1 - k) + tail, lane.dtype) for k in range(bits)]
        scratch += shapes[:-1] + shapes
    scratch += [
        pltpu.VMEM((2, spots, tall, width), jnp.bfloat16),
        pltpu.VMEM((2, spots, tall, width), jnp.bfloat16),
        pltpu.SemaphoreType.DMA((2, 2)),
        pltpu.SemaphoreType.DMA((count, steps)),
        pltpu.SemaphoreType.DMA((count, steps)),
        pltpu.SemaphoreType.DMA((2, bits)),
        pltpu.SemaphoreType.DMA((2, bits)),
    ]
    return pl.pallas_call(
        functools.partial(
            reduce_kernel, groups=groups, labels=labels, weight_order=weight_order, share=share
        ),
        out_shape=(
            jax.ShapeDtypeStruct((count, share, width), jnp.float32),
            jax.ShapeDtypeStruct((count, (tall - share) * (width // share), share), jnp.float32),
            jax.ShapeDtypeStruct(weights.shape[bits:], jnp.float32),
            jax.ShapeDtypeStruct(gains.shape[bits:], jnp.float32),
        ),
        in_specs=[anywhere] * (1 + len(came)) + [vmem] * 2,
        out_specs=[vmem] * 4,
        scratch_shapes=scratch,
        compiler_params=pltpu.CompilerParams(
            collective_id=0, has_side_effects=True, vmem_limit_bytes=67 * 1000 * 1000
        ),
        name="reduce_rest",
    )(keep, *came, weights, gains)


def on_device(
    tokens,
    segments,
    routes,
    attn_gain,
    w_query,
    w_key,
    w_value,
    w_out,
    mlp_gain,
    w_router,
    w_gate_up,
    w_down,
    cotangent,
    *,
    n_ep,
    n_rep,
):
    inputs = tokens[0]
    own_routes = routes[0]
    grad_output = cotangent[0]
    rows_dev, model_width = inputs.shape
    everyone = ("ep", "rep")
    heads = HEADS // n_rep
    head_width = heads * HEAD_DIM
    shared = max(1, n_rep // KV_HEADS)
    query_width = w_query.shape[1]
    key_width = w_key.shape[1]
    experts_all = w_router.shape[1]
    half_dim = HEAD_DIM // 2

    pack_ids = lax.all_gather(segments[0], "rep", axis=0, tiled=True)
    length = pack_ids.shape[0]
    blocks = length // BLOCK
    offset = lax.axis_index("rep") * rows_dev
    doc_start = jnp.sum((pack_ids[None, :] < pack_ids[:, None]).astype(jnp.int32), 1)
    position = (jnp.arange(length, dtype=jnp.int32) - doc_start).astype(jnp.float32)
    angles = (
        position[:, None]
        * jnp.exp(jnp.arange(half_dim, dtype=jnp.float32) * (-math.log(10000.0) / half_dim))[
            None, :
        ]
    )
    cosine = jnp.cos(angles)
    sine = jnp.sin(angles)
    cosine = jnp.concatenate([cosine, cosine], 1)
    sine = jnp.concatenate([-sine, sine], 1)
    own_cosine = lax.dynamic_slice_in_dim(cosine, offset, rows_dev, 0)
    own_sine = lax.dynamic_slice_in_dim(sine, offset, rows_dev, 0)
    starts = doc_start.reshape(blocks, 1, BLOCK)
    lows = doc_start[::BLOCK] // BLOCK

    joined = jnp.concatenate([w_query, w_key, w_value, w_out, w_router], 1)
    full = lax.all_gather(joined, everyone, axis=0, tiled=True)
    rotated_width = query_width + key_width
    input_width = rotated_width + key_width
    full_in = full[:, :input_width]
    full_out = full[:, input_width : input_width + model_width]
    full_router = full[:, input_width + model_width :]

    normed, factor_one = rms_norm(inputs, attn_gain)
    normed_b = normed.astype(jnp.bfloat16)
    mixed_in = product(normed_b, full_in)
    turn = mixed_in[:, :rotated_width]
    times = rotated_width // HEAD_DIM
    turned = turn * jnp.tile(own_cosine, (1, times)) + swap_halves(turn) * jnp.tile(
        own_sine, (1, times)
    )
    turned_b = turned.astype(jnp.bfloat16)
    value_b = mixed_in[:, rotated_width:].astype(jnp.bfloat16)
    query_part = turned_b[:, :query_width].reshape(rows_dev, n_rep, head_width)
    key_part = turned_b[:, query_width:].reshape(rows_dev, KV_HEADS, HEAD_DIM)
    value_part = value_b.reshape(rows_dev, KV_HEADS, HEAD_DIM)
    if shared > 1:
        key_part = jnp.repeat(key_part, shared, 1)
        value_part = jnp.repeat(value_part, shared, 1)
    sending = jnp.concatenate([query_part, key_part, value_part], 2).transpose(1, 0, 2)
    head_rows = lax.all_to_all(sending, "rep", split_axis=0, concat_axis=0, tiled=True)
    head_rows = head_rows.reshape(length, head_width + 2 * HEAD_DIM)
    mixed, mixed_out, totals = attend_forward(head_rows, starts, lows, heads)
    mixed_rows = lax.all_to_all(
        mixed.reshape(n_rep, rows_dev, head_width), "rep", split_axis=0, concat_axis=0, tiled=True
    )
    mixed_rows = mixed_rows.transpose(1, 0, 2).reshape(rows_dev, query_width)
    hidden = inputs + branch_scale * product(mixed_rows, full_out)

    normed_two, factor_two = rms_norm(hidden, mlp_gain)
    normed_two_b = normed_two.astype(jnp.bfloat16)
    router_f = full_router.astype(jnp.float32)
    logits = product(normed_two_b, full_router)
    numbers = jnp.arange(experts_all, dtype=jnp.int32)
    onehot = jnp.sum((own_routes[:, :, None] == numbers).astype(jnp.float32), 1)
    chosen = onehot > 0.5
    peak = jnp.max(jnp.where(chosen, logits, far_below), 1, keepdims=True)
    raised = jnp.where(chosen, jnp.exp(jnp.minimum(logits - peak, 0.0)), 0.0)
    probs = raised / jnp.sum(raised, 1, keepdims=True)
    before = (
        lax.broadcasted_iota(jnp.int32, (rows_dev, rows_dev), 0)
        > lax.broadcasted_iota(jnp.int32, (rows_dev, rows_dev), 1)
    ).astype(jnp.bfloat16)
    rank = product(before, onehot.astype(jnp.bfloat16))
    kept = chosen & (rank < CAP)
    rank_sent = jnp.where(kept, rank, -1.0).T
    probs_sent = probs.T
    both_sent = jnp.concatenate(
        [rank_sent.reshape(n_ep, -1, rows_dev), probs_sent.reshape(n_ep, -1, rows_dev)], 1
    )
    both_all = lax.all_to_all(both_sent, "ep", split_axis=0, concat_axis=0, tiled=True)
    ranks = both_all[:, : experts_all // n_ep]
    prob_all = both_all[:, experts_all // n_ep :]
    expert_rows = lax.all_gather(normed_two_b, "ep", axis=0, tiled=True)
    expert_cots = lax.all_gather(grad_output.astype(jnp.bfloat16), "ep", axis=0, tiled=True)
    rep_bits = [("rep", b) for b in range(bits_of(n_rep))]
    ep_bits = [("ep", b) for b in range(bits_of(n_ep))]
    count = experts_all // n_ep
    sizes = [(count - count // 4) // 2, count - count // 4 - (count - count // 4) // 2, count // 4]
    groups = []
    for g, size in enumerate(sizes):
        lead = [0, len(rep_bits) - 2, len(rep_bits) - 1][g]
        groups.append(
            (sum(sizes[:g]), size, [lead] + [b for b in range(len(rep_bits)) if b != lead])
        )
    out_sum, grad_sum, inner, grad_keep, *grad_send = experts(
        lax.axis_index("rep").astype(jnp.int32).reshape(1),
        expert_rows,
        expert_cots,
        ranks,
        prob_all,
        w_gate_up,
        w_down,
        n_rep,
        groups,
    )
    came = [swap(sent, "rep", order[0]) for sent, (_, _, order) in zip(grad_send, groups)]
    out_back = lax.all_to_all(
        out_sum.reshape(n_ep, rows_dev, model_width), "ep", split_axis=0, concat_axis=0, tiled=True
    )
    grad_back = lax.all_to_all(
        grad_sum.reshape(n_ep, rows_dev, model_width), "ep", split_axis=0, concat_axis=0, tiled=True
    )
    inner_back = lax.all_to_all(inner, "ep", split_axis=0, concat_axis=0, tiled=True)
    output = hidden + branch_scale * jnp.sum(out_back.astype(jnp.float32), 0)
    grad_probs = inner_back.reshape(experts_all, rows_dev).T
    grad_logits = probs * (grad_probs - jnp.sum(grad_probs * probs, -1, keepdims=True))
    normed_two_f = normed_two_b.astype(jnp.float32)
    grad_router = jnp.dot(normed_two_f.T, grad_logits, precision=lax.Precision.HIGHEST)
    grad_normed_two = jnp.sum(grad_back.astype(jnp.float32), 0) + jnp.dot(
        grad_logits, router_f.T, precision=lax.Precision.HIGHEST
    )
    grad_hidden_norm, grad_mlp_gain = norm_back(grad_normed_two, hidden, factor_two, mlp_gain)
    grad_hidden = grad_output + grad_hidden_norm
    grad_attn = (branch_scale * grad_hidden).astype(jnp.bfloat16)
    grad_out_w = dot_tn(mixed_rows, grad_attn)
    grad_mixed = dot_nt(grad_attn, full_out).astype(jnp.bfloat16)
    grad_heads = lax.all_to_all(
        grad_mixed.reshape(rows_dev, n_rep, head_width).transpose(1, 0, 2),
        "rep",
        split_axis=0,
        concat_axis=0,
        tiled=True,
    ).reshape(length, head_width)
    grad_query, grad_key, grad_value = attend_backward(
        head_rows, grad_heads, mixed_out, totals, starts, lows, heads
    )
    turn_back = jnp.concatenate([grad_query, grad_key], 1)
    turn_back = turn_back * jnp.tile(cosine, (1, heads + 1)) - swap_halves(turn_back) * jnp.tile(
        sine, (1, heads + 1)
    )
    returning = jnp.concatenate([turn_back, grad_value], 1).astype(jnp.bfloat16)
    returned = lax.all_to_all(
        returning.reshape(n_rep, rows_dev, head_width + 2 * HEAD_DIM),
        "rep",
        split_axis=0,
        concat_axis=0,
        tiled=True,
    ).transpose(1, 0, 2)
    grad_query_rows = returned[:, :, :head_width].reshape(rows_dev, query_width)
    key_back = returned[:, :, head_width : head_width + HEAD_DIM]
    value_back = returned[:, :, head_width + HEAD_DIM :]
    if shared > 1:
        key_back = jnp.sum(
            key_back.reshape(rows_dev, KV_HEADS, shared, HEAD_DIM).astype(jnp.float32), 2
        ).astype(jnp.bfloat16)
        value_back = jnp.sum(
            value_back.reshape(rows_dev, KV_HEADS, shared, HEAD_DIM).astype(jnp.float32), 2
        ).astype(jnp.bfloat16)
    grad_in_rows = jnp.concatenate(
        [
            grad_query_rows,
            key_back.reshape(rows_dev, key_width),
            value_back.reshape(rows_dev, key_width),
        ],
        1,
    )
    grad_w_in = dot_tn(normed_b, grad_in_rows)
    grad_normed = dot_nt(grad_in_rows, full_in)
    grad_inputs_norm, grad_attn_gain = norm_back(grad_normed, inputs, factor_one, attn_gain)
    grad_inputs = grad_hidden + grad_inputs_norm
    everything = n_ep * n_rep
    gains = jnp.concatenate(
        [grad_attn_gain.reshape(everything, -1), grad_mlp_gain.reshape(everything, -1)], 1
    )
    labels = ep_bits[::-1] + rep_bits[::-1]
    shape = (2,) * len(labels)
    weight_grads = jnp.concatenate([grad_w_in, grad_out_w, grad_router], 1).astype(jnp.bfloat16)
    expert_up, expert_down, weights, gains = reduce_rest(
        grad_keep,
        came,
        weight_grads.reshape(shape + (-1, weight_grads.shape[1])),
        gains.reshape(shape + (1, -1)),
        [(begin, size, [("rep", b) for b in order]) for begin, size, order in groups],
        labels,
        ep_bits + rep_bits,
        model_width // n_rep,
    )
    gains = gains[0]
    part = model_width // everything
    return (
        output[None],
        grad_inputs[None],
        gains[:part],
        weights[:, :query_width],
        weights[:, query_width:rotated_width],
        weights[:, rotated_width:input_width],
        weights[:, input_width : input_width + model_width],
        gains[part:],
        weights[:, input_width + model_width :],
        expert_up,
        expert_down,
    )


def solution(mesh):
    placed = (
        P("ep", "rep", None),
        P("ep", "rep"),
        P("ep", "rep", None),
        P(),
        P(("ep", "rep"), None),
        P(("ep", "rep"), None),
        P(("ep", "rep"), None),
        P(("ep", "rep"), None),
        P(),
        P(("ep", "rep"), None),
        P("ep", None, None),
        P("ep", None, None),
        P("ep", "rep", None),
    )
    return jax.shard_map(
        functools.partial(on_device, n_ep=mesh.shape["ep"], n_rep=mesh.shape["rep"]),
        mesh=mesh,
        in_specs=placed,
        out_specs=(
            P("ep", "rep", None),
            P("ep", "rep", None),
            P(("ep", "rep")),
            P(("ep", "rep"), None),
            P(("ep", "rep"), None),
            P(("ep", "rep"), None),
            P(("ep", "rep"), None),
            P(("ep", "rep")),
            P(("ep", "rep"), None),
            P("ep", "rep", None),
            P("ep", None, "rep"),
        ),
        check_vma=False,
    )
```

```python
import functools
import math

import jax
import jax.numpy as jnp
from jax import lax
from jax.experimental import pallas as pl
from jax.experimental.pallas import tpu as pltpu
from jax.sharding import PartitionSpec as P

HEADS = 16
KV_HEADS = 8
HEAD_DIM = 64
CAP = 80
BLOCK = 256

epsilon = 1e-06
score_scale = 0.015625
branch_scale = 0.22
far_below = -1e30

NT = (((1,), (1,)), ((), ()))
TN = (((0,), (0,)), ((), ()))


def product(left, right):
    return jnp.dot(left, right, preferred_element_type=jnp.float32)


def dot_nt(left, right):
    return lax.dot_general(left, right, NT, preferred_element_type=jnp.float32)


def dot_tn(left, right):
    return lax.dot_general(left, right, TN, preferred_element_type=jnp.float32)


def rms_norm(values, gain):
    factor = lax.rsqrt(jnp.mean(values * values, -1, keepdims=True) + epsilon)
    return (values * factor * gain, factor)


def norm_back(grad_normed, values, factor, gain):
    scaled = grad_normed * gain
    gain_part = jnp.sum(grad_normed * values * factor, 0)
    inner_sum = jnp.mean(scaled * values, -1, keepdims=True)
    return (factor * scaled - values * (factor * factor * factor) * inner_sum, gain_part)


def swap_halves(values):
    count, width = values.shape
    half_dim = HEAD_DIM // 2
    lane = lax.broadcasted_iota(jnp.int32, values.shape, 1)
    return jnp.where(
        lane % HEAD_DIM < half_dim,
        jnp.roll(values, -half_dim, 1),
        jnp.roll(values, half_dim, 1),
    )


def attend_forward_kernel(
    low_ref, rows_ref, start_ref, mixed_ref, out_ref, total_ref, key_s, value_s, *, heads
):
    step = pl.program_id(0)
    width = heads * HEAD_DIM

    @pl.when(step == 0)
    def _():
        key_s[...] = rows_ref[:, width : width + HEAD_DIM]
        value_s[...] = rows_ref[:, width + HEAD_DIM : width + 2 * HEAD_DIM]

    block_rows = rows_ref[pl.ds(pl.multiple_of(step * BLOCK, BLOCK), BLOCK), :]
    queries = [
        block_rows[:, h * HEAD_DIM : (h + 1) * HEAD_DIM] * jnp.bfloat16(score_scale)
        for h in range(heads)
    ]
    starts = start_ref[0]
    at = step * BLOCK + lax.broadcasted_iota(jnp.int32, (1, BLOCK), 1)

    def one(j, carry):
        rows = pl.ds(pl.multiple_of(j * BLOCK, BLOCK), BLOCK)
        key_block = key_s[rows, :]
        value_block = value_s[rows, :]
        place = j * BLOCK + lax.broadcasted_iota(jnp.int32, (BLOCK, BLOCK), 0)
        allowed = (place >= starts) & (place <= at)
        result = []
        for h in range(heads):
            peak, total, mixed = carry[h]
            scores = jnp.where(allowed, dot_nt(key_block, queries[h]), far_below)
            new_peak = jnp.maximum(peak, jnp.max(scores, 0, keepdims=True))
            fade = jnp.exp(peak - new_peak)
            raised = jnp.exp(scores - new_peak)
            total = fade * total + jnp.sum(raised, 0, keepdims=True)
            mixed = fade * mixed + dot_tn(value_block, raised.astype(jnp.bfloat16))
            result.append((new_peak, total, mixed))
        return tuple(result)

    first = tuple(
        (
            jnp.full((1, BLOCK), far_below, jnp.float32),
            jnp.zeros((1, BLOCK), jnp.float32),
            jnp.zeros((HEAD_DIM, BLOCK), jnp.float32),
        )
        for _ in range(heads)
    )
    done = lax.fori_loop(low_ref[step], step + 1, one, first)
    for h in range(heads):
        peak, total, mixed = done[h]
        mixed = mixed / total
        out_ref[h * HEAD_DIM : (h + 1) * HEAD_DIM, :] = mixed
        total_ref[0, h : h + 1, :] = peak + jnp.log(total)
        mixed_ref[:, h * HEAD_DIM : (h + 1) * HEAD_DIM] = mixed.T.astype(jnp.bfloat16)


def attend_forward(rows, starts, lows, heads):
    length, width = rows.shape
    blocks = length // BLOCK
    whole = lambda i, low: (0, 0)
    return pl.pallas_call(
        functools.partial(attend_forward_kernel, heads=heads),
        out_shape=(
            jax.ShapeDtypeStruct((length, heads * HEAD_DIM), jnp.bfloat16),
            jax.ShapeDtypeStruct((heads * HEAD_DIM, length), jnp.float32),
            jax.ShapeDtypeStruct((blocks, heads, BLOCK), jnp.float32),
        ),
        grid_spec=pltpu.PrefetchScalarGridSpec(
            num_scalar_prefetch=1,
            grid=(blocks,),
            in_specs=[
                pl.BlockSpec((length, width), whole),
                pl.BlockSpec((1, 1, BLOCK), lambda i, low: (i, 0, 0)),
            ],
            out_specs=[
                pl.BlockSpec((BLOCK, heads * HEAD_DIM), lambda i, low: (i, 0)),
                pl.BlockSpec((heads * HEAD_DIM, BLOCK), lambda i, low: (0, i)),
                pl.BlockSpec((1, heads, BLOCK), lambda i, low: (i, 0, 0)),
            ],
            scratch_shapes=[
                pltpu.VMEM((length, HEAD_DIM), jnp.bfloat16),
                pltpu.VMEM((length, HEAD_DIM), jnp.bfloat16),
            ],
        ),
        name="attend_forward",
    )(lows, rows, starts)


def attend_backward_kernel(
    low_ref,
    rows_ref,
    grad_ref,
    out_ref,
    total_ref,
    start_ref,
    grad_query_ref,
    grad_key_ref,
    grad_value_ref,
    key_s,
    value_s,
    *,
    heads,
):
    step = pl.program_id(0)
    width = heads * HEAD_DIM

    @pl.when(step == 0)
    def _():
        key_s[...] = rows_ref[:, width : width + HEAD_DIM]
        value_s[...] = rows_ref[:, width + HEAD_DIM : width + 2 * HEAD_DIM]
        grad_key_ref[...] = jnp.zeros_like(grad_key_ref)
        grad_value_ref[...] = jnp.zeros_like(grad_value_ref)

    own = pl.ds(pl.multiple_of(step * BLOCK, BLOCK), BLOCK)
    block_rows = rows_ref[own, :]
    grads_all = grad_ref[...]
    starts = start_ref[0]
    at = step * BLOCK + lax.broadcasted_iota(jnp.int32, (1, BLOCK), 1)
    queries, scaled, grads, inners, totals = [], [], [], [], []
    for h in range(heads):
        span = slice(h * HEAD_DIM, (h + 1) * HEAD_DIM)
        queries.append(block_rows[:, span])
        scaled.append(block_rows[:, span] * jnp.bfloat16(score_scale))
        grads.append(grads_all[:, span])
        turned = grads_all[:, span].astype(jnp.float32).T
        inners.append(jnp.sum(turned * out_ref[span, :], 0, keepdims=True))
        totals.append(total_ref[0, h : h + 1, :])

    def one(j, carry):
        rows = pl.ds(pl.multiple_of(j * BLOCK, BLOCK), BLOCK)
        key_block = key_s[rows, :]
        value_block = value_s[rows, :]
        place = j * BLOCK + lax.broadcasted_iota(jnp.int32, (BLOCK, BLOCK), 0)
        allowed = (place >= starts) & (place <= at)
        result = []
        key_sum = grad_key_ref[rows, :]
        value_sum = grad_value_ref[rows, :]
        for h in range(heads):
            scores = jnp.where(allowed, dot_nt(key_block, scaled[h]), far_below)
            prob = jnp.exp(scores - totals[h])
            grad_prob = dot_nt(value_block, grads[h])
            grad_scores = (prob * (grad_prob - inners[h]) * score_scale).astype(jnp.bfloat16)
            value_sum = value_sum + product(prob.astype(jnp.bfloat16), grads[h])
            key_sum = key_sum + product(grad_scores, queries[h])
            result.append(carry[h] + dot_tn(grad_scores, key_block))
        grad_key_ref[rows, :] = key_sum
        grad_value_ref[rows, :] = value_sum
        return tuple(result)

    first = tuple(jnp.zeros((BLOCK, HEAD_DIM), jnp.float32) for _ in range(heads))
    done = lax.fori_loop(low_ref[step], step + 1, one, first)
    for h in range(heads):
        grad_query_ref[:, h * HEAD_DIM : (h + 1) * HEAD_DIM] = done[h]


def attend_backward(rows, grads, outs, totals, starts, lows, heads):
    length, width = rows.shape
    blocks = length // BLOCK
    whole = lambda i, low: (0, 0)
    return pl.pallas_call(
        functools.partial(attend_backward_kernel, heads=heads),
        out_shape=(
            jax.ShapeDtypeStruct((length, heads * HEAD_DIM), jnp.float32),
            jax.ShapeDtypeStruct((length, HEAD_DIM), jnp.float32),
            jax.ShapeDtypeStruct((length, HEAD_DIM), jnp.float32),
        ),
        grid_spec=pltpu.PrefetchScalarGridSpec(
            num_scalar_prefetch=1,
            grid=(blocks,),
            in_specs=[
                pl.BlockSpec((length, width), whole),
                pl.BlockSpec((BLOCK, heads * HEAD_DIM), lambda i, low: (i, 0)),
                pl.BlockSpec((heads * HEAD_DIM, BLOCK), lambda i, low: (0, i)),
                pl.BlockSpec((1, heads, BLOCK), lambda i, low: (i, 0, 0)),
                pl.BlockSpec((1, 1, BLOCK), lambda i, low: (i, 0, 0)),
            ],
            out_specs=[
                pl.BlockSpec((BLOCK, heads * HEAD_DIM), lambda i, low: (i, 0)),
                pl.BlockSpec((length, HEAD_DIM), whole),
                pl.BlockSpec((length, HEAD_DIM), whole),
            ],
            scratch_shapes=[
                pltpu.VMEM((length, HEAD_DIM), jnp.bfloat16),
                pltpu.VMEM((length, HEAD_DIM), jnp.bfloat16),
            ],
        ),
        name="attend_backward",
    )(lows, rows, grads, outs, totals, starts)


def bits_of(size):
    return max(size.bit_length() - 1, 0)


def swap(sent, axis, bit):
    size = lax.axis_size(axis)
    return lax.ppermute(sent, axis, [(i, i ^ (1 << bit)) for i in range(size)])


def side(axis, bit):
    index = lax.axis_index(axis)
    mine = (index // (1 << bit)) % 2
    return (mine, index + (1 - 2 * mine) * (1 << bit))


def pick(dim, index):
    return (slice(None),) * dim + (index,)


def digits(number, count):
    return tuple((number // (1 << (count - 1 - k))) % 2 for k in range(count))


def mesh_copy(source, target, sends, gets, axis, partner):
    return pltpu.make_async_remote_copy(
        src_ref=source,
        dst_ref=target,
        send_sem=sends,
        recv_sem=gets,
        device_id={axis: partner},
        device_id_type=pl.DeviceIdType.MESH,
    )


def greet(partners):
    barrier = pltpu.get_barrier_semaphore()
    for axis, partner in partners:
        pl.semaphore_signal(
            barrier, inc=1, device_id={axis: partner}, device_id_type=pl.DeviceIdType.MESH
        )
    pl.semaphore_wait(barrier, len(partners))


class Lane:
    def __init__(self, labels, order, first, refs, sends, gets, rows=None):
        bits = len(labels)
        self.order, self.first, self.sends, self.gets = (order, first, sends, gets)
        self.sums, self.got = (refs[: bits - 1], refs[bits - 1 : 2 * bits - 1])
        self.labels = [list(labels)]
        for label in order:
            self.labels.append([other for other in self.labels[-1] if other != label])
        self.rows = rows

    @staticmethod
    def scratch(bits, tail, dtype):
        shapes = [pltpu.VMEM((2,) * (bits - 1 - k) + tail, dtype) for k in range(bits)]
        return shapes[:-1] + shapes

    def source(self, k):
        return self.first if k == 0 else self.sums[k - 1]

    def copy(self, k):
        axis, bit = self.order[k]
        mine, partner = side(axis, bit)
        dim = self.labels[k].index((axis, bit))
        return mesh_copy(
            self.source(k).at[pick(dim, 1 - mine)],
            self.got[k],
            self.sends.at[k],
            self.gets.at[k],
            axis,
            partner,
        )

    def start(self, k):
        self.copy(k).start()

    def add(self, k, out=None):
        axis, bit = self.order[k]
        mine, _ = side(axis, bit)
        dim = self.labels[k].index((axis, bit))
        left = len(self.order) - 1 - k
        self.copy(k).wait_recv()
        source, got = (self.source(k), self.got[k])
        target = out if left == 0 else self.sums[k]
        height = got.shape[left]
        rows = self.rows or height
        blocks = height // rows

        def body(i, carry):
            at = digits(i // blocks, left)
            own = pl.ds(pl.multiple_of((i % blocks) * rows, rows), rows)
            if blocks == 1:
                own = slice(None)
            here = at[:dim] + (mine,) + at[dim:]
            total = source[here + (own,)].astype(jnp.float32) + got[at + (own,)].astype(
                jnp.float32
            )
            target[at + (own,)] = total.astype(target.dtype)
            return carry

        lax.fori_loop(0, blocks << left, body, 0)

    def finish(self):
        for k in range(len(self.order)):
            self.copy(k).wait_send()


def reduce_kernel(*refs, units, n_came, labels, weight_order, share):
    keep_ref, *refs = refs
    came_refs, refs = (refs[:n_came], refs[n_came:])
    weight_ref, gain_ref, up_ref, down_ref, weight_out, gain_out, *refs = refs
    steps = len(units[0][3]) - 1
    sends, keeps, gets = ([], [], [])
    for _ in range(steps):
        sends.append(refs[0])
        keeps.append(refs[1])
        gets.append(refs[2])
        refs = refs[3:]
    bits = len(labels)
    lane_refs, refs = (refs[: 2 * (2 * bits - 1)], refs[2 * (2 * bits - 1) :])
    load_keep, load_came, load_sem, unit_send, unit_get, lane_send, lane_get = refs
    lanes = [
        Lane(
            labels,
            weight_order,
            first,
            lane_refs[number * (2 * bits - 1) : (number + 1) * (2 * bits - 1)],
            lane_send.at[number],
            lane_get.at[number],
        )
        for number, first in enumerate((weight_ref, gain_ref))
    ]
    count, spots, tall, width = keep_ref.shape
    rows = 32 if tall % 32 == 0 else tall
    blocks = tall // rows

    greet([(axis, side(axis, bit)[1]) for axis, bit in weight_order])

    def lane_start(k):
        for lane in lanes:
            lane.start(k)

    def lane_add(k):
        for lane, out in zip(lanes, (weight_out, gain_out)):
            lane.add(k, out)

    lane_start(0)

    def loads(n):
        unit, g, place, _ = units[n]
        slot = n % 2
        return (
            pltpu.make_async_copy(keep_ref.at[unit], load_keep.at[slot], load_sem.at[slot, 0]),
            pltpu.make_async_copy(
                came_refs[g].at[place], load_came.at[slot], load_sem.at[slot, 1]
            ),
        )

    def unit_copy(unit, order, k):
        axis, bit = order[k + 1]
        return mesh_copy(
            sends[k].at[unit],
            gets[k].at[unit],
            unit_send.at[unit, k],
            unit_get.at[unit, k],
            axis,
            side(axis, bit)[1],
        )

    def unit_add(unit, order, k, left, right):
        mine, _ = side(*order[k + 1])
        half = spots >> (k + 1)

        def fill(target, which):
            def body(i, carry):
                piece = i // blocks
                own = pl.ds(pl.multiple_of((i % blocks) * rows, rows), rows)
                total = left[which * half + piece, own, :].astype(jnp.float32) + right[
                    which * half + piece, own, :
                ].astype(jnp.float32)
                target[unit, piece, own, :] = total.astype(jnp.bfloat16)
                return carry

            lax.fori_loop(0, half * blocks, body, 0)

        fill(sends[k], 1 - mine)
        unit_copy(unit, order, k).start()
        fill(keeps[k], mine)

    def begin_unit(n):
        unit, _, _, order = units[n]
        for copy in loads(n):
            copy.wait()
        unit_add(unit, order, 0, load_keep.at[n % 2], load_came.at[n % 2])
        if n + 2 < len(units):
            for copy in loads(n + 2):
                copy.start()

    def next_unit(n, k):
        unit, _, _, order = units[n]
        unit_copy(unit, order, k - 1).wait_recv()
        unit_add(unit, order, k, keeps[k - 1].at[unit], gets[k - 1].at[unit])

    def end_unit(n):
        unit, _, _, order = units[n]
        unit_copy(unit, order, steps - 1).wait_recv()
        total = keeps[-1][unit, 0].astype(jnp.float32) + gets[-1][unit, 0].astype(jnp.float32)
        up_ref[unit] = total[:share]
        pieces = width // share
        rest = tall - share
        for p in range(pieces):
            down_ref[unit, p * rest : (p + 1) * rest, :] = total[
                share:, p * share : (p + 1) * share
            ]

    for n in range(min(2, len(units))):
        for copy in loads(n):
            copy.start()
    work = [functools.partial(begin_unit, n) for n in range(len(units))]
    for k in range(1, steps):
        work += [functools.partial(next_unit, n, k) for n in range(len(units))]
    work += [functools.partial(end_unit, n) for n in range(len(units))]
    marks = [len(units) + (len(work) - len(units)) * k // bits for k in range(bits)]
    for number, job in enumerate(work):
        for k, mark in enumerate(marks[:-1]):
            if number == mark:
                lane_add(k)
                lane_start(k + 1)
        job()
    lane_add(bits - 1)
    for unit, _, _, order in units:
        for k in range(steps):
            unit_copy(unit, order, k).wait_send()
    for lane in lanes:
        lane.finish()


def reduce_rest(keep, came, weights, gains, units, labels, weight_order, share):
    count, spots, tall, width = keep.shape
    bits = len(labels)
    steps = len(units[0][3]) - 1
    anywhere = pl.BlockSpec(memory_space=pl.ANY)
    vmem = pl.BlockSpec(memory_space=pltpu.VMEM)
    scratch = []
    for k in range(steps):
        scratch += [pltpu.VMEM((count, spots >> (k + 1), tall, width), jnp.bfloat16)] * 3
    for lane in (weights, gains):
        scratch += Lane.scratch(bits, lane.shape[bits:], lane.dtype)
    scratch += [
        pltpu.VMEM((2, spots, tall, width), jnp.bfloat16),
        pltpu.VMEM((2, spots, tall, width), jnp.bfloat16),
        pltpu.SemaphoreType.DMA((2, 2)),
        pltpu.SemaphoreType.DMA((count, steps)),
        pltpu.SemaphoreType.DMA((count, steps)),
        pltpu.SemaphoreType.DMA((2, bits)),
        pltpu.SemaphoreType.DMA((2, bits)),
    ]
    return pl.pallas_call(
        functools.partial(
            reduce_kernel,
            units=units,
            n_came=len(came),
            labels=labels,
            weight_order=weight_order,
            share=share,
        ),
        out_shape=(
            jax.ShapeDtypeStruct((count, share, width), jnp.float32),
            jax.ShapeDtypeStruct((count, (tall - share) * (width // share), share), jnp.float32),
            jax.ShapeDtypeStruct(weights.shape[bits:], jnp.float32),
            jax.ShapeDtypeStruct(gains.shape[bits:], jnp.float32),
        ),
        in_specs=[anywhere] * (1 + len(came)) + [vmem] * 2,
        out_specs=[vmem] * 4,
        scratch_shapes=scratch,
        compiler_params=pltpu.CompilerParams(
            collective_id=0, has_side_effects=True, vmem_limit_bytes=67 * 1000 * 1000
        ),
        name="reduce_rest",
    )(keep, *came, weights, gains)


def experts_kernel(
    *refs, sources, rows_dev, count, copies, orders, near, labels, ep_order
):
    rows_hbm, cot_hbm, rank_ref, prob_ref, gate_up_ref, down_ref, *refs = refs
    out_ref, grad_ref, inner_ref, keep_ref, came_ref, *refs = refs
    far = count - near
    sent_refs, refs = (refs[:far], refs[far:])
    rows_s, cot_s, picks_s, out_s, grad_s, send_s, inner_s, inner_got, *refs = refs
    bits = len(labels)
    lane_refs, refs = (refs[: 2 * (2 * bits - 1)], refs[2 * (2 * bits - 1) :])
    load_sem, unit_send, unit_get, lane_send, lane_get, inner_send, inner_take = refs
    me = lax.axis_index("ep")
    step = pl.program_id(0)
    grad_lane, out_lane = [
        Lane(
            labels,
            ep_order,
            first,
            lane_refs[number * (2 * bits - 1) : (number + 1) * (2 * bits - 1)],
            lane_send.at[number],
            lane_get.at[number],
            rows=32,
        )
        for number, first in enumerate((cot_s, rows_s))
    ]

    def unit_copy(e):
        bit = orders[e][0]
        if e < near:
            return mesh_copy(
                send_s.at[e],
                came_ref.at[e],
                unit_send.at[e],
                unit_get.at[e],
                "rep",
                side("rep", bit)[1],
            )
        return pltpu.make_async_copy(send_s.at[e], sent_refs[e - near], unit_send.at[e])

    def inner_copy(d):
        peer = (me + d) % sources
        return mesh_copy(
            inner_s.at[peer],
            inner_got.at[me],
            inner_send.at[d - 1],
            inner_take.at[d - 1],
            "ep",
            peer,
        )

    @pl.when(step == 0)
    def _():
        loads = [
            pltpu.make_async_copy(rows_hbm, rows_s, load_sem.at[0]),
            pltpu.make_async_copy(cot_hbm, cot_s, load_sem.at[1]),
        ]
        for copy in loads:
            copy.start()
        partners = [("ep", (me + d) % sources) for d in range(1, sources)]
        for bit in sorted({order[0] for order in orders[:near]}):
            partners.append(("rep", side("rep", bit)[1]))
        greet(partners)
        for copy in loads:
            copy.wait()

    slots = pl.ds(pl.multiple_of(step * CAP, 16), CAP)
    numbers = lax.broadcasted_iota(jnp.int32, (CAP, rows_dev), 0).astype(jnp.float32)
    rows_in, cots, weights, picks = [], [], [], []
    for s in range(sources):
        rank = rank_ref[s, pl.ds(step, 1), :]
        pick_table = jnp.where(rank == numbers, 1.0, 0.0)
        weights.append(jnp.sum(pick_table * prob_ref[s, pl.ds(step, 1), :], 1, keepdims=True))
        pick_b = pick_table.astype(jnp.bfloat16)
        picks.append(pick_table)
        picks_s[s, slots, :] = pick_b
        rows_in.append(product(pick_b, rows_s[digits(s, bits)]).astype(jnp.bfloat16))
        cots.append(product(pick_b, cot_s[digits(s, bits)]))
    arrived = jnp.concatenate(rows_in, 0)
    weight = jnp.concatenate(weights, 0)
    grad_mix = branch_scale * jnp.concatenate(cots, 0)
    gate_up = gate_up_ref[0]
    down = down_ref[0]
    hidden_units = down.shape[0]
    both = product(arrived, gate_up)
    gate_part = both[:, :hidden_units]
    up_part = both[:, hidden_units:]
    sigmoid_gate = jax.nn.sigmoid(gate_part)
    active = (gate_part * sigmoid_gate * up_part).astype(jnp.bfloat16)
    produced = product(active, down).astype(jnp.bfloat16).astype(jnp.float32)
    inner = jnp.sum(grad_mix * produced, 1, keepdims=True)
    sent_out = (weight * produced).astype(jnp.bfloat16)
    grad_out = (weight * grad_mix).astype(jnp.bfloat16)
    grad_active = dot_nt(grad_out, down)
    grad_down = dot_tn(active, grad_out).astype(jnp.bfloat16)
    grad_gate = grad_active * up_part * sigmoid_gate * (1.0 + gate_part * (1.0 - sigmoid_gate))
    grad_up = grad_active * gate_part * sigmoid_gate
    grad_both = jnp.concatenate([grad_gate, grad_up], 1).astype(jnp.bfloat16)
    grad_gate_up = dot_tn(arrived, grad_both).astype(jnp.bfloat16)
    share = grad_down.shape[1] // copies
    tall = hidden_units // copies

    def put(order, mine):
        bit, *later = order
        for r in range(copies):
            spot = 0
            for b in later:
                spot = 2 * spot + ((r >> b) & 1)
            ref = keep_ref.at[0] if (r >> bit) & 1 == mine else send_s.at[step]
            ref[spot, :share, :] = grad_gate_up[r * share : (r + 1) * share]
            for k in range(copies):
                ref[spot, share : share + tall, k * share : (k + 1) * share] = grad_down[
                    k * tall : (k + 1) * tall, r * share : (r + 1) * share
                ]

    for order in {tuple(order): order for order in orders}.values():
        members = [e for e in range(count) if orders[e] == order]
        here = functools.reduce(jnp.logical_or, [step == e for e in members])
        side_mine, _ = side("rep", order[0])
        for mine in range(2):

            @pl.when(here & (side_mine == mine))
            def _(order=order, mine=mine):
                put(order, mine)

    grad_in = dot_nt(grad_both, gate_up).astype(jnp.bfloat16)
    for s in range(sources):
        part = slice(s * CAP, (s + 1) * CAP)
        out_s[s, slots, :] = sent_out[part]
        grad_s[s, slots, :] = grad_in[part]
        inner_s[s, pl.ds(step, 1), :] = jnp.sum(picks[s] * inner[part], 0, keepdims=True)
    for e in range(count):

        @pl.when(step == e)
        def _(e=e):
            unit_copy(e).start()

    @pl.when(step == count - 1)
    def _():
        for table_of, target, lane in ((grad_s, cot_s, grad_lane), (out_s, rows_s, out_lane)):
            for s in range(sources):
                target[digits(s, bits)] = dot_tn(picks_s[s], table_of[s]).astype(jnp.bfloat16)
            lane.start(0)
        for d in range(1, sources):
            inner_copy(d).start()
        for k in range(bits):
            for lane, total in ((grad_lane, grad_ref), (out_lane, out_ref)):
                lane.add(k, total)
                if k + 1 < bits:
                    lane.start(k + 1)
        inner_got[me] = inner_s[me]
        for d in range(1, sources):
            inner_copy(d).wait_recv()
        inner_ref[...] = inner_got[...]
        for d in range(1, sources):
            inner_copy(d).wait_send()
        grad_lane.finish()
        out_lane.finish()
        for e in range(count):
            unit_copy(e).wait()


def experts(rows, cots, ranks, probs, w_gate_up, w_down, copies, orders, near, labels, ep_order):
    sources, count, rows_dev = ranks.shape
    total, model_width = rows.shape
    hidden_units = w_down.shape[1]
    bits = len(labels)
    tall = model_width // copies + hidden_units // copies
    flat = lambda i: (0, 0)
    cube = lambda i: (0, 0, 0)
    once = pl.Buffered(1)
    anywhere = pl.BlockSpec(memory_space=pl.ANY)
    far = count - near
    shape = (2,) * bits + (rows_dev, model_width)
    piece = (copies // 2, tall, model_width)
    return pl.pallas_call(
        functools.partial(
            experts_kernel,
            sources=sources,
            rows_dev=rows_dev,
            count=count,
            copies=copies,
            orders=orders,
            near=near,
            labels=labels,
            ep_order=ep_order,
        ),
        out_shape=(
            jax.ShapeDtypeStruct((rows_dev, model_width), jnp.float32),
            jax.ShapeDtypeStruct((rows_dev, model_width), jnp.float32),
            jax.ShapeDtypeStruct((sources, count, rows_dev), jnp.float32),
            jax.ShapeDtypeStruct((count,) + piece, jnp.bfloat16),
            jax.ShapeDtypeStruct((near,) + piece, jnp.bfloat16),
        )
        + (jax.ShapeDtypeStruct(piece, jnp.bfloat16),) * far,
        grid=(count,),
        in_specs=[
            anywhere,
            anywhere,
            pl.BlockSpec((sources, count, rows_dev), cube, pipeline_mode=once),
            pl.BlockSpec((sources, count, rows_dev), cube, pipeline_mode=once),
            pl.BlockSpec((1, model_width, 2 * hidden_units), lambda i: (i, 0, 0)),
            pl.BlockSpec((1, hidden_units, model_width), lambda i: (i, 0, 0)),
        ],
        out_specs=[
            pl.BlockSpec((rows_dev, model_width), flat, pipeline_mode=once),
            pl.BlockSpec((rows_dev, model_width), flat, pipeline_mode=once),
            pl.BlockSpec((sources, count, rows_dev), cube, pipeline_mode=once),
            pl.BlockSpec((1,) + piece, lambda i: (i, 0, 0, 0)),
            anywhere,
        ]
        + [anywhere] * far,
        scratch_shapes=[
            pltpu.VMEM(shape, jnp.bfloat16),
            pltpu.VMEM(shape, jnp.bfloat16),
            pltpu.VMEM((sources, count * CAP, rows_dev), jnp.bfloat16),
            pltpu.VMEM((sources, count * CAP, model_width), jnp.bfloat16),
            pltpu.VMEM((sources, count * CAP, model_width), jnp.bfloat16),
            pltpu.VMEM((count,) + piece, jnp.bfloat16),
            pltpu.VMEM((sources, count, rows_dev), jnp.float32),
            pltpu.VMEM((sources, count, rows_dev), jnp.float32),
        ]
        + Lane.scratch(bits, (rows_dev, model_width), jnp.bfloat16) * 2
        + [
            pltpu.SemaphoreType.DMA((2,)),
            pltpu.SemaphoreType.DMA((count,)),
            pltpu.SemaphoreType.DMA((near,)),
            pltpu.SemaphoreType.DMA((2, bits)),
            pltpu.SemaphoreType.DMA((2, bits)),
            pltpu.SemaphoreType.DMA((sources - 1,)),
            pltpu.SemaphoreType.DMA((sources - 1,)),
        ],
        compiler_params=pltpu.CompilerParams(
            collective_id=1, has_side_effects=True, vmem_limit_bytes=67 * 1000 * 1000
        ),
        name="experts",
    )(rows.reshape(shape), cots.reshape(shape), ranks, probs, w_gate_up, w_down)


def on_device(
    tokens,
    segments,
    routes,
    attn_gain,
    w_query,
    w_key,
    w_value,
    w_out,
    mlp_gain,
    w_router,
    w_gate_up,
    w_down,
    cotangent,
    *,
    n_ep,
    n_rep,
):
    inputs = tokens[0]
    own_routes = routes[0]
    grad_output = cotangent[0]
    rows_dev, model_width = inputs.shape
    everyone = ("ep", "rep")
    heads = HEADS // n_rep
    head_width = heads * HEAD_DIM
    shared = max(1, n_rep // KV_HEADS)
    query_width = w_query.shape[1]
    key_width = w_key.shape[1]
    experts_all = w_router.shape[1]
    half_dim = HEAD_DIM // 2

    pack_ids = lax.all_gather(segments[0], "rep", axis=0, tiled=True)
    length = pack_ids.shape[0]
    blocks = length // BLOCK
    offset = lax.axis_index("rep") * rows_dev
    doc_start = jnp.sum((pack_ids[None, :] < pack_ids[:, None]).astype(jnp.int32), 1)
    position = (jnp.arange(length, dtype=jnp.int32) - doc_start).astype(jnp.float32)
    angles = (
        position[:, None]
        * jnp.exp(jnp.arange(half_dim, dtype=jnp.float32) * (-math.log(10000.0) / half_dim))[
            None, :
        ]
    )
    cosine = jnp.cos(angles)
    sine = jnp.sin(angles)
    cosine = jnp.concatenate([cosine, cosine], 1)
    sine = jnp.concatenate([-sine, sine], 1)
    own_cosine = lax.dynamic_slice_in_dim(cosine, offset, rows_dev, 0)
    own_sine = lax.dynamic_slice_in_dim(sine, offset, rows_dev, 0)
    starts = doc_start.reshape(blocks, 1, BLOCK)
    lows = doc_start[::BLOCK] // BLOCK

    joined = jnp.concatenate([w_query, w_key, w_value, w_out, w_router], 1)
    full = lax.all_gather(joined, everyone, axis=0, tiled=True)
    rotated_width = query_width + key_width
    input_width = rotated_width + key_width
    full_in = full[:, :input_width]
    full_out = full[:, input_width : input_width + model_width]
    full_router = full[:, input_width + model_width :]

    normed, factor_one = rms_norm(inputs, attn_gain)
    normed_b = normed.astype(jnp.bfloat16)
    mixed_in = product(normed_b, full_in)
    turn = mixed_in[:, :rotated_width]
    times = rotated_width // HEAD_DIM
    turned = turn * jnp.tile(own_cosine, (1, times)) + swap_halves(turn) * jnp.tile(
        own_sine, (1, times)
    )
    turned_b = turned.astype(jnp.bfloat16)
    value_b = mixed_in[:, rotated_width:].astype(jnp.bfloat16)
    query_part = turned_b[:, :query_width].reshape(rows_dev, n_rep, head_width)
    key_part = turned_b[:, query_width:].reshape(rows_dev, KV_HEADS, HEAD_DIM)
    value_part = value_b.reshape(rows_dev, KV_HEADS, HEAD_DIM)
    if shared > 1:
        key_part = jnp.repeat(key_part, shared, 1)
        value_part = jnp.repeat(value_part, shared, 1)
    sending = jnp.concatenate([query_part, key_part, value_part], 2).transpose(1, 0, 2)
    head_rows = lax.all_to_all(sending, "rep", split_axis=0, concat_axis=0, tiled=True)
    head_rows = head_rows.reshape(length, head_width + 2 * HEAD_DIM)
    mixed, mixed_out, totals = attend_forward(head_rows, starts, lows, heads)
    mixed_rows = lax.all_to_all(
        mixed.reshape(n_rep, rows_dev, head_width), "rep", split_axis=0, concat_axis=0, tiled=True
    )
    mixed_rows = mixed_rows.transpose(1, 0, 2).reshape(rows_dev, query_width)
    hidden = inputs + branch_scale * product(mixed_rows, full_out)

    normed_two, factor_two = rms_norm(hidden, mlp_gain)
    normed_two_b = normed_two.astype(jnp.bfloat16)
    router_f = full_router.astype(jnp.float32)
    logits = product(normed_two_b, full_router)
    numbers = jnp.arange(experts_all, dtype=jnp.int32)
    onehot = jnp.sum((own_routes[:, :, None] == numbers).astype(jnp.float32), 1)
    chosen = onehot > 0.5
    peak = jnp.max(jnp.where(chosen, logits, far_below), 1, keepdims=True)
    raised = jnp.where(chosen, jnp.exp(jnp.minimum(logits - peak, 0.0)), 0.0)
    probs = raised / jnp.sum(raised, 1, keepdims=True)
    before = (
        lax.broadcasted_iota(jnp.int32, (rows_dev, rows_dev), 0)
        > lax.broadcasted_iota(jnp.int32, (rows_dev, rows_dev), 1)
    ).astype(jnp.bfloat16)
    rank = product(before, onehot.astype(jnp.bfloat16))
    kept = chosen & (rank < CAP)
    rank_sent = jnp.where(kept, rank, -1.0).T
    probs_sent = probs.T
    both_sent = jnp.concatenate(
        [rank_sent.reshape(n_ep, -1, rows_dev), probs_sent.reshape(n_ep, -1, rows_dev)], 1
    )
    both_all = lax.all_to_all(both_sent, "ep", split_axis=0, concat_axis=0, tiled=True)
    ranks = both_all[:, : experts_all // n_ep]
    prob_all = both_all[:, experts_all // n_ep :]
    expert_rows = lax.all_gather(normed_two_b, "ep", axis=0, tiled=True)
    expert_cots = lax.all_gather(grad_output.astype(jnp.bfloat16), "ep", axis=0, tiled=True)
    rep_bits = [("rep", b) for b in range(bits_of(n_rep))]
    ep_bits = [("ep", b) for b in range(bits_of(n_ep))]
    count = experts_all // n_ep
    near = count * 5 // 8
    kinds = [2, 0, 1, 0, 1][:near] + [0, 1, 2][near - count :]
    leads = [0, len(rep_bits) - 2, len(rep_bits) - 1]
    orders = [
        [leads[kind]] + [b for b in range(len(rep_bits)) if b != leads[kind]] for kind in kinds
    ]
    out_sum, grad_sum, inner_back, grad_keep, came_near, *sent = experts(
        expert_rows,
        expert_cots,
        ranks,
        prob_all,
        w_gate_up,
        w_down,
        n_rep,
        orders,
        near,
        ep_bits[::-1],
        ep_bits,
    )
    came = [came_near] + [
        swap(half, "rep", order[0])[None] for half, order in zip(sent, orders[near:])
    ]
    units = [(e, 0, e, [("rep", b) for b in orders[e]]) for e in range(near)]
    units += [
        (e, 1 + e - near, 0, [("rep", b) for b in orders[e]]) for e in range(near, count)
    ]
    units = units[1:3] + units[:1] + units[3:]
    output = hidden + branch_scale * out_sum
    grad_probs = inner_back.reshape(experts_all, rows_dev).T
    grad_logits = probs * (grad_probs - jnp.sum(grad_probs * probs, -1, keepdims=True))
    normed_two_f = normed_two_b.astype(jnp.float32)
    grad_router = jnp.dot(normed_two_f.T, grad_logits, precision=lax.Precision.HIGHEST)
    grad_normed_two = grad_sum + jnp.dot(
        grad_logits, router_f.T, precision=lax.Precision.HIGHEST
    )
    grad_hidden_norm, grad_mlp_gain = norm_back(grad_normed_two, hidden, factor_two, mlp_gain)
    grad_hidden = grad_output + grad_hidden_norm
    grad_attn = (branch_scale * grad_hidden).astype(jnp.bfloat16)
    grad_out_w = dot_tn(mixed_rows, grad_attn)
    grad_mixed = dot_nt(grad_attn, full_out).astype(jnp.bfloat16)
    grad_heads = lax.all_to_all(
        grad_mixed.reshape(rows_dev, n_rep, head_width).transpose(1, 0, 2),
        "rep",
        split_axis=0,
        concat_axis=0,
        tiled=True,
    ).reshape(length, head_width)
    grad_query, grad_key, grad_value = attend_backward(
        head_rows, grad_heads, mixed_out, totals, starts, lows, heads
    )
    turn_back = jnp.concatenate([grad_query, grad_key], 1)
    turn_back = turn_back * jnp.tile(cosine, (1, heads + 1)) - swap_halves(turn_back) * jnp.tile(
        sine, (1, heads + 1)
    )
    returning = jnp.concatenate([turn_back, grad_value], 1).astype(jnp.bfloat16)
    returned = lax.all_to_all(
        returning.reshape(n_rep, rows_dev, head_width + 2 * HEAD_DIM),
        "rep",
        split_axis=0,
        concat_axis=0,
        tiled=True,
    ).transpose(1, 0, 2)
    grad_query_rows = returned[:, :, :head_width].reshape(rows_dev, query_width)
    key_back = returned[:, :, head_width : head_width + HEAD_DIM]
    value_back = returned[:, :, head_width + HEAD_DIM :]
    if shared > 1:
        key_back = jnp.sum(
            key_back.reshape(rows_dev, KV_HEADS, shared, HEAD_DIM).astype(jnp.float32), 2
        ).astype(jnp.bfloat16)
        value_back = jnp.sum(
            value_back.reshape(rows_dev, KV_HEADS, shared, HEAD_DIM).astype(jnp.float32), 2
        ).astype(jnp.bfloat16)
    grad_in_rows = jnp.concatenate(
        [
            grad_query_rows,
            key_back.reshape(rows_dev, key_width),
            value_back.reshape(rows_dev, key_width),
        ],
        1,
    )
    grad_w_in = dot_tn(normed_b, grad_in_rows)
    grad_normed = dot_nt(grad_in_rows, full_in)
    grad_inputs_norm, grad_attn_gain = norm_back(grad_normed, inputs, factor_one, attn_gain)
    grad_inputs = grad_hidden + grad_inputs_norm
    everything = n_ep * n_rep
    gains = jnp.concatenate(
        [grad_attn_gain.reshape(everything, -1), grad_mlp_gain.reshape(everything, -1)], 1
    )
    labels = ep_bits[::-1] + rep_bits[::-1]
    shape = (2,) * len(labels)
    weight_grads = jnp.concatenate([grad_w_in, grad_out_w, grad_router], 1).astype(jnp.bfloat16)
    expert_up, expert_down, weights, gains = reduce_rest(
        grad_keep,
        came,
        weight_grads.reshape(shape + (-1, weight_grads.shape[1])),
        gains.reshape(shape + (1, -1)),
        units,
        labels,
        ep_bits + rep_bits,
        model_width // n_rep,
    )
    gains = gains[0]
    part = model_width // everything
    return (
        output[None],
        grad_inputs[None],
        gains[:part],
        weights[:, :query_width],
        weights[:, query_width:rotated_width],
        weights[:, rotated_width:input_width],
        weights[:, input_width : input_width + model_width],
        gains[part:],
        weights[:, input_width + model_width :],
        expert_up,
        expert_down,
    )


def solution(mesh):
    placed = (
        P("ep", "rep", None),
        P("ep", "rep"),
        P("ep", "rep", None),
        P(),
        P(("ep", "rep"), None),
        P(("ep", "rep"), None),
        P(("ep", "rep"), None),
        P(("ep", "rep"), None),
        P(),
        P(("ep", "rep"), None),
        P("ep", None, None),
        P("ep", None, None),
        P("ep", "rep", None),
    )
    return jax.shard_map(
        functools.partial(on_device, n_ep=mesh.shape["ep"], n_rep=mesh.shape["rep"]),
        mesh=mesh,
        in_specs=placed,
        out_specs=(
            P("ep", "rep", None),
            P("ep", "rep", None),
            P(("ep", "rep")),
            P(("ep", "rep"), None),
            P(("ep", "rep"), None),
            P(("ep", "rep"), None),
            P(("ep", "rep"), None),
            P(("ep", "rep")),
            P(("ep", "rep"), None),
            P("ep", "rep", None),
            P("ep", None, "rep"),
        ),
        check_vma=False,
    )
```

```python
import functools
import math

import jax
import jax.numpy as jnp
from jax import lax
from jax.experimental import pallas as pl
from jax.experimental.pallas import tpu as pltpu
from jax.sharding import PartitionSpec as P

HEADS = 16
KV_HEADS = 8
HEAD_DIM = 64
CAP = 80
BLOCK = 256

epsilon = 1e-06
score_scale = 0.015625
branch_scale = 0.22
far_below = -1e30

NT = (((1,), (1,)), ((), ()))
TN = (((0,), (0,)), ((), ()))


def product(left, right):
    return jnp.dot(left, right, preferred_element_type=jnp.float32)


def dot_nt(left, right):
    return lax.dot_general(left, right, NT, preferred_element_type=jnp.float32)


def dot_tn(left, right):
    return lax.dot_general(left, right, TN, preferred_element_type=jnp.float32)


def rms_norm(values, gain):
    factor = lax.rsqrt(jnp.mean(values * values, -1, keepdims=True) + epsilon)
    return (values * factor * gain, factor)


def norm_back(grad_normed, values, factor, gain):
    scaled = grad_normed * gain
    gain_part = jnp.sum(grad_normed * values * factor, 0)
    inner_sum = jnp.mean(scaled * values, -1, keepdims=True)
    return (factor * scaled - values * (factor * factor * factor) * inner_sum, gain_part)


def swap_halves(values):
    count, width = values.shape
    half_dim = HEAD_DIM // 2
    lane = lax.broadcasted_iota(jnp.int32, values.shape, 1)
    return jnp.where(
        lane % HEAD_DIM < half_dim,
        jnp.roll(values, -half_dim, 1),
        jnp.roll(values, half_dim, 1),
    )


def attend_forward_kernel(
    low_ref, rows_ref, start_ref, mixed_ref, out_ref, total_ref, key_s, value_s, *, heads
):
    step = pl.program_id(0)
    width = heads * HEAD_DIM

    @pl.when(step == 0)
    def _():
        key_s[...] = rows_ref[:, width : width + HEAD_DIM]
        value_s[...] = rows_ref[:, width + HEAD_DIM : width + 2 * HEAD_DIM]

    block_rows = rows_ref[pl.ds(pl.multiple_of(step * BLOCK, BLOCK), BLOCK), :]
    queries = [
        block_rows[:, h * HEAD_DIM : (h + 1) * HEAD_DIM] * jnp.bfloat16(score_scale)
        for h in range(heads)
    ]
    starts = start_ref[0]
    at = step * BLOCK + lax.broadcasted_iota(jnp.int32, (1, BLOCK), 1)

    def one(j, carry):
        rows = pl.ds(pl.multiple_of(j * BLOCK, BLOCK), BLOCK)
        key_block = key_s[rows, :]
        value_block = value_s[rows, :]
        place = j * BLOCK + lax.broadcasted_iota(jnp.int32, (BLOCK, BLOCK), 0)
        allowed = (place >= starts) & (place <= at)
        result = []
        for h in range(heads):
            peak, total, mixed = carry[h]
            scores = jnp.where(allowed, dot_nt(key_block, queries[h]), far_below)
            new_peak = jnp.maximum(peak, jnp.max(scores, 0, keepdims=True))
            fade = jnp.exp(peak - new_peak)
            raised = jnp.exp(scores - new_peak)
            total = fade * total + jnp.sum(raised, 0, keepdims=True)
            mixed = fade * mixed + dot_tn(value_block, raised.astype(jnp.bfloat16))
            result.append((new_peak, total, mixed))
        return tuple(result)

    first = tuple(
        (
            jnp.full((1, BLOCK), far_below, jnp.float32),
            jnp.zeros((1, BLOCK), jnp.float32),
            jnp.zeros((HEAD_DIM, BLOCK), jnp.float32),
        )
        for _ in range(heads)
    )
    done = lax.fori_loop(low_ref[step], step + 1, one, first)
    for h in range(heads):
        peak, total, mixed = done[h]
        mixed = mixed / total
        out_ref[h * HEAD_DIM : (h + 1) * HEAD_DIM, :] = mixed
        total_ref[0, h : h + 1, :] = peak + jnp.log(total)
        mixed_ref[:, h * HEAD_DIM : (h + 1) * HEAD_DIM] = mixed.T.astype(jnp.bfloat16)


def attend_forward(rows, starts, lows, heads):
    length, width = rows.shape
    blocks = length // BLOCK
    whole = lambda i, low: (0, 0)
    return pl.pallas_call(
        functools.partial(attend_forward_kernel, heads=heads),
        out_shape=(
            jax.ShapeDtypeStruct((length, heads * HEAD_DIM), jnp.bfloat16),
            jax.ShapeDtypeStruct((heads * HEAD_DIM, length), jnp.float32),
            jax.ShapeDtypeStruct((blocks, heads, BLOCK), jnp.float32),
        ),
        grid_spec=pltpu.PrefetchScalarGridSpec(
            num_scalar_prefetch=1,
            grid=(blocks,),
            in_specs=[
                pl.BlockSpec((length, width), whole),
                pl.BlockSpec((1, 1, BLOCK), lambda i, low: (i, 0, 0)),
            ],
            out_specs=[
                pl.BlockSpec((BLOCK, heads * HEAD_DIM), lambda i, low: (i, 0)),
                pl.BlockSpec((heads * HEAD_DIM, BLOCK), lambda i, low: (0, i)),
                pl.BlockSpec((1, heads, BLOCK), lambda i, low: (i, 0, 0)),
            ],
            scratch_shapes=[
                pltpu.VMEM((length, HEAD_DIM), jnp.bfloat16),
                pltpu.VMEM((length, HEAD_DIM), jnp.bfloat16),
            ],
        ),
        name="attend_forward",
    )(lows, rows, starts)


def attend_backward_kernel(
    low_ref,
    rows_ref,
    grad_ref,
    out_ref,
    total_ref,
    start_ref,
    cosine_ref,
    sine_ref,
    back_ref,
    key_s,
    value_s,
    grad_query_s,
    grad_key_s,
    grad_value_s,
    *,
    heads,
    blocks,
):
    step = pl.program_id(0)
    width = heads * HEAD_DIM

    @pl.when(step == 0)
    def _():
        key_s[...] = rows_ref[:, width : width + HEAD_DIM]
        value_s[...] = rows_ref[:, width + HEAD_DIM : width + 2 * HEAD_DIM]
        grad_key_s[...] = jnp.zeros_like(grad_key_s)
        grad_value_s[...] = jnp.zeros_like(grad_value_s)

    own = pl.ds(pl.multiple_of(step * BLOCK, BLOCK), BLOCK)
    block_rows = rows_ref[own, :]
    grads_all = grad_ref[...]
    starts = start_ref[0]
    at = step * BLOCK + lax.broadcasted_iota(jnp.int32, (1, BLOCK), 1)
    queries, scaled, grads, inners, totals = [], [], [], [], []
    for h in range(heads):
        span = slice(h * HEAD_DIM, (h + 1) * HEAD_DIM)
        queries.append(block_rows[:, span])
        scaled.append(block_rows[:, span] * jnp.bfloat16(score_scale))
        grads.append(grads_all[:, span])
        turned = grads_all[:, span].astype(jnp.float32).T
        inners.append(jnp.sum(turned * out_ref[span, :], 0, keepdims=True))
        totals.append(total_ref[0, h : h + 1, :])

    def one(j, carry):
        rows = pl.ds(pl.multiple_of(j * BLOCK, BLOCK), BLOCK)
        key_block = key_s[rows, :]
        value_block = value_s[rows, :]
        place = j * BLOCK + lax.broadcasted_iota(jnp.int32, (BLOCK, BLOCK), 0)
        allowed = (place >= starts) & (place <= at)
        result = []
        key_sum = grad_key_s[rows, :]
        value_sum = grad_value_s[rows, :]
        for h in range(heads):
            scores = jnp.where(allowed, dot_nt(key_block, scaled[h]), far_below)
            prob = jnp.exp(scores - totals[h])
            grad_prob = dot_nt(value_block, grads[h])
            grad_scores = (prob * (grad_prob - inners[h]) * score_scale).astype(jnp.bfloat16)
            value_sum = value_sum + product(prob.astype(jnp.bfloat16), grads[h])
            key_sum = key_sum + product(grad_scores, queries[h])
            result.append(carry[h] + dot_tn(grad_scores, key_block))
        grad_key_s[rows, :] = key_sum
        grad_value_s[rows, :] = value_sum
        return tuple(result)

    first = tuple(jnp.zeros((BLOCK, HEAD_DIM), jnp.float32) for _ in range(heads))
    done = lax.fori_loop(low_ref[step], step + 1, one, first)
    for h in range(heads):
        grad_query_s[own, h * HEAD_DIM : (h + 1) * HEAD_DIM] = done[h]

    @pl.when(step == blocks - 1)
    def _():
        def turn(j, carry):
            rows = pl.ds(pl.multiple_of(j * BLOCK, BLOCK), BLOCK)
            cosine = cosine_ref[rows, :]
            sine = sine_ref[rows, :]
            parts = [
                grad_query_s[rows, h * HEAD_DIM : (h + 1) * HEAD_DIM] for h in range(heads)
            ]
            parts.append(grad_key_s[rows, :])
            half = HEAD_DIM // 2
            turned = [
                part * cosine - jnp.concatenate([part[:, half:], part[:, :half]], 1) * sine
                for part in parts
            ]
            turned.append(grad_value_s[rows, :])
            back_ref[rows, :] = jnp.concatenate(turned, 1).astype(jnp.bfloat16)
            return carry

        lax.fori_loop(0, blocks, turn, 0)


def attend_backward(rows, grads, outs, totals, starts, lows, cosine, sine, heads):
    length, width = rows.shape
    blocks = length // BLOCK
    whole = lambda i, low: (0, 0)
    once = pl.Buffered(1)
    return pl.pallas_call(
        functools.partial(attend_backward_kernel, heads=heads, blocks=blocks),
        out_shape=jax.ShapeDtypeStruct((length, width), jnp.bfloat16),
        grid_spec=pltpu.PrefetchScalarGridSpec(
            num_scalar_prefetch=1,
            grid=(blocks,),
            in_specs=[
                pl.BlockSpec((length, width), whole),
                pl.BlockSpec((BLOCK, heads * HEAD_DIM), lambda i, low: (i, 0)),
                pl.BlockSpec((heads * HEAD_DIM, BLOCK), lambda i, low: (0, i)),
                pl.BlockSpec((1, heads, BLOCK), lambda i, low: (i, 0, 0)),
                pl.BlockSpec((1, 1, BLOCK), lambda i, low: (i, 0, 0)),
                pl.BlockSpec((length, HEAD_DIM), whole, pipeline_mode=once),
                pl.BlockSpec((length, HEAD_DIM), whole, pipeline_mode=once),
            ],
            out_specs=pl.BlockSpec((length, width), whole),
            scratch_shapes=[
                pltpu.VMEM((length, HEAD_DIM), jnp.bfloat16),
                pltpu.VMEM((length, HEAD_DIM), jnp.bfloat16),
                pltpu.VMEM((length, heads * HEAD_DIM), jnp.float32),
                pltpu.VMEM((length, HEAD_DIM), jnp.float32),
                pltpu.VMEM((length, HEAD_DIM), jnp.float32),
            ],
        ),
        name="attend_backward",
    )(lows, rows, grads, outs, totals, starts, cosine, sine)


def after(value, *others):
    return lax.optimization_barrier((value, *others))[0]


def bits_of(size):
    return max(size.bit_length() - 1, 0)


def swap(sent, axis, bit):
    size = lax.axis_size(axis)
    return lax.ppermute(sent, axis, [(i, i ^ (1 << bit)) for i in range(size)])


def side(axis, bit):
    index = lax.axis_index(axis)
    mine = (index // (1 << bit)) % 2
    return (mine, index + (1 - 2 * mine) * (1 << bit))


def pick(dim, index):
    return (slice(None),) * dim + (index,)


def digits(number, count):
    return tuple((number // (1 << (count - 1 - k))) % 2 for k in range(count))


def mesh_copy(source, target, sends, gets, axis, partner):
    return pltpu.make_async_remote_copy(
        src_ref=source,
        dst_ref=target,
        send_sem=sends,
        recv_sem=gets,
        device_id={axis: partner},
        device_id_type=pl.DeviceIdType.MESH,
    )


def greet(partners):
    barrier = pltpu.get_barrier_semaphore()
    for axis, partner in partners:
        pl.semaphore_signal(
            barrier, inc=1, device_id={axis: partner}, device_id_type=pl.DeviceIdType.MESH
        )
    pl.semaphore_wait(barrier, len(partners))


class Lane:
    def __init__(self, labels, order, first, refs, sends, gets, rows=None):
        bits = len(labels)
        self.order, self.first, self.sends, self.gets = (order, first, sends, gets)
        self.sums, self.got = (refs[: bits - 1], refs[bits - 1 : 2 * bits - 1])
        self.labels = [list(labels)]
        for label in order:
            self.labels.append([other for other in self.labels[-1] if other != label])
        self.rows = rows

    @staticmethod
    def scratch(bits, tail, dtype):
        shapes = [pltpu.VMEM((2,) * (bits - 1 - k) + tail, dtype) for k in range(bits)]
        return shapes[:-1] + shapes

    def source(self, k):
        return self.first if k == 0 else self.sums[k - 1]

    def copy(self, k):
        axis, bit = self.order[k]
        mine, partner = side(axis, bit)
        dim = self.labels[k].index((axis, bit))
        return mesh_copy(
            self.source(k).at[pick(dim, 1 - mine)],
            self.got[k],
            self.sends.at[k],
            self.gets.at[k],
            axis,
            partner,
        )

    def start(self, k):
        self.copy(k).start()

    def add(self, k, out=None):
        axis, bit = self.order[k]
        mine, _ = side(axis, bit)
        dim = self.labels[k].index((axis, bit))
        left = len(self.order) - 1 - k
        self.copy(k).wait_recv()
        source, got = (self.source(k), self.got[k])
        target = out if left == 0 else self.sums[k]
        height = got.shape[left]
        rows = self.rows or height
        blocks = height // rows

        def body(i, carry):
            at = digits(i // blocks, left)
            own = pl.ds(pl.multiple_of((i % blocks) * rows, rows), rows)
            if blocks == 1:
                own = slice(None)
            here = at[:dim] + (mine,) + at[dim:]
            total = source[here + (own,)].astype(jnp.float32) + got[at + (own,)].astype(
                jnp.float32
            )
            target[at + (own,)] = total.astype(target.dtype)
            return carry

        lax.fori_loop(0, blocks << left, body, 0)

    def finish(self):
        for k in range(len(self.order)):
            self.copy(k).wait_send()


def reduce_kernel(*refs, units, n_came, labels, weight_order, share):
    keep_ref, *refs = refs
    came_refs, refs = (refs[:n_came], refs[n_came:])
    weight_ref, gain_ref, up_ref, down_ref, weight_out, gain_out, *refs = refs
    steps = len(units[0][3]) - 1
    sends, keeps, gets = ([], [], [])
    for _ in range(steps):
        sends.append(refs[0])
        keeps.append(refs[1])
        gets.append(refs[2])
        refs = refs[3:]
    bits = len(labels)
    lane_refs, refs = (refs[: 2 * (2 * bits - 1)], refs[2 * (2 * bits - 1) :])
    load_keep, load_came, load_sem, unit_send, unit_get, lane_send, lane_get = refs
    lanes = [
        Lane(
            labels,
            weight_order,
            first,
            lane_refs[number * (2 * bits - 1) : (number + 1) * (2 * bits - 1)],
            lane_send.at[number],
            lane_get.at[number],
        )
        for number, first in enumerate((weight_ref, gain_ref))
    ]
    count, spots, tall, width = keep_ref.shape
    rows = 32 if tall % 32 == 0 else tall
    blocks = tall // rows

    greet([(axis, side(axis, bit)[1]) for axis, bit in weight_order])

    def lane_start(k):
        for lane in lanes:
            lane.start(k)

    def lane_add(k):
        for lane, out in zip(lanes, (weight_out, gain_out)):
            lane.add(k, out)

    lane_start(0)

    def loads(n):
        unit, g, place, _ = units[n]
        slot = n % 2
        return (
            pltpu.make_async_copy(keep_ref.at[unit], load_keep.at[slot], load_sem.at[slot, 0]),
            pltpu.make_async_copy(
                came_refs[g].at[place], load_came.at[slot], load_sem.at[slot, 1]
            ),
        )

    def unit_copy(unit, order, k):
        axis, bit = order[k + 1]
        return mesh_copy(
            sends[k].at[unit],
            gets[k].at[unit],
            unit_send.at[unit, k],
            unit_get.at[unit, k],
            axis,
            side(axis, bit)[1],
        )

    def unit_add(unit, order, k, left, right):
        mine, _ = side(*order[k + 1])
        half = spots >> (k + 1)

        def fill(target, which):
            def body(i, carry):
                piece = i // blocks
                own = pl.ds(pl.multiple_of((i % blocks) * rows, rows), rows)
                total = left[which * half + piece, own, :].astype(jnp.float32) + right[
                    which * half + piece, own, :
                ].astype(jnp.float32)
                target[unit, piece, own, :] = total.astype(jnp.bfloat16)
                return carry

            lax.fori_loop(0, half * blocks, body, 0)

        fill(sends[k], 1 - mine)
        unit_copy(unit, order, k).start()
        fill(keeps[k], mine)

    def begin_unit(n):
        unit, _, _, order = units[n]
        for copy in loads(n):
            copy.wait()
        unit_add(unit, order, 0, load_keep.at[n % 2], load_came.at[n % 2])
        if n + 2 < len(units):
            for copy in loads(n + 2):
                copy.start()

    def next_unit(n, k):
        unit, _, _, order = units[n]
        unit_copy(unit, order, k - 1).wait_recv()
        unit_add(unit, order, k, keeps[k - 1].at[unit], gets[k - 1].at[unit])

    def end_unit(n):
        unit, _, _, order = units[n]
        unit_copy(unit, order, steps - 1).wait_recv()
        total = keeps[-1][unit, 0].astype(jnp.float32) + gets[-1][unit, 0].astype(jnp.float32)
        up_ref[unit] = total[:share]
        pieces = width // share
        rest = tall - share
        for p in range(pieces):
            down_ref[unit, p * rest : (p + 1) * rest, :] = total[
                share:, p * share : (p + 1) * share
            ]

    for n in range(min(2, len(units))):
        for copy in loads(n):
            copy.start()
    work = [functools.partial(begin_unit, n) for n in range(len(units))]
    for k in range(1, steps):
        work += [functools.partial(next_unit, n, k) for n in range(len(units))]
    work += [functools.partial(end_unit, n) for n in range(len(units))]
    marks = [len(units) + (len(work) - len(units)) * k // bits for k in range(bits)]
    for number, job in enumerate(work):
        for k, mark in enumerate(marks[:-1]):
            if number == mark:
                lane_add(k)
                lane_start(k + 1)
        job()
    lane_add(bits - 1)
    for unit, _, _, order in units:
        for k in range(steps):
            unit_copy(unit, order, k).wait_send()
    for lane in lanes:
        lane.finish()


def reduce_rest(keep, came, weights, gains, units, labels, weight_order, share):
    count, spots, tall, width = keep.shape
    bits = len(labels)
    steps = len(units[0][3]) - 1
    anywhere = pl.BlockSpec(memory_space=pl.ANY)
    vmem = pl.BlockSpec(memory_space=pltpu.VMEM)
    scratch = []
    for k in range(steps):
        scratch += [pltpu.VMEM((count, spots >> (k + 1), tall, width), jnp.bfloat16)] * 3
    for lane in (weights, gains):
        scratch += Lane.scratch(bits, lane.shape[bits:], lane.dtype)
    scratch += [
        pltpu.VMEM((2, spots, tall, width), jnp.bfloat16),
        pltpu.VMEM((2, spots, tall, width), jnp.bfloat16),
        pltpu.SemaphoreType.DMA((2, 2)),
        pltpu.SemaphoreType.DMA((count, steps)),
        pltpu.SemaphoreType.DMA((count, steps)),
        pltpu.SemaphoreType.DMA((2, bits)),
        pltpu.SemaphoreType.DMA((2, bits)),
    ]
    return pl.pallas_call(
        functools.partial(
            reduce_kernel,
            units=units,
            n_came=len(came),
            labels=labels,
            weight_order=weight_order,
            share=share,
        ),
        out_shape=(
            jax.ShapeDtypeStruct((count, share, width), jnp.float32),
            jax.ShapeDtypeStruct((count, (tall - share) * (width // share), share), jnp.float32),
            jax.ShapeDtypeStruct(weights.shape[bits:], jnp.float32),
            jax.ShapeDtypeStruct(gains.shape[bits:], jnp.float32),
        ),
        in_specs=[anywhere] * (1 + len(came)) + [vmem] * 2,
        out_specs=[vmem] * 4,
        scratch_shapes=scratch,
        compiler_params=pltpu.CompilerParams(
            collective_id=0, has_side_effects=True, vmem_limit_bytes=67 * 1000 * 1000
        ),
        name="reduce_rest",
    )(keep, *came, weights, gains)


def experts_kernel(
    *refs, sources, rows_dev, count, copies, orders, near, labels, ep_order
):
    rows_hbm, cot_hbm, rank_ref, prob_ref, gate_up_ref, down_ref, *refs = refs
    out_ref, grad_ref, inner_ref, keep_ref, came_ref, *refs = refs
    far = count - near
    sent_refs, refs = (refs[:far], refs[far:])
    rows_s, cot_s, picks_s, out_s, grad_s, send_s, inner_s, inner_got, *refs = refs
    bits = len(labels)
    lane_refs, refs = (refs[: 2 * (2 * bits - 1)], refs[2 * (2 * bits - 1) :])
    load_sem, unit_send, unit_get, lane_send, lane_get, inner_send, inner_take = refs
    me = lax.axis_index("ep")
    step = pl.program_id(0)
    grad_lane, out_lane = [
        Lane(
            labels,
            ep_order,
            first,
            lane_refs[number * (2 * bits - 1) : (number + 1) * (2 * bits - 1)],
            lane_send.at[number],
            lane_get.at[number],
            rows=32,
        )
        for number, first in enumerate((cot_s, rows_s))
    ]

    def unit_copy(e):
        bit = orders[e][0]
        if e < near:
            return mesh_copy(
                send_s.at[e],
                came_ref.at[e],
                unit_send.at[e],
                unit_get.at[e],
                "rep",
                side("rep", bit)[1],
            )
        return pltpu.make_async_copy(send_s.at[e], sent_refs[e - near], unit_send.at[e])

    def inner_copy(d):
        peer = (me + d) % sources
        return mesh_copy(
            inner_s.at[peer],
            inner_got.at[me],
            inner_send.at[d - 1],
            inner_take.at[d - 1],
            "ep",
            peer,
        )

    @pl.when(step == 0)
    def _():
        loads = [
            pltpu.make_async_copy(rows_hbm, rows_s, load_sem.at[0]),
            pltpu.make_async_copy(cot_hbm, cot_s, load_sem.at[1]),
        ]
        for copy in loads:
            copy.start()
        partners = [("ep", (me + d) % sources) for d in range(1, sources)]
        for bit in sorted({order[0] for order in orders[:near]}):
            partners.append(("rep", side("rep", bit)[1]))
        greet(partners)
        for copy in loads:
            copy.wait()

    slots = pl.ds(pl.multiple_of(step * CAP, 16), CAP)
    numbers = lax.broadcasted_iota(jnp.int32, (CAP, rows_dev), 0).astype(jnp.float32)
    rows_in, cots, weights, picks = [], [], [], []
    for s in range(sources):
        rank = rank_ref[s, pl.ds(step, 1), :]
        pick_table = jnp.where(rank == numbers, 1.0, 0.0)
        weights.append(jnp.sum(pick_table * prob_ref[s, pl.ds(step, 1), :], 1, keepdims=True))
        pick_b = pick_table.astype(jnp.bfloat16)
        picks.append(pick_table)
        picks_s[s, slots, :] = pick_b
        rows_in.append(product(pick_b, rows_s[digits(s, bits)]).astype(jnp.bfloat16))
        cots.append(product(pick_b, cot_s[digits(s, bits)]))
    arrived = jnp.concatenate(rows_in, 0)
    weight = jnp.concatenate(weights, 0)
    grad_mix = branch_scale * jnp.concatenate(cots, 0)
    gate_up = gate_up_ref[0]
    down = down_ref[0]
    hidden_units = down.shape[0]
    both = product(arrived, gate_up)
    gate_part = both[:, :hidden_units]
    up_part = both[:, hidden_units:]
    sigmoid_gate = jax.nn.sigmoid(gate_part)
    active = (gate_part * sigmoid_gate * up_part).astype(jnp.bfloat16)
    produced = product(active, down).astype(jnp.bfloat16).astype(jnp.float32)
    inner = jnp.sum(grad_mix * produced, 1, keepdims=True)
    sent_out = (weight * produced).astype(jnp.bfloat16)
    grad_out = (weight * grad_mix).astype(jnp.bfloat16)
    grad_active = dot_nt(grad_out, down)
    grad_down = dot_tn(active, grad_out).astype(jnp.bfloat16)
    grad_gate = grad_active * up_part * sigmoid_gate * (1.0 + gate_part * (1.0 - sigmoid_gate))
    grad_up = grad_active * gate_part * sigmoid_gate
    grad_both = jnp.concatenate([grad_gate, grad_up], 1).astype(jnp.bfloat16)
    grad_gate_up = dot_tn(arrived, grad_both).astype(jnp.bfloat16)
    share = grad_down.shape[1] // copies
    tall = hidden_units // copies

    def put(order, mine):
        bit, *later = order
        for r in range(copies):
            spot = 0
            for b in later:
                spot = 2 * spot + ((r >> b) & 1)
            ref = keep_ref.at[0] if (r >> bit) & 1 == mine else send_s.at[step]
            ref[spot, :share, :] = grad_gate_up[r * share : (r + 1) * share]
            for k in range(copies):
                ref[spot, share : share + tall, k * share : (k + 1) * share] = grad_down[
                    k * tall : (k + 1) * tall, r * share : (r + 1) * share
                ]

    for order in {tuple(order): order for order in orders}.values():
        members = [e for e in range(count) if orders[e] == order]
        here = functools.reduce(jnp.logical_or, [step == e for e in members])
        side_mine, _ = side("rep", order[0])
        for mine in range(2):

            @pl.when(here & (side_mine == mine))
            def _(order=order, mine=mine):
                put(order, mine)

    grad_in = dot_nt(grad_both, gate_up).astype(jnp.bfloat16)
    for s in range(sources):
        part = slice(s * CAP, (s + 1) * CAP)
        out_s[s, slots, :] = sent_out[part]
        grad_s[s, slots, :] = grad_in[part]
        inner_s[s, pl.ds(step, 1), :] = jnp.sum(picks[s] * inner[part], 0, keepdims=True)
    for e in range(count):

        @pl.when(step == e)
        def _(e=e):
            unit_copy(e).start()

    @pl.when(step == count - 1)
    def _():
        for table_of, target, lane in ((grad_s, cot_s, grad_lane), (out_s, rows_s, out_lane)):
            for s in range(sources):
                target[digits(s, bits)] = dot_tn(picks_s[s], table_of[s]).astype(jnp.bfloat16)
            lane.start(0)
        for d in range(1, sources):
            inner_copy(d).start()
        for k in range(bits):
            for lane, total in ((grad_lane, grad_ref), (out_lane, out_ref)):
                lane.add(k, total)
                if k + 1 < bits:
                    lane.start(k + 1)
        inner_got[me] = inner_s[me]
        for d in range(1, sources):
            inner_copy(d).wait_recv()
        inner_ref[...] = inner_got[...]
        for d in range(1, sources):
            inner_copy(d).wait_send()
        grad_lane.finish()
        out_lane.finish()
        for e in range(count):
            unit_copy(e).wait()


def experts(rows, cots, ranks, probs, w_gate_up, w_down, copies, orders, near, labels, ep_order):
    sources, count, rows_dev = ranks.shape
    total, model_width = rows.shape
    hidden_units = w_down.shape[1]
    bits = len(labels)
    tall = model_width // copies + hidden_units // copies
    flat = lambda i: (0, 0)
    cube = lambda i: (0, 0, 0)
    once = pl.Buffered(1)
    anywhere = pl.BlockSpec(memory_space=pl.ANY)
    far = count - near
    shape = (2,) * bits + (rows_dev, model_width)
    piece = (copies // 2, tall, model_width)
    return pl.pallas_call(
        functools.partial(
            experts_kernel,
            sources=sources,
            rows_dev=rows_dev,
            count=count,
            copies=copies,
            orders=orders,
            near=near,
            labels=labels,
            ep_order=ep_order,
        ),
        out_shape=(
            jax.ShapeDtypeStruct((rows_dev, model_width), jnp.float32),
            jax.ShapeDtypeStruct((rows_dev, model_width), jnp.float32),
            jax.ShapeDtypeStruct((sources, count, rows_dev), jnp.float32),
            jax.ShapeDtypeStruct((count,) + piece, jnp.bfloat16),
            jax.ShapeDtypeStruct((near,) + piece, jnp.bfloat16),
        )
        + (jax.ShapeDtypeStruct(piece, jnp.bfloat16),) * far,
        grid=(count,),
        in_specs=[
            anywhere,
            anywhere,
            pl.BlockSpec((sources, count, rows_dev), cube, pipeline_mode=once),
            pl.BlockSpec((sources, count, rows_dev), cube, pipeline_mode=once),
            pl.BlockSpec((1, model_width, 2 * hidden_units), lambda i: (i, 0, 0)),
            pl.BlockSpec((1, hidden_units, model_width), lambda i: (i, 0, 0)),
        ],
        out_specs=[
            pl.BlockSpec((rows_dev, model_width), flat, pipeline_mode=once),
            pl.BlockSpec((rows_dev, model_width), flat, pipeline_mode=once),
            pl.BlockSpec((sources, count, rows_dev), cube, pipeline_mode=once),
            pl.BlockSpec((1,) + piece, lambda i: (i, 0, 0, 0)),
            anywhere,
        ]
        + [anywhere] * far,
        scratch_shapes=[
            pltpu.VMEM(shape, jnp.bfloat16),
            pltpu.VMEM(shape, jnp.bfloat16),
            pltpu.VMEM((sources, count * CAP, rows_dev), jnp.bfloat16),
            pltpu.VMEM((sources, count * CAP, model_width), jnp.bfloat16),
            pltpu.VMEM((sources, count * CAP, model_width), jnp.bfloat16),
            pltpu.VMEM((count,) + piece, jnp.bfloat16),
            pltpu.VMEM((sources, count, rows_dev), jnp.float32),
            pltpu.VMEM((sources, count, rows_dev), jnp.float32),
        ]
        + Lane.scratch(bits, (rows_dev, model_width), jnp.bfloat16) * 2
        + [
            pltpu.SemaphoreType.DMA((2,)),
            pltpu.SemaphoreType.DMA((count,)),
            pltpu.SemaphoreType.DMA((near,)),
            pltpu.SemaphoreType.DMA((2, bits)),
            pltpu.SemaphoreType.DMA((2, bits)),
            pltpu.SemaphoreType.DMA((sources - 1,)),
            pltpu.SemaphoreType.DMA((sources - 1,)),
        ],
        compiler_params=pltpu.CompilerParams(
            collective_id=1, has_side_effects=True, vmem_limit_bytes=67 * 1000 * 1000
        ),
        name="experts",
    )(rows.reshape(shape), cots.reshape(shape), ranks, probs, w_gate_up, w_down)


def on_device(
    tokens,
    segments,
    routes,
    attn_gain,
    w_query,
    w_key,
    w_value,
    w_out,
    mlp_gain,
    w_router,
    w_gate_up,
    w_down,
    cotangent,
    *,
    n_ep,
    n_rep,
):
    inputs = tokens[0]
    own_routes = routes[0]
    grad_output = cotangent[0]
    rows_dev, model_width = inputs.shape
    everyone = ("ep", "rep")
    heads = HEADS // n_rep
    head_width = heads * HEAD_DIM
    shared = max(1, n_rep // KV_HEADS)
    query_width = w_query.shape[1]
    key_width = w_key.shape[1]
    experts_all = w_router.shape[1]
    half_dim = HEAD_DIM // 2

    pack_ids = lax.all_gather(segments[0], "rep", axis=0, tiled=True)
    length = pack_ids.shape[0]
    blocks = length // BLOCK
    offset = lax.axis_index("rep") * rows_dev
    doc_start = jnp.sum((pack_ids[None, :] < pack_ids[:, None]).astype(jnp.int32), 1)
    position = (jnp.arange(length, dtype=jnp.int32) - doc_start).astype(jnp.float32)
    angles = (
        position[:, None]
        * jnp.exp(jnp.arange(half_dim, dtype=jnp.float32) * (-math.log(10000.0) / half_dim))[
            None, :
        ]
    )
    cosine = jnp.cos(angles)
    sine = jnp.sin(angles)
    cosine = jnp.concatenate([cosine, cosine], 1)
    sine = jnp.concatenate([-sine, sine], 1)
    own_cosine = lax.dynamic_slice_in_dim(cosine, offset, rows_dev, 0)
    own_sine = lax.dynamic_slice_in_dim(sine, offset, rows_dev, 0)
    starts = doc_start.reshape(blocks, 1, BLOCK)
    lows = doc_start[::BLOCK] // BLOCK

    joined = jnp.concatenate([w_query, w_key, w_value, w_out, w_router], 1)
    full = lax.all_gather(joined, everyone, axis=0, tiled=True)
    rotated_width = query_width + key_width
    input_width = rotated_width + key_width
    full_in = full[:, :input_width]
    full_out = full[:, input_width : input_width + model_width]
    full_router = full[:, input_width + model_width :]

    normed, factor_one = rms_norm(inputs, attn_gain)
    normed_b = normed.astype(jnp.bfloat16)
    mixed_in = product(normed_b, full_in)
    turn = mixed_in[:, :rotated_width]
    times = rotated_width // HEAD_DIM
    turned = turn * jnp.tile(own_cosine, (1, times)) + swap_halves(turn) * jnp.tile(
        own_sine, (1, times)
    )
    turned_b = turned.astype(jnp.bfloat16)
    value_b = mixed_in[:, rotated_width:].astype(jnp.bfloat16)
    query_part = turned_b[:, :query_width].reshape(rows_dev, n_rep, head_width)
    key_part = turned_b[:, query_width:].reshape(rows_dev, KV_HEADS, HEAD_DIM)
    value_part = value_b.reshape(rows_dev, KV_HEADS, HEAD_DIM)
    if shared > 1:
        key_part = jnp.repeat(key_part, shared, 1)
        value_part = jnp.repeat(value_part, shared, 1)
    sending = jnp.concatenate([query_part, key_part, value_part], 2).transpose(1, 0, 2)
    head_rows = lax.all_to_all(sending, "rep", split_axis=0, concat_axis=0, tiled=True)
    head_rows = head_rows.reshape(length, head_width + 2 * HEAD_DIM)
    mixed, mixed_out, totals = attend_forward(head_rows, starts, lows, heads)
    mixed_rows = lax.all_to_all(
        mixed.reshape(n_rep, rows_dev, head_width), "rep", split_axis=0, concat_axis=0, tiled=True
    )
    mixed_rows = mixed_rows.transpose(1, 0, 2).reshape(rows_dev, query_width)
    hidden = inputs + branch_scale * product(mixed_rows, full_out)

    normed_two, factor_two = rms_norm(hidden, mlp_gain)
    normed_two_b = normed_two.astype(jnp.bfloat16)
    router_f = full_router.astype(jnp.float32)
    logits = product(normed_two_b, full_router)
    numbers = jnp.arange(experts_all, dtype=jnp.int32)
    onehot = jnp.sum((own_routes[:, :, None] == numbers).astype(jnp.float32), 1)
    chosen = onehot > 0.5
    peak = jnp.max(jnp.where(chosen, logits, far_below), 1, keepdims=True)
    raised = jnp.where(chosen, jnp.exp(jnp.minimum(logits - peak, 0.0)), 0.0)
    probs = raised / jnp.sum(raised, 1, keepdims=True)
    before = (
        lax.broadcasted_iota(jnp.int32, (rows_dev, rows_dev), 0)
        > lax.broadcasted_iota(jnp.int32, (rows_dev, rows_dev), 1)
    ).astype(jnp.bfloat16)
    rank = product(before, onehot.astype(jnp.bfloat16))
    kept = chosen & (rank < CAP)
    rank_sent = jnp.where(kept, rank, -1.0).T
    probs_sent = probs.T
    both_sent = jnp.concatenate(
        [rank_sent.reshape(n_ep, -1, rows_dev), probs_sent.reshape(n_ep, -1, rows_dev)], 1
    )
    both_all = lax.all_to_all(both_sent, "ep", split_axis=0, concat_axis=0, tiled=True)
    ranks = both_all[:, : experts_all // n_ep]
    prob_all = both_all[:, experts_all // n_ep :]
    expert_rows = lax.all_gather(normed_two_b, "ep", axis=0, tiled=True)
    expert_cots = lax.all_gather(grad_output.astype(jnp.bfloat16), "ep", axis=0, tiled=True)
    rep_bits = [("rep", b) for b in range(bits_of(n_rep))]
    ep_bits = [("ep", b) for b in range(bits_of(n_ep))]
    count = experts_all // n_ep
    near = count * 5 // 8
    kinds = [0, 1, 0, 1, 0][:near] + [0, 1, 0][near - count :]
    leads = [0, len(rep_bits) - 2]
    orders = [
        [leads[kind]] + [b for b in range(len(rep_bits)) if b != leads[kind]] for kind in kinds
    ]
    out_sum, grad_sum, inner_back, grad_keep, came_near, *sent = experts(
        expert_rows,
        expert_cots,
        ranks,
        prob_all,
        w_gate_up,
        w_down,
        n_rep,
        orders,
        near,
        ep_bits[::-1],
        ep_bits,
    )
    units = [(e, 0, e, [("rep", b) for b in orders[e]]) for e in range(near)]
    units += [
        (e, 1 + e - near, 0, [("rep", b) for b in orders[e]]) for e in range(near, count)
    ]
    output = hidden + branch_scale * out_sum
    grad_probs = inner_back.reshape(experts_all, rows_dev).T
    grad_logits = probs * (grad_probs - jnp.sum(grad_probs * probs, -1, keepdims=True))
    normed_two_f = normed_two_b.astype(jnp.float32)
    grad_router = jnp.dot(normed_two_f.T, grad_logits, precision=lax.Precision.HIGHEST)
    grad_normed_two = grad_sum + jnp.dot(
        grad_logits, router_f.T, precision=lax.Precision.HIGHEST
    )
    grad_hidden_norm, grad_mlp_gain = norm_back(grad_normed_two, hidden, factor_two, mlp_gain)
    grad_hidden = grad_output + grad_hidden_norm
    grad_attn = (branch_scale * grad_hidden).astype(jnp.bfloat16)
    grad_out_w = dot_tn(mixed_rows, grad_attn)
    grad_mixed = dot_nt(grad_attn, full_out).astype(jnp.bfloat16)
    grad_heads = lax.all_to_all(
        grad_mixed.reshape(rows_dev, n_rep, head_width).transpose(1, 0, 2),
        "rep",
        split_axis=0,
        concat_axis=0,
        tiled=True,
    ).reshape(length, head_width)
    beside = [
        swap(after(sent[k], grad_heads), "rep", orders[near + k][0])[None]
        for k in range(len(sent) - 1)
    ]
    returning = attend_backward(
        head_rows, grad_heads, mixed_out, totals, starts, lows, cosine, sine, heads
    )
    returning = after(returning, *beside)
    returned = lax.all_to_all(
        returning.reshape(n_rep, rows_dev, head_width + 2 * HEAD_DIM),
        "rep",
        split_axis=0,
        concat_axis=0,
        tiled=True,
    ).transpose(1, 0, 2)
    last = swap(after(sent[-1], returned), "rep", orders[-1][0])[None]
    came = [came_near] + beside + [last]
    grad_query_rows = returned[:, :, :head_width].reshape(rows_dev, query_width)
    key_back = returned[:, :, head_width : head_width + HEAD_DIM]
    value_back = returned[:, :, head_width + HEAD_DIM :]
    if shared > 1:
        key_back = jnp.sum(
            key_back.reshape(rows_dev, KV_HEADS, shared, HEAD_DIM).astype(jnp.float32), 2
        ).astype(jnp.bfloat16)
        value_back = jnp.sum(
            value_back.reshape(rows_dev, KV_HEADS, shared, HEAD_DIM).astype(jnp.float32), 2
        ).astype(jnp.bfloat16)
    grad_in_rows = jnp.concatenate(
        [
            grad_query_rows,
            key_back.reshape(rows_dev, key_width),
            value_back.reshape(rows_dev, key_width),
        ],
        1,
    )
    grad_w_in = dot_tn(normed_b, grad_in_rows)
    grad_normed = dot_nt(grad_in_rows, full_in)
    grad_inputs_norm, grad_attn_gain = norm_back(grad_normed, inputs, factor_one, attn_gain)
    grad_inputs = grad_hidden + grad_inputs_norm
    everything = n_ep * n_rep
    gains = jnp.concatenate(
        [grad_attn_gain.reshape(everything, -1), grad_mlp_gain.reshape(everything, -1)], 1
    )
    labels = ep_bits[::-1] + rep_bits[::-1]
    shape = (2,) * len(labels)
    weight_grads = jnp.concatenate([grad_w_in, grad_out_w, grad_router], 1).astype(jnp.bfloat16)
    expert_up, expert_down, weights, gains = reduce_rest(
        grad_keep,
        came,
        weight_grads.reshape(shape + (-1, weight_grads.shape[1])),
        gains.reshape(shape + (1, -1)),
        units,
        labels,
        ep_bits + rep_bits,
        model_width // n_rep,
    )
    gains = gains[0]
    part = model_width // everything
    return (
        output[None],
        grad_inputs[None],
        gains[:part],
        weights[:, :query_width],
        weights[:, query_width:rotated_width],
        weights[:, rotated_width:input_width],
        weights[:, input_width : input_width + model_width],
        gains[part:],
        weights[:, input_width + model_width :],
        expert_up,
        expert_down,
    )


def solution(mesh):
    placed = (
        P("ep", "rep", None),
        P("ep", "rep"),
        P("ep", "rep", None),
        P(),
        P(("ep", "rep"), None),
        P(("ep", "rep"), None),
        P(("ep", "rep"), None),
        P(("ep", "rep"), None),
        P(),
        P(("ep", "rep"), None),
        P("ep", None, None),
        P("ep", None, None),
        P("ep", "rep", None),
    )
    return jax.shard_map(
        functools.partial(on_device, n_ep=mesh.shape["ep"], n_rep=mesh.shape["rep"]),
        mesh=mesh,
        in_specs=placed,
        out_specs=(
            P("ep", "rep", None),
            P("ep", "rep", None),
            P(("ep", "rep")),
            P(("ep", "rep"), None),
            P(("ep", "rep"), None),
            P(("ep", "rep"), None),
            P(("ep", "rep"), None),
            P(("ep", "rep")),
            P(("ep", "rep"), None),
            P("ep", "rep", None),
            P("ep", None, "rep"),
        ),
        check_vma=False,
    )
```

```python
import functools
import math

import jax
import jax.numpy as jnp
from jax import lax
from jax.experimental import pallas as pl
from jax.experimental.pallas import tpu as pltpu
from jax.sharding import PartitionSpec as P

HEADS = 16
KV_HEADS = 8
HEAD_DIM = 64
CAP = 80
BLOCK = 256

epsilon = 1e-06
score_scale = 0.015625
branch_scale = 0.22
far_below = -1e30

NT = (((1,), (1,)), ((), ()))
TN = (((0,), (0,)), ((), ()))


def product(left, right):
    return jnp.dot(left, right, preferred_element_type=jnp.float32)


def dot_nt(left, right):
    return lax.dot_general(left, right, NT, preferred_element_type=jnp.float32)


def dot_tn(left, right):
    return lax.dot_general(left, right, TN, preferred_element_type=jnp.float32)


def rms_norm(values, gain):
    factor = lax.rsqrt(jnp.mean(values * values, -1, keepdims=True) + epsilon)
    return (values * factor * gain, factor)


def norm_back(grad_normed, values, factor, gain):
    scaled = grad_normed * gain
    gain_part = jnp.sum(grad_normed * values * factor, 0)
    inner_sum = jnp.mean(scaled * values, -1, keepdims=True)
    return (factor * scaled - values * (factor * factor * factor) * inner_sum, gain_part)


def swap_halves(values):
    count, width = values.shape
    half_dim = HEAD_DIM // 2
    lane = lax.broadcasted_iota(jnp.int32, values.shape, 1)
    return jnp.where(
        lane % HEAD_DIM < half_dim,
        jnp.roll(values, -half_dim, 1),
        jnp.roll(values, half_dim, 1),
    )


def attend_forward_kernel(
    low_ref, rows_ref, start_ref, mixed_ref, out_ref, total_ref, key_s, value_s, *, heads
):
    step = pl.program_id(0)
    width = heads * HEAD_DIM

    @pl.when(step == 0)
    def _():
        key_s[...] = rows_ref[:, width : width + HEAD_DIM]
        value_s[...] = rows_ref[:, width + HEAD_DIM : width + 2 * HEAD_DIM]

    block_rows = rows_ref[pl.ds(pl.multiple_of(step * BLOCK, BLOCK), BLOCK), :]
    queries = [
        block_rows[:, h * HEAD_DIM : (h + 1) * HEAD_DIM] * jnp.bfloat16(score_scale)
        for h in range(heads)
    ]
    starts = start_ref[0]
    at = step * BLOCK + lax.broadcasted_iota(jnp.int32, (1, BLOCK), 1)

    def one(j, carry):
        rows = pl.ds(pl.multiple_of(j * BLOCK, BLOCK), BLOCK)
        key_block = key_s[rows, :]
        value_block = value_s[rows, :]
        place = j * BLOCK + lax.broadcasted_iota(jnp.int32, (BLOCK, BLOCK), 0)
        allowed = (place >= starts) & (place <= at)
        result = []
        for h in range(heads):
            peak, total, mixed = carry[h]
            scores = jnp.where(allowed, dot_nt(key_block, queries[h]), far_below)
            new_peak = jnp.maximum(peak, jnp.max(scores, 0, keepdims=True))
            fade = jnp.exp(peak - new_peak)
            raised = jnp.exp(scores - new_peak)
            total = fade * total + jnp.sum(raised, 0, keepdims=True)
            mixed = fade * mixed + dot_tn(value_block, raised.astype(jnp.bfloat16))
            result.append((new_peak, total, mixed))
        return tuple(result)

    first = tuple(
        (
            jnp.full((1, BLOCK), far_below, jnp.float32),
            jnp.zeros((1, BLOCK), jnp.float32),
            jnp.zeros((HEAD_DIM, BLOCK), jnp.float32),
        )
        for _ in range(heads)
    )
    done = lax.fori_loop(low_ref[step], step + 1, one, first)
    for h in range(heads):
        peak, total, mixed = done[h]
        mixed = mixed / total
        out_ref[h * HEAD_DIM : (h + 1) * HEAD_DIM, :] = mixed
        total_ref[0, h : h + 1, :] = peak + jnp.log(total)
        mixed_ref[:, h * HEAD_DIM : (h + 1) * HEAD_DIM] = mixed.T.astype(jnp.bfloat16)


def attend_forward(rows, starts, lows, heads):
    length, width = rows.shape
    blocks = length // BLOCK
    whole = lambda i, low: (0, 0)
    return pl.pallas_call(
        functools.partial(attend_forward_kernel, heads=heads),
        out_shape=(
            jax.ShapeDtypeStruct((length, heads * HEAD_DIM), jnp.bfloat16),
            jax.ShapeDtypeStruct((heads * HEAD_DIM, length), jnp.float32),
            jax.ShapeDtypeStruct((blocks, heads, BLOCK), jnp.float32),
        ),
        grid_spec=pltpu.PrefetchScalarGridSpec(
            num_scalar_prefetch=1,
            grid=(blocks,),
            in_specs=[
                pl.BlockSpec((length, width), whole),
                pl.BlockSpec((1, 1, BLOCK), lambda i, low: (i, 0, 0)),
            ],
            out_specs=[
                pl.BlockSpec((BLOCK, heads * HEAD_DIM), lambda i, low: (i, 0)),
                pl.BlockSpec((heads * HEAD_DIM, BLOCK), lambda i, low: (0, i)),
                pl.BlockSpec((1, heads, BLOCK), lambda i, low: (i, 0, 0)),
            ],
            scratch_shapes=[
                pltpu.VMEM((length, HEAD_DIM), jnp.bfloat16),
                pltpu.VMEM((length, HEAD_DIM), jnp.bfloat16),
            ],
        ),
        name="attend_forward",
    )(lows, rows, starts)


def attend_backward_kernel(
    low_ref,
    rows_ref,
    grad_ref,
    out_ref,
    total_ref,
    start_ref,
    cosine_ref,
    sine_ref,
    back_ref,
    key_s,
    value_s,
    grad_query_s,
    grad_key_s,
    grad_value_s,
    *,
    heads,
    blocks,
):
    step = pl.program_id(0)
    width = heads * HEAD_DIM

    @pl.when(step == 0)
    def _():
        key_s[...] = rows_ref[:, width : width + HEAD_DIM]
        value_s[...] = rows_ref[:, width + HEAD_DIM : width + 2 * HEAD_DIM]
        grad_key_s[...] = jnp.zeros_like(grad_key_s)
        grad_value_s[...] = jnp.zeros_like(grad_value_s)

    own = pl.ds(pl.multiple_of(step * BLOCK, BLOCK), BLOCK)
    block_rows = rows_ref[own, :]
    grads_all = grad_ref[...]
    starts = start_ref[0]
    at = step * BLOCK + lax.broadcasted_iota(jnp.int32, (1, BLOCK), 1)
    queries, scaled, grads, inners, totals = [], [], [], [], []
    for h in range(heads):
        span = slice(h * HEAD_DIM, (h + 1) * HEAD_DIM)
        queries.append(block_rows[:, span])
        scaled.append(block_rows[:, span] * jnp.bfloat16(score_scale))
        grads.append(grads_all[:, span])
        turned = grads_all[:, span].astype(jnp.float32).T
        inners.append(jnp.sum(turned * out_ref[span, :], 0, keepdims=True))
        totals.append(total_ref[0, h : h + 1, :])

    def one(j, carry):
        rows = pl.ds(pl.multiple_of(j * BLOCK, BLOCK), BLOCK)
        key_block = key_s[rows, :]
        value_block = value_s[rows, :]
        place = j * BLOCK + lax.broadcasted_iota(jnp.int32, (BLOCK, BLOCK), 0)
        allowed = (place >= starts) & (place <= at)
        result = []
        key_sum = grad_key_s[rows, :]
        value_sum = grad_value_s[rows, :]
        for h in range(heads):
            scores = jnp.where(allowed, dot_nt(key_block, scaled[h]), far_below)
            prob = jnp.exp(scores - totals[h])
            grad_prob = dot_nt(value_block, grads[h])
            grad_scores = (prob * (grad_prob - inners[h]) * score_scale).astype(jnp.bfloat16)
            value_sum = value_sum + product(prob.astype(jnp.bfloat16), grads[h])
            key_sum = key_sum + product(grad_scores, queries[h])
            result.append(carry[h] + dot_tn(grad_scores, key_block))
        grad_key_s[rows, :] = key_sum
        grad_value_s[rows, :] = value_sum
        return tuple(result)

    first = tuple(jnp.zeros((BLOCK, HEAD_DIM), jnp.float32) for _ in range(heads))
    done = lax.fori_loop(low_ref[step], step + 1, one, first)
    for h in range(heads):
        grad_query_s[own, h * HEAD_DIM : (h + 1) * HEAD_DIM] = done[h]

    @pl.when(step == blocks - 1)
    def _():
        def turn(j, carry):
            rows = pl.ds(pl.multiple_of(j * BLOCK, BLOCK), BLOCK)
            cosine = cosine_ref[rows, :]
            sine = sine_ref[rows, :]
            parts = [
                grad_query_s[rows, h * HEAD_DIM : (h + 1) * HEAD_DIM] for h in range(heads)
            ]
            parts.append(grad_key_s[rows, :])
            half = HEAD_DIM // 2
            turned = [
                part * cosine - jnp.concatenate([part[:, half:], part[:, :half]], 1) * sine
                for part in parts
            ]
            turned.append(grad_value_s[rows, :])
            back_ref[rows, :] = jnp.concatenate(turned, 1).astype(jnp.bfloat16)
            return carry

        lax.fori_loop(0, blocks, turn, 0)


def attend_backward(rows, grads, outs, totals, starts, lows, cosine, sine, heads):
    length, width = rows.shape
    blocks = length // BLOCK
    whole = lambda i, low: (0, 0)
    once = pl.Buffered(1)
    return pl.pallas_call(
        functools.partial(attend_backward_kernel, heads=heads, blocks=blocks),
        out_shape=jax.ShapeDtypeStruct((length, width), jnp.bfloat16),
        grid_spec=pltpu.PrefetchScalarGridSpec(
            num_scalar_prefetch=1,
            grid=(blocks,),
            in_specs=[
                pl.BlockSpec((length, width), whole),
                pl.BlockSpec((BLOCK, heads * HEAD_DIM), lambda i, low: (i, 0)),
                pl.BlockSpec((heads * HEAD_DIM, BLOCK), lambda i, low: (0, i)),
                pl.BlockSpec((1, heads, BLOCK), lambda i, low: (i, 0, 0)),
                pl.BlockSpec((1, 1, BLOCK), lambda i, low: (i, 0, 0)),
                pl.BlockSpec((length, HEAD_DIM), whole, pipeline_mode=once),
                pl.BlockSpec((length, HEAD_DIM), whole, pipeline_mode=once),
            ],
            out_specs=pl.BlockSpec((length, width), whole),
            scratch_shapes=[
                pltpu.VMEM((length, HEAD_DIM), jnp.bfloat16),
                pltpu.VMEM((length, HEAD_DIM), jnp.bfloat16),
                pltpu.VMEM((length, heads * HEAD_DIM), jnp.float32),
                pltpu.VMEM((length, HEAD_DIM), jnp.float32),
                pltpu.VMEM((length, HEAD_DIM), jnp.float32),
            ],
        ),
        name="attend_backward",
    )(lows, rows, grads, outs, totals, starts, cosine, sine)


def after(value, *others):
    return lax.optimization_barrier((value, *others))[0]


def bits_of(size):
    return max(size.bit_length() - 1, 0)


def swap(sent, axis, bit):
    size = lax.axis_size(axis)
    return lax.ppermute(sent, axis, [(i, i ^ (1 << bit)) for i in range(size)])


def side(axis, bit):
    index = lax.axis_index(axis)
    mine = (index // (1 << bit)) % 2
    return (mine, index + (1 - 2 * mine) * (1 << bit))


def pick(dim, index):
    return (slice(None),) * dim + (index,)


def digits(number, count):
    return tuple((number // (1 << (count - 1 - k))) % 2 for k in range(count))


def mesh_copy(source, target, sends, gets, axis, partner):
    return pltpu.make_async_remote_copy(
        src_ref=source,
        dst_ref=target,
        send_sem=sends,
        recv_sem=gets,
        device_id={axis: partner},
        device_id_type=pl.DeviceIdType.MESH,
    )


def greet(partners):
    barrier = pltpu.get_barrier_semaphore()
    for axis, partner in partners:
        pl.semaphore_signal(
            barrier, inc=1, device_id={axis: partner}, device_id_type=pl.DeviceIdType.MESH
        )
    pl.semaphore_wait(barrier, len(partners))


class Lane:
    def __init__(self, labels, order, first, refs, sends, gets, rows=None):
        bits = len(labels)
        self.order, self.first, self.sends, self.gets = (order, first, sends, gets)
        self.sums, self.got = (refs[: bits - 1], refs[bits - 1 : 2 * bits - 1])
        self.labels = [list(labels)]
        for label in order:
            self.labels.append([other for other in self.labels[-1] if other != label])
        self.rows = rows

    @staticmethod
    def scratch(bits, tail, dtype):
        shapes = [pltpu.VMEM((2,) * (bits - 1 - k) + tail, dtype) for k in range(bits)]
        return shapes[:-1] + shapes

    def source(self, k):
        return self.first if k == 0 else self.sums[k - 1]

    def copy(self, k):
        axis, bit = self.order[k]
        mine, partner = side(axis, bit)
        dim = self.labels[k].index((axis, bit))
        return mesh_copy(
            self.source(k).at[pick(dim, 1 - mine)],
            self.got[k],
            self.sends.at[k],
            self.gets.at[k],
            axis,
            partner,
        )

    def start(self, k):
        self.copy(k).start()

    def add(self, k, out=None):
        axis, bit = self.order[k]
        mine, _ = side(axis, bit)
        dim = self.labels[k].index((axis, bit))
        left = len(self.order) - 1 - k
        self.copy(k).wait_recv()
        source, got = (self.source(k), self.got[k])
        target = out if left == 0 else self.sums[k]
        height = got.shape[left]
        rows = self.rows or height
        blocks = height // rows

        def body(i, carry):
            at = digits(i // blocks, left)
            own = pl.ds(pl.multiple_of((i % blocks) * rows, rows), rows)
            if blocks == 1:
                own = slice(None)
            here = at[:dim] + (mine,) + at[dim:]
            total = source[here + (own,)].astype(jnp.float32) + got[at + (own,)].astype(
                jnp.float32
            )
            target[at + (own,)] = total.astype(target.dtype)
            return carry

        lax.fori_loop(0, blocks << left, body, 0)

    def finish(self):
        for k in range(len(self.order)):
            self.copy(k).wait_send()


def reduce_kernel(*refs, units, n_parts, labels, weight_order, share):
    part_refs, refs = (refs[:n_parts], refs[n_parts:])
    weight_ref, gain_ref, up_ref, down_ref, weight_out, gain_out, *refs = refs
    steps = len(units[0][2]) - 1
    sends, keeps, gets = ([], [], [])
    for _ in range(steps):
        sends.append(refs[0])
        keeps.append(refs[1])
        gets.append(refs[2])
        refs = refs[3:]
    bits = len(labels)
    lane_refs, refs = (refs[: 2 * (2 * bits - 1)], refs[2 * (2 * bits - 1) :])
    load_keep, load_came, load_sem, unit_send, unit_get, lane_send, lane_get = refs
    lanes = [
        Lane(
            labels,
            weight_order,
            first,
            lane_refs[number * (2 * bits - 1) : (number + 1) * (2 * bits - 1)],
            lane_send.at[number],
            lane_get.at[number],
        )
        for number, first in enumerate((weight_ref, gain_ref))
    ]
    _, spots, tall, width = load_keep.shape
    rows = 32 if tall % 32 == 0 else tall
    blocks = tall // rows

    greet([(axis, side(axis, bit)[1]) for axis, bit in weight_order])

    def lane_start(k):
        for lane in lanes:
            lane.start(k)

    def lane_add(k):
        for lane, out in zip(lanes, (weight_out, gain_out)):
            lane.add(k, out)

    lane_start(0)

    sequence = [
        n for k in range(steps + 1) for n, unit in enumerate(units) if unit[3] == k
    ]

    def loads(turn):
        _, parts, _, skip = units[sequence[turn]]
        slot = turn % 2
        size = spots >> skip
        return [
            pltpu.make_async_copy(
                part_refs[which].at[place],
                buffer.at[slot, pl.ds(0, size)],
                load_sem.at[slot, number],
            )
            for number, ((which, place), buffer) in enumerate(
                zip(parts, (load_keep, load_came))
            )
        ]

    def unit_copy(unit, order, k):
        axis, bit = order[k + 1]
        return mesh_copy(
            sends[k].at[unit],
            gets[k].at[unit],
            unit_send.at[unit, k],
            unit_get.at[unit, k],
            axis,
            side(axis, bit)[1],
        )

    def unit_add(unit, order, k, left, right):
        mine, _ = side(*order[k + 1])
        half = spots >> (k + 1)

        def fill(target, which):
            def body(i, carry):
                piece = i // blocks
                own = pl.ds(pl.multiple_of((i % blocks) * rows, rows), rows)
                total = left[which * half + piece, own, :].astype(jnp.float32) + right[
                    which * half + piece, own, :
                ].astype(jnp.float32)
                target[unit, piece, own, :] = total.astype(jnp.bfloat16)
                return carry

            lax.fori_loop(0, half * blocks, body, 0)

        fill(sends[k], 1 - mine)
        unit_copy(unit, order, k).start()
        fill(keeps[k], mine)

    def begin_unit(n):
        unit, _, order, skip = units[n]
        turn = sequence.index(n)
        for copy in loads(turn):
            copy.wait()
        left, right = (load_keep.at[turn % 2], load_came.at[turn % 2])
        if skip < steps:
            unit_add(unit, order, skip, left, right)
        else:
            give(unit, left[0].astype(jnp.float32) + right[0].astype(jnp.float32))
        if turn + 2 < len(units):
            for copy in loads(turn + 2):
                copy.start()

    def next_unit(n, k):
        unit, _, order, _ = units[n]
        unit_copy(unit, order, k - 1).wait_recv()
        unit_add(unit, order, k, keeps[k - 1].at[unit], gets[k - 1].at[unit])

    def end_unit(n):
        unit, _, order, _ = units[n]
        unit_copy(unit, order, steps - 1).wait_recv()
        give(unit, keeps[-1][unit, 0].astype(jnp.float32) + gets[-1][unit, 0].astype(jnp.float32))

    def give(unit, total):
        up_ref[unit] = total[:share]
        pieces = width // share
        rest = tall - share
        for p in range(pieces):
            down_ref[unit, p * rest : (p + 1) * rest, :] = total[
                share:, p * share : (p + 1) * share
            ]

    for turn in range(min(2, len(units))):
        for copy in loads(turn):
            copy.start()
    work = []
    first_jobs = 0
    for k in range(steps):
        for n, unit in enumerate(units):
            if unit[3] == k:
                work.append(functools.partial(begin_unit, n))
            elif unit[3] < k:
                work.append(functools.partial(next_unit, n, k))
        first_jobs = first_jobs or len(work)
    for last in (True, False):
        for n, unit in enumerate(units):
            if (unit[3] == steps) == last:
                work.append(functools.partial(begin_unit if last else end_unit, n))
    marks = [first_jobs + (len(work) - first_jobs) * k // bits for k in range(bits)]
    for number, job in enumerate(work):
        for k, mark in enumerate(marks[:-1]):
            if number == mark:
                lane_add(k)
                lane_start(k + 1)
        job()
    lane_add(bits - 1)
    for unit, _, order, skip in units:
        for k in range(skip, steps):
            unit_copy(unit, order, k).wait_send()
    for lane in lanes:
        lane.finish()


def reduce_rest(parts, weights, gains, units, labels, weight_order, share):
    _, spots, tall, width = parts[0].shape
    count = len(units)
    bits = len(labels)
    steps = len(units[0][2]) - 1
    anywhere = pl.BlockSpec(memory_space=pl.ANY)
    vmem = pl.BlockSpec(memory_space=pltpu.VMEM)
    scratch = []
    for k in range(steps):
        scratch += [pltpu.VMEM((count, spots >> (k + 1), tall, width), jnp.bfloat16)] * 3
    for lane in (weights, gains):
        scratch += Lane.scratch(bits, lane.shape[bits:], lane.dtype)
    scratch += [
        pltpu.VMEM((2, spots, tall, width), jnp.bfloat16),
        pltpu.VMEM((2, spots, tall, width), jnp.bfloat16),
        pltpu.SemaphoreType.DMA((2, 2)),
        pltpu.SemaphoreType.DMA((count, steps)),
        pltpu.SemaphoreType.DMA((count, steps)),
        pltpu.SemaphoreType.DMA((2, bits)),
        pltpu.SemaphoreType.DMA((2, bits)),
    ]
    return pl.pallas_call(
        functools.partial(
            reduce_kernel,
            units=units,
            n_parts=len(parts),
            labels=labels,
            weight_order=weight_order,
            share=share,
        ),
        out_shape=(
            jax.ShapeDtypeStruct((count, share, width), jnp.float32),
            jax.ShapeDtypeStruct((count, (tall - share) * (width // share), share), jnp.float32),
            jax.ShapeDtypeStruct(weights.shape[bits:], jnp.float32),
            jax.ShapeDtypeStruct(gains.shape[bits:], jnp.float32),
        ),
        in_specs=[anywhere] * len(parts) + [vmem] * 2,
        out_specs=[vmem] * 4,
        scratch_shapes=scratch,
        compiler_params=pltpu.CompilerParams(
            collective_id=0, has_side_effects=True, vmem_limit_bytes=67 * 1000 * 1000
        ),
        name="reduce_rest",
    )(*parts, weights, gains)


def experts_kernel(
    *refs, sources, rows_dev, count, copies, orders, near, labels, ep_order
):
    rows_hbm, cot_hbm, rank_ref, prob_ref, gate_up_ref, down_ref, *refs = refs
    out_ref, grad_ref, inner_ref, keep_ref, came_ref, *refs = refs
    far = count - near
    sent_refs, refs = (refs[:far], refs[far:])
    rows_s, cot_s, picks_s, out_s, grad_s, send_s, inner_s, inner_got, *refs = refs
    bits = len(labels)
    lane_refs, refs = (refs[: 2 * (2 * bits - 1)], refs[2 * (2 * bits - 1) :])
    load_sem, unit_send, unit_get, lane_send, lane_get, inner_send, inner_take = refs
    me = lax.axis_index("ep")
    step = pl.program_id(0)
    grad_lane, out_lane = [
        Lane(
            labels,
            ep_order,
            first,
            lane_refs[number * (2 * bits - 1) : (number + 1) * (2 * bits - 1)],
            lane_send.at[number],
            lane_get.at[number],
            rows=32,
        )
        for number, first in enumerate((cot_s, rows_s))
    ]

    def unit_copy(e):
        bit = orders[e][0]
        if e < near:
            return mesh_copy(
                send_s.at[e],
                came_ref.at[e],
                unit_send.at[e],
                unit_get.at[e],
                "rep",
                side("rep", bit)[1],
            )
        return pltpu.make_async_copy(send_s.at[e], sent_refs[e - near], unit_send.at[e])

    def inner_copy(d):
        peer = (me + d) % sources
        return mesh_copy(
            inner_s.at[peer],
            inner_got.at[me],
            inner_send.at[d - 1],
            inner_take.at[d - 1],
            "ep",
            peer,
        )

    @pl.when(step == 0)
    def _():
        loads = [
            pltpu.make_async_copy(rows_hbm, rows_s, load_sem.at[0]),
            pltpu.make_async_copy(cot_hbm, cot_s, load_sem.at[1]),
        ]
        for copy in loads:
            copy.start()
        partners = [("ep", (me + d) % sources) for d in range(1, sources)]
        for bit in sorted({order[0] for order in orders[:near]}):
            partners.append(("rep", side("rep", bit)[1]))
        greet(partners)
        for copy in loads:
            copy.wait()

    slots = pl.ds(pl.multiple_of(step * CAP, 16), CAP)
    numbers = lax.broadcasted_iota(jnp.int32, (CAP, rows_dev), 0).astype(jnp.float32)
    rows_in, cots, weights, picks = [], [], [], []
    for s in range(sources):
        rank = rank_ref[s, pl.ds(step, 1), :]
        pick_table = jnp.where(rank == numbers, 1.0, 0.0)
        weights.append(jnp.sum(pick_table * prob_ref[s, pl.ds(step, 1), :], 1, keepdims=True))
        pick_b = pick_table.astype(jnp.bfloat16)
        picks.append(pick_table)
        picks_s[s, slots, :] = pick_b
        rows_in.append(product(pick_b, rows_s[digits(s, bits)]).astype(jnp.bfloat16))
        cots.append(product(pick_b, cot_s[digits(s, bits)]))
    arrived = jnp.concatenate(rows_in, 0)
    weight = jnp.concatenate(weights, 0)
    grad_mix = branch_scale * jnp.concatenate(cots, 0)
    gate_up = gate_up_ref[0]
    down = down_ref[0]
    hidden_units = down.shape[0]
    both = product(arrived, gate_up)
    gate_part = both[:, :hidden_units]
    up_part = both[:, hidden_units:]
    sigmoid_gate = jax.nn.sigmoid(gate_part)
    active = (gate_part * sigmoid_gate * up_part).astype(jnp.bfloat16)
    produced = product(active, down).astype(jnp.bfloat16).astype(jnp.float32)
    inner = jnp.sum(grad_mix * produced, 1, keepdims=True)
    sent_out = (weight * produced).astype(jnp.bfloat16)
    grad_out = (weight * grad_mix).astype(jnp.bfloat16)
    grad_active = dot_nt(grad_out, down)
    grad_down = dot_tn(active, grad_out).astype(jnp.bfloat16)
    grad_gate = grad_active * up_part * sigmoid_gate * (1.0 + gate_part * (1.0 - sigmoid_gate))
    grad_up = grad_active * gate_part * sigmoid_gate
    grad_both = jnp.concatenate([grad_gate, grad_up], 1).astype(jnp.bfloat16)
    grad_gate_up = dot_tn(arrived, grad_both).astype(jnp.bfloat16)
    share = grad_down.shape[1] // copies
    tall = hidden_units // copies

    def put(order, mine):
        bit, *later = order
        for r in range(copies):
            spot = 0
            for b in later:
                spot = 2 * spot + ((r >> b) & 1)
            ref = keep_ref.at[0] if (r >> bit) & 1 == mine else send_s.at[step]
            ref[spot, :share, :] = grad_gate_up[r * share : (r + 1) * share]
            for k in range(copies):
                ref[spot, share : share + tall, k * share : (k + 1) * share] = grad_down[
                    k * tall : (k + 1) * tall, r * share : (r + 1) * share
                ]

    for order in {tuple(order): order for order in orders}.values():
        members = [e for e in range(count) if orders[e] == order]
        here = functools.reduce(jnp.logical_or, [step == e for e in members])
        side_mine, _ = side("rep", order[0])
        for mine in range(2):

            @pl.when(here & (side_mine == mine))
            def _(order=order, mine=mine):
                put(order, mine)

    grad_in = dot_nt(grad_both, gate_up).astype(jnp.bfloat16)
    for s in range(sources):
        part = slice(s * CAP, (s + 1) * CAP)
        out_s[s, slots, :] = sent_out[part]
        grad_s[s, slots, :] = grad_in[part]
        inner_s[s, pl.ds(step, 1), :] = jnp.sum(picks[s] * inner[part], 0, keepdims=True)
    for e in range(count):

        @pl.when(step == e)
        def _(e=e):
            unit_copy(e).start()

    @pl.when(step == count - 1)
    def _():
        for table_of, target, lane in ((grad_s, cot_s, grad_lane), (out_s, rows_s, out_lane)):
            for s in range(sources):
                target[digits(s, bits)] = dot_tn(picks_s[s], table_of[s]).astype(jnp.bfloat16)
            lane.start(0)
        for d in range(1, sources):
            inner_copy(d).start()
        for k in range(bits):
            for lane, total in ((grad_lane, grad_ref), (out_lane, out_ref)):
                lane.add(k, total)
                if k + 1 < bits:
                    lane.start(k + 1)
        inner_got[me] = inner_s[me]
        for d in range(1, sources):
            inner_copy(d).wait_recv()
        inner_ref[...] = inner_got[...]
        for d in range(1, sources):
            inner_copy(d).wait_send()
        grad_lane.finish()
        out_lane.finish()
        for e in range(count):
            unit_copy(e).wait()


def experts(rows, cots, ranks, probs, w_gate_up, w_down, copies, orders, near, labels, ep_order):
    sources, count, rows_dev = ranks.shape
    total, model_width = rows.shape
    hidden_units = w_down.shape[1]
    bits = len(labels)
    tall = model_width // copies + hidden_units // copies
    flat = lambda i: (0, 0)
    cube = lambda i: (0, 0, 0)
    once = pl.Buffered(1)
    anywhere = pl.BlockSpec(memory_space=pl.ANY)
    far = count - near
    shape = (2,) * bits + (rows_dev, model_width)
    piece = (copies // 2, tall, model_width)
    return pl.pallas_call(
        functools.partial(
            experts_kernel,
            sources=sources,
            rows_dev=rows_dev,
            count=count,
            copies=copies,
            orders=orders,
            near=near,
            labels=labels,
            ep_order=ep_order,
        ),
        out_shape=(
            jax.ShapeDtypeStruct((rows_dev, model_width), jnp.float32),
            jax.ShapeDtypeStruct((rows_dev, model_width), jnp.float32),
            jax.ShapeDtypeStruct((sources, count, rows_dev), jnp.float32),
            jax.ShapeDtypeStruct((count,) + piece, jnp.bfloat16),
            jax.ShapeDtypeStruct((near,) + piece, jnp.bfloat16),
        )
        + (jax.ShapeDtypeStruct(piece, jnp.bfloat16),) * far,
        grid=(count,),
        in_specs=[
            anywhere,
            anywhere,
            pl.BlockSpec((sources, count, rows_dev), cube, pipeline_mode=once),
            pl.BlockSpec((sources, count, rows_dev), cube, pipeline_mode=once),
            pl.BlockSpec((1, model_width, 2 * hidden_units), lambda i: (i, 0, 0)),
            pl.BlockSpec((1, hidden_units, model_width), lambda i: (i, 0, 0)),
        ],
        out_specs=[
            pl.BlockSpec((rows_dev, model_width), flat, pipeline_mode=once),
            pl.BlockSpec((rows_dev, model_width), flat, pipeline_mode=once),
            pl.BlockSpec((sources, count, rows_dev), cube, pipeline_mode=once),
            pl.BlockSpec((1,) + piece, lambda i: (i, 0, 0, 0)),
            anywhere,
        ]
        + [anywhere] * far,
        scratch_shapes=[
            pltpu.VMEM(shape, jnp.bfloat16),
            pltpu.VMEM(shape, jnp.bfloat16),
            pltpu.VMEM((sources, count * CAP, rows_dev), jnp.bfloat16),
            pltpu.VMEM((sources, count * CAP, model_width), jnp.bfloat16),
            pltpu.VMEM((sources, count * CAP, model_width), jnp.bfloat16),
            pltpu.VMEM((count,) + piece, jnp.bfloat16),
            pltpu.VMEM((sources, count, rows_dev), jnp.float32),
            pltpu.VMEM((sources, count, rows_dev), jnp.float32),
        ]
        + Lane.scratch(bits, (rows_dev, model_width), jnp.bfloat16) * 2
        + [
            pltpu.SemaphoreType.DMA((2,)),
            pltpu.SemaphoreType.DMA((count,)),
            pltpu.SemaphoreType.DMA((near,)),
            pltpu.SemaphoreType.DMA((2, bits)),
            pltpu.SemaphoreType.DMA((2, bits)),
            pltpu.SemaphoreType.DMA((sources - 1,)),
            pltpu.SemaphoreType.DMA((sources - 1,)),
        ],
        compiler_params=pltpu.CompilerParams(
            collective_id=1, has_side_effects=True, vmem_limit_bytes=67 * 1000 * 1000
        ),
        name="experts",
    )(rows.reshape(shape), cots.reshape(shape), ranks, probs, w_gate_up, w_down)


def on_device(
    tokens,
    segments,
    routes,
    attn_gain,
    w_query,
    w_key,
    w_value,
    w_out,
    mlp_gain,
    w_router,
    w_gate_up,
    w_down,
    cotangent,
    *,
    n_ep,
    n_rep,
):
    inputs = tokens[0]
    own_routes = routes[0]
    grad_output = cotangent[0]
    rows_dev, model_width = inputs.shape
    everyone = ("ep", "rep")
    heads = HEADS // n_rep
    head_width = heads * HEAD_DIM
    shared = max(1, n_rep // KV_HEADS)
    query_width = w_query.shape[1]
    key_width = w_key.shape[1]
    experts_all = w_router.shape[1]
    half_dim = HEAD_DIM // 2

    pack_ids = lax.all_gather(segments[0], "rep", axis=0, tiled=True)
    length = pack_ids.shape[0]
    blocks = length // BLOCK
    offset = lax.axis_index("rep") * rows_dev
    doc_start = jnp.sum((pack_ids[None, :] < pack_ids[:, None]).astype(jnp.int32), 1)
    position = (jnp.arange(length, dtype=jnp.int32) - doc_start).astype(jnp.float32)
    angles = (
        position[:, None]
        * jnp.exp(jnp.arange(half_dim, dtype=jnp.float32) * (-math.log(10000.0) / half_dim))[
            None, :
        ]
    )
    cosine = jnp.cos(angles)
    sine = jnp.sin(angles)
    cosine = jnp.concatenate([cosine, cosine], 1)
    sine = jnp.concatenate([-sine, sine], 1)
    own_cosine = lax.dynamic_slice_in_dim(cosine, offset, rows_dev, 0)
    own_sine = lax.dynamic_slice_in_dim(sine, offset, rows_dev, 0)
    starts = doc_start.reshape(blocks, 1, BLOCK)
    lows = doc_start[::BLOCK] // BLOCK

    joined = jnp.concatenate([w_query, w_key, w_value, w_out, w_router], 1)
    full = lax.all_gather(joined, everyone, axis=0, tiled=True)
    rotated_width = query_width + key_width
    input_width = rotated_width + key_width
    full_in = full[:, :input_width]
    full_out = full[:, input_width : input_width + model_width]
    full_router = full[:, input_width + model_width :]

    normed, factor_one = rms_norm(inputs, attn_gain)
    normed_b = normed.astype(jnp.bfloat16)
    mixed_in = product(normed_b, full_in)
    turn = mixed_in[:, :rotated_width]
    times = rotated_width // HEAD_DIM
    turned = turn * jnp.tile(own_cosine, (1, times)) + swap_halves(turn) * jnp.tile(
        own_sine, (1, times)
    )
    turned_b = turned.astype(jnp.bfloat16)
    value_b = mixed_in[:, rotated_width:].astype(jnp.bfloat16)
    query_part = turned_b[:, :query_width].reshape(rows_dev, n_rep, head_width)
    key_part = turned_b[:, query_width:].reshape(rows_dev, KV_HEADS, HEAD_DIM)
    value_part = value_b.reshape(rows_dev, KV_HEADS, HEAD_DIM)
    if shared > 1:
        key_part = jnp.repeat(key_part, shared, 1)
        value_part = jnp.repeat(value_part, shared, 1)
    sending = jnp.concatenate([query_part, key_part, value_part], 2).transpose(1, 0, 2)
    head_rows = lax.all_to_all(sending, "rep", split_axis=0, concat_axis=0, tiled=True)
    head_rows = head_rows.reshape(length, head_width + 2 * HEAD_DIM)
    mixed, mixed_out, totals = attend_forward(head_rows, starts, lows, heads)
    mixed_rows = lax.all_to_all(
        mixed.reshape(n_rep, rows_dev, head_width), "rep", split_axis=0, concat_axis=0, tiled=True
    )
    mixed_rows = mixed_rows.transpose(1, 0, 2).reshape(rows_dev, query_width)
    hidden = inputs + branch_scale * product(mixed_rows, full_out)

    normed_two, factor_two = rms_norm(hidden, mlp_gain)
    normed_two_b = normed_two.astype(jnp.bfloat16)
    router_f = full_router.astype(jnp.float32)
    logits = product(normed_two_b, full_router)
    numbers = jnp.arange(experts_all, dtype=jnp.int32)
    onehot = jnp.sum((own_routes[:, :, None] == numbers).astype(jnp.float32), 1)
    chosen = onehot > 0.5
    peak = jnp.max(jnp.where(chosen, logits, far_below), 1, keepdims=True)
    raised = jnp.where(chosen, jnp.exp(jnp.minimum(logits - peak, 0.0)), 0.0)
    probs = raised / jnp.sum(raised, 1, keepdims=True)
    before = (
        lax.broadcasted_iota(jnp.int32, (rows_dev, rows_dev), 0)
        > lax.broadcasted_iota(jnp.int32, (rows_dev, rows_dev), 1)
    ).astype(jnp.bfloat16)
    rank = product(before, onehot.astype(jnp.bfloat16))
    kept = chosen & (rank < CAP)
    rank_sent = jnp.where(kept, rank, -1.0).T
    probs_sent = probs.T
    both_sent = jnp.concatenate(
        [rank_sent.reshape(n_ep, -1, rows_dev), probs_sent.reshape(n_ep, -1, rows_dev)], 1
    )
    both_all = lax.all_to_all(both_sent, "ep", split_axis=0, concat_axis=0, tiled=True)
    ranks = both_all[:, : experts_all // n_ep]
    prob_all = both_all[:, experts_all // n_ep :]
    expert_rows = lax.all_gather(normed_two_b, "ep", axis=0, tiled=True)
    expert_cots = lax.all_gather(grad_output.astype(jnp.bfloat16), "ep", axis=0, tiled=True)
    rep_bits = [("rep", b) for b in range(bits_of(n_rep))]
    ep_bits = [("ep", b) for b in range(bits_of(n_ep))]
    count = experts_all // n_ep
    near = count * 3 // 4
    kinds = [k % 2 for k in range(near)] + [0] * (count - near)
    leads = [0, len(rep_bits) - 2]
    orders = [
        [leads[kind]] + [b for b in range(len(rep_bits)) if b != leads[kind]] for kind in kinds
    ]
    out_sum, grad_sum, inner_back, grad_keep, came_near, *sent = experts(
        expert_rows,
        expert_cots,
        ranks,
        prob_all,
        w_gate_up,
        w_down,
        n_rep,
        orders,
        near,
        ep_bits[::-1],
        ep_bits,
    )
    rep_orders = [[("rep", b) for b in order] for order in orders]
    early = list(range(0, near, 2))
    late = early[2:]
    early = early[:2]

    def halves(left, right, label, e=None):
        mine, _ = side(*label)
        half = left.shape[-3] // 2

        def total(which):
            parts = []
            for stack in (left, right):
                start = [jnp.int32(0)] * stack.ndim
                start[-3] = (which * half).astype(jnp.int32)
                size = stack.shape[-3:]
                if e is not None:
                    start[0] = jnp.int32(e)
                part = lax.dynamic_slice(
                    stack, start, (1,) * (stack.ndim - 3) + (half,) + size[1:]
                )
                parts.append(part.reshape((half,) + size[1:]).astype(jnp.float32))
            return (parts[0] + parts[1]).astype(jnp.bfloat16)

        return (total(1 - mine), total(mine))

    output = hidden + branch_scale * out_sum
    grad_probs = inner_back.reshape(experts_all, rows_dev).T
    grad_logits = probs * (grad_probs - jnp.sum(grad_probs * probs, -1, keepdims=True))
    normed_two_f = normed_two_b.astype(jnp.float32)
    grad_router = jnp.dot(normed_two_f.T, grad_logits, precision=lax.Precision.HIGHEST)
    grad_normed_two = grad_sum + jnp.dot(
        grad_logits, router_f.T, precision=lax.Precision.HIGHEST
    )
    grad_hidden_norm, grad_mlp_gain = norm_back(grad_normed_two, hidden, factor_two, mlp_gain)
    grad_hidden = grad_output + grad_hidden_norm
    grad_attn = (branch_scale * grad_hidden).astype(jnp.bfloat16)
    grad_out_w = dot_tn(mixed_rows, grad_attn)
    grad_mixed = dot_nt(grad_attn, full_out).astype(jnp.bfloat16)
    grad_heads = lax.all_to_all(
        grad_mixed.reshape(rows_dev, n_rep, head_width).transpose(1, 0, 2),
        "rep",
        split_axis=0,
        concat_axis=0,
        tiled=True,
    ).reshape(length, head_width)
    beside = [swap(after(sent[0], grad_heads), *rep_orders[near][0])]
    second = {}
    for e in early:
        give, own = halves(grad_keep, came_near, rep_orders[e][1], e)
        second[e] = (own, swap(after(give, grad_heads), *rep_orders[e][1]))
        beside.append(second[e][1])
    returning = attend_backward(
        head_rows, grad_heads, mixed_out, totals, starts, lows, cosine, sine, heads
    )
    returning = after(returning, *beside)
    returned = lax.all_to_all(
        returning.reshape(n_rep, rows_dev, head_width + 2 * HEAD_DIM),
        "rep",
        split_axis=0,
        concat_axis=0,
        tiled=True,
    ).transpose(1, 0, 2)
    parts = [grad_keep, came_near]
    steps_of = {e: ((0, e), (1, e), 0) for e in range(near)}

    def put_by(e, own, got, skip):
        steps_of[e] = ((len(parts), 0), (len(parts) + 1, 0), skip)
        parts.extend([own[None], got[None]])

    for k, half in enumerate(sent):
        got = beside[0] if k == 0 else swap(after(half, returned), *rep_orders[near + k][0])
        steps_of[near + k] = ((0, near + k), (len(parts), 0), 0)
        parts.append(got[None])
    for e in late:
        give, own = halves(grad_keep, came_near, rep_orders[e][1], e)
        put_by(e, own, swap(after(give, returned), *rep_orders[e][1]), 1)
    for e in early:
        give, own = halves(*second[e], rep_orders[e][2])
        put_by(e, own, swap(after(give, returned), *rep_orders[e][2]), 2)
    units = [
        (e, steps_of[e][:2], rep_orders[e], steps_of[e][2])
        for e in sorted(range(count), key=lambda e: (e < near, e))
    ]
    grad_query_rows = returned[:, :, :head_width].reshape(rows_dev, query_width)
    key_back = returned[:, :, head_width : head_width + HEAD_DIM]
    value_back = returned[:, :, head_width + HEAD_DIM :]
    if shared > 1:
        key_back = jnp.sum(
            key_back.reshape(rows_dev, KV_HEADS, shared, HEAD_DIM).astype(jnp.float32), 2
        ).astype(jnp.bfloat16)
        value_back = jnp.sum(
            value_back.reshape(rows_dev, KV_HEADS, shared, HEAD_DIM).astype(jnp.float32), 2
        ).astype(jnp.bfloat16)
    grad_in_rows = jnp.concatenate(
        [
            grad_query_rows,
            key_back.reshape(rows_dev, key_width),
            value_back.reshape(rows_dev, key_width),
        ],
        1,
    )
    grad_w_in = dot_tn(normed_b, grad_in_rows)
    grad_normed = dot_nt(grad_in_rows, full_in)
    grad_inputs_norm, grad_attn_gain = norm_back(grad_normed, inputs, factor_one, attn_gain)
    grad_inputs = grad_hidden + grad_inputs_norm
    everything = n_ep * n_rep
    gains = jnp.concatenate(
        [grad_attn_gain.reshape(everything, -1), grad_mlp_gain.reshape(everything, -1)], 1
    )
    labels = ep_bits[::-1] + rep_bits[::-1]
    shape = (2,) * len(labels)
    weight_grads = jnp.concatenate([grad_w_in, grad_out_w, grad_router], 1).astype(jnp.bfloat16)
    expert_up, expert_down, weights, gains = reduce_rest(
        parts,
        weight_grads.reshape(shape + (-1, weight_grads.shape[1])),
        gains.reshape(shape + (1, -1)),
        units,
        labels,
        ep_bits + rep_bits,
        model_width // n_rep,
    )
    gains = gains[0]
    part = model_width // everything
    return (
        output[None],
        grad_inputs[None],
        gains[:part],
        weights[:, :query_width],
        weights[:, query_width:rotated_width],
        weights[:, rotated_width:input_width],
        weights[:, input_width : input_width + model_width],
        gains[part:],
        weights[:, input_width + model_width :],
        expert_up,
        expert_down,
    )


def solution(mesh):
    placed = (
        P("ep", "rep", None),
        P("ep", "rep"),
        P("ep", "rep", None),
        P(),
        P(("ep", "rep"), None),
        P(("ep", "rep"), None),
        P(("ep", "rep"), None),
        P(("ep", "rep"), None),
        P(),
        P(("ep", "rep"), None),
        P("ep", None, None),
        P("ep", None, None),
        P("ep", "rep", None),
    )
    return jax.shard_map(
        functools.partial(on_device, n_ep=mesh.shape["ep"], n_rep=mesh.shape["rep"]),
        mesh=mesh,
        in_specs=placed,
        out_specs=(
            P("ep", "rep", None),
            P("ep", "rep", None),
            P(("ep", "rep")),
            P(("ep", "rep"), None),
            P(("ep", "rep"), None),
            P(("ep", "rep"), None),
            P(("ep", "rep"), None),
            P(("ep", "rep")),
            P(("ep", "rep"), None),
            P("ep", "rep", None),
            P("ep", None, "rep"),
        ),
        check_vma=False,
    )
```

```python
import functools
import math

import jax
import jax.numpy as jnp
from jax import lax
from jax.experimental import pallas as pl
from jax.experimental.pallas import tpu as pltpu
from jax.sharding import PartitionSpec as P

HEADS = 16
KV_HEADS = 8
HEAD_DIM = 64
CAP = 80
BLOCK = 256

epsilon = 1e-06
score_scale = 0.015625
branch_scale = 0.22
far_below = -1e30

NT = (((1,), (1,)), ((), ()))
TN = (((0,), (0,)), ((), ()))


def product(left, right):
    return jnp.dot(left, right, preferred_element_type=jnp.float32)


def dot_nt(left, right):
    return lax.dot_general(left, right, NT, preferred_element_type=jnp.float32)


def dot_tn(left, right):
    return lax.dot_general(left, right, TN, preferred_element_type=jnp.float32)


def rms_norm(values, gain):
    factor = lax.rsqrt(jnp.mean(values * values, -1, keepdims=True) + epsilon)
    return (values * factor * gain, factor)


def norm_back(grad_normed, values, factor, gain):
    scaled = grad_normed * gain
    gain_part = jnp.sum(grad_normed * values * factor, 0)
    inner_sum = jnp.mean(scaled * values, -1, keepdims=True)
    return (factor * scaled - values * (factor * factor * factor) * inner_sum, gain_part)


def swap_halves(values):
    count, width = values.shape
    half_dim = HEAD_DIM // 2
    lane = lax.broadcasted_iota(jnp.int32, values.shape, 1)
    return jnp.where(
        lane % HEAD_DIM < half_dim,
        jnp.roll(values, -half_dim, 1),
        jnp.roll(values, half_dim, 1),
    )


def attend_forward_kernel(
    low_ref, rows_ref, start_ref, mixed_ref, out_ref, total_ref, key_s, value_s, *, heads
):
    step = pl.program_id(0)
    width = heads * HEAD_DIM

    @pl.when(step == 0)
    def _():
        key_s[...] = rows_ref[:, width : width + HEAD_DIM]
        value_s[...] = rows_ref[:, width + HEAD_DIM : width + 2 * HEAD_DIM]

    block_rows = rows_ref[pl.ds(pl.multiple_of(step * BLOCK, BLOCK), BLOCK), :]
    queries = [
        block_rows[:, h * HEAD_DIM : (h + 1) * HEAD_DIM] * jnp.bfloat16(score_scale)
        for h in range(heads)
    ]
    starts = start_ref[0]
    at = step * BLOCK + lax.broadcasted_iota(jnp.int32, (1, BLOCK), 1)

    def one(j, carry):
        rows = pl.ds(pl.multiple_of(j * BLOCK, BLOCK), BLOCK)
        key_block = key_s[rows, :]
        value_block = value_s[rows, :]
        place = j * BLOCK + lax.broadcasted_iota(jnp.int32, (BLOCK, BLOCK), 0)
        allowed = (place >= starts) & (place <= at)
        result = []
        for h in range(heads):
            peak, total, mixed = carry[h]
            scores = jnp.where(allowed, dot_nt(key_block, queries[h]), far_below)
            new_peak = jnp.maximum(peak, jnp.max(scores, 0, keepdims=True))
            fade = jnp.exp(peak - new_peak)
            raised = jnp.exp(scores - new_peak)
            total = fade * total + jnp.sum(raised, 0, keepdims=True)
            mixed = fade * mixed + dot_tn(value_block, raised.astype(jnp.bfloat16))
            result.append((new_peak, total, mixed))
        return tuple(result)

    first = tuple(
        (
            jnp.full((1, BLOCK), far_below, jnp.float32),
            jnp.zeros((1, BLOCK), jnp.float32),
            jnp.zeros((HEAD_DIM, BLOCK), jnp.float32),
        )
        for _ in range(heads)
    )
    done = lax.fori_loop(low_ref[step], step + 1, one, first)
    for h in range(heads):
        peak, total, mixed = done[h]
        mixed = mixed / total
        out_ref[h * HEAD_DIM : (h + 1) * HEAD_DIM, :] = mixed
        total_ref[0, h : h + 1, :] = peak + jnp.log(total)
        mixed_ref[:, h * HEAD_DIM : (h + 1) * HEAD_DIM] = mixed.T.astype(jnp.bfloat16)


def attend_forward(rows, starts, lows, heads):
    length, width = rows.shape
    blocks = length // BLOCK
    whole = lambda i, low: (0, 0)
    return pl.pallas_call(
        functools.partial(attend_forward_kernel, heads=heads),
        out_shape=(
            jax.ShapeDtypeStruct((length, heads * HEAD_DIM), jnp.bfloat16),
            jax.ShapeDtypeStruct((heads * HEAD_DIM, length), jnp.float32),
            jax.ShapeDtypeStruct((blocks, heads, BLOCK), jnp.float32),
        ),
        grid_spec=pltpu.PrefetchScalarGridSpec(
            num_scalar_prefetch=1,
            grid=(blocks,),
            in_specs=[
                pl.BlockSpec((length, width), whole),
                pl.BlockSpec((1, 1, BLOCK), lambda i, low: (i, 0, 0)),
            ],
            out_specs=[
                pl.BlockSpec((BLOCK, heads * HEAD_DIM), lambda i, low: (i, 0)),
                pl.BlockSpec((heads * HEAD_DIM, BLOCK), lambda i, low: (0, i)),
                pl.BlockSpec((1, heads, BLOCK), lambda i, low: (i, 0, 0)),
            ],
            scratch_shapes=[
                pltpu.VMEM((length, HEAD_DIM), jnp.bfloat16),
                pltpu.VMEM((length, HEAD_DIM), jnp.bfloat16),
            ],
        ),
        name="attend_forward",
    )(lows, rows, starts)


def attend_backward_kernel(
    low_ref,
    rows_ref,
    grad_ref,
    out_ref,
    total_ref,
    start_ref,
    cosine_ref,
    sine_ref,
    back_ref,
    key_s,
    value_s,
    grad_query_s,
    grad_key_s,
    grad_value_s,
    *,
    heads,
    blocks,
):
    step = pl.program_id(0)
    width = heads * HEAD_DIM

    @pl.when(step == 0)
    def _():
        key_s[...] = rows_ref[:, width : width + HEAD_DIM]
        value_s[...] = rows_ref[:, width + HEAD_DIM : width + 2 * HEAD_DIM]
        grad_key_s[...] = jnp.zeros_like(grad_key_s)
        grad_value_s[...] = jnp.zeros_like(grad_value_s)

    own = pl.ds(pl.multiple_of(step * BLOCK, BLOCK), BLOCK)
    block_rows = rows_ref[own, :]
    grads_all = grad_ref[...]
    starts = start_ref[0]
    at = step * BLOCK + lax.broadcasted_iota(jnp.int32, (1, BLOCK), 1)
    queries, scaled, grads, inners, totals = [], [], [], [], []
    for h in range(heads):
        span = slice(h * HEAD_DIM, (h + 1) * HEAD_DIM)
        queries.append(block_rows[:, span])
        scaled.append(block_rows[:, span] * jnp.bfloat16(score_scale))
        grads.append(grads_all[:, span])
        turned = grads_all[:, span].astype(jnp.float32).T
        inners.append(jnp.sum(turned * out_ref[span, :], 0, keepdims=True))
        totals.append(total_ref[0, h : h + 1, :])

    def one(j, carry):
        rows = pl.ds(pl.multiple_of(j * BLOCK, BLOCK), BLOCK)
        key_block = key_s[rows, :]
        value_block = value_s[rows, :]
        place = j * BLOCK + lax.broadcasted_iota(jnp.int32, (BLOCK, BLOCK), 0)
        allowed = (place >= starts) & (place <= at)
        result = []
        key_sum = grad_key_s[rows, :]
        value_sum = grad_value_s[rows, :]
        for h in range(heads):
            scores = jnp.where(allowed, dot_nt(key_block, scaled[h]), far_below)
            prob = jnp.exp(scores - totals[h])
            grad_prob = dot_nt(value_block, grads[h])
            grad_scores = (prob * (grad_prob - inners[h]) * score_scale).astype(jnp.bfloat16)
            value_sum = value_sum + product(prob.astype(jnp.bfloat16), grads[h])
            key_sum = key_sum + product(grad_scores, queries[h])
            result.append(carry[h] + dot_tn(grad_scores, key_block))
        grad_key_s[rows, :] = key_sum
        grad_value_s[rows, :] = value_sum
        return tuple(result)

    first = tuple(jnp.zeros((BLOCK, HEAD_DIM), jnp.float32) for _ in range(heads))
    done = lax.fori_loop(low_ref[step], step + 1, one, first)
    for h in range(heads):
        grad_query_s[own, h * HEAD_DIM : (h + 1) * HEAD_DIM] = done[h]

    @pl.when(step == blocks - 1)
    def _():
        def turn(j, carry):
            rows = pl.ds(pl.multiple_of(j * BLOCK, BLOCK), BLOCK)
            cosine = cosine_ref[rows, :]
            sine = sine_ref[rows, :]
            parts = [
                grad_query_s[rows, h * HEAD_DIM : (h + 1) * HEAD_DIM] for h in range(heads)
            ]
            parts.append(grad_key_s[rows, :])
            half = HEAD_DIM // 2
            turned = [
                part * cosine - jnp.concatenate([part[:, half:], part[:, :half]], 1) * sine
                for part in parts
            ]
            turned.append(grad_value_s[rows, :])
            back_ref[rows, :] = jnp.concatenate(turned, 1).astype(jnp.bfloat16)
            return carry

        lax.fori_loop(0, blocks, turn, 0)


def attend_backward(rows, grads, outs, totals, starts, lows, cosine, sine, heads):
    length, width = rows.shape
    blocks = length // BLOCK
    whole = lambda i, low: (0, 0)
    once = pl.Buffered(1)
    return pl.pallas_call(
        functools.partial(attend_backward_kernel, heads=heads, blocks=blocks),
        out_shape=jax.ShapeDtypeStruct((length, width), jnp.bfloat16),
        grid_spec=pltpu.PrefetchScalarGridSpec(
            num_scalar_prefetch=1,
            grid=(blocks,),
            in_specs=[
                pl.BlockSpec((length, width), whole),
                pl.BlockSpec((BLOCK, heads * HEAD_DIM), lambda i, low: (i, 0)),
                pl.BlockSpec((heads * HEAD_DIM, BLOCK), lambda i, low: (0, i)),
                pl.BlockSpec((1, heads, BLOCK), lambda i, low: (i, 0, 0)),
                pl.BlockSpec((1, 1, BLOCK), lambda i, low: (i, 0, 0)),
                pl.BlockSpec((length, HEAD_DIM), whole, pipeline_mode=once),
                pl.BlockSpec((length, HEAD_DIM), whole, pipeline_mode=once),
            ],
            out_specs=pl.BlockSpec((length, width), whole),
            scratch_shapes=[
                pltpu.VMEM((length, HEAD_DIM), jnp.bfloat16),
                pltpu.VMEM((length, HEAD_DIM), jnp.bfloat16),
                pltpu.VMEM((length, heads * HEAD_DIM), jnp.float32),
                pltpu.VMEM((length, HEAD_DIM), jnp.float32),
                pltpu.VMEM((length, HEAD_DIM), jnp.float32),
            ],
        ),
        name="attend_backward",
    )(lows, rows, grads, outs, totals, starts, cosine, sine)


def after(value, *others):
    return lax.optimization_barrier((value, *others))[0]


def bits_of(size):
    return max(size.bit_length() - 1, 0)


def swap(sent, axis, bit):
    size = lax.axis_size(axis)
    return lax.ppermute(sent, axis, [(i, i ^ (1 << bit)) for i in range(size)])


def side(axis, bit):
    index = lax.axis_index(axis)
    mine = (index // (1 << bit)) % 2
    return (mine, index + (1 - 2 * mine) * (1 << bit))


def pick(dim, index):
    return (slice(None),) * dim + (index,)


def digits(number, count):
    return tuple((number // (1 << (count - 1 - k))) % 2 for k in range(count))


def mesh_copy(source, target, sends, gets, axis, partner):
    return pltpu.make_async_remote_copy(
        src_ref=source,
        dst_ref=target,
        send_sem=sends,
        recv_sem=gets,
        device_id={axis: partner},
        device_id_type=pl.DeviceIdType.MESH,
    )


def greet(partners):
    barrier = pltpu.get_barrier_semaphore()
    for axis, partner in partners:
        pl.semaphore_signal(
            barrier, inc=1, device_id={axis: partner}, device_id_type=pl.DeviceIdType.MESH
        )
    pl.semaphore_wait(barrier, len(partners))


class Lane:
    def __init__(self, labels, order, first, refs, sends, gets, rows=None):
        bits = len(labels)
        self.order, self.first, self.sends, self.gets = (order, first, sends, gets)
        self.sums, self.got = (refs[: bits - 1], refs[bits - 1 : 2 * bits - 1])
        self.labels = [list(labels)]
        for label in order:
            self.labels.append([other for other in self.labels[-1] if other != label])
        self.rows = rows

    @staticmethod
    def scratch(bits, tail, dtype):
        shapes = [pltpu.VMEM((2,) * (bits - 1 - k) + tail, dtype) for k in range(bits)]
        return shapes[:-1] + shapes

    def source(self, k):
        return self.first if k == 0 else self.sums[k - 1]

    def copy(self, k):
        axis, bit = self.order[k]
        mine, partner = side(axis, bit)
        dim = self.labels[k].index((axis, bit))
        return mesh_copy(
            self.source(k).at[pick(dim, 1 - mine)],
            self.got[k],
            self.sends.at[k],
            self.gets.at[k],
            axis,
            partner,
        )

    def start(self, k):
        self.copy(k).start()

    def add(self, k, out=None):
        axis, bit = self.order[k]
        mine, _ = side(axis, bit)
        dim = self.labels[k].index((axis, bit))
        left = len(self.order) - 1 - k
        self.copy(k).wait_recv()
        source, got = (self.source(k), self.got[k])
        target = out if left == 0 else self.sums[k]
        height = got.shape[left]
        rows = self.rows or height
        blocks = height // rows

        def body(i, carry):
            at = digits(i // blocks, left)
            own = pl.ds(pl.multiple_of((i % blocks) * rows, rows), rows)
            if blocks == 1:
                own = slice(None)
            here = at[:dim] + (mine,) + at[dim:]
            total = source[here + (own,)].astype(jnp.float32) + got[at + (own,)].astype(
                jnp.float32
            )
            target[at + (own,)] = total.astype(target.dtype)
            return carry

        lax.fori_loop(0, blocks << left, body, 0)

    def finish(self):
        for k in range(len(self.order)):
            self.copy(k).wait_send()


def reduce_kernel(*refs, units, n_parts, labels, weight_order, share):
    part_refs, refs = (refs[:n_parts], refs[n_parts:])
    weight_ref, gain_ref, up_ref, down_ref, weight_out, gain_out, late_ref, *refs = refs
    steps = len(units[0][2]) - 1
    sends, keeps, gets = ([], [], [])
    for _ in range(steps):
        sends.append(refs[0])
        keeps.append(refs[1])
        gets.append(refs[2])
        refs = refs[3:]
    bits = len(labels)
    lane_refs, refs = (refs[: 2 * (2 * bits - 1)], refs[2 * (2 * bits - 1) :])
    load_keep, load_came, load_sem, unit_send, unit_get, lane_send, lane_get, late_sem = refs
    lanes = [
        Lane(
            labels,
            weight_order,
            first,
            lane_refs[number * (2 * bits - 1) : (number + 1) * (2 * bits - 1)],
            lane_send.at[number],
            lane_get.at[number],
        )
        for number, first in enumerate((weight_ref, gain_ref))
    ]
    _, spots, tall, width = load_keep.shape
    rows = 32 if tall % 32 == 0 else tall
    blocks = tall // rows

    greet([(axis, side(axis, bit)[1]) for axis, bit in weight_order])

    def lane_start(k):
        for lane in lanes:
            lane.start(k)

    def lane_add(k):
        for lane, out in zip(lanes, (weight_out, gain_out)):
            lane.add(k, out)

    lane_start(0)

    late = [n for n, unit in enumerate(units) if unit[3] < 0]
    half_way = [n for n, unit in enumerate(units) if 0 < unit[3] < steps]
    fresh = [n for n, unit in enumerate(units) if unit[3] == 0]
    done = [n for n, unit in enumerate(units) if unit[3] == steps]
    sequence = half_way + fresh + late + done

    def late_copy(n):
        _, ((_, _), (which, place)), order, _ = units[n]
        axis, bit = order[0]
        return mesh_copy(
            part_refs[which].at[place],
            late_ref.at[late.index(n)],
            late_sem.at[0, late.index(n)],
            late_sem.at[1, late.index(n)],
            axis,
            side(axis, bit)[1],
        )

    def loads(turn):
        n = sequence[turn]
        _, parts, _, skip = units[n]
        slot = turn % 2
        size = spots >> max(skip, 0)
        sources = [part_refs[which].at[place] for which, place in parts]
        if skip < 0:
            sources[1] = late_ref.at[late.index(n)]
        return [
            pltpu.make_async_copy(
                source, buffer.at[slot, pl.ds(0, size)], load_sem.at[slot, number]
            )
            for number, (source, buffer) in enumerate(zip(sources, (load_keep, load_came)))
        ]

    def load(turn):
        if turn < len(units) and units[sequence[turn]][3] >= 0:
            for copy in loads(turn):
                copy.start()

    def unit_copy(unit, order, k):
        axis, bit = order[k + 1]
        return mesh_copy(
            sends[k].at[unit],
            gets[k].at[unit],
            unit_send.at[unit, k],
            unit_get.at[unit, k],
            axis,
            side(axis, bit)[1],
        )

    def unit_add(unit, order, k, left, right):
        mine, _ = side(*order[k + 1])
        half = spots >> (k + 1)

        def fill(target, which):
            def body(i, carry):
                piece = i // blocks
                own = pl.ds(pl.multiple_of((i % blocks) * rows, rows), rows)
                total = left[which * half + piece, own, :].astype(jnp.float32) + right[
                    which * half + piece, own, :
                ].astype(jnp.float32)
                target[unit, piece, own, :] = total.astype(jnp.bfloat16)
                return carry

            lax.fori_loop(0, half * blocks, body, 0)

        fill(sends[k], 1 - mine)
        unit_copy(unit, order, k).start()
        fill(keeps[k], mine)

    def begin_unit(n):
        unit, _, order, skip = units[n]
        turn = sequence.index(n)
        if skip < 0:
            late_copy(n).wait_recv()
            for copy in loads(turn):
                copy.start()
        for copy in loads(turn):
            copy.wait()
        left, right = (load_keep.at[turn % 2], load_came.at[turn % 2])
        if skip < steps:
            unit_add(unit, order, max(skip, 0), left, right)
        else:
            give(unit, left[0].astype(jnp.float32) + right[0].astype(jnp.float32))
        load(turn + 2)

    def next_unit(n, k):
        unit, _, order, _ = units[n]
        unit_copy(unit, order, k - 1).wait_recv()
        unit_add(unit, order, k, keeps[k - 1].at[unit], gets[k - 1].at[unit])

    def end_unit(n):
        unit, _, order, _ = units[n]
        unit_copy(unit, order, steps - 1).wait_recv()
        give(unit, keeps[-1][unit, 0].astype(jnp.float32) + gets[-1][unit, 0].astype(jnp.float32))

    def give(unit, total):
        up_ref[unit] = total[:share]
        pieces = width // share
        rest = tall - share
        for p in range(pieces):
            down_ref[unit, p * rest : (p + 1) * rest, :] = total[
                share:, p * share : (p + 1) * share
            ]

    load(0)
    load(1)
    def late_start():
        for n in late:
            late_copy(n).start()

    def lane_turn(k):
        lane_add(k)
        if k + 1 < bits:
            lane_start(k + 1)

    work = [(begin_unit, n) for n in half_way + fresh[:1]] + [(lane_turn, 0)]
    work += [(begin_unit, n) for n in fresh[1:2]] + [(late_start,)]
    work += [(begin_unit, n) for n in fresh[2:]]
    for k in range(1, steps):
        onward = [n for n in half_way if units[n][3] < k] + fresh
        work += [(next_unit, n, k) for n in onward[:2]]
        if k == 1:
            work += [(lane_turn, 1)] + [(begin_unit, n) for n in late]
        work += [(next_unit, n, k) for n in onward[2:3]]
        work += [(next_unit, n, k) for n in late]
        work += [(next_unit, n, k) for n in onward[3:]]
    work += [(begin_unit, n) for n in done]
    work += [(end_unit, n) for n in half_way + fresh[:2] + late] + [(lane_turn, 2)]
    work += [(end_unit, n) for n in fresh[2:3]] + [(lane_turn, 3)]
    work += [(end_unit, n) for n in fresh[3:]]
    work += [(lane_turn, k) for k in range(4, bits)]
    for job, *arguments in work:
        job(*arguments)
    for unit, _, order, skip in units:
        for k in range(max(skip, 0), steps):
            unit_copy(unit, order, k).wait_send()
    for n in late:
        late_copy(n).wait_send()
    for lane in lanes:
        lane.finish()


def reduce_rest(parts, weights, gains, units, labels, weight_order, share):
    _, spots, tall, width = parts[0].shape
    count = len(units)
    bits = len(labels)
    steps = len(units[0][2]) - 1
    late = max(1, len([unit for unit in units if unit[3] < 0]))
    anywhere = pl.BlockSpec(memory_space=pl.ANY)
    vmem = pl.BlockSpec(memory_space=pltpu.VMEM)
    scratch = []
    for k in range(steps):
        scratch += [pltpu.VMEM((count, spots >> (k + 1), tall, width), jnp.bfloat16)] * 3
    for lane in (weights, gains):
        scratch += Lane.scratch(bits, lane.shape[bits:], lane.dtype)
    scratch += [
        pltpu.VMEM((2, spots, tall, width), jnp.bfloat16),
        pltpu.VMEM((2, spots, tall, width), jnp.bfloat16),
        pltpu.SemaphoreType.DMA((2, 2)),
        pltpu.SemaphoreType.DMA((count, steps)),
        pltpu.SemaphoreType.DMA((count, steps)),
        pltpu.SemaphoreType.DMA((2, bits)),
        pltpu.SemaphoreType.DMA((2, bits)),
        pltpu.SemaphoreType.DMA((2, late)),
    ]
    return pl.pallas_call(
        functools.partial(
            reduce_kernel,
            units=units,
            n_parts=len(parts),
            labels=labels,
            weight_order=weight_order,
            share=share,
        ),
        out_shape=(
            jax.ShapeDtypeStruct((count, share, width), jnp.float32),
            jax.ShapeDtypeStruct((count, (tall - share) * (width // share), share), jnp.float32),
            jax.ShapeDtypeStruct(weights.shape[bits:], jnp.float32),
            jax.ShapeDtypeStruct(gains.shape[bits:], jnp.float32),
            jax.ShapeDtypeStruct((late, spots, tall, width), jnp.bfloat16),
        ),
        in_specs=[anywhere] * len(parts) + [vmem] * 2,
        out_specs=[vmem] * 4 + [anywhere],
        scratch_shapes=scratch,
        compiler_params=pltpu.CompilerParams(
            collective_id=0, has_side_effects=True, vmem_limit_bytes=67 * 1000 * 1000
        ),
        name="reduce_rest",
    )(*parts, weights, gains)


def experts_kernel(
    *refs, sources, rows_dev, count, copies, orders, near, labels, ep_order
):
    rows_hbm, cot_hbm, rank_ref, prob_ref, gate_up_ref, down_ref, *refs = refs
    out_ref, grad_ref, inner_ref, keep_ref, came_ref, *refs = refs
    far = count - near
    sent_refs, refs = (refs[:far], refs[far:])
    rows_s, cot_s, picks_s, out_s, grad_s, send_s, inner_s, inner_got, *refs = refs
    bits = len(labels)
    lane_refs, refs = (refs[: 2 * (2 * bits - 1)], refs[2 * (2 * bits - 1) :])
    load_sem, unit_send, unit_get, lane_send, lane_get, inner_send, inner_take = refs
    me = lax.axis_index("ep")
    step = pl.program_id(0)
    grad_lane, out_lane = [
        Lane(
            labels,
            ep_order,
            first,
            lane_refs[number * (2 * bits - 1) : (number + 1) * (2 * bits - 1)],
            lane_send.at[number],
            lane_get.at[number],
            rows=32,
        )
        for number, first in enumerate((cot_s, rows_s))
    ]

    def unit_copy(e):
        bit = orders[e][0]
        if e < near:
            return mesh_copy(
                send_s.at[e],
                came_ref.at[e],
                unit_send.at[e],
                unit_get.at[e],
                "rep",
                side("rep", bit)[1],
            )
        return pltpu.make_async_copy(send_s.at[e], sent_refs[e - near], unit_send.at[e])

    def inner_copy(d):
        peer = (me + d) % sources
        return mesh_copy(
            inner_s.at[peer],
            inner_got.at[me],
            inner_send.at[d - 1],
            inner_take.at[d - 1],
            "ep",
            peer,
        )

    @pl.when(step == 0)
    def _():
        loads = [
            pltpu.make_async_copy(rows_hbm, rows_s, load_sem.at[0]),
            pltpu.make_async_copy(cot_hbm, cot_s, load_sem.at[1]),
        ]
        for copy in loads:
            copy.start()
        partners = [("ep", (me + d) % sources) for d in range(1, sources)]
        for bit in sorted({order[0] for order in orders[:near]}):
            partners.append(("rep", side("rep", bit)[1]))
        greet(partners)
        for copy in loads:
            copy.wait()

    slots = pl.ds(pl.multiple_of(step * CAP, 16), CAP)
    numbers = lax.broadcasted_iota(jnp.int32, (CAP, rows_dev), 0).astype(jnp.float32)
    rows_in, cots, weights, picks = [], [], [], []
    for s in range(sources):
        rank = rank_ref[s, pl.ds(step, 1), :]
        pick_table = jnp.where(rank == numbers, 1.0, 0.0)
        weights.append(jnp.sum(pick_table * prob_ref[s, pl.ds(step, 1), :], 1, keepdims=True))
        pick_b = pick_table.astype(jnp.bfloat16)
        picks.append(pick_table)
        picks_s[s, slots, :] = pick_b
        rows_in.append(product(pick_b, rows_s[digits(s, bits)]).astype(jnp.bfloat16))
        cots.append(product(pick_b, cot_s[digits(s, bits)]))
    arrived = jnp.concatenate(rows_in, 0)
    weight = jnp.concatenate(weights, 0)
    grad_mix = branch_scale * jnp.concatenate(cots, 0)
    gate_up = gate_up_ref[0]
    down = down_ref[0]
    hidden_units = down.shape[0]
    both = product(arrived, gate_up)
    gate_part = both[:, :hidden_units]
    up_part = both[:, hidden_units:]
    sigmoid_gate = jax.nn.sigmoid(gate_part)
    active = (gate_part * sigmoid_gate * up_part).astype(jnp.bfloat16)
    produced = product(active, down).astype(jnp.bfloat16).astype(jnp.float32)
    inner = jnp.sum(grad_mix * produced, 1, keepdims=True)
    sent_out = (weight * produced).astype(jnp.bfloat16)
    grad_out = (weight * grad_mix).astype(jnp.bfloat16)
    grad_active = dot_nt(grad_out, down)
    grad_down = dot_tn(active, grad_out).astype(jnp.bfloat16)
    grad_gate = grad_active * up_part * sigmoid_gate * (1.0 + gate_part * (1.0 - sigmoid_gate))
    grad_up = grad_active * gate_part * sigmoid_gate
    grad_both = jnp.concatenate([grad_gate, grad_up], 1).astype(jnp.bfloat16)
    grad_gate_up = dot_tn(arrived, grad_both).astype(jnp.bfloat16)
    share = grad_down.shape[1] // copies
    tall = hidden_units // copies

    def put(order, mine):
        bit, *later = order
        for r in range(copies):
            spot = 0
            for b in later:
                spot = 2 * spot + ((r >> b) & 1)
            ref = keep_ref.at[0] if (r >> bit) & 1 == mine else send_s.at[step]
            ref[spot, :share, :] = grad_gate_up[r * share : (r + 1) * share]
            for k in range(copies):
                ref[spot, share : share + tall, k * share : (k + 1) * share] = grad_down[
                    k * tall : (k + 1) * tall, r * share : (r + 1) * share
                ]

    for order in {tuple(order): order for order in orders}.values():
        members = [e for e in range(count) if orders[e] == order]
        here = functools.reduce(jnp.logical_or, [step == e for e in members])
        side_mine, _ = side("rep", order[0])
        for mine in range(2):

            @pl.when(here & (side_mine == mine))
            def _(order=order, mine=mine):
                put(order, mine)

    grad_in = dot_nt(grad_both, gate_up).astype(jnp.bfloat16)
    for s in range(sources):
        part = slice(s * CAP, (s + 1) * CAP)
        out_s[s, slots, :] = sent_out[part]
        grad_s[s, slots, :] = grad_in[part]
        inner_s[s, pl.ds(step, 1), :] = jnp.sum(picks[s] * inner[part], 0, keepdims=True)
    for e in range(count):

        @pl.when(step == e)
        def _(e=e):
            unit_copy(e).start()

    @pl.when(step == count - 1)
    def _():
        for table_of, target, lane in ((grad_s, cot_s, grad_lane), (out_s, rows_s, out_lane)):
            for s in range(sources):
                target[digits(s, bits)] = dot_tn(picks_s[s], table_of[s]).astype(jnp.bfloat16)
            lane.start(0)
        for d in range(1, sources):
            inner_copy(d).start()
        for k in range(bits):
            for lane, total in ((grad_lane, grad_ref), (out_lane, out_ref)):
                lane.add(k, total)
                if k + 1 < bits:
                    lane.start(k + 1)
        inner_got[me] = inner_s[me]
        for d in range(1, sources):
            inner_copy(d).wait_recv()
        inner_ref[...] = inner_got[...]
        for d in range(1, sources):
            inner_copy(d).wait_send()
        grad_lane.finish()
        out_lane.finish()
        for e in range(count):
            unit_copy(e).wait()


def experts(rows, cots, ranks, probs, w_gate_up, w_down, copies, orders, near, labels, ep_order):
    sources, count, rows_dev = ranks.shape
    total, model_width = rows.shape
    hidden_units = w_down.shape[1]
    bits = len(labels)
    tall = model_width // copies + hidden_units // copies
    flat = lambda i: (0, 0)
    cube = lambda i: (0, 0, 0)
    once = pl.Buffered(1)
    anywhere = pl.BlockSpec(memory_space=pl.ANY)
    far = count - near
    shape = (2,) * bits + (rows_dev, model_width)
    piece = (copies // 2, tall, model_width)
    return pl.pallas_call(
        functools.partial(
            experts_kernel,
            sources=sources,
            rows_dev=rows_dev,
            count=count,
            copies=copies,
            orders=orders,
            near=near,
            labels=labels,
            ep_order=ep_order,
        ),
        out_shape=(
            jax.ShapeDtypeStruct((rows_dev, model_width), jnp.float32),
            jax.ShapeDtypeStruct((rows_dev, model_width), jnp.float32),
            jax.ShapeDtypeStruct((sources, count, rows_dev), jnp.float32),
            jax.ShapeDtypeStruct((count,) + piece, jnp.bfloat16),
            jax.ShapeDtypeStruct((near,) + piece, jnp.bfloat16),
        )
        + (jax.ShapeDtypeStruct(piece, jnp.bfloat16),) * far,
        grid=(count,),
        in_specs=[
            anywhere,
            anywhere,
            pl.BlockSpec((sources, count, rows_dev), cube, pipeline_mode=once),
            pl.BlockSpec((sources, count, rows_dev), cube, pipeline_mode=once),
            pl.BlockSpec((1, model_width, 2 * hidden_units), lambda i: (i, 0, 0)),
            pl.BlockSpec((1, hidden_units, model_width), lambda i: (i, 0, 0)),
        ],
        out_specs=[
            pl.BlockSpec((rows_dev, model_width), flat, pipeline_mode=once),
            pl.BlockSpec((rows_dev, model_width), flat, pipeline_mode=once),
            pl.BlockSpec((sources, count, rows_dev), cube, pipeline_mode=once),
            pl.BlockSpec((1,) + piece, lambda i: (i, 0, 0, 0)),
            anywhere,
        ]
        + [anywhere] * far,
        scratch_shapes=[
            pltpu.VMEM(shape, jnp.bfloat16),
            pltpu.VMEM(shape, jnp.bfloat16),
            pltpu.VMEM((sources, count * CAP, rows_dev), jnp.bfloat16),
            pltpu.VMEM((sources, count * CAP, model_width), jnp.bfloat16),
            pltpu.VMEM((sources, count * CAP, model_width), jnp.bfloat16),
            pltpu.VMEM((count,) + piece, jnp.bfloat16),
            pltpu.VMEM((sources, count, rows_dev), jnp.float32),
            pltpu.VMEM((sources, count, rows_dev), jnp.float32),
        ]
        + Lane.scratch(bits, (rows_dev, model_width), jnp.bfloat16) * 2
        + [
            pltpu.SemaphoreType.DMA((2,)),
            pltpu.SemaphoreType.DMA((count,)),
            pltpu.SemaphoreType.DMA((near,)),
            pltpu.SemaphoreType.DMA((2, bits)),
            pltpu.SemaphoreType.DMA((2, bits)),
            pltpu.SemaphoreType.DMA((sources - 1,)),
            pltpu.SemaphoreType.DMA((sources - 1,)),
        ],
        compiler_params=pltpu.CompilerParams(
            collective_id=1, has_side_effects=True, vmem_limit_bytes=67 * 1000 * 1000
        ),
        name="experts",
    )(rows.reshape(shape), cots.reshape(shape), ranks, probs, w_gate_up, w_down)


def on_device(
    tokens,
    segments,
    routes,
    attn_gain,
    w_query,
    w_key,
    w_value,
    w_out,
    mlp_gain,
    w_router,
    w_gate_up,
    w_down,
    cotangent,
    *,
    n_ep,
    n_rep,
):
    inputs = tokens[0]
    own_routes = routes[0]
    grad_output = cotangent[0]
    rows_dev, model_width = inputs.shape
    everyone = ("ep", "rep")
    heads = HEADS // n_rep
    head_width = heads * HEAD_DIM
    shared = max(1, n_rep // KV_HEADS)
    query_width = w_query.shape[1]
    key_width = w_key.shape[1]
    experts_all = w_router.shape[1]
    half_dim = HEAD_DIM // 2

    pack_ids = lax.all_gather(segments[0], "rep", axis=0, tiled=True)
    length = pack_ids.shape[0]
    blocks = length // BLOCK
    offset = lax.axis_index("rep") * rows_dev
    doc_start = jnp.sum((pack_ids[None, :] < pack_ids[:, None]).astype(jnp.int32), 1)
    position = (jnp.arange(length, dtype=jnp.int32) - doc_start).astype(jnp.float32)
    angles = (
        position[:, None]
        * jnp.exp(jnp.arange(half_dim, dtype=jnp.float32) * (-math.log(10000.0) / half_dim))[
            None, :
        ]
    )
    cosine = jnp.cos(angles)
    sine = jnp.sin(angles)
    cosine = jnp.concatenate([cosine, cosine], 1)
    sine = jnp.concatenate([-sine, sine], 1)
    own_cosine = lax.dynamic_slice_in_dim(cosine, offset, rows_dev, 0)
    own_sine = lax.dynamic_slice_in_dim(sine, offset, rows_dev, 0)
    starts = doc_start.reshape(blocks, 1, BLOCK)
    lows = doc_start[::BLOCK] // BLOCK

    rotated_width = query_width + key_width
    input_width = rotated_width + key_width
    full_in = lax.all_gather(
        jnp.concatenate([w_query, w_key, w_value], 1), everyone, axis=0, tiled=True
    )
    full = lax.all_gather(jnp.concatenate([w_out, w_router], 1), everyone, axis=0, tiled=True)
    full_out = full[:, :model_width]
    full_router = full[:, model_width:]

    normed, factor_one = rms_norm(inputs, attn_gain)
    normed_b = normed.astype(jnp.bfloat16)
    mixed_in = product(normed_b, full_in)
    turn = mixed_in[:, :rotated_width]
    times = rotated_width // HEAD_DIM
    turned = turn * jnp.tile(own_cosine, (1, times)) + swap_halves(turn) * jnp.tile(
        own_sine, (1, times)
    )
    turned_b = turned.astype(jnp.bfloat16)
    value_b = mixed_in[:, rotated_width:].astype(jnp.bfloat16)
    query_part = turned_b[:, :query_width].reshape(rows_dev, n_rep, head_width)
    key_part = turned_b[:, query_width:].reshape(rows_dev, KV_HEADS, HEAD_DIM)
    value_part = value_b.reshape(rows_dev, KV_HEADS, HEAD_DIM)
    if shared > 1:
        key_part = jnp.repeat(key_part, shared, 1)
        value_part = jnp.repeat(value_part, shared, 1)
    sending = jnp.concatenate([query_part, key_part, value_part], 2).transpose(1, 0, 2)
    head_rows = lax.all_to_all(sending, "rep", split_axis=0, concat_axis=0, tiled=True)
    head_rows = head_rows.reshape(length, head_width + 2 * HEAD_DIM)
    mixed, mixed_out, totals = attend_forward(head_rows, starts, lows, heads)
    mixed_rows = lax.all_to_all(
        mixed.reshape(n_rep, rows_dev, head_width), "rep", split_axis=0, concat_axis=0, tiled=True
    )
    mixed_rows = mixed_rows.transpose(1, 0, 2).reshape(rows_dev, query_width)
    hidden = inputs + branch_scale * product(mixed_rows, full_out)

    normed_two, factor_two = rms_norm(hidden, mlp_gain)
    normed_two_b = normed_two.astype(jnp.bfloat16)
    router_f = full_router.astype(jnp.float32)
    logits = product(normed_two_b, full_router)
    numbers = jnp.arange(experts_all, dtype=jnp.int32)
    onehot = jnp.sum((own_routes[:, :, None] == numbers).astype(jnp.float32), 1)
    chosen = onehot > 0.5
    peak = jnp.max(jnp.where(chosen, logits, far_below), 1, keepdims=True)
    raised = jnp.where(chosen, jnp.exp(jnp.minimum(logits - peak, 0.0)), 0.0)
    probs = raised / jnp.sum(raised, 1, keepdims=True)
    before = (
        lax.broadcasted_iota(jnp.int32, (rows_dev, rows_dev), 0)
        > lax.broadcasted_iota(jnp.int32, (rows_dev, rows_dev), 1)
    ).astype(jnp.bfloat16)
    rank = product(before, onehot.astype(jnp.bfloat16))
    kept = chosen & (rank < CAP)
    rank_sent = jnp.where(kept, rank, -1.0).T
    probs_sent = probs.T
    both_sent = jnp.concatenate(
        [rank_sent.reshape(n_ep, -1, rows_dev), probs_sent.reshape(n_ep, -1, rows_dev)], 1
    )
    both_all = lax.all_to_all(both_sent, "ep", split_axis=0, concat_axis=0, tiled=True)
    ranks = both_all[:, : experts_all // n_ep]
    prob_all = both_all[:, experts_all // n_ep :]
    expert_rows = lax.all_gather(normed_two_b, "ep", axis=0, tiled=True)
    expert_cots = lax.all_gather(grad_output.astype(jnp.bfloat16), "ep", axis=0, tiled=True)
    rep_bits = [("rep", b) for b in range(bits_of(n_rep))]
    ep_bits = [("ep", b) for b in range(bits_of(n_ep))]
    count = experts_all // n_ep
    near = count * 3 // 4
    kinds = [k % 2 for k in range(near)] + [0] * (count - near)
    leads = [0, len(rep_bits) - 2]
    orders = [
        [leads[kind]] + [b for b in range(len(rep_bits)) if b != leads[kind]] for kind in kinds
    ]
    out_sum, grad_sum, inner_back, grad_keep, came_near, *sent = experts(
        expert_rows,
        expert_cots,
        ranks,
        prob_all,
        w_gate_up,
        w_down,
        n_rep,
        orders,
        near,
        ep_bits[::-1],
        ep_bits,
    )
    rep_orders = [[("rep", b) for b in order] for order in orders]
    early = list(range(0, near, 2))
    late = early[2:]
    early = early[:2]

    def halves(left, right, label, e=None):
        mine, _ = side(*label)
        half = left.shape[-3] // 2

        def total(which):
            parts = []
            for stack in (left, right):
                start = [jnp.int32(0)] * stack.ndim
                start[-3] = (which * half).astype(jnp.int32)
                size = stack.shape[-3:]
                if e is not None:
                    start[0] = jnp.int32(e)
                part = lax.dynamic_slice(
                    stack, start, (1,) * (stack.ndim - 3) + (half,) + size[1:]
                )
                parts.append(part.reshape((half,) + size[1:]).astype(jnp.float32))
            return (parts[0] + parts[1]).astype(jnp.bfloat16)

        return (total(1 - mine), total(mine))

    output = hidden + branch_scale * out_sum
    grad_probs = inner_back.reshape(experts_all, rows_dev).T
    grad_logits = probs * (grad_probs - jnp.sum(grad_probs * probs, -1, keepdims=True))
    normed_two_f = normed_two_b.astype(jnp.float32)
    grad_router = jnp.dot(normed_two_f.T, grad_logits, precision=lax.Precision.HIGHEST)
    grad_normed_two = grad_sum + jnp.dot(
        grad_logits, router_f.T, precision=lax.Precision.HIGHEST
    )
    grad_hidden_norm, grad_mlp_gain = norm_back(grad_normed_two, hidden, factor_two, mlp_gain)
    grad_hidden = grad_output + grad_hidden_norm
    grad_attn = (branch_scale * grad_hidden).astype(jnp.bfloat16)
    grad_out_w = dot_tn(mixed_rows, grad_attn)
    grad_mixed = dot_nt(grad_attn, full_out).astype(jnp.bfloat16)
    grad_heads = lax.all_to_all(
        grad_mixed.reshape(rows_dev, n_rep, head_width).transpose(1, 0, 2),
        "rep",
        split_axis=0,
        concat_axis=0,
        tiled=True,
    ).reshape(length, head_width)
    beside = [swap(after(sent[0], grad_heads), *rep_orders[near][0])]
    second = {}
    for e in early:
        give, own = halves(grad_keep, came_near, rep_orders[e][1], e)
        second[e] = (own, swap(after(give, grad_heads), *rep_orders[e][1]))
        beside.append(second[e][1])
    returning = attend_backward(
        head_rows, grad_heads, mixed_out, totals, starts, lows, cosine, sine, heads
    )
    returning = after(returning, *beside)
    returned = lax.all_to_all(
        returning.reshape(n_rep, rows_dev, head_width + 2 * HEAD_DIM),
        "rep",
        split_axis=0,
        concat_axis=0,
        tiled=True,
    ).transpose(1, 0, 2)
    parts = [grad_keep, came_near]
    steps_of = {e: ((0, e), (1, e), 0) for e in range(near)}

    def put_by(e, own, got, skip):
        steps_of[e] = ((len(parts), 0), (len(parts) + 1, 0), skip)
        parts.extend([own[None], got[None]])

    for k, half in enumerate(sent):
        steps_of[near + k] = ((0, near + k), (len(parts), 0), 0 if k == 0 else -1)
        parts.append((beside[0] if k == 0 else half)[None])
    for e in late:
        give, own = halves(grad_keep, came_near, rep_orders[e][1], e)
        put_by(e, own, swap(after(give, returned), *rep_orders[e][1]), 1)
    for e in early:
        give, own = halves(*second[e], rep_orders[e][2])
        put_by(e, own, swap(after(give, returned), *rep_orders[e][2]), 2)
    units = [
        (e, steps_of[e][:2], rep_orders[e], steps_of[e][2])
        for e in sorted(range(count), key=lambda e: (e < near, e))
    ]
    grad_query_rows = returned[:, :, :head_width].reshape(rows_dev, query_width)
    key_back = returned[:, :, head_width : head_width + HEAD_DIM]
    value_back = returned[:, :, head_width + HEAD_DIM :]
    if shared > 1:
        key_back = jnp.sum(
            key_back.reshape(rows_dev, KV_HEADS, shared, HEAD_DIM).astype(jnp.float32), 2
        ).astype(jnp.bfloat16)
        value_back = jnp.sum(
            value_back.reshape(rows_dev, KV_HEADS, shared, HEAD_DIM).astype(jnp.float32), 2
        ).astype(jnp.bfloat16)
    grad_in_rows = jnp.concatenate(
        [
            grad_query_rows,
            key_back.reshape(rows_dev, key_width),
            value_back.reshape(rows_dev, key_width),
        ],
        1,
    )
    grad_w_in = dot_tn(normed_b, grad_in_rows)
    grad_normed = dot_nt(grad_in_rows, full_in)
    grad_inputs_norm, grad_attn_gain = norm_back(grad_normed, inputs, factor_one, attn_gain)
    grad_inputs = grad_hidden + grad_inputs_norm
    everything = n_ep * n_rep
    gains = jnp.concatenate(
        [grad_attn_gain.reshape(everything, -1), grad_mlp_gain.reshape(everything, -1)], 1
    )
    labels = ep_bits[::-1] + rep_bits[::-1]
    shape = (2,) * len(labels)
    weight_grads = jnp.concatenate([grad_w_in, grad_out_w, grad_router], 1).astype(jnp.bfloat16)
    expert_up, expert_down, weights, gains, _ = reduce_rest(
        parts,
        weight_grads.reshape(shape + (-1, weight_grads.shape[1])),
        gains.reshape(shape + (1, -1)),
        units,
        labels,
        ep_bits + rep_bits,
        model_width // n_rep,
    )
    gains = gains[0]
    part = model_width // everything
    return (
        output[None],
        grad_inputs[None],
        gains[:part],
        weights[:, :query_width],
        weights[:, query_width:rotated_width],
        weights[:, rotated_width:input_width],
        weights[:, input_width : input_width + model_width],
        gains[part:],
        weights[:, input_width + model_width :],
        expert_up,
        expert_down,
    )


def solution(mesh):
    placed = (
        P("ep", "rep", None),
        P("ep", "rep"),
        P("ep", "rep", None),
        P(),
        P(("ep", "rep"), None),
        P(("ep", "rep"), None),
        P(("ep", "rep"), None),
        P(("ep", "rep"), None),
        P(),
        P(("ep", "rep"), None),
        P("ep", None, None),
        P("ep", None, None),
        P("ep", "rep", None),
    )
    return jax.shard_map(
        functools.partial(on_device, n_ep=mesh.shape["ep"], n_rep=mesh.shape["rep"]),
        mesh=mesh,
        in_specs=placed,
        out_specs=(
            P("ep", "rep", None),
            P("ep", "rep", None),
            P(("ep", "rep")),
            P(("ep", "rep"), None),
            P(("ep", "rep"), None),
            P(("ep", "rep"), None),
            P(("ep", "rep"), None),
            P(("ep", "rep")),
            P(("ep", "rep"), None),
            P("ep", "rep", None),
            P("ep", None, "rep"),
        ),
        check_vma=False,
    )
```

```python
import functools
import math

import jax
import jax.numpy as jnp
from jax import lax
from jax.experimental import pallas as pl
from jax.experimental.pallas import tpu as pltpu
from jax.sharding import PartitionSpec as P

HEADS = 16
KV_HEADS = 8
HEAD_DIM = 64
CAP = 80
BLOCK = 256

epsilon = 1e-06
score_scale = 0.015625
branch_scale = 0.22
far_below = -1e30

NT = (((1,), (1,)), ((), ()))
TN = (((0,), (0,)), ((), ()))


def product(left, right):
    return jnp.dot(left, right, preferred_element_type=jnp.float32)


def dot_nt(left, right):
    return lax.dot_general(left, right, NT, preferred_element_type=jnp.float32)


def dot_tn(left, right):
    return lax.dot_general(left, right, TN, preferred_element_type=jnp.float32)


def rms_norm(values, gain):
    factor = lax.rsqrt(jnp.mean(values * values, -1, keepdims=True) + epsilon)
    return (values * factor * gain, factor)


def norm_back(grad_normed, values, factor, gain):
    scaled = grad_normed * gain
    gain_part = jnp.sum(grad_normed * values * factor, 0)
    inner_sum = jnp.mean(scaled * values, -1, keepdims=True)
    return (factor * scaled - values * (factor * factor * factor) * inner_sum, gain_part)


def swap_halves(values):
    count, width = values.shape
    half_dim = HEAD_DIM // 2
    lane = lax.broadcasted_iota(jnp.int32, values.shape, 1)
    return jnp.where(
        lane % HEAD_DIM < half_dim,
        jnp.roll(values, -half_dim, 1),
        jnp.roll(values, half_dim, 1),
    )


def attend_forward_kernel(
    low_ref, rows_ref, start_ref, mixed_ref, out_ref, total_ref, key_s, value_s, *, heads
):
    step = pl.program_id(0)
    width = heads * HEAD_DIM

    @pl.when(step == 0)
    def _():
        key_s[...] = rows_ref[:, width : width + HEAD_DIM]
        value_s[...] = rows_ref[:, width + HEAD_DIM : width + 2 * HEAD_DIM]

    block_rows = rows_ref[pl.ds(pl.multiple_of(step * BLOCK, BLOCK), BLOCK), :]
    queries = [
        block_rows[:, h * HEAD_DIM : (h + 1) * HEAD_DIM] * jnp.bfloat16(score_scale)
        for h in range(heads)
    ]
    starts = start_ref[0]
    at = step * BLOCK + lax.broadcasted_iota(jnp.int32, (1, BLOCK), 1)

    def one(j, carry):
        rows = pl.ds(pl.multiple_of(j * BLOCK, BLOCK), BLOCK)
        key_block = key_s[rows, :]
        value_block = value_s[rows, :]
        place = j * BLOCK + lax.broadcasted_iota(jnp.int32, (BLOCK, BLOCK), 0)
        allowed = (place >= starts) & (place <= at)
        result = []
        for h in range(heads):
            peak, total, mixed = carry[h]
            scores = jnp.where(allowed, dot_nt(key_block, queries[h]), far_below)
            new_peak = jnp.maximum(peak, jnp.max(scores, 0, keepdims=True))
            fade = jnp.exp(peak - new_peak)
            raised = jnp.exp(scores - new_peak)
            total = fade * total + jnp.sum(raised, 0, keepdims=True)
            mixed = fade * mixed + dot_tn(value_block, raised.astype(jnp.bfloat16))
            result.append((new_peak, total, mixed))
        return tuple(result)

    first = tuple(
        (
            jnp.full((1, BLOCK), far_below, jnp.float32),
            jnp.zeros((1, BLOCK), jnp.float32),
            jnp.zeros((HEAD_DIM, BLOCK), jnp.float32),
        )
        for _ in range(heads)
    )
    done = lax.fori_loop(low_ref[step], step + 1, one, first)
    for h in range(heads):
        peak, total, mixed = done[h]
        mixed = mixed / total
        out_ref[h * HEAD_DIM : (h + 1) * HEAD_DIM, :] = mixed
        total_ref[0, h : h + 1, :] = peak + jnp.log(total)
        mixed_ref[:, h * HEAD_DIM : (h + 1) * HEAD_DIM] = mixed.T.astype(jnp.bfloat16)


def attend_forward(rows, starts, lows, heads):
    length, width = rows.shape
    blocks = length // BLOCK
    whole = lambda i, low: (0, 0)
    return pl.pallas_call(
        functools.partial(attend_forward_kernel, heads=heads),
        out_shape=(
            jax.ShapeDtypeStruct((length, heads * HEAD_DIM), jnp.bfloat16),
            jax.ShapeDtypeStruct((heads * HEAD_DIM, length), jnp.float32),
            jax.ShapeDtypeStruct((blocks, heads, BLOCK), jnp.float32),
        ),
        grid_spec=pltpu.PrefetchScalarGridSpec(
            num_scalar_prefetch=1,
            grid=(blocks,),
            in_specs=[
                pl.BlockSpec((length, width), whole),
                pl.BlockSpec((1, 1, BLOCK), lambda i, low: (i, 0, 0)),
            ],
            out_specs=[
                pl.BlockSpec((BLOCK, heads * HEAD_DIM), lambda i, low: (i, 0)),
                pl.BlockSpec((heads * HEAD_DIM, BLOCK), lambda i, low: (0, i)),
                pl.BlockSpec((1, heads, BLOCK), lambda i, low: (i, 0, 0)),
            ],
            scratch_shapes=[
                pltpu.VMEM((length, HEAD_DIM), jnp.bfloat16),
                pltpu.VMEM((length, HEAD_DIM), jnp.bfloat16),
            ],
        ),
        name="attend_forward",
    )(lows, rows, starts)


def attend_backward_kernel(
    low_ref,
    rows_ref,
    grad_ref,
    out_ref,
    total_ref,
    start_ref,
    cosine_ref,
    sine_ref,
    back_ref,
    key_s,
    value_s,
    grad_query_s,
    grad_key_s,
    grad_value_s,
    *,
    heads,
    blocks,
):
    step = pl.program_id(0)
    width = heads * HEAD_DIM

    @pl.when(step == 0)
    def _():
        key_s[...] = rows_ref[:, width : width + HEAD_DIM]
        value_s[...] = rows_ref[:, width + HEAD_DIM : width + 2 * HEAD_DIM]
        grad_key_s[...] = jnp.zeros_like(grad_key_s)
        grad_value_s[...] = jnp.zeros_like(grad_value_s)

    own = pl.ds(pl.multiple_of(step * BLOCK, BLOCK), BLOCK)
    block_rows = rows_ref[own, :]
    grads_all = grad_ref[...]
    starts = start_ref[0]
    at = step * BLOCK + lax.broadcasted_iota(jnp.int32, (1, BLOCK), 1)
    queries, scaled, grads, inners, totals = [], [], [], [], []
    for h in range(heads):
        span = slice(h * HEAD_DIM, (h + 1) * HEAD_DIM)
        queries.append(block_rows[:, span])
        scaled.append(block_rows[:, span] * jnp.bfloat16(score_scale))
        grads.append(grads_all[:, span])
        turned = grads_all[:, span].astype(jnp.float32).T
        inners.append(jnp.sum(turned * out_ref[span, :], 0, keepdims=True))
        totals.append(total_ref[0, h : h + 1, :])

    def one(j, carry):
        rows = pl.ds(pl.multiple_of(j * BLOCK, BLOCK), BLOCK)
        key_block = key_s[rows, :]
        value_block = value_s[rows, :]
        place = j * BLOCK + lax.broadcasted_iota(jnp.int32, (BLOCK, BLOCK), 0)
        allowed = (place >= starts) & (place <= at)
        result = []
        key_sum = grad_key_s[rows, :]
        value_sum = grad_value_s[rows, :]
        for h in range(heads):
            scores = jnp.where(allowed, dot_nt(key_block, scaled[h]), far_below)
            prob = jnp.exp(scores - totals[h])
            grad_prob = dot_nt(value_block, grads[h])
            grad_scores = (prob * (grad_prob - inners[h]) * score_scale).astype(jnp.bfloat16)
            value_sum = value_sum + product(prob.astype(jnp.bfloat16), grads[h])
            key_sum = key_sum + product(grad_scores, queries[h])
            result.append(carry[h] + dot_tn(grad_scores, key_block))
        grad_key_s[rows, :] = key_sum
        grad_value_s[rows, :] = value_sum
        return tuple(result)

    first = tuple(jnp.zeros((BLOCK, HEAD_DIM), jnp.float32) for _ in range(heads))
    done = lax.fori_loop(low_ref[step], step + 1, one, first)
    for h in range(heads):
        grad_query_s[own, h * HEAD_DIM : (h + 1) * HEAD_DIM] = done[h]

    @pl.when(step == blocks - 1)
    def _():
        def turn(j, carry):
            rows = pl.ds(pl.multiple_of(j * BLOCK, BLOCK), BLOCK)
            cosine = cosine_ref[rows, :]
            sine = sine_ref[rows, :]
            parts = [
                grad_query_s[rows, h * HEAD_DIM : (h + 1) * HEAD_DIM] for h in range(heads)
            ]
            parts.append(grad_key_s[rows, :])
            half = HEAD_DIM // 2
            turned = [
                part * cosine - jnp.concatenate([part[:, half:], part[:, :half]], 1) * sine
                for part in parts
            ]
            turned.append(grad_value_s[rows, :])
            back_ref[rows, :] = jnp.concatenate(turned, 1).astype(jnp.bfloat16)
            return carry

        lax.fori_loop(0, blocks, turn, 0)


def attend_backward(rows, grads, outs, totals, starts, lows, cosine, sine, heads):
    length, width = rows.shape
    blocks = length // BLOCK
    whole = lambda i, low: (0, 0)
    once = pl.Buffered(1)
    return pl.pallas_call(
        functools.partial(attend_backward_kernel, heads=heads, blocks=blocks),
        out_shape=jax.ShapeDtypeStruct((length, width), jnp.bfloat16),
        grid_spec=pltpu.PrefetchScalarGridSpec(
            num_scalar_prefetch=1,
            grid=(blocks,),
            in_specs=[
                pl.BlockSpec((length, width), whole),
                pl.BlockSpec((BLOCK, heads * HEAD_DIM), lambda i, low: (i, 0)),
                pl.BlockSpec((heads * HEAD_DIM, BLOCK), lambda i, low: (0, i)),
                pl.BlockSpec((1, heads, BLOCK), lambda i, low: (i, 0, 0)),
                pl.BlockSpec((1, 1, BLOCK), lambda i, low: (i, 0, 0)),
                pl.BlockSpec((length, HEAD_DIM), whole, pipeline_mode=once),
                pl.BlockSpec((length, HEAD_DIM), whole, pipeline_mode=once),
            ],
            out_specs=pl.BlockSpec((length, width), whole),
            scratch_shapes=[
                pltpu.VMEM((length, HEAD_DIM), jnp.bfloat16),
                pltpu.VMEM((length, HEAD_DIM), jnp.bfloat16),
                pltpu.VMEM((length, heads * HEAD_DIM), jnp.float32),
                pltpu.VMEM((length, HEAD_DIM), jnp.float32),
                pltpu.VMEM((length, HEAD_DIM), jnp.float32),
            ],
        ),
        name="attend_backward",
    )(lows, rows, grads, outs, totals, starts, cosine, sine)


def after(value, *others):
    return lax.optimization_barrier((value, *others))[0]


def bits_of(size):
    return max(size.bit_length() - 1, 0)


def swap(sent, axis, bit):
    size = lax.axis_size(axis)
    return lax.ppermute(sent, axis, [(i, i ^ (1 << bit)) for i in range(size)])


def side(axis, bit):
    index = lax.axis_index(axis)
    mine = (index // (1 << bit)) % 2
    return (mine, index + (1 - 2 * mine) * (1 << bit))


def pick(dim, index):
    return (slice(None),) * dim + (index,)


def digits(number, count):
    return tuple((number // (1 << (count - 1 - k))) % 2 for k in range(count))


def mesh_copy(source, target, sends, gets, axis, partner):
    return pltpu.make_async_remote_copy(
        src_ref=source,
        dst_ref=target,
        send_sem=sends,
        recv_sem=gets,
        device_id={axis: partner},
        device_id_type=pl.DeviceIdType.MESH,
    )


def greet(partners):
    barrier = pltpu.get_barrier_semaphore()
    for axis, partner in partners:
        pl.semaphore_signal(
            barrier, inc=1, device_id={axis: partner}, device_id_type=pl.DeviceIdType.MESH
        )
    pl.semaphore_wait(barrier, len(partners))


class Lane:
    def __init__(self, labels, order, first, refs, sends, gets, rows=None):
        bits = len(labels)
        self.order, self.first, self.sends, self.gets = (order, first, sends, gets)
        self.sums, self.got = (refs[: bits - 1], refs[bits - 1 : 2 * bits - 1])
        self.labels = [list(labels)]
        for label in order:
            self.labels.append([other for other in self.labels[-1] if other != label])
        self.rows = rows

    @staticmethod
    def scratch(bits, tail, dtype):
        shapes = [pltpu.VMEM((2,) * (bits - 1 - k) + tail, dtype) for k in range(bits)]
        return shapes[:-1] + shapes

    def source(self, k):
        return self.first if k == 0 else self.sums[k - 1]

    def copy(self, k):
        axis, bit = self.order[k]
        mine, partner = side(axis, bit)
        dim = self.labels[k].index((axis, bit))
        return mesh_copy(
            self.source(k).at[pick(dim, 1 - mine)],
            self.got[k],
            self.sends.at[k],
            self.gets.at[k],
            axis,
            partner,
        )

    def start(self, k):
        self.copy(k).start()

    def add(self, k, out=None):
        axis, bit = self.order[k]
        mine, _ = side(axis, bit)
        dim = self.labels[k].index((axis, bit))
        left = len(self.order) - 1 - k
        self.copy(k).wait_recv()
        source, got = (self.source(k), self.got[k])
        target = out if left == 0 else self.sums[k]
        height = got.shape[left]
        rows = self.rows or height
        blocks = height // rows

        def body(i, carry):
            at = digits(i // blocks, left)
            own = pl.ds(pl.multiple_of((i % blocks) * rows, rows), rows)
            if blocks == 1:
                own = slice(None)
            here = at[:dim] + (mine,) + at[dim:]
            total = source[here + (own,)].astype(jnp.float32) + got[at + (own,)].astype(
                jnp.float32
            )
            target[at + (own,)] = total.astype(target.dtype)
            return carry

        lax.fori_loop(0, blocks << left, body, 0)

    def finish(self):
        for k in range(len(self.order)):
            self.copy(k).wait_send()


def reduce_kernel(*refs, units, n_parts, n_lanes, labels, weight_order, share):
    part_refs, refs = (refs[:n_parts], refs[n_parts:])
    lane_ins, (up_ref, down_ref, *refs) = (refs[:n_lanes], refs[n_lanes:])
    lane_outs, (late_ref, *refs) = (refs[:n_lanes], refs[n_lanes:])
    steps = len(units[0][2]) - 1
    sends, keeps, gets = ([], [], [])
    for _ in range(steps):
        sends.append(refs[0])
        keeps.append(refs[1])
        gets.append(refs[2])
        refs = refs[3:]
    bits = len(labels)
    each = 2 * bits - 1
    lane_refs, refs = (refs[: n_lanes * each], refs[n_lanes * each :])
    load_keep, load_came, load_sem, unit_send, unit_get, lane_send, lane_get, late_sem = refs
    lanes = [
        Lane(
            labels,
            weight_order,
            first,
            lane_refs[number * each : (number + 1) * each],
            lane_send.at[number],
            lane_get.at[number],
        )
        for number, first in enumerate(lane_ins)
    ]
    _, spots, tall, width = load_keep.shape
    rows = 32 if tall % 32 == 0 else tall
    blocks = tall // rows

    greet([(axis, side(axis, bit)[1]) for axis, bit in weight_order])

    def lane_start(k):
        for lane in lanes:
            lane.start(k)

    def lane_add(k):
        for lane, out in zip(lanes, lane_outs):
            lane.add(k, out)

    lane_start(0)

    late = [n for n, unit in enumerate(units) if unit[3] < 0]
    half_way = [n for n, unit in enumerate(units) if 0 < unit[3] < steps]
    fresh = [n for n, unit in enumerate(units) if unit[3] == 0]
    done = [n for n, unit in enumerate(units) if unit[3] == steps]
    sequence = half_way + fresh + late + done

    def late_copy(n):
        _, ((_, _), (which, place)), order, _ = units[n]
        axis, bit = order[0]
        return mesh_copy(
            part_refs[which].at[place],
            late_ref.at[late.index(n)],
            late_sem.at[0, late.index(n)],
            late_sem.at[1, late.index(n)],
            axis,
            side(axis, bit)[1],
        )

    def loads(turn):
        n = sequence[turn]
        _, parts, _, skip = units[n]
        slot = turn % 2
        size = spots >> max(skip, 0)
        sources = [part_refs[which].at[place] for which, place in parts]
        if skip < 0:
            sources[1] = late_ref.at[late.index(n)]
        return [
            pltpu.make_async_copy(
                source, buffer.at[slot, pl.ds(0, size)], load_sem.at[slot, number]
            )
            for number, (source, buffer) in enumerate(zip(sources, (load_keep, load_came)))
        ]

    def load(turn):
        if turn < len(units) and units[sequence[turn]][3] >= 0:
            for copy in loads(turn):
                copy.start()

    def unit_copy(unit, order, k):
        axis, bit = order[k + 1]
        return mesh_copy(
            sends[k].at[unit],
            gets[k].at[unit],
            unit_send.at[unit, k],
            unit_get.at[unit, k],
            axis,
            side(axis, bit)[1],
        )

    def unit_add(unit, order, k, left, right):
        mine, _ = side(*order[k + 1])
        half = spots >> (k + 1)

        def fill(target, which):
            def body(i, carry):
                piece = i // blocks
                own = pl.ds(pl.multiple_of((i % blocks) * rows, rows), rows)
                total = left[which * half + piece, own, :].astype(jnp.float32) + right[
                    which * half + piece, own, :
                ].astype(jnp.float32)
                target[unit, piece, own, :] = total.astype(jnp.bfloat16)
                return carry

            lax.fori_loop(0, half * blocks, body, 0)

        fill(sends[k], 1 - mine)
        unit_copy(unit, order, k).start()
        fill(keeps[k], mine)

    def begin_unit(n):
        unit, _, order, skip = units[n]
        turn = sequence.index(n)
        if skip < 0:
            late_copy(n).wait_recv()
            for copy in loads(turn):
                copy.start()
        for copy in loads(turn):
            copy.wait()
        left, right = (load_keep.at[turn % 2], load_came.at[turn % 2])
        if skip < steps:
            unit_add(unit, order, max(skip, 0), left, right)
        else:
            give(unit, left[0].astype(jnp.float32) + right[0].astype(jnp.float32))
        load(turn + 2)

    def next_unit(n, k):
        unit, _, order, _ = units[n]
        unit_copy(unit, order, k - 1).wait_recv()
        unit_add(unit, order, k, keeps[k - 1].at[unit], gets[k - 1].at[unit])

    def end_unit(n):
        unit, _, order, _ = units[n]
        unit_copy(unit, order, steps - 1).wait_recv()
        give(unit, keeps[-1][unit, 0].astype(jnp.float32) + gets[-1][unit, 0].astype(jnp.float32))

    def give(unit, total):
        up_ref[unit] = total[:share]
        pieces = width // share
        rest = tall - share
        for p in range(pieces):
            down_ref[unit, p * rest : (p + 1) * rest, :] = total[
                share:, p * share : (p + 1) * share
            ]

    load(0)
    load(1)
    def late_start():
        for n in late:
            late_copy(n).start()

    def lane_turn(k):
        lane_add(k)
        if k + 1 < bits:
            lane_start(k + 1)

    work = [(begin_unit, n) for n in half_way + fresh[:1]] + [(lane_turn, 0)]
    work += [(begin_unit, n) for n in fresh[1:2]] + [(late_start,)]
    work += [(begin_unit, n) for n in fresh[2:]]
    for k in range(1, steps):
        onward = [n for n in half_way if units[n][3] < k] + fresh
        work += [(next_unit, n, k) for n in onward[:3]]
        if k == 1:
            work += [(lane_turn, 1)] + [(begin_unit, n) for n in late]
        work += [(next_unit, n, k) for n in onward[3:4]]
        work += [(next_unit, n, k) for n in late]
        work += [(next_unit, n, k) for n in onward[4:]]
    work += [(begin_unit, n) for n in done]
    work += [(end_unit, n) for n in half_way + fresh[:3] + late] + [(lane_turn, 2)]
    work += [(end_unit, n) for n in fresh[3:4]] + [(lane_turn, 3)]
    work += [(end_unit, n) for n in fresh[4:]]
    work += [(lane_turn, k) for k in range(4, bits)]
    for job, *arguments in work:
        job(*arguments)
    for unit, _, order, skip in units:
        for k in range(max(skip, 0), steps):
            unit_copy(unit, order, k).wait_send()
    for n in late:
        late_copy(n).wait_send()
    for lane in lanes:
        lane.finish()


def reduce_rest(parts, lanes, units, labels, weight_order, share):
    _, spots, tall, width = parts[0].shape
    count = len(units)
    bits = len(labels)
    steps = len(units[0][2]) - 1
    late = max(1, len([unit for unit in units if unit[3] < 0]))
    anywhere = pl.BlockSpec(memory_space=pl.ANY)
    vmem = pl.BlockSpec(memory_space=pltpu.VMEM)
    scratch = []
    for k in range(steps):
        scratch += [pltpu.VMEM((count, spots >> (k + 1), tall, width), jnp.bfloat16)] * 3
    for lane in lanes:
        scratch += Lane.scratch(bits, lane.shape[bits:], lane.dtype)
    scratch += [
        pltpu.VMEM((2, spots, tall, width), jnp.bfloat16),
        pltpu.VMEM((2, spots, tall, width), jnp.bfloat16),
        pltpu.SemaphoreType.DMA((2, 2)),
        pltpu.SemaphoreType.DMA((count, steps)),
        pltpu.SemaphoreType.DMA((count, steps)),
        pltpu.SemaphoreType.DMA((len(lanes), bits)),
        pltpu.SemaphoreType.DMA((len(lanes), bits)),
        pltpu.SemaphoreType.DMA((2, late)),
    ]
    return pl.pallas_call(
        functools.partial(
            reduce_kernel,
            units=units,
            n_parts=len(parts),
            n_lanes=len(lanes),
            labels=labels,
            weight_order=weight_order,
            share=share,
        ),
        out_shape=(
            jax.ShapeDtypeStruct((count, share, width), jnp.float32),
            jax.ShapeDtypeStruct((count, (tall - share) * (width // share), share), jnp.float32),
        )
        + tuple(jax.ShapeDtypeStruct(lane.shape[bits:], jnp.float32) for lane in lanes)
        + (jax.ShapeDtypeStruct((late, spots, tall, width), jnp.bfloat16),),
        in_specs=[anywhere] * len(parts) + [vmem] * len(lanes),
        out_specs=[vmem] * (2 + len(lanes)) + [anywhere],
        scratch_shapes=scratch,
        compiler_params=pltpu.CompilerParams(
            collective_id=0, has_side_effects=True, vmem_limit_bytes=67 * 1000 * 1000
        ),
        name="reduce_rest",
    )(*parts, *lanes)


def experts_kernel(
    *refs, sources, rows_dev, count, copies, orders, near, labels, ep_order
):
    rows_hbm, cot_hbm, rank_ref, prob_ref, gate_up_ref, down_ref, *refs = refs
    out_ref, grad_ref, inner_ref, keep_ref, came_ref, *refs = refs
    far = count - near
    sent_refs, refs = (refs[:far], refs[far:])
    rows_s, cot_s, picks_s, out_s, grad_s, send_s, inner_s, inner_got, *refs = refs
    bits = len(labels)
    lane_refs, refs = (refs[: 2 * (2 * bits - 1)], refs[2 * (2 * bits - 1) :])
    load_sem, unit_send, unit_get, lane_send, lane_get, inner_send, inner_take = refs
    me = lax.axis_index("ep")
    step = pl.program_id(0)
    grad_lane, out_lane = [
        Lane(
            labels,
            ep_order,
            first,
            lane_refs[number * (2 * bits - 1) : (number + 1) * (2 * bits - 1)],
            lane_send.at[number],
            lane_get.at[number],
            rows=32,
        )
        for number, first in enumerate((cot_s, rows_s))
    ]

    def unit_copy(e):
        bit = orders[e][0]
        if e < near:
            return mesh_copy(
                send_s.at[e],
                came_ref.at[e],
                unit_send.at[e],
                unit_get.at[e],
                "rep",
                side("rep", bit)[1],
            )
        return pltpu.make_async_copy(send_s.at[e], sent_refs[e - near], unit_send.at[e])

    def inner_copy(d):
        peer = (me + d) % sources
        return mesh_copy(
            inner_s.at[peer],
            inner_got.at[me],
            inner_send.at[d - 1],
            inner_take.at[d - 1],
            "ep",
            peer,
        )

    @pl.when(step == 0)
    def _():
        loads = [
            pltpu.make_async_copy(rows_hbm, rows_s, load_sem.at[0]),
            pltpu.make_async_copy(cot_hbm, cot_s, load_sem.at[1]),
        ]
        for copy in loads:
            copy.start()
        partners = [("ep", (me + d) % sources) for d in range(1, sources)]
        for bit in sorted({order[0] for order in orders[:near]}):
            partners.append(("rep", side("rep", bit)[1]))
        greet(partners)
        for copy in loads:
            copy.wait()

    slots = pl.ds(pl.multiple_of(step * CAP, 16), CAP)
    numbers = lax.broadcasted_iota(jnp.int32, (CAP, rows_dev), 0).astype(jnp.float32)
    rows_in, cots, weights, picks = [], [], [], []
    for s in range(sources):
        rank = rank_ref[s, pl.ds(step, 1), :]
        pick_table = jnp.where(rank == numbers, 1.0, 0.0)
        weights.append(jnp.sum(pick_table * prob_ref[s, pl.ds(step, 1), :], 1, keepdims=True))
        pick_b = pick_table.astype(jnp.bfloat16)
        picks.append(pick_table)
        picks_s[s, slots, :] = pick_b
        rows_in.append(product(pick_b, rows_s[digits(s, bits)]).astype(jnp.bfloat16))
        cots.append(product(pick_b, cot_s[digits(s, bits)]))
    arrived = jnp.concatenate(rows_in, 0)
    weight = jnp.concatenate(weights, 0)
    grad_mix = branch_scale * jnp.concatenate(cots, 0)
    gate_up = gate_up_ref[0]
    down = down_ref[0]
    hidden_units = down.shape[0]
    both = product(arrived, gate_up)
    gate_part = both[:, :hidden_units]
    up_part = both[:, hidden_units:]
    sigmoid_gate = jax.nn.sigmoid(gate_part)
    active = (gate_part * sigmoid_gate * up_part).astype(jnp.bfloat16)
    produced = product(active, down).astype(jnp.bfloat16).astype(jnp.float32)
    inner = jnp.sum(grad_mix * produced, 1, keepdims=True)
    sent_out = (weight * produced).astype(jnp.bfloat16)
    grad_out = (weight * grad_mix).astype(jnp.bfloat16)
    grad_active = dot_nt(grad_out, down)
    grad_down = dot_tn(active, grad_out).astype(jnp.bfloat16)
    grad_gate = grad_active * up_part * sigmoid_gate * (1.0 + gate_part * (1.0 - sigmoid_gate))
    grad_up = grad_active * gate_part * sigmoid_gate
    grad_both = jnp.concatenate([grad_gate, grad_up], 1).astype(jnp.bfloat16)
    grad_gate_up = dot_tn(arrived, grad_both).astype(jnp.bfloat16)
    share = grad_down.shape[1] // copies
    tall = hidden_units // copies

    def put(order, mine):
        bit, *later = order
        for r in range(copies):
            spot = 0
            for b in later:
                spot = 2 * spot + ((r >> b) & 1)
            ref = keep_ref.at[0] if (r >> bit) & 1 == mine else send_s.at[step]
            ref[spot, :share, :] = grad_gate_up[r * share : (r + 1) * share]
            for k in range(copies):
                ref[spot, share : share + tall, k * share : (k + 1) * share] = grad_down[
                    k * tall : (k + 1) * tall, r * share : (r + 1) * share
                ]

    for order in {tuple(order): order for order in orders}.values():
        members = [e for e in range(count) if orders[e] == order]
        here = functools.reduce(jnp.logical_or, [step == e for e in members])
        side_mine, _ = side("rep", order[0])
        for mine in range(2):

            @pl.when(here & (side_mine == mine))
            def _(order=order, mine=mine):
                put(order, mine)

    grad_in = dot_nt(grad_both, gate_up).astype(jnp.bfloat16)
    for s in range(sources):
        part = slice(s * CAP, (s + 1) * CAP)
        out_s[s, slots, :] = sent_out[part]
        grad_s[s, slots, :] = grad_in[part]
        inner_s[s, pl.ds(step, 1), :] = jnp.sum(picks[s] * inner[part], 0, keepdims=True)
    for e in range(count):

        @pl.when(step == e)
        def _(e=e):
            unit_copy(e).start()

    @pl.when(step == count - 1)
    def _():
        for table_of, target, lane in ((grad_s, cot_s, grad_lane), (out_s, rows_s, out_lane)):
            for s in range(sources):
                target[digits(s, bits)] = dot_tn(picks_s[s], table_of[s]).astype(jnp.bfloat16)
            lane.start(0)
        for d in range(1, sources):
            inner_copy(d).start()
        for k in range(bits):
            for lane, total in ((grad_lane, grad_ref), (out_lane, out_ref)):
                lane.add(k, total)
                if k + 1 < bits:
                    lane.start(k + 1)
        inner_got[me] = inner_s[me]
        for d in range(1, sources):
            inner_copy(d).wait_recv()
        inner_ref[...] = inner_got[...]
        for d in range(1, sources):
            inner_copy(d).wait_send()
        grad_lane.finish()
        out_lane.finish()
        for e in range(count):
            unit_copy(e).wait()


def experts(rows, cots, ranks, probs, w_gate_up, w_down, copies, orders, near, labels, ep_order):
    sources, count, rows_dev = ranks.shape
    total, model_width = rows.shape
    hidden_units = w_down.shape[1]
    bits = len(labels)
    tall = model_width // copies + hidden_units // copies
    flat = lambda i: (0, 0)
    cube = lambda i: (0, 0, 0)
    once = pl.Buffered(1)
    anywhere = pl.BlockSpec(memory_space=pl.ANY)
    far = count - near
    shape = (2,) * bits + (rows_dev, model_width)
    piece = (copies // 2, tall, model_width)
    return pl.pallas_call(
        functools.partial(
            experts_kernel,
            sources=sources,
            rows_dev=rows_dev,
            count=count,
            copies=copies,
            orders=orders,
            near=near,
            labels=labels,
            ep_order=ep_order,
        ),
        out_shape=(
            jax.ShapeDtypeStruct((rows_dev, model_width), jnp.float32),
            jax.ShapeDtypeStruct((rows_dev, model_width), jnp.float32),
            jax.ShapeDtypeStruct((sources, count, rows_dev), jnp.float32),
            jax.ShapeDtypeStruct((count,) + piece, jnp.bfloat16),
            jax.ShapeDtypeStruct((near,) + piece, jnp.bfloat16),
        )
        + (jax.ShapeDtypeStruct(piece, jnp.bfloat16),) * far,
        grid=(count,),
        in_specs=[
            anywhere,
            anywhere,
            pl.BlockSpec((sources, count, rows_dev), cube, pipeline_mode=once),
            pl.BlockSpec((sources, count, rows_dev), cube, pipeline_mode=once),
            pl.BlockSpec((1, model_width, 2 * hidden_units), lambda i: (i, 0, 0)),
            pl.BlockSpec((1, hidden_units, model_width), lambda i: (i, 0, 0)),
        ],
        out_specs=[
            pl.BlockSpec((rows_dev, model_width), flat, pipeline_mode=once),
            pl.BlockSpec((rows_dev, model_width), flat, pipeline_mode=once),
            pl.BlockSpec((sources, count, rows_dev), cube, pipeline_mode=once),
            pl.BlockSpec((1,) + piece, lambda i: (i, 0, 0, 0)),
            anywhere,
        ]
        + [anywhere] * far,
        scratch_shapes=[
            pltpu.VMEM(shape, jnp.bfloat16),
            pltpu.VMEM(shape, jnp.bfloat16),
            pltpu.VMEM((sources, count * CAP, rows_dev), jnp.bfloat16),
            pltpu.VMEM((sources, count * CAP, model_width), jnp.bfloat16),
            pltpu.VMEM((sources, count * CAP, model_width), jnp.bfloat16),
            pltpu.VMEM((count,) + piece, jnp.bfloat16),
            pltpu.VMEM((sources, count, rows_dev), jnp.float32),
            pltpu.VMEM((sources, count, rows_dev), jnp.float32),
        ]
        + Lane.scratch(bits, (rows_dev, model_width), jnp.bfloat16) * 2
        + [
            pltpu.SemaphoreType.DMA((2,)),
            pltpu.SemaphoreType.DMA((count,)),
            pltpu.SemaphoreType.DMA((near,)),
            pltpu.SemaphoreType.DMA((2, bits)),
            pltpu.SemaphoreType.DMA((2, bits)),
            pltpu.SemaphoreType.DMA((sources - 1,)),
            pltpu.SemaphoreType.DMA((sources - 1,)),
        ],
        compiler_params=pltpu.CompilerParams(
            collective_id=1, has_side_effects=True, vmem_limit_bytes=67 * 1000 * 1000
        ),
        name="experts",
    )(rows.reshape(shape), cots.reshape(shape), ranks, probs, w_gate_up, w_down)


def on_device(
    tokens,
    segments,
    routes,
    attn_gain,
    w_query,
    w_key,
    w_value,
    w_out,
    mlp_gain,
    w_router,
    w_gate_up,
    w_down,
    cotangent,
    *,
    n_ep,
    n_rep,
):
    inputs = tokens[0]
    own_routes = routes[0]
    grad_output = cotangent[0]
    rows_dev, model_width = inputs.shape
    everyone = ("ep", "rep")
    heads = HEADS // n_rep
    head_width = heads * HEAD_DIM
    shared = max(1, n_rep // KV_HEADS)
    query_width = w_query.shape[1]
    key_width = w_key.shape[1]
    experts_all = w_router.shape[1]
    half_dim = HEAD_DIM // 2

    pack_ids = lax.all_gather(segments[0], "rep", axis=0, tiled=True)
    length = pack_ids.shape[0]
    blocks = length // BLOCK
    offset = lax.axis_index("rep") * rows_dev
    doc_start = jnp.sum((pack_ids[None, :] < pack_ids[:, None]).astype(jnp.int32), 1)
    position = (jnp.arange(length, dtype=jnp.int32) - doc_start).astype(jnp.float32)
    angles = (
        position[:, None]
        * jnp.exp(jnp.arange(half_dim, dtype=jnp.float32) * (-math.log(10000.0) / half_dim))[
            None, :
        ]
    )
    cosine = jnp.cos(angles)
    sine = jnp.sin(angles)
    cosine = jnp.concatenate([cosine, cosine], 1)
    sine = jnp.concatenate([-sine, sine], 1)
    own_cosine = lax.dynamic_slice_in_dim(cosine, offset, rows_dev, 0)
    own_sine = lax.dynamic_slice_in_dim(sine, offset, rows_dev, 0)
    starts = doc_start.reshape(blocks, 1, BLOCK)
    lows = doc_start[::BLOCK] // BLOCK

    rotated_width = query_width + key_width
    input_width = rotated_width + key_width
    joined = jnp.concatenate([w_query, w_key, w_value, w_out, w_router], 1)
    full = lax.all_gather(joined, everyone, axis=0, tiled=True)
    full_in = full[:, :input_width]
    full_out = full[:, input_width : input_width + model_width]
    full_router = full[:, input_width + model_width :]

    normed, factor_one = rms_norm(inputs, attn_gain)
    normed_b = normed.astype(jnp.bfloat16)
    mixed_in = product(normed_b, full_in)
    turn = mixed_in[:, :rotated_width]
    times = rotated_width // HEAD_DIM
    turned = turn * jnp.tile(own_cosine, (1, times)) + swap_halves(turn) * jnp.tile(
        own_sine, (1, times)
    )
    turned_b = turned.astype(jnp.bfloat16)
    value_b = mixed_in[:, rotated_width:].astype(jnp.bfloat16)
    query_part = turned_b[:, :query_width].reshape(rows_dev, n_rep, head_width)
    key_part = turned_b[:, query_width:].reshape(rows_dev, KV_HEADS, HEAD_DIM)
    value_part = value_b.reshape(rows_dev, KV_HEADS, HEAD_DIM)
    if shared > 1:
        key_part = jnp.repeat(key_part, shared, 1)
        value_part = jnp.repeat(value_part, shared, 1)
    sending = jnp.concatenate([query_part, key_part, value_part], 2).transpose(1, 0, 2)
    head_rows = lax.all_to_all(sending, "rep", split_axis=0, concat_axis=0, tiled=True)
    head_rows = head_rows.reshape(length, head_width + 2 * HEAD_DIM)
    mixed, mixed_out, totals = attend_forward(head_rows, starts, lows, heads)
    mixed_rows = lax.all_to_all(
        mixed.reshape(n_rep, rows_dev, head_width), "rep", split_axis=0, concat_axis=0, tiled=True
    )
    mixed_rows = mixed_rows.transpose(1, 0, 2).reshape(rows_dev, query_width)
    hidden = inputs + branch_scale * product(mixed_rows, full_out)

    normed_two, factor_two = rms_norm(hidden, mlp_gain)
    normed_two_b = normed_two.astype(jnp.bfloat16)
    router_f = full_router.astype(jnp.float32)
    logits = product(normed_two_b, full_router)
    numbers = jnp.arange(experts_all, dtype=jnp.int32)
    onehot = jnp.sum((own_routes[:, :, None] == numbers).astype(jnp.float32), 1)
    chosen = onehot > 0.5
    peak = jnp.max(jnp.where(chosen, logits, far_below), 1, keepdims=True)
    raised = jnp.where(chosen, jnp.exp(jnp.minimum(logits - peak, 0.0)), 0.0)
    probs = raised / jnp.sum(raised, 1, keepdims=True)
    before = (
        lax.broadcasted_iota(jnp.int32, (rows_dev, rows_dev), 0)
        > lax.broadcasted_iota(jnp.int32, (rows_dev, rows_dev), 1)
    ).astype(jnp.bfloat16)
    rank = product(before, onehot.astype(jnp.bfloat16))
    kept = chosen & (rank < CAP)
    rank_sent = jnp.where(kept, rank, -1.0).T
    probs_sent = probs.T
    both_sent = jnp.concatenate(
        [rank_sent.reshape(n_ep, -1, rows_dev), probs_sent.reshape(n_ep, -1, rows_dev)], 1
    )
    both_all = lax.all_to_all(both_sent, "ep", split_axis=0, concat_axis=0, tiled=True)
    ranks = both_all[:, : experts_all // n_ep]
    prob_all = both_all[:, experts_all // n_ep :]
    expert_rows = lax.all_gather(normed_two_b, "ep", axis=0, tiled=True)
    expert_cots = lax.all_gather(grad_output.astype(jnp.bfloat16), "ep", axis=0, tiled=True)
    rep_bits = [("rep", b) for b in range(bits_of(n_rep))]
    ep_bits = [("ep", b) for b in range(bits_of(n_ep))]
    count = experts_all // n_ep
    near = count * 3 // 4
    kinds = [k % 2 for k in range(near)] + [0] * (count - near)
    leads = [0, len(rep_bits) - 2]
    orders = [
        [leads[kind]] + [b for b in range(len(rep_bits)) if b != leads[kind]] for kind in kinds
    ]
    out_sum, grad_sum, inner_back, grad_keep, came_near, *sent = experts(
        expert_rows,
        expert_cots,
        ranks,
        prob_all,
        w_gate_up,
        w_down,
        n_rep,
        orders,
        near,
        ep_bits[::-1],
        ep_bits,
    )
    rep_orders = [[("rep", b) for b in order] for order in orders]
    early = list(range(0, near, 2))
    early = early[:2]

    def halves(left, right, label, e=None):
        mine, _ = side(*label)
        half = left.shape[-3] // 2

        def total(which):
            parts = []
            for stack in (left, right):
                start = [jnp.int32(0)] * stack.ndim
                start[-3] = (which * half).astype(jnp.int32)
                size = stack.shape[-3:]
                if e is not None:
                    start[0] = jnp.int32(e)
                part = lax.dynamic_slice(
                    stack, start, (1,) * (stack.ndim - 3) + (half,) + size[1:]
                )
                parts.append(part.reshape((half,) + size[1:]).astype(jnp.float32))
            return (parts[0] + parts[1]).astype(jnp.bfloat16)

        return (total(1 - mine), total(mine))

    output = hidden + branch_scale * out_sum
    grad_probs = inner_back.reshape(experts_all, rows_dev).T
    grad_logits = probs * (grad_probs - jnp.sum(grad_probs * probs, -1, keepdims=True))
    normed_two_f = normed_two_b.astype(jnp.float32)
    grad_router = jnp.dot(normed_two_f.T, grad_logits, precision=lax.Precision.HIGHEST)
    grad_normed_two = grad_sum + jnp.dot(
        grad_logits, router_f.T, precision=lax.Precision.HIGHEST
    )
    grad_hidden_norm, grad_mlp_gain = norm_back(grad_normed_two, hidden, factor_two, mlp_gain)
    grad_hidden = grad_output + grad_hidden_norm
    grad_attn = (branch_scale * grad_hidden).astype(jnp.bfloat16)
    grad_out_w = dot_tn(mixed_rows, grad_attn)
    grad_mixed = dot_nt(grad_attn, full_out).astype(jnp.bfloat16)
    grad_heads = lax.all_to_all(
        grad_mixed.reshape(rows_dev, n_rep, head_width).transpose(1, 0, 2),
        "rep",
        split_axis=0,
        concat_axis=0,
        tiled=True,
    ).reshape(length, head_width)
    beside = [swap(after(sent[0], grad_heads), *rep_orders[near][0])]
    second = {}
    for e in early:
        give, own = halves(grad_keep, came_near, rep_orders[e][1], e)
        second[e] = (own, swap(after(give, grad_heads), *rep_orders[e][1]))
        beside.append(second[e][1])
    returning = attend_backward(
        head_rows, grad_heads, mixed_out, totals, starts, lows, cosine, sine, heads
    )
    returning = after(returning, *beside)
    returned = lax.all_to_all(
        returning.reshape(n_rep, rows_dev, head_width + 2 * HEAD_DIM),
        "rep",
        split_axis=0,
        concat_axis=0,
        tiled=True,
    ).transpose(1, 0, 2)
    parts = [grad_keep, came_near]
    steps_of = {e: ((0, e), (1, e), 0) for e in range(near)}

    def put_by(e, own, got, skip):
        steps_of[e] = ((len(parts), 0), (len(parts) + 1, 0), skip)
        parts.extend([own[None], got[None]])

    for k, half in enumerate(sent):
        steps_of[near + k] = ((0, near + k), (len(parts), 0), 0 if k == 0 else -1)
        parts.append((beside[0] if k == 0 else half)[None])
    for e in early[1:]:
        put_by(e, *second[e], 1)
    for e in early[:1]:
        give, own = halves(*second[e], rep_orders[e][2])
        put_by(e, own, swap(after(give, returned), *rep_orders[e][2]), 2)
    units = [
        (e, steps_of[e][:2], rep_orders[e], steps_of[e][2])
        for e in sorted(range(count), key=lambda e: (e < near, e > 1 and e % 2, e))
    ]
    grad_query_rows = returned[:, :, :head_width].reshape(rows_dev, query_width)
    key_back = returned[:, :, head_width : head_width + HEAD_DIM]
    value_back = returned[:, :, head_width + HEAD_DIM :]
    if shared > 1:
        key_back = jnp.sum(
            key_back.reshape(rows_dev, KV_HEADS, shared, HEAD_DIM).astype(jnp.float32), 2
        ).astype(jnp.bfloat16)
        value_back = jnp.sum(
            value_back.reshape(rows_dev, KV_HEADS, shared, HEAD_DIM).astype(jnp.float32), 2
        ).astype(jnp.bfloat16)
    grad_in_rows = jnp.concatenate(
        [
            grad_query_rows,
            key_back.reshape(rows_dev, key_width),
            value_back.reshape(rows_dev, key_width),
        ],
        1,
    )
    grad_w_in = dot_tn(normed_b, grad_in_rows)
    grad_normed = dot_nt(grad_in_rows, full_in)
    grad_inputs_norm, grad_attn_gain = norm_back(grad_normed, inputs, factor_one, attn_gain)
    grad_inputs = grad_hidden + grad_inputs_norm
    everything = n_ep * n_rep
    gains = jnp.concatenate(
        [grad_attn_gain.reshape(everything, -1), grad_mlp_gain.reshape(everything, -1)], 1
    )
    labels = ep_bits[::-1] + rep_bits[::-1]
    shape = (2,) * len(labels)
    grads = [grad.astype(jnp.bfloat16) for grad in (grad_w_in, grad_out_w, grad_router)]
    lanes = [grad.reshape(shape + (-1, grad.shape[1])) for grad in grads]
    lanes.append(gains.reshape(shape + (1, -1)))
    expert_up, expert_down, weights, weights_out, weights_router, gains, _ = reduce_rest(
        parts,
        lanes,
        units,
        labels,
        ep_bits + rep_bits,
        model_width // n_rep,
    )
    gains = gains[0]
    part = model_width // everything
    return (
        output[None],
        grad_inputs[None],
        gains[:part],
        weights[:, :query_width],
        weights[:, query_width:rotated_width],
        weights[:, rotated_width:input_width],
        weights_out,
        gains[part:],
        weights_router,
        expert_up,
        expert_down,
    )


def solution(mesh):
    placed = (
        P("ep", "rep", None),
        P("ep", "rep"),
        P("ep", "rep", None),
        P(),
        P(("ep", "rep"), None),
        P(("ep", "rep"), None),
        P(("ep", "rep"), None),
        P(("ep", "rep"), None),
        P(),
        P(("ep", "rep"), None),
        P("ep", None, None),
        P("ep", None, None),
        P("ep", "rep", None),
    )
    return jax.shard_map(
        functools.partial(on_device, n_ep=mesh.shape["ep"], n_rep=mesh.shape["rep"]),
        mesh=mesh,
        in_specs=placed,
        out_specs=(
            P("ep", "rep", None),
            P("ep", "rep", None),
            P(("ep", "rep")),
            P(("ep", "rep"), None),
            P(("ep", "rep"), None),
            P(("ep", "rep"), None),
            P(("ep", "rep"), None),
            P(("ep", "rep")),
            P(("ep", "rep"), None),
            P("ep", "rep", None),
            P("ep", None, "rep"),
        ),
        check_vma=False,
    )
```

```python
import functools
import math

import jax
import jax.numpy as jnp
from jax import lax
from jax.experimental import pallas as pl
from jax.experimental.pallas import tpu as pltpu
from jax.sharding import PartitionSpec as P

HEADS = 16
KV_HEADS = 8
HEAD_DIM = 64
CAP = 80
BLOCK = 256

epsilon = 1e-06
score_scale = 0.015625
branch_scale = 0.22
far_below = -1e30

NT = (((1,), (1,)), ((), ()))
TN = (((0,), (0,)), ((), ()))


def product(left, right):
    return jnp.dot(left, right, preferred_element_type=jnp.float32)


def dot_nt(left, right):
    return lax.dot_general(left, right, NT, preferred_element_type=jnp.float32)


def dot_tn(left, right):
    return lax.dot_general(left, right, TN, preferred_element_type=jnp.float32)


def rms_norm(values, gain):
    factor = lax.rsqrt(jnp.mean(values * values, -1, keepdims=True) + epsilon)
    return (values * factor * gain, factor)


def norm_back(grad_normed, values, factor, gain):
    scaled = grad_normed * gain
    gain_part = jnp.sum(grad_normed * values * factor, 0)
    inner_sum = jnp.mean(scaled * values, -1, keepdims=True)
    return (factor * scaled - values * (factor * factor * factor) * inner_sum, gain_part)


def swap_halves(values):
    count, width = values.shape
    half_dim = HEAD_DIM // 2
    lane = lax.broadcasted_iota(jnp.int32, values.shape, 1)
    return jnp.where(
        lane % HEAD_DIM < half_dim,
        jnp.roll(values, -half_dim, 1),
        jnp.roll(values, half_dim, 1),
    )


def attend_forward_kernel(
    low_ref, rows_ref, start_ref, mixed_ref, out_ref, total_ref, key_s, value_s, *, heads
):
    step = pl.program_id(0)
    width = heads * HEAD_DIM

    @pl.when(step == 0)
    def _():
        key_s[...] = rows_ref[:, width : width + HEAD_DIM]
        value_s[...] = rows_ref[:, width + HEAD_DIM : width + 2 * HEAD_DIM]

    block_rows = rows_ref[pl.ds(pl.multiple_of(step * BLOCK, BLOCK), BLOCK), :]
    queries = [
        block_rows[:, h * HEAD_DIM : (h + 1) * HEAD_DIM] * jnp.bfloat16(score_scale)
        for h in range(heads)
    ]
    starts = start_ref[0]
    at = step * BLOCK + lax.broadcasted_iota(jnp.int32, (1, BLOCK), 1)

    def one(j, carry):
        rows = pl.ds(pl.multiple_of(j * BLOCK, BLOCK), BLOCK)
        key_block = key_s[rows, :]
        value_block = value_s[rows, :]
        place = j * BLOCK + lax.broadcasted_iota(jnp.int32, (BLOCK, BLOCK), 0)
        allowed = (place >= starts) & (place <= at)
        result = []
        for h in range(heads):
            peak, total, mixed = carry[h]
            scores = jnp.where(allowed, dot_nt(key_block, queries[h]), far_below)
            new_peak = jnp.maximum(peak, jnp.max(scores, 0, keepdims=True))
            fade = jnp.exp(peak - new_peak)
            raised = jnp.exp(scores - new_peak)
            total = fade * total + jnp.sum(raised, 0, keepdims=True)
            mixed = fade * mixed + dot_tn(value_block, raised.astype(jnp.bfloat16))
            result.append((new_peak, total, mixed))
        return tuple(result)

    first = tuple(
        (
            jnp.full((1, BLOCK), far_below, jnp.float32),
            jnp.zeros((1, BLOCK), jnp.float32),
            jnp.zeros((HEAD_DIM, BLOCK), jnp.float32),
        )
        for _ in range(heads)
    )
    done = lax.fori_loop(low_ref[step], step + 1, one, first)
    for h in range(heads):
        peak, total, mixed = done[h]
        mixed = mixed / total
        out_ref[h * HEAD_DIM : (h + 1) * HEAD_DIM, :] = mixed
        total_ref[0, h : h + 1, :] = peak + jnp.log(total)
        mixed_ref[:, h * HEAD_DIM : (h + 1) * HEAD_DIM] = mixed.T.astype(jnp.bfloat16)


def attend_forward(rows, starts, lows, heads):
    length, width = rows.shape
    blocks = length // BLOCK
    whole = lambda i, low: (0, 0)
    return pl.pallas_call(
        functools.partial(attend_forward_kernel, heads=heads),
        out_shape=(
            jax.ShapeDtypeStruct((length, heads * HEAD_DIM), jnp.bfloat16),
            jax.ShapeDtypeStruct((heads * HEAD_DIM, length), jnp.float32),
            jax.ShapeDtypeStruct((blocks, heads, BLOCK), jnp.float32),
        ),
        grid_spec=pltpu.PrefetchScalarGridSpec(
            num_scalar_prefetch=1,
            grid=(blocks,),
            in_specs=[
                pl.BlockSpec((length, width), whole),
                pl.BlockSpec((1, 1, BLOCK), lambda i, low: (i, 0, 0)),
            ],
            out_specs=[
                pl.BlockSpec((BLOCK, heads * HEAD_DIM), lambda i, low: (i, 0)),
                pl.BlockSpec((heads * HEAD_DIM, BLOCK), lambda i, low: (0, i)),
                pl.BlockSpec((1, heads, BLOCK), lambda i, low: (i, 0, 0)),
            ],
            scratch_shapes=[
                pltpu.VMEM((length, HEAD_DIM), jnp.bfloat16),
                pltpu.VMEM((length, HEAD_DIM), jnp.bfloat16),
            ],
        ),
        name="attend_forward",
    )(lows, rows, starts)


def attend_backward_kernel(
    low_ref,
    rows_ref,
    grad_ref,
    out_ref,
    total_ref,
    start_ref,
    cosine_ref,
    sine_ref,
    back_ref,
    key_s,
    value_s,
    grad_query_s,
    grad_key_s,
    grad_value_s,
    *,
    heads,
    blocks,
):
    step = pl.program_id(0)
    width = heads * HEAD_DIM

    @pl.when(step == 0)
    def _():
        key_s[...] = rows_ref[:, width : width + HEAD_DIM]
        value_s[...] = rows_ref[:, width + HEAD_DIM : width + 2 * HEAD_DIM]
        grad_key_s[...] = jnp.zeros_like(grad_key_s)
        grad_value_s[...] = jnp.zeros_like(grad_value_s)

    own = pl.ds(pl.multiple_of(step * BLOCK, BLOCK), BLOCK)
    block_rows = rows_ref[own, :]
    grads_all = grad_ref[...]
    starts = start_ref[0]
    at = step * BLOCK + lax.broadcasted_iota(jnp.int32, (1, BLOCK), 1)
    queries, scaled, grads, inners, totals = [], [], [], [], []
    for h in range(heads):
        span = slice(h * HEAD_DIM, (h + 1) * HEAD_DIM)
        queries.append(block_rows[:, span])
        scaled.append(block_rows[:, span] * jnp.bfloat16(score_scale))
        grads.append(grads_all[:, span])
        turned = grads_all[:, span].astype(jnp.float32).T
        inners.append(jnp.sum(turned * out_ref[span, :], 0, keepdims=True))
        totals.append(total_ref[0, h : h + 1, :])

    def one(j, carry):
        rows = pl.ds(pl.multiple_of(j * BLOCK, BLOCK), BLOCK)
        key_block = key_s[rows, :]
        value_block = value_s[rows, :]
        place = j * BLOCK + lax.broadcasted_iota(jnp.int32, (BLOCK, BLOCK), 0)
        allowed = (place >= starts) & (place <= at)
        result = []
        key_sum = grad_key_s[rows, :]
        value_sum = grad_value_s[rows, :]
        for h in range(heads):
            scores = jnp.where(allowed, dot_nt(key_block, scaled[h]), far_below)
            prob = jnp.exp(scores - totals[h])
            grad_prob = dot_nt(value_block, grads[h])
            grad_scores = (prob * (grad_prob - inners[h]) * score_scale).astype(jnp.bfloat16)
            value_sum = value_sum + product(prob.astype(jnp.bfloat16), grads[h])
            key_sum = key_sum + product(grad_scores, queries[h])
            result.append(carry[h] + dot_tn(grad_scores, key_block))
        grad_key_s[rows, :] = key_sum
        grad_value_s[rows, :] = value_sum
        return tuple(result)

    first = tuple(jnp.zeros((BLOCK, HEAD_DIM), jnp.float32) for _ in range(heads))
    done = lax.fori_loop(low_ref[step], step + 1, one, first)
    for h in range(heads):
        grad_query_s[own, h * HEAD_DIM : (h + 1) * HEAD_DIM] = done[h]

    @pl.when(step == blocks - 1)
    def _():
        def turn(j, carry):
            rows = pl.ds(pl.multiple_of(j * BLOCK, BLOCK), BLOCK)
            cosine = cosine_ref[rows, :]
            sine = sine_ref[rows, :]
            parts = [
                grad_query_s[rows, h * HEAD_DIM : (h + 1) * HEAD_DIM] for h in range(heads)
            ]
            parts.append(grad_key_s[rows, :])
            half = HEAD_DIM // 2
            turned = [
                part * cosine - jnp.concatenate([part[:, half:], part[:, :half]], 1) * sine
                for part in parts
            ]
            turned.append(grad_value_s[rows, :])
            back_ref[rows, :] = jnp.concatenate(turned, 1).astype(jnp.bfloat16)
            return carry

        lax.fori_loop(0, blocks, turn, 0)


def attend_backward(rows, grads, outs, totals, starts, lows, cosine, sine, heads):
    length, width = rows.shape
    blocks = length // BLOCK
    whole = lambda i, low: (0, 0)
    once = pl.Buffered(1)
    return pl.pallas_call(
        functools.partial(attend_backward_kernel, heads=heads, blocks=blocks),
        out_shape=jax.ShapeDtypeStruct((length, width), jnp.bfloat16),
        grid_spec=pltpu.PrefetchScalarGridSpec(
            num_scalar_prefetch=1,
            grid=(blocks,),
            in_specs=[
                pl.BlockSpec((length, width), whole),
                pl.BlockSpec((BLOCK, heads * HEAD_DIM), lambda i, low: (i, 0)),
                pl.BlockSpec((heads * HEAD_DIM, BLOCK), lambda i, low: (0, i)),
                pl.BlockSpec((1, heads, BLOCK), lambda i, low: (i, 0, 0)),
                pl.BlockSpec((1, 1, BLOCK), lambda i, low: (i, 0, 0)),
                pl.BlockSpec((length, HEAD_DIM), whole, pipeline_mode=once),
                pl.BlockSpec((length, HEAD_DIM), whole, pipeline_mode=once),
            ],
            out_specs=pl.BlockSpec((length, width), whole),
            scratch_shapes=[
                pltpu.VMEM((length, HEAD_DIM), jnp.bfloat16),
                pltpu.VMEM((length, HEAD_DIM), jnp.bfloat16),
                pltpu.VMEM((length, heads * HEAD_DIM), jnp.float32),
                pltpu.VMEM((length, HEAD_DIM), jnp.float32),
                pltpu.VMEM((length, HEAD_DIM), jnp.float32),
            ],
        ),
        name="attend_backward",
    )(lows, rows, grads, outs, totals, starts, cosine, sine)


def after(value, *others):
    return lax.optimization_barrier((value, *others))[0]


def bits_of(size):
    return max(size.bit_length() - 1, 0)


def swap(sent, axis, bit):
    size = lax.axis_size(axis)
    return lax.ppermute(sent, axis, [(i, i ^ (1 << bit)) for i in range(size)])


def side(axis, bit):
    index = lax.axis_index(axis)
    mine = (index // (1 << bit)) % 2
    return (mine, index + (1 - 2 * mine) * (1 << bit))


def pick(dim, index):
    return (slice(None),) * dim + (index,)


def digits(number, count):
    return tuple((number // (1 << (count - 1 - k))) % 2 for k in range(count))


def mesh_copy(source, target, sends, gets, axis, partner):
    return pltpu.make_async_remote_copy(
        src_ref=source,
        dst_ref=target,
        send_sem=sends,
        recv_sem=gets,
        device_id={axis: partner},
        device_id_type=pl.DeviceIdType.MESH,
    )


def greet(partners):
    barrier = pltpu.get_barrier_semaphore()
    for axis, partner in partners:
        pl.semaphore_signal(
            barrier, inc=1, device_id={axis: partner}, device_id_type=pl.DeviceIdType.MESH
        )
    pl.semaphore_wait(barrier, len(partners))


class Lane:
    def __init__(self, labels, order, first, refs, sends, gets, rows=None):
        bits = len(labels)
        self.order, self.first, self.sends, self.gets = (order, first, sends, gets)
        self.sums, self.got = (refs[: bits - 1], refs[bits - 1 : 2 * bits - 1])
        self.labels = [list(labels)]
        for label in order:
            self.labels.append([other for other in self.labels[-1] if other != label])
        self.rows = rows

    @staticmethod
    def scratch(bits, tail, dtype):
        shapes = [pltpu.VMEM((2,) * (bits - 1 - k) + tail, dtype) for k in range(bits)]
        return shapes[:-1] + shapes

    def source(self, k):
        return self.first if k == 0 else self.sums[k - 1]

    def copy(self, k):
        axis, bit = self.order[k]
        mine, partner = side(axis, bit)
        dim = self.labels[k].index((axis, bit))
        return mesh_copy(
            self.source(k).at[pick(dim, 1 - mine)],
            self.got[k],
            self.sends.at[k],
            self.gets.at[k],
            axis,
            partner,
        )

    def start(self, k):
        self.copy(k).start()

    def add(self, k, out=None):
        axis, bit = self.order[k]
        mine, _ = side(axis, bit)
        dim = self.labels[k].index((axis, bit))
        left = len(self.order) - 1 - k
        self.copy(k).wait_recv()
        source, got = (self.source(k), self.got[k])
        target = out if left == 0 else self.sums[k]
        height = got.shape[left]
        rows = self.rows or height
        blocks = height // rows

        def body(i, carry):
            at = digits(i // blocks, left)
            own = pl.ds(pl.multiple_of((i % blocks) * rows, rows), rows)
            if blocks == 1:
                own = slice(None)
            here = at[:dim] + (mine,) + at[dim:]
            total = source[here + (own,)].astype(jnp.float32) + got[at + (own,)].astype(
                jnp.float32
            )
            target[at + (own,)] = total.astype(target.dtype)
            return carry

        lax.fori_loop(0, blocks << left, body, 0)

    def finish(self):
        for k in range(len(self.order)):
            self.copy(k).wait_send()


def gather_kernel(*refs, lanes, partners):
    count = len(lanes)
    ins, outs = (refs[:count], refs[count : 2 * count])
    sends, gets = refs[2 * count :]
    greet([(axis, side(axis, bit)[1]) for axis, bit in partners])

    def copy(number, k):
        labels, order = lanes[number]
        region = tuple(
            slice(None) if label in order[:k] else side(*label)[0] for label in labels
        )
        target = outs[number].at[region]
        axis, bit = order[k]
        return mesh_copy(
            ins[number] if k == 0 else target,
            target,
            sends.at[number, k],
            gets.at[number, k],
            axis,
            side(axis, bit)[1],
        )

    most = max(len(order) for _, order in lanes)
    for k in range(most + 1):
        for number, (labels, order) in enumerate(lanes):
            if 0 < k <= len(order):
                copy(number, k - 1).wait_recv()
            if k < len(order):
                copy(number, k).start()
            if k == 0:
                outs[number][tuple(side(*label)[0] for label in labels)] = ins[number][...]
    for number, (_, order) in enumerate(lanes):
        for k in range(len(order)):
            copy(number, k).wait_send()


def gather(arrays, lanes, partners):
    vmem = pl.BlockSpec(memory_space=pltpu.VMEM)
    most = max(len(order) for _, order in lanes)
    return pl.pallas_call(
        functools.partial(gather_kernel, lanes=lanes, partners=partners),
        out_shape=[
            jax.ShapeDtypeStruct((2,) * len(order) + array.shape, array.dtype)
            for array, (_, order) in zip(arrays, lanes)
        ],
        in_specs=[vmem] * len(arrays),
        out_specs=[vmem] * len(arrays),
        scratch_shapes=[
            pltpu.SemaphoreType.DMA((len(arrays), most)),
            pltpu.SemaphoreType.DMA((len(arrays), most)),
        ],
        compiler_params=pltpu.CompilerParams(collective_id=2, has_side_effects=True),
        name="gather",
    )(*arrays)


def reduce_kernel(*refs, units, n_parts, n_lanes, labels, weight_order, share):
    part_refs, refs = (refs[:n_parts], refs[n_parts:])
    lane_ins, (up_ref, down_ref, *refs) = (refs[:n_lanes], refs[n_lanes:])
    lane_outs, (late_ref, *refs) = (refs[:n_lanes], refs[n_lanes:])
    steps = len(units[0][2]) - 1
    sends, keeps, gets = ([], [], [])
    for _ in range(steps):
        sends.append(refs[0])
        keeps.append(refs[1])
        gets.append(refs[2])
        refs = refs[3:]
    bits = len(labels)
    each = 2 * bits - 1
    lane_refs, refs = (refs[: n_lanes * each], refs[n_lanes * each :])
    load_keep, load_came, load_sem, unit_send, unit_get, lane_send, lane_get, late_sem = refs
    lanes = [
        Lane(
            labels,
            weight_order,
            first,
            lane_refs[number * each : (number + 1) * each],
            lane_send.at[number],
            lane_get.at[number],
        )
        for number, first in enumerate(lane_ins)
    ]
    _, spots, tall, width = load_keep.shape
    rows = 32 if tall % 32 == 0 else tall
    blocks = tall // rows

    greet([(axis, side(axis, bit)[1]) for axis, bit in weight_order])

    def lane_start(k):
        for lane in lanes:
            lane.start(k)

    def lane_add(k):
        for lane, out in zip(lanes, lane_outs):
            lane.add(k, out)

    lane_start(0)

    late = [n for n, unit in enumerate(units) if unit[3] < 0]
    half_way = [n for n, unit in enumerate(units) if 0 < unit[3] < steps]
    fresh = [n for n, unit in enumerate(units) if unit[3] == 0]
    done = [n for n, unit in enumerate(units) if unit[3] == steps]
    sequence = half_way + fresh + late + done

    def late_copy(n):
        _, ((_, _), (which, place)), order, _ = units[n]
        axis, bit = order[0]
        return mesh_copy(
            part_refs[which].at[place],
            late_ref.at[late.index(n)],
            late_sem.at[0, late.index(n)],
            late_sem.at[1, late.index(n)],
            axis,
            side(axis, bit)[1],
        )

    def loads(turn):
        n = sequence[turn]
        _, parts, _, skip = units[n]
        slot = turn % 2
        size = spots >> max(skip, 0)
        sources = [part_refs[which].at[place] for which, place in parts]
        if skip < 0:
            sources[1] = late_ref.at[late.index(n)]
        return [
            pltpu.make_async_copy(
                source, buffer.at[slot, pl.ds(0, size)], load_sem.at[slot, number]
            )
            for number, (source, buffer) in enumerate(zip(sources, (load_keep, load_came)))
        ]

    def load(turn):
        if turn < len(units) and units[sequence[turn]][3] >= 0:
            for copy in loads(turn):
                copy.start()

    def unit_copy(unit, order, k):
        axis, bit = order[k + 1]
        return mesh_copy(
            sends[k].at[unit],
            gets[k].at[unit],
            unit_send.at[unit, k],
            unit_get.at[unit, k],
            axis,
            side(axis, bit)[1],
        )

    def unit_add(unit, order, k, left, right):
        mine, _ = side(*order[k + 1])
        half = spots >> (k + 1)

        def fill(target, which):
            def body(i, carry):
                piece = i // blocks
                own = pl.ds(pl.multiple_of((i % blocks) * rows, rows), rows)
                total = left[which * half + piece, own, :].astype(jnp.float32) + right[
                    which * half + piece, own, :
                ].astype(jnp.float32)
                target[unit, piece, own, :] = total.astype(jnp.bfloat16)
                return carry

            lax.fori_loop(0, half * blocks, body, 0)

        fill(sends[k], 1 - mine)
        unit_copy(unit, order, k).start()
        fill(keeps[k], mine)

    def begin_unit(n):
        unit, _, order, skip = units[n]
        turn = sequence.index(n)
        if skip < 0:
            late_copy(n).wait_recv()
            for copy in loads(turn):
                copy.start()
        for copy in loads(turn):
            copy.wait()
        left, right = (load_keep.at[turn % 2], load_came.at[turn % 2])
        if skip < steps:
            unit_add(unit, order, max(skip, 0), left, right)
        else:
            give(unit, left[0].astype(jnp.float32) + right[0].astype(jnp.float32))
        load(turn + 2)

    def next_unit(n, k):
        unit, _, order, _ = units[n]
        unit_copy(unit, order, k - 1).wait_recv()
        unit_add(unit, order, k, keeps[k - 1].at[unit], gets[k - 1].at[unit])

    def end_unit(n):
        unit, _, order, _ = units[n]
        unit_copy(unit, order, steps - 1).wait_recv()
        give(unit, keeps[-1][unit, 0].astype(jnp.float32) + gets[-1][unit, 0].astype(jnp.float32))

    def give(unit, total):
        up_ref[unit] = total[:share]
        pieces = width // share
        rest = tall - share
        for p in range(pieces):
            down_ref[unit, p * rest : (p + 1) * rest, :] = total[
                share:, p * share : (p + 1) * share
            ]

    load(0)
    load(1)
    def late_start():
        for n in late:
            late_copy(n).start()

    def lane_turn(k):
        lane_add(k)
        if k + 1 < bits:
            lane_start(k + 1)

    work = [(begin_unit, n) for n in half_way + fresh[:1]] + [(lane_turn, 0)]
    work += [(begin_unit, n) for n in fresh[1:2]] + [(late_start,)]
    work += [(begin_unit, n) for n in fresh[2:]]
    for k in range(1, steps):
        onward = [n for n in half_way if units[n][3] < k] + fresh
        work += [(next_unit, n, k) for n in onward[:3]]
        if k == 1:
            work += [(lane_turn, 1)] + [(begin_unit, n) for n in late]
        work += [(next_unit, n, k) for n in onward[3:4]]
        work += [(next_unit, n, k) for n in late]
        work += [(next_unit, n, k) for n in onward[4:]]
    work += [(begin_unit, n) for n in done]
    work += [(end_unit, n) for n in half_way + fresh[:3] + late] + [(lane_turn, 2)]
    work += [(end_unit, n) for n in fresh[3:4]] + [(lane_turn, 3)]
    work += [(end_unit, n) for n in fresh[4:]]
    work += [(lane_turn, k) for k in range(4, bits)]
    for job, *arguments in work:
        job(*arguments)
    for unit, _, order, skip in units:
        for k in range(max(skip, 0), steps):
            unit_copy(unit, order, k).wait_send()
    for n in late:
        late_copy(n).wait_send()
    for lane in lanes:
        lane.finish()


def reduce_rest(parts, lanes, units, labels, weight_order, share):
    _, spots, tall, width = parts[0].shape
    count = len(units)
    bits = len(labels)
    steps = len(units[0][2]) - 1
    late = max(1, len([unit for unit in units if unit[3] < 0]))
    anywhere = pl.BlockSpec(memory_space=pl.ANY)
    vmem = pl.BlockSpec(memory_space=pltpu.VMEM)
    scratch = []
    for k in range(steps):
        scratch += [pltpu.VMEM((count, spots >> (k + 1), tall, width), jnp.bfloat16)] * 3
    for lane in lanes:
        scratch += Lane.scratch(bits, lane.shape[bits:], lane.dtype)
    scratch += [
        pltpu.VMEM((2, spots, tall, width), jnp.bfloat16),
        pltpu.VMEM((2, spots, tall, width), jnp.bfloat16),
        pltpu.SemaphoreType.DMA((2, 2)),
        pltpu.SemaphoreType.DMA((count, steps)),
        pltpu.SemaphoreType.DMA((count, steps)),
        pltpu.SemaphoreType.DMA((len(lanes), bits)),
        pltpu.SemaphoreType.DMA((len(lanes), bits)),
        pltpu.SemaphoreType.DMA((2, late)),
    ]
    return pl.pallas_call(
        functools.partial(
            reduce_kernel,
            units=units,
            n_parts=len(parts),
            n_lanes=len(lanes),
            labels=labels,
            weight_order=weight_order,
            share=share,
        ),
        out_shape=(
            jax.ShapeDtypeStruct((count, share, width), jnp.float32),
            jax.ShapeDtypeStruct((count, (tall - share) * (width // share), share), jnp.float32),
        )
        + tuple(jax.ShapeDtypeStruct(lane.shape[bits:], jnp.float32) for lane in lanes)
        + (jax.ShapeDtypeStruct((late, spots, tall, width), jnp.bfloat16),),
        in_specs=[anywhere] * len(parts) + [vmem] * len(lanes),
        out_specs=[vmem] * (2 + len(lanes)) + [anywhere],
        scratch_shapes=scratch,
        compiler_params=pltpu.CompilerParams(
            collective_id=0, has_side_effects=True, vmem_limit_bytes=67 * 1000 * 1000
        ),
        name="reduce_rest",
    )(*parts, *lanes)


def experts_kernel(
    *refs, sources, rows_dev, count, copies, orders, near, labels, ep_order
):
    rows_hbm, cot_hbm, rank_ref, prob_ref, gate_up_ref, down_ref, *refs = refs
    out_ref, grad_ref, inner_ref, keep_ref, came_ref, *refs = refs
    far = count - near
    sent_refs, refs = (refs[:far], refs[far:])
    rows_s, cot_s, picks_s, out_s, grad_s, send_s, inner_s, inner_got, *refs = refs
    bits = len(labels)
    lane_refs, refs = (refs[: 2 * (2 * bits - 1)], refs[2 * (2 * bits - 1) :])
    load_sem, unit_send, unit_get, lane_send, lane_get, inner_send, inner_take = refs
    me = lax.axis_index("ep")
    step = pl.program_id(0)
    grad_lane, out_lane = [
        Lane(
            labels,
            ep_order,
            first,
            lane_refs[number * (2 * bits - 1) : (number + 1) * (2 * bits - 1)],
            lane_send.at[number],
            lane_get.at[number],
            rows=32,
        )
        for number, first in enumerate((cot_s, rows_s))
    ]

    def unit_copy(e):
        bit = orders[e][0]
        if e < near:
            return mesh_copy(
                send_s.at[e],
                came_ref.at[e],
                unit_send.at[e],
                unit_get.at[e],
                "rep",
                side("rep", bit)[1],
            )
        return pltpu.make_async_copy(send_s.at[e], sent_refs[e - near], unit_send.at[e])

    def inner_copy(d):
        peer = (me + d) % sources
        return mesh_copy(
            inner_s.at[peer],
            inner_got.at[me],
            inner_send.at[d - 1],
            inner_take.at[d - 1],
            "ep",
            peer,
        )

    @pl.when(step == 0)
    def _():
        loads = [
            pltpu.make_async_copy(rows_hbm, rows_s, load_sem.at[0]),
            pltpu.make_async_copy(cot_hbm, cot_s, load_sem.at[1]),
        ]
        for copy in loads:
            copy.start()
        partners = [("ep", (me + d) % sources) for d in range(1, sources)]
        for bit in sorted({order[0] for order in orders[:near]}):
            partners.append(("rep", side("rep", bit)[1]))
        greet(partners)
        for copy in loads:
            copy.wait()

    slots = pl.ds(pl.multiple_of(step * CAP, 16), CAP)
    numbers = lax.broadcasted_iota(jnp.int32, (CAP, rows_dev), 0).astype(jnp.float32)
    rows_in, cots, weights, picks = [], [], [], []
    for s in range(sources):
        rank = rank_ref[s, pl.ds(step, 1), :]
        pick_table = jnp.where(rank == numbers, 1.0, 0.0)
        weights.append(jnp.sum(pick_table * prob_ref[s, pl.ds(step, 1), :], 1, keepdims=True))
        pick_b = pick_table.astype(jnp.bfloat16)
        picks.append(pick_table)
        picks_s[s, slots, :] = pick_b
        rows_in.append(product(pick_b, rows_s[digits(s, bits)]).astype(jnp.bfloat16))
        cots.append(product(pick_b, cot_s[digits(s, bits)]))
    arrived = jnp.concatenate(rows_in, 0)
    weight = jnp.concatenate(weights, 0)
    grad_mix = branch_scale * jnp.concatenate(cots, 0)
    gate_up = gate_up_ref[0]
    down = down_ref[0]
    hidden_units = down.shape[0]
    both = product(arrived, gate_up)
    gate_part = both[:, :hidden_units]
    up_part = both[:, hidden_units:]
    sigmoid_gate = jax.nn.sigmoid(gate_part)
    active = (gate_part * sigmoid_gate * up_part).astype(jnp.bfloat16)
    produced = product(active, down).astype(jnp.bfloat16).astype(jnp.float32)
    inner = jnp.sum(grad_mix * produced, 1, keepdims=True)
    sent_out = (weight * produced).astype(jnp.bfloat16)
    grad_out = (weight * grad_mix).astype(jnp.bfloat16)
    grad_active = dot_nt(grad_out, down)
    grad_down = dot_tn(active, grad_out).astype(jnp.bfloat16)
    grad_gate = grad_active * up_part * sigmoid_gate * (1.0 + gate_part * (1.0 - sigmoid_gate))
    grad_up = grad_active * gate_part * sigmoid_gate
    grad_both = jnp.concatenate([grad_gate, grad_up], 1).astype(jnp.bfloat16)
    grad_gate_up = dot_tn(arrived, grad_both).astype(jnp.bfloat16)
    share = grad_down.shape[1] // copies
    tall = hidden_units // copies

    def put(order, mine):
        bit, *later = order
        for r in range(copies):
            spot = 0
            for b in later:
                spot = 2 * spot + ((r >> b) & 1)
            ref = keep_ref.at[0] if (r >> bit) & 1 == mine else send_s.at[step]
            ref[spot, :share, :] = grad_gate_up[r * share : (r + 1) * share]
            for k in range(copies):
                ref[spot, share : share + tall, k * share : (k + 1) * share] = grad_down[
                    k * tall : (k + 1) * tall, r * share : (r + 1) * share
                ]

    for order in {tuple(order): order for order in orders}.values():
        members = [e for e in range(count) if orders[e] == order]
        here = functools.reduce(jnp.logical_or, [step == e for e in members])
        side_mine, _ = side("rep", order[0])
        for mine in range(2):

            @pl.when(here & (side_mine == mine))
            def _(order=order, mine=mine):
                put(order, mine)

    grad_in = dot_nt(grad_both, gate_up).astype(jnp.bfloat16)
    for s in range(sources):
        part = slice(s * CAP, (s + 1) * CAP)
        out_s[s, slots, :] = sent_out[part]
        grad_s[s, slots, :] = grad_in[part]
        inner_s[s, pl.ds(step, 1), :] = jnp.sum(picks[s] * inner[part], 0, keepdims=True)
    for e in range(count):

        @pl.when(step == e)
        def _(e=e):
            unit_copy(e).start()

    @pl.when(step == count - 1)
    def _():
        for table_of, target, lane in ((grad_s, cot_s, grad_lane), (out_s, rows_s, out_lane)):
            for s in range(sources):
                target[digits(s, bits)] = dot_tn(picks_s[s], table_of[s]).astype(jnp.bfloat16)
            lane.start(0)
        for d in range(1, sources):
            inner_copy(d).start()
        for k in range(bits):
            for lane, total in ((grad_lane, grad_ref), (out_lane, out_ref)):
                lane.add(k, total)
                if k + 1 < bits:
                    lane.start(k + 1)
        inner_got[me] = inner_s[me]
        for d in range(1, sources):
            inner_copy(d).wait_recv()
        inner_ref[...] = inner_got[...]
        for d in range(1, sources):
            inner_copy(d).wait_send()
        grad_lane.finish()
        out_lane.finish()
        for e in range(count):
            unit_copy(e).wait()


def experts(rows, cots, ranks, probs, w_gate_up, w_down, copies, orders, near, labels, ep_order):
    sources, count, rows_dev = ranks.shape
    total, model_width = rows.shape
    hidden_units = w_down.shape[1]
    bits = len(labels)
    tall = model_width // copies + hidden_units // copies
    flat = lambda i: (0, 0)
    cube = lambda i: (0, 0, 0)
    once = pl.Buffered(1)
    anywhere = pl.BlockSpec(memory_space=pl.ANY)
    far = count - near
    shape = (2,) * bits + (rows_dev, model_width)
    piece = (copies // 2, tall, model_width)
    return pl.pallas_call(
        functools.partial(
            experts_kernel,
            sources=sources,
            rows_dev=rows_dev,
            count=count,
            copies=copies,
            orders=orders,
            near=near,
            labels=labels,
            ep_order=ep_order,
        ),
        out_shape=(
            jax.ShapeDtypeStruct((rows_dev, model_width), jnp.float32),
            jax.ShapeDtypeStruct((rows_dev, model_width), jnp.float32),
            jax.ShapeDtypeStruct((sources, count, rows_dev), jnp.float32),
            jax.ShapeDtypeStruct((count,) + piece, jnp.bfloat16),
            jax.ShapeDtypeStruct((near,) + piece, jnp.bfloat16),
        )
        + (jax.ShapeDtypeStruct(piece, jnp.bfloat16),) * far,
        grid=(count,),
        in_specs=[
            anywhere,
            anywhere,
            pl.BlockSpec((sources, count, rows_dev), cube, pipeline_mode=once),
            pl.BlockSpec((sources, count, rows_dev), cube, pipeline_mode=once),
            pl.BlockSpec((1, model_width, 2 * hidden_units), lambda i: (i, 0, 0)),
            pl.BlockSpec((1, hidden_units, model_width), lambda i: (i, 0, 0)),
        ],
        out_specs=[
            pl.BlockSpec((rows_dev, model_width), flat, pipeline_mode=once),
            pl.BlockSpec((rows_dev, model_width), flat, pipeline_mode=once),
            pl.BlockSpec((sources, count, rows_dev), cube, pipeline_mode=once),
            pl.BlockSpec((1,) + piece, lambda i: (i, 0, 0, 0)),
            anywhere,
        ]
        + [anywhere] * far,
        scratch_shapes=[
            pltpu.VMEM(shape, jnp.bfloat16),
            pltpu.VMEM(shape, jnp.bfloat16),
            pltpu.VMEM((sources, count * CAP, rows_dev), jnp.bfloat16),
            pltpu.VMEM((sources, count * CAP, model_width), jnp.bfloat16),
            pltpu.VMEM((sources, count * CAP, model_width), jnp.bfloat16),
            pltpu.VMEM((count,) + piece, jnp.bfloat16),
            pltpu.VMEM((sources, count, rows_dev), jnp.float32),
            pltpu.VMEM((sources, count, rows_dev), jnp.float32),
        ]
        + Lane.scratch(bits, (rows_dev, model_width), jnp.bfloat16) * 2
        + [
            pltpu.SemaphoreType.DMA((2,)),
            pltpu.SemaphoreType.DMA((count,)),
            pltpu.SemaphoreType.DMA((near,)),
            pltpu.SemaphoreType.DMA((2, bits)),
            pltpu.SemaphoreType.DMA((2, bits)),
            pltpu.SemaphoreType.DMA((sources - 1,)),
            pltpu.SemaphoreType.DMA((sources - 1,)),
        ],
        compiler_params=pltpu.CompilerParams(
            collective_id=1, has_side_effects=True, vmem_limit_bytes=67 * 1000 * 1000
        ),
        name="experts",
    )(rows.reshape(shape), cots.reshape(shape), ranks, probs, w_gate_up, w_down)


def on_device(
    tokens,
    segments,
    routes,
    attn_gain,
    w_query,
    w_key,
    w_value,
    w_out,
    mlp_gain,
    w_router,
    w_gate_up,
    w_down,
    cotangent,
    *,
    n_ep,
    n_rep,
):
    inputs = tokens[0]
    own_routes = routes[0]
    grad_output = cotangent[0]
    rows_dev, model_width = inputs.shape
    everyone = ("ep", "rep")
    heads = HEADS // n_rep
    head_width = heads * HEAD_DIM
    shared = max(1, n_rep // KV_HEADS)
    query_width = w_query.shape[1]
    key_width = w_key.shape[1]
    experts_all = w_router.shape[1]
    half_dim = HEAD_DIM // 2

    rep_bits = [("rep", b) for b in range(bits_of(n_rep))]
    ep_bits = [("ep", b) for b in range(bits_of(n_ep))]
    labels = ep_bits[::-1] + rep_bits[::-1]
    rep_down, ep_down = (rep_bits[::-1], ep_bits[::-1])
    full_query, full_rest, pack_ids = gather(
        [w_query, jnp.concatenate([w_key, w_value], 1), segments],
        [
            (labels, rep_down + ep_down),
            (labels, rep_down[:-1] + ep_down[:-1] + rep_bits[:1] + ep_bits[:1]),
            (rep_down, rep_down),
        ],
        labels,
    )
    full_query = full_query.reshape(model_width, -1)
    full_rest = full_rest.reshape(model_width, -1)
    pack_ids = pack_ids.reshape(-1)
    rotated_width = query_width + key_width
    input_width = rotated_width + key_width
    joined = after(jnp.concatenate([w_out, w_router], 1), full_query)
    full = lax.all_gather(joined, everyone, axis=0, tiled=True)
    full_out = full[:, :model_width]
    full_router = full[:, model_width:]

    length = pack_ids.shape[0]
    blocks = length // BLOCK
    offset = lax.axis_index("rep") * rows_dev
    doc_start = jnp.sum((pack_ids[None, :] < pack_ids[:, None]).astype(jnp.int32), 1)
    starts = doc_start.reshape(blocks, 1, BLOCK)
    lows = doc_start[::BLOCK] // BLOCK
    pace = jnp.exp(jnp.arange(half_dim, dtype=jnp.float32) * (-math.log(10000.0) / half_dim))

    def rope_tables(first, begins):
        places = first + jnp.arange(begins.shape[0], dtype=jnp.int32)
        angles = (places - begins).astype(jnp.float32)[:, None] * pace[None, :]
        cosine = jnp.cos(angles)
        sine = jnp.sin(angles)
        return (jnp.concatenate([cosine, cosine], 1), jnp.concatenate([-sine, sine], 1))

    own_starts = jnp.sum((pack_ids[None, :] < segments[0][:, None]).astype(jnp.int32), 1)
    own_cosine, own_sine = rope_tables(offset, own_starts)

    normed, factor_one = rms_norm(inputs, attn_gain)
    normed_b = normed.astype(jnp.bfloat16)
    mixed_in = jnp.concatenate([product(normed_b, full_query), product(normed_b, full_rest)], 1)
    turn = mixed_in[:, :rotated_width]
    times = rotated_width // HEAD_DIM
    turned = turn * jnp.tile(own_cosine, (1, times)) + swap_halves(turn) * jnp.tile(
        own_sine, (1, times)
    )
    turned_b = turned.astype(jnp.bfloat16)
    value_b = mixed_in[:, rotated_width:].astype(jnp.bfloat16)
    query_part = turned_b[:, :query_width].reshape(rows_dev, n_rep, head_width)
    key_part = turned_b[:, query_width:].reshape(rows_dev, KV_HEADS, HEAD_DIM)
    value_part = value_b.reshape(rows_dev, KV_HEADS, HEAD_DIM)
    if shared > 1:
        key_part = jnp.repeat(key_part, shared, 1)
        value_part = jnp.repeat(value_part, shared, 1)
    sending = jnp.concatenate([query_part, key_part, value_part], 2).transpose(1, 0, 2)
    head_rows = lax.all_to_all(sending, "rep", split_axis=0, concat_axis=0, tiled=True)
    head_rows = head_rows.reshape(length, head_width + 2 * HEAD_DIM)
    mixed, mixed_out, totals = attend_forward(head_rows, starts, lows, heads)
    cosine, sine = rope_tables(0, after(doc_start, mixed))
    mixed_rows = lax.all_to_all(
        mixed.reshape(n_rep, rows_dev, head_width), "rep", split_axis=0, concat_axis=0, tiled=True
    )
    mixed_rows = mixed_rows.transpose(1, 0, 2).reshape(rows_dev, query_width)
    hidden = inputs + branch_scale * product(mixed_rows, full_out)

    normed_two, factor_two = rms_norm(hidden, mlp_gain)
    normed_two_b = normed_two.astype(jnp.bfloat16)
    router_f = full_router.astype(jnp.float32)
    logits = product(normed_two_b, full_router)
    numbers = jnp.arange(experts_all, dtype=jnp.int32)
    onehot = jnp.sum((own_routes[:, :, None] == numbers).astype(jnp.float32), 1)
    chosen = onehot > 0.5
    peak = jnp.max(jnp.where(chosen, logits, far_below), 1, keepdims=True)
    raised = jnp.where(chosen, jnp.exp(jnp.minimum(logits - peak, 0.0)), 0.0)
    probs = raised / jnp.sum(raised, 1, keepdims=True)
    before = (
        lax.broadcasted_iota(jnp.int32, (rows_dev, rows_dev), 0)
        > lax.broadcasted_iota(jnp.int32, (rows_dev, rows_dev), 1)
    ).astype(jnp.bfloat16)
    rank = product(before, onehot.astype(jnp.bfloat16))
    kept = chosen & (rank < CAP)
    rank_sent = jnp.where(kept, rank, -1.0).T
    probs_sent = probs.T
    both_sent = jnp.concatenate(
        [rank_sent.reshape(n_ep, -1, rows_dev), probs_sent.reshape(n_ep, -1, rows_dev)], 1
    )
    both_all = lax.all_to_all(both_sent, "ep", split_axis=0, concat_axis=0, tiled=True)
    ranks = both_all[:, : experts_all // n_ep]
    prob_all = both_all[:, experts_all // n_ep :]
    expert_rows = lax.all_gather(normed_two_b, "ep", axis=0, tiled=True)
    expert_cots = lax.all_gather(grad_output.astype(jnp.bfloat16), "ep", axis=0, tiled=True)
    count = experts_all // n_ep
    near = count * 3 // 4
    kinds = [k % 2 for k in range(near)] + [0] * (count - near)
    leads = [0, len(rep_bits) - 2]
    orders = [
        [leads[kind]] + [b for b in range(len(rep_bits)) if b != leads[kind]] for kind in kinds
    ]
    out_sum, grad_sum, inner_back, grad_keep, came_near, *sent = experts(
        expert_rows,
        expert_cots,
        ranks,
        prob_all,
        w_gate_up,
        w_down,
        n_rep,
        orders,
        near,
        ep_bits[::-1],
        ep_bits,
    )
    rep_orders = [[("rep", b) for b in order] for order in orders]
    early = list(range(0, near, 2))
    early = early[:2]

    def halves(left, right, label, e=None):
        mine, _ = side(*label)
        half = left.shape[-3] // 2

        def total(which):
            parts = []
            for stack in (left, right):
                start = [jnp.int32(0)] * stack.ndim
                start[-3] = (which * half).astype(jnp.int32)
                size = stack.shape[-3:]
                if e is not None:
                    start[0] = jnp.int32(e)
                part = lax.dynamic_slice(
                    stack, start, (1,) * (stack.ndim - 3) + (half,) + size[1:]
                )
                parts.append(part.reshape((half,) + size[1:]).astype(jnp.float32))
            return (parts[0] + parts[1]).astype(jnp.bfloat16)

        return (total(1 - mine), total(mine))

    output = hidden + branch_scale * out_sum
    grad_probs = inner_back.reshape(experts_all, rows_dev).T
    grad_logits = probs * (grad_probs - jnp.sum(grad_probs * probs, -1, keepdims=True))
    normed_two_f = normed_two_b.astype(jnp.float32)
    grad_router = jnp.dot(normed_two_f.T, grad_logits, precision=lax.Precision.HIGHEST)
    grad_normed_two = grad_sum + jnp.dot(
        grad_logits, router_f.T, precision=lax.Precision.HIGHEST
    )
    grad_hidden_norm, grad_mlp_gain = norm_back(grad_normed_two, hidden, factor_two, mlp_gain)
    grad_hidden = grad_output + grad_hidden_norm
    grad_attn = (branch_scale * grad_hidden).astype(jnp.bfloat16)
    grad_out_w = dot_tn(mixed_rows, grad_attn)
    grad_mixed = dot_nt(grad_attn, full_out).astype(jnp.bfloat16)
    grad_heads = lax.all_to_all(
        grad_mixed.reshape(rows_dev, n_rep, head_width).transpose(1, 0, 2),
        "rep",
        split_axis=0,
        concat_axis=0,
        tiled=True,
    ).reshape(length, head_width)
    beside = [swap(after(sent[0], grad_heads), *rep_orders[near][0])]
    second = {}
    for e in early:
        give, own = halves(grad_keep, came_near, rep_orders[e][1], e)
        second[e] = (own, swap(after(give, grad_heads), *rep_orders[e][1]))
        beside.append(second[e][1])
    returning = attend_backward(
        head_rows, grad_heads, mixed_out, totals, starts, lows, cosine, sine, heads
    )
    returning = after(returning, *beside)
    returned = lax.all_to_all(
        returning.reshape(n_rep, rows_dev, head_width + 2 * HEAD_DIM),
        "rep",
        split_axis=0,
        concat_axis=0,
        tiled=True,
    ).transpose(1, 0, 2)
    parts = [grad_keep, came_near]
    steps_of = {e: ((0, e), (1, e), 0) for e in range(near)}

    def put_by(e, own, got, skip):
        steps_of[e] = ((len(parts), 0), (len(parts) + 1, 0), skip)
        parts.extend([own[None], got[None]])

    for k, half in enumerate(sent):
        steps_of[near + k] = ((0, near + k), (len(parts), 0), 0 if k == 0 else -1)
        parts.append((beside[0] if k == 0 else half)[None])
    for e in early[1:]:
        put_by(e, *second[e], 1)
    for e in early[:1]:
        give, own = halves(*second[e], rep_orders[e][2])
        put_by(e, own, swap(after(give, returned), *rep_orders[e][2]), 2)
    units = [
        (e, steps_of[e][:2], rep_orders[e], steps_of[e][2])
        for e in sorted(range(count), key=lambda e: (e < near, e > 1 and e % 2, e))
    ]
    grad_query_rows = returned[:, :, :head_width].reshape(rows_dev, query_width)
    key_back = returned[:, :, head_width : head_width + HEAD_DIM]
    value_back = returned[:, :, head_width + HEAD_DIM :]
    if shared > 1:
        key_back = jnp.sum(
            key_back.reshape(rows_dev, KV_HEADS, shared, HEAD_DIM).astype(jnp.float32), 2
        ).astype(jnp.bfloat16)
        value_back = jnp.sum(
            value_back.reshape(rows_dev, KV_HEADS, shared, HEAD_DIM).astype(jnp.float32), 2
        ).astype(jnp.bfloat16)
    grad_in_rows = jnp.concatenate(
        [
            grad_query_rows,
            key_back.reshape(rows_dev, key_width),
            value_back.reshape(rows_dev, key_width),
        ],
        1,
    )
    grad_w_in = dot_tn(normed_b, grad_in_rows)
    grad_normed = dot_nt(grad_in_rows[:, :query_width], full_query) + dot_nt(
        grad_in_rows[:, query_width:], full_rest
    )
    grad_inputs_norm, grad_attn_gain = norm_back(grad_normed, inputs, factor_one, attn_gain)
    grad_inputs = grad_hidden + grad_inputs_norm
    everything = n_ep * n_rep
    gains = jnp.concatenate(
        [grad_attn_gain.reshape(everything, -1), grad_mlp_gain.reshape(everything, -1)], 1
    )
    shape = (2,) * len(labels)
    grads = [grad.astype(jnp.bfloat16) for grad in (grad_w_in, grad_out_w, grad_router)]
    lanes = [grad.reshape(shape + (-1, grad.shape[1])) for grad in grads]
    lanes.append(gains.reshape(shape + (1, -1)))
    expert_up, expert_down, weights, weights_out, weights_router, gains, _ = reduce_rest(
        parts,
        lanes,
        units,
        labels,
        ep_bits + rep_bits,
        model_width // n_rep,
    )
    gains = gains[0]
    part = model_width // everything
    return (
        output[None],
        grad_inputs[None],
        gains[:part],
        weights[:, :query_width],
        weights[:, query_width:rotated_width],
        weights[:, rotated_width:input_width],
        weights_out,
        gains[part:],
        weights_router,
        expert_up,
        expert_down,
    )


def solution(mesh):
    placed = (
        P("ep", "rep", None),
        P("ep", "rep"),
        P("ep", "rep", None),
        P(),
        P(("ep", "rep"), None),
        P(("ep", "rep"), None),
        P(("ep", "rep"), None),
        P(("ep", "rep"), None),
        P(),
        P(("ep", "rep"), None),
        P("ep", None, None),
        P("ep", None, None),
        P("ep", "rep", None),
    )
    return jax.shard_map(
        functools.partial(on_device, n_ep=mesh.shape["ep"], n_rep=mesh.shape["rep"]),
        mesh=mesh,
        in_specs=placed,
        out_specs=(
            P("ep", "rep", None),
            P("ep", "rep", None),
            P(("ep", "rep")),
            P(("ep", "rep"), None),
            P(("ep", "rep"), None),
            P(("ep", "rep"), None),
            P(("ep", "rep"), None),
            P(("ep", "rep")),
            P(("ep", "rep"), None),
            P("ep", "rep", None),
            P("ep", None, "rep"),
        ),
        check_vma=False,
    )
```

```python
import functools
import math

import jax
import jax.numpy as jnp
from jax import lax
from jax.experimental import pallas as pl
from jax.experimental.pallas import tpu as pltpu
from jax.sharding import PartitionSpec as P

HEADS = 16
KV_HEADS = 8
HEAD_DIM = 64
CAP = 80
BLOCK = 256

epsilon = 1e-06
score_scale = 0.015625
branch_scale = 0.22
far_below = -1e30

NT = (((1,), (1,)), ((), ()))
TN = (((0,), (0,)), ((), ()))


def product(left, right):
    return jnp.dot(left, right, preferred_element_type=jnp.float32)


def dot_nt(left, right):
    return lax.dot_general(left, right, NT, preferred_element_type=jnp.float32)


def dot_tn(left, right):
    return lax.dot_general(left, right, TN, preferred_element_type=jnp.float32)


def rms_norm(values, gain):
    factor = lax.rsqrt(jnp.mean(values * values, -1, keepdims=True) + epsilon)
    return (values * factor * gain, factor)


def norm_back(grad_normed, values, factor, gain):
    scaled = grad_normed * gain
    gain_part = jnp.sum(grad_normed * values * factor, 0)
    inner_sum = jnp.mean(scaled * values, -1, keepdims=True)
    return (factor * scaled - values * (factor * factor * factor) * inner_sum, gain_part)


def swap_halves(values):
    count, width = values.shape
    half_dim = HEAD_DIM // 2
    lane = lax.broadcasted_iota(jnp.int32, values.shape, 1)
    return jnp.where(
        lane % HEAD_DIM < half_dim,
        jnp.roll(values, -half_dim, 1),
        jnp.roll(values, half_dim, 1),
    )


def attend_forward_kernel(
    low_ref, rows_ref, start_ref, mixed_ref, out_ref, total_ref, key_s, value_s, *, heads
):
    step = pl.program_id(0)
    width = heads * HEAD_DIM

    @pl.when(step == 0)
    def _():
        key_s[...] = rows_ref[:, width : width + HEAD_DIM]
        value_s[...] = rows_ref[:, width + HEAD_DIM : width + 2 * HEAD_DIM]

    block_rows = rows_ref[pl.ds(pl.multiple_of(step * BLOCK, BLOCK), BLOCK), :]
    queries = [
        block_rows[:, h * HEAD_DIM : (h + 1) * HEAD_DIM] * jnp.bfloat16(score_scale)
        for h in range(heads)
    ]
    starts = start_ref[0]
    at = step * BLOCK + lax.broadcasted_iota(jnp.int32, (1, BLOCK), 1)

    def one(j, carry):
        rows = pl.ds(pl.multiple_of(j * BLOCK, BLOCK), BLOCK)
        key_block = key_s[rows, :]
        value_block = value_s[rows, :]
        place = j * BLOCK + lax.broadcasted_iota(jnp.int32, (BLOCK, BLOCK), 0)
        allowed = (place >= starts) & (place <= at)
        result = []
        for h in range(heads):
            peak, total, mixed = carry[h]
            scores = jnp.where(allowed, dot_nt(key_block, queries[h]), far_below)
            new_peak = jnp.maximum(peak, jnp.max(scores, 0, keepdims=True))
            fade = jnp.exp(peak - new_peak)
            raised = jnp.exp(scores - new_peak)
            total = fade * total + jnp.sum(raised, 0, keepdims=True)
            mixed = fade * mixed + dot_tn(value_block, raised.astype(jnp.bfloat16))
            result.append((new_peak, total, mixed))
        return tuple(result)

    first = tuple(
        (
            jnp.full((1, BLOCK), far_below, jnp.float32),
            jnp.zeros((1, BLOCK), jnp.float32),
            jnp.zeros((HEAD_DIM, BLOCK), jnp.float32),
        )
        for _ in range(heads)
    )
    done = lax.fori_loop(low_ref[step], step + 1, one, first)
    for h in range(heads):
        peak, total, mixed = done[h]
        mixed = mixed / total
        out_ref[h * HEAD_DIM : (h + 1) * HEAD_DIM, :] = mixed
        total_ref[0, h : h + 1, :] = peak + jnp.log(total)
        mixed_ref[:, h * HEAD_DIM : (h + 1) * HEAD_DIM] = mixed.T.astype(jnp.bfloat16)


def attend_forward(rows, starts, lows, heads):
    length, width = rows.shape
    blocks = length // BLOCK
    whole = lambda i, low: (0, 0)
    return pl.pallas_call(
        functools.partial(attend_forward_kernel, heads=heads),
        out_shape=(
            jax.ShapeDtypeStruct((length, heads * HEAD_DIM), jnp.bfloat16),
            jax.ShapeDtypeStruct((heads * HEAD_DIM, length), jnp.float32),
            jax.ShapeDtypeStruct((blocks, heads, BLOCK), jnp.float32),
        ),
        grid_spec=pltpu.PrefetchScalarGridSpec(
            num_scalar_prefetch=1,
            grid=(blocks,),
            in_specs=[
                pl.BlockSpec((length, width), whole),
                pl.BlockSpec((1, 1, BLOCK), lambda i, low: (i, 0, 0)),
            ],
            out_specs=[
                pl.BlockSpec((BLOCK, heads * HEAD_DIM), lambda i, low: (i, 0)),
                pl.BlockSpec((heads * HEAD_DIM, BLOCK), lambda i, low: (0, i)),
                pl.BlockSpec((1, heads, BLOCK), lambda i, low: (i, 0, 0)),
            ],
            scratch_shapes=[
                pltpu.VMEM((length, HEAD_DIM), jnp.bfloat16),
                pltpu.VMEM((length, HEAD_DIM), jnp.bfloat16),
            ],
        ),
        name="attend_forward",
    )(lows, rows, starts)


def attend_backward_kernel(
    low_ref,
    rows_ref,
    grad_ref,
    out_ref,
    total_ref,
    start_ref,
    cosine_ref,
    sine_ref,
    back_ref,
    key_s,
    value_s,
    grad_query_s,
    grad_key_s,
    grad_value_s,
    *,
    heads,
    blocks,
):
    step = pl.program_id(0)
    width = heads * HEAD_DIM

    @pl.when(step == 0)
    def _():
        key_s[...] = rows_ref[:, width : width + HEAD_DIM]
        value_s[...] = rows_ref[:, width + HEAD_DIM : width + 2 * HEAD_DIM]
        grad_key_s[...] = jnp.zeros_like(grad_key_s)
        grad_value_s[...] = jnp.zeros_like(grad_value_s)

    own = pl.ds(pl.multiple_of(step * BLOCK, BLOCK), BLOCK)
    block_rows = rows_ref[own, :]
    grads_all = grad_ref[...]
    starts = start_ref[0]
    at = step * BLOCK + lax.broadcasted_iota(jnp.int32, (1, BLOCK), 1)
    queries, scaled, grads, inners, totals = [], [], [], [], []
    for h in range(heads):
        span = slice(h * HEAD_DIM, (h + 1) * HEAD_DIM)
        queries.append(block_rows[:, span])
        scaled.append(block_rows[:, span] * jnp.bfloat16(score_scale))
        grads.append(grads_all[:, span])
        turned = grads_all[:, span].astype(jnp.float32).T
        inners.append(jnp.sum(turned * out_ref[span, :], 0, keepdims=True))
        totals.append(total_ref[0, h : h + 1, :])

    def one(j, carry):
        rows = pl.ds(pl.multiple_of(j * BLOCK, BLOCK), BLOCK)
        key_block = key_s[rows, :]
        value_block = value_s[rows, :]
        place = j * BLOCK + lax.broadcasted_iota(jnp.int32, (BLOCK, BLOCK), 0)
        allowed = (place >= starts) & (place <= at)
        result = []
        key_sum = grad_key_s[rows, :]
        value_sum = grad_value_s[rows, :]
        for h in range(heads):
            scores = jnp.where(allowed, dot_nt(key_block, scaled[h]), far_below)
            prob = jnp.exp(scores - totals[h])
            grad_prob = dot_nt(value_block, grads[h])
            grad_scores = (prob * (grad_prob - inners[h]) * score_scale).astype(jnp.bfloat16)
            value_sum = value_sum + product(prob.astype(jnp.bfloat16), grads[h])
            key_sum = key_sum + product(grad_scores, queries[h])
            result.append(carry[h] + dot_tn(grad_scores, key_block))
        grad_key_s[rows, :] = key_sum
        grad_value_s[rows, :] = value_sum
        return tuple(result)

    first = tuple(jnp.zeros((BLOCK, HEAD_DIM), jnp.float32) for _ in range(heads))
    done = lax.fori_loop(low_ref[step], step + 1, one, first)
    for h in range(heads):
        grad_query_s[own, h * HEAD_DIM : (h + 1) * HEAD_DIM] = done[h]

    @pl.when(step == blocks - 1)
    def _():
        def turn(j, carry):
            rows = pl.ds(pl.multiple_of(j * BLOCK, BLOCK), BLOCK)
            cosine = cosine_ref[rows, :]
            sine = sine_ref[rows, :]
            parts = [
                grad_query_s[rows, h * HEAD_DIM : (h + 1) * HEAD_DIM] for h in range(heads)
            ]
            parts.append(grad_key_s[rows, :])
            half = HEAD_DIM // 2
            turned = [
                part * cosine - jnp.concatenate([part[:, half:], part[:, :half]], 1) * sine
                for part in parts
            ]
            turned.append(grad_value_s[rows, :])
            back_ref[rows, :] = jnp.concatenate(turned, 1).astype(jnp.bfloat16)
            return carry

        lax.fori_loop(0, blocks, turn, 0)


def attend_backward(rows, grads, outs, totals, starts, lows, cosine, sine, heads):
    length, width = rows.shape
    blocks = length // BLOCK
    whole = lambda i, low: (0, 0)
    once = pl.Buffered(1)
    return pl.pallas_call(
        functools.partial(attend_backward_kernel, heads=heads, blocks=blocks),
        out_shape=jax.ShapeDtypeStruct((length, width), jnp.bfloat16),
        grid_spec=pltpu.PrefetchScalarGridSpec(
            num_scalar_prefetch=1,
            grid=(blocks,),
            in_specs=[
                pl.BlockSpec((length, width), whole),
                pl.BlockSpec((BLOCK, heads * HEAD_DIM), lambda i, low: (i, 0)),
                pl.BlockSpec((heads * HEAD_DIM, BLOCK), lambda i, low: (0, i)),
                pl.BlockSpec((1, heads, BLOCK), lambda i, low: (i, 0, 0)),
                pl.BlockSpec((1, 1, BLOCK), lambda i, low: (i, 0, 0)),
                pl.BlockSpec((length, HEAD_DIM), whole, pipeline_mode=once),
                pl.BlockSpec((length, HEAD_DIM), whole, pipeline_mode=once),
            ],
            out_specs=pl.BlockSpec((length, width), whole),
            scratch_shapes=[
                pltpu.VMEM((length, HEAD_DIM), jnp.bfloat16),
                pltpu.VMEM((length, HEAD_DIM), jnp.bfloat16),
                pltpu.VMEM((length, heads * HEAD_DIM), jnp.float32),
                pltpu.VMEM((length, HEAD_DIM), jnp.float32),
                pltpu.VMEM((length, HEAD_DIM), jnp.float32),
            ],
        ),
        name="attend_backward",
    )(lows, rows, grads, outs, totals, starts, cosine, sine)


def after(value, *others):
    return lax.optimization_barrier((value, *others))[0]


def bits_of(size):
    return max(size.bit_length() - 1, 0)


def swap(sent, axis, bit):
    size = lax.axis_size(axis)
    return lax.ppermute(sent, axis, [(i, i ^ (1 << bit)) for i in range(size)])


def side(axis, bit):
    index = lax.axis_index(axis)
    mine = (index // (1 << bit)) % 2
    return (mine, index + (1 - 2 * mine) * (1 << bit))


def pick(dim, index):
    return (slice(None),) * dim + (index,)


def digits(number, count):
    return tuple((number // (1 << (count - 1 - k))) % 2 for k in range(count))


def mesh_copy(source, target, sends, gets, axis, partner):
    return pltpu.make_async_remote_copy(
        src_ref=source,
        dst_ref=target,
        send_sem=sends,
        recv_sem=gets,
        device_id={axis: partner},
        device_id_type=pl.DeviceIdType.MESH,
    )


def greet(partners):
    barrier = pltpu.get_barrier_semaphore()
    for axis, partner in partners:
        pl.semaphore_signal(
            barrier, inc=1, device_id={axis: partner}, device_id_type=pl.DeviceIdType.MESH
        )
    pl.semaphore_wait(barrier, len(partners))


class Lane:
    def __init__(self, labels, order, first, refs, sends, gets, rows=None):
        bits = len(labels)
        self.order, self.first, self.sends, self.gets = (order, first, sends, gets)
        self.sums, self.got = (refs[: bits - 1], refs[bits - 1 : 2 * bits - 1])
        self.labels = [list(labels)]
        for label in order:
            self.labels.append([other for other in self.labels[-1] if other != label])
        self.rows = rows

    @staticmethod
    def scratch(bits, tail, dtype):
        shapes = [pltpu.VMEM((2,) * (bits - 1 - k) + tail, dtype) for k in range(bits)]
        return shapes[:-1] + shapes

    def source(self, k):
        return self.first if k == 0 else self.sums[k - 1]

    def copy(self, k):
        axis, bit = self.order[k]
        mine, partner = side(axis, bit)
        dim = self.labels[k].index((axis, bit))
        return mesh_copy(
            self.source(k).at[pick(dim, 1 - mine)],
            self.got[k],
            self.sends.at[k],
            self.gets.at[k],
            axis,
            partner,
        )

    def start(self, k):
        self.copy(k).start()

    def add(self, k, out=None):
        axis, bit = self.order[k]
        mine, _ = side(axis, bit)
        dim = self.labels[k].index((axis, bit))
        left = len(self.order) - 1 - k
        self.copy(k).wait_recv()
        source, got = (self.source(k), self.got[k])
        target = out if left == 0 else self.sums[k]
        height = got.shape[left]
        rows = self.rows or height
        blocks = height // rows

        def body(i, carry):
            at = digits(i // blocks, left)
            own = pl.ds(pl.multiple_of((i % blocks) * rows, rows), rows)
            if blocks == 1:
                own = slice(None)
            here = at[:dim] + (mine,) + at[dim:]
            total = source[here + (own,)].astype(jnp.float32) + got[at + (own,)].astype(
                jnp.float32
            )
            target[at + (own,)] = total.astype(target.dtype)
            return carry

        lax.fori_loop(0, blocks << left, body, 0)

    def finish(self):
        for k in range(len(self.order)):
            self.copy(k).wait_send()


def gather_kernel(*refs, lanes, partners):
    count = len(lanes)
    ins, outs = (refs[:count], refs[count : 2 * count])
    sends, gets = refs[2 * count :]
    greet([(axis, side(axis, bit)[1]) for axis, bit in partners])

    def copy(number, k):
        labels, order = lanes[number]
        region = tuple(
            slice(None) if label in order[:k] else side(*label)[0] for label in labels
        )
        target = outs[number].at[region]
        axis, bit = order[k]
        return mesh_copy(
            ins[number] if k == 0 else target,
            target,
            sends.at[number, k],
            gets.at[number, k],
            axis,
            side(axis, bit)[1],
        )

    most = max(len(order) for _, order in lanes)
    for k in range(most + 1):
        for number, (labels, order) in enumerate(lanes):
            if 0 < k <= len(order):
                copy(number, k - 1).wait_recv()
            if k < len(order):
                copy(number, k).start()
            if k == 0:
                outs[number][tuple(side(*label)[0] for label in labels)] = ins[number][...]
    for number, (_, order) in enumerate(lanes):
        for k in range(len(order)):
            copy(number, k).wait_send()


def gather(arrays, lanes, partners):
    vmem = pl.BlockSpec(memory_space=pltpu.VMEM)
    most = max(len(order) for _, order in lanes)
    return pl.pallas_call(
        functools.partial(gather_kernel, lanes=lanes, partners=partners),
        out_shape=[
            jax.ShapeDtypeStruct((2,) * len(order) + array.shape, array.dtype)
            for array, (_, order) in zip(arrays, lanes)
        ],
        in_specs=[vmem] * len(arrays),
        out_specs=[vmem] * len(arrays),
        scratch_shapes=[
            pltpu.SemaphoreType.DMA((len(arrays), most)),
            pltpu.SemaphoreType.DMA((len(arrays), most)),
        ],
        compiler_params=pltpu.CompilerParams(collective_id=2, has_side_effects=True),
        name="gather",
    )(*arrays)


def reduce_kernel(*refs, units, n_parts, n_lanes, labels, weight_order, share):
    part_refs, refs = (refs[:n_parts], refs[n_parts:])
    lane_ins, (up_ref, down_ref, *refs) = (refs[:n_lanes], refs[n_lanes:])
    lane_outs, (late_ref, *refs) = (refs[:n_lanes], refs[n_lanes:])
    steps = len(units[0][2]) - 1
    sends, keeps, gets = ([], [], [])
    for _ in range(steps):
        sends.append(refs[0])
        keeps.append(refs[1])
        gets.append(refs[2])
        refs = refs[3:]
    bits = len(labels)
    each = 2 * bits - 1
    lane_refs, refs = (refs[: n_lanes * each], refs[n_lanes * each :])
    load_keep, load_came, load_sem, unit_send, unit_get, lane_send, lane_get, late_sem = refs
    lanes = [
        Lane(
            labels,
            weight_order,
            first,
            lane_refs[number * each : (number + 1) * each],
            lane_send.at[number],
            lane_get.at[number],
        )
        for number, first in enumerate(lane_ins)
    ]
    _, spots, tall, width = load_keep.shape
    rows = 32 if tall % 32 == 0 else tall
    blocks = tall // rows

    greet([(axis, side(axis, bit)[1]) for axis, bit in weight_order])

    def lane_start(k):
        for lane in lanes:
            lane.start(k)

    def lane_add(k):
        for lane, out in zip(lanes, lane_outs):
            lane.add(k, out)

    lane_start(0)

    late = [n for n, unit in enumerate(units) if unit[3] < 0]
    half_way = [n for n, unit in enumerate(units) if 0 < unit[3] < steps]
    fresh = [n for n, unit in enumerate(units) if unit[3] == 0]
    done = [n for n, unit in enumerate(units) if unit[3] == steps]
    sequence = half_way + fresh + late + done

    def late_copy(n):
        _, ((_, _), (which, place)), order, _ = units[n]
        axis, bit = order[0]
        return mesh_copy(
            part_refs[which].at[place],
            late_ref.at[late.index(n)],
            late_sem.at[0, late.index(n)],
            late_sem.at[1, late.index(n)],
            axis,
            side(axis, bit)[1],
        )

    def loads(turn):
        n = sequence[turn]
        _, parts, _, skip = units[n]
        slot = turn % 2
        size = spots >> max(skip, 0)
        sources = [part_refs[which].at[place] for which, place in parts]
        if skip < 0:
            sources[1] = late_ref.at[late.index(n)]
        return [
            pltpu.make_async_copy(
                source, buffer.at[slot, pl.ds(0, size)], load_sem.at[slot, number]
            )
            for number, (source, buffer) in enumerate(zip(sources, (load_keep, load_came)))
        ]

    def load(turn):
        if turn < len(units) and units[sequence[turn]][3] >= 0:
            for copy in loads(turn):
                copy.start()

    def unit_copy(unit, order, k):
        axis, bit = order[k + 1]
        return mesh_copy(
            sends[k].at[unit],
            gets[k].at[unit],
            unit_send.at[unit, k],
            unit_get.at[unit, k],
            axis,
            side(axis, bit)[1],
        )

    def unit_add(unit, order, k, left, right):
        mine, _ = side(*order[k + 1])
        half = spots >> (k + 1)

        def fill(target, which):
            def body(i, carry):
                piece = i // blocks
                own = pl.ds(pl.multiple_of((i % blocks) * rows, rows), rows)
                total = left[which * half + piece, own, :].astype(jnp.float32) + right[
                    which * half + piece, own, :
                ].astype(jnp.float32)
                target[unit, piece, own, :] = total.astype(jnp.bfloat16)
                return carry

            lax.fori_loop(0, half * blocks, body, 0)

        fill(sends[k], 1 - mine)
        unit_copy(unit, order, k).start()
        fill(keeps[k], mine)

    def begin_unit(n):
        unit, _, order, skip = units[n]
        turn = sequence.index(n)
        if skip < 0:
            late_copy(n).wait_recv()
            for copy in loads(turn):
                copy.start()
        for copy in loads(turn):
            copy.wait()
        left, right = (load_keep.at[turn % 2], load_came.at[turn % 2])
        if skip < steps:
            unit_add(unit, order, max(skip, 0), left, right)
        else:
            give(unit, left[0].astype(jnp.float32) + right[0].astype(jnp.float32))
        load(turn + 2)

    def next_unit(n, k):
        unit, _, order, _ = units[n]
        unit_copy(unit, order, k - 1).wait_recv()
        unit_add(unit, order, k, keeps[k - 1].at[unit], gets[k - 1].at[unit])

    def end_unit(n):
        unit, _, order, _ = units[n]
        unit_copy(unit, order, steps - 1).wait_recv()
        give(unit, keeps[-1][unit, 0].astype(jnp.float32) + gets[-1][unit, 0].astype(jnp.float32))

    def give(unit, total):
        up_ref[unit] = total[:share]
        pieces = width // share
        rest = tall - share
        for p in range(pieces):
            down_ref[unit, p * rest : (p + 1) * rest, :] = total[
                share:, p * share : (p + 1) * share
            ]

    load(0)
    load(1)
    def late_start():
        for n in late:
            late_copy(n).start()

    def lane_turn(k):
        lane_add(k)
        if k + 1 < bits:
            lane_start(k + 1)

    work = [(begin_unit, n) for n in half_way + fresh[:1]] + [(lane_turn, 0)]
    work += [(begin_unit, n) for n in fresh[1:2]] + [(late_start,)]
    work += [(begin_unit, n) for n in fresh[2:]]
    for k in range(1, steps):
        onward = [n for n in half_way if units[n][3] < k] + fresh
        work += [(next_unit, n, k) for n in onward[:3]]
        if k == 1:
            work += [(lane_turn, 1)] + [(begin_unit, n) for n in late]
        work += [(next_unit, n, k) for n in onward[3:4]]
        work += [(next_unit, n, k) for n in late]
        work += [(next_unit, n, k) for n in onward[4:]]
    work += [(begin_unit, n) for n in done]
    work += [(end_unit, n) for n in half_way + fresh[:3] + late] + [(lane_turn, 2)]
    work += [(end_unit, n) for n in fresh[3:4]] + [(lane_turn, 3)]
    work += [(end_unit, n) for n in fresh[4:]]
    work += [(lane_turn, k) for k in range(4, bits)]
    for job, *arguments in work:
        job(*arguments)
    for unit, _, order, skip in units:
        for k in range(max(skip, 0), steps):
            unit_copy(unit, order, k).wait_send()
    for n in late:
        late_copy(n).wait_send()
    for lane in lanes:
        lane.finish()


def reduce_rest(parts, lanes, units, labels, weight_order, share):
    _, spots, tall, width = parts[0].shape
    count = len(units)
    bits = len(labels)
    steps = len(units[0][2]) - 1
    late = max(1, len([unit for unit in units if unit[3] < 0]))
    anywhere = pl.BlockSpec(memory_space=pl.ANY)
    vmem = pl.BlockSpec(memory_space=pltpu.VMEM)
    scratch = []
    for k in range(steps):
        scratch += [pltpu.VMEM((count, spots >> (k + 1), tall, width), jnp.bfloat16)] * 3
    for lane in lanes:
        scratch += Lane.scratch(bits, lane.shape[bits:], lane.dtype)
    scratch += [
        pltpu.VMEM((2, spots, tall, width), jnp.bfloat16),
        pltpu.VMEM((2, spots, tall, width), jnp.bfloat16),
        pltpu.SemaphoreType.DMA((2, 2)),
        pltpu.SemaphoreType.DMA((count, steps)),
        pltpu.SemaphoreType.DMA((count, steps)),
        pltpu.SemaphoreType.DMA((len(lanes), bits)),
        pltpu.SemaphoreType.DMA((len(lanes), bits)),
        pltpu.SemaphoreType.DMA((2, late)),
    ]
    return pl.pallas_call(
        functools.partial(
            reduce_kernel,
            units=units,
            n_parts=len(parts),
            n_lanes=len(lanes),
            labels=labels,
            weight_order=weight_order,
            share=share,
        ),
        out_shape=(
            jax.ShapeDtypeStruct((count, share, width), jnp.float32),
            jax.ShapeDtypeStruct((count, (tall - share) * (width // share), share), jnp.float32),
        )
        + tuple(jax.ShapeDtypeStruct(lane.shape[bits:], jnp.float32) for lane in lanes)
        + (jax.ShapeDtypeStruct((late, spots, tall, width), jnp.bfloat16),),
        in_specs=[anywhere] * len(parts) + [vmem] * len(lanes),
        out_specs=[vmem] * (2 + len(lanes)) + [anywhere],
        scratch_shapes=scratch,
        compiler_params=pltpu.CompilerParams(
            collective_id=0, has_side_effects=True, vmem_limit_bytes=67 * 1000 * 1000
        ),
        name="reduce_rest",
    )(*parts, *lanes)


def experts_kernel(
    *refs, sources, rows_dev, count, copies, orders, near, labels, ep_order
):
    rows_hbm, cot_hbm, rank_ref, prob_ref, gate_up_ref, down_ref, *refs = refs
    out_ref, grad_ref, inner_ref, keep_ref, came_ref, *refs = refs
    far = count - near
    sent_refs, refs = (refs[:far], refs[far:])
    rows_s, cot_s, picks_s, out_s, grad_s, send_s, inner_s, inner_got, *refs = refs
    bits = len(labels)
    lane_refs, refs = (refs[: 2 * (2 * bits - 1)], refs[2 * (2 * bits - 1) :])
    load_sem, unit_send, unit_get, lane_send, lane_get, inner_send, inner_take = refs
    me = lax.axis_index("ep")
    step = pl.program_id(0)
    grad_lane, out_lane = [
        Lane(
            labels,
            ep_order,
            first,
            lane_refs[number * (2 * bits - 1) : (number + 1) * (2 * bits - 1)],
            lane_send.at[number],
            lane_get.at[number],
            rows=32,
        )
        for number, first in enumerate((cot_s, rows_s))
    ]

    def unit_copy(e):
        bit = orders[e][0]
        if e < near:
            return mesh_copy(
                send_s.at[e],
                came_ref.at[e],
                unit_send.at[e],
                unit_get.at[e],
                "rep",
                side("rep", bit)[1],
            )
        return pltpu.make_async_copy(send_s.at[e], sent_refs[e - near], unit_send.at[e])

    def inner_copy(d):
        peer = (me + d) % sources
        return mesh_copy(
            inner_s.at[peer],
            inner_got.at[me],
            inner_send.at[d - 1],
            inner_take.at[d - 1],
            "ep",
            peer,
        )

    @pl.when(step == 0)
    def _():
        loads = [
            pltpu.make_async_copy(rows_hbm, rows_s, load_sem.at[0]),
            pltpu.make_async_copy(cot_hbm, cot_s, load_sem.at[1]),
        ]
        for copy in loads:
            copy.start()
        partners = [("ep", (me + d) % sources) for d in range(1, sources)]
        for bit in sorted({order[0] for order in orders[:near]}):
            partners.append(("rep", side("rep", bit)[1]))
        greet(partners)
        for copy in loads:
            copy.wait()

    slots = pl.ds(pl.multiple_of(step * CAP, 16), CAP)
    numbers = lax.broadcasted_iota(jnp.int32, (CAP, rows_dev), 0).astype(jnp.float32)
    rows_in, cots, weights, picks = [], [], [], []
    for s in range(sources):
        rank = rank_ref[s, pl.ds(step, 1), :]
        pick_table = jnp.where(rank == numbers, 1.0, 0.0)
        weights.append(jnp.sum(pick_table * prob_ref[s, pl.ds(step, 1), :], 1, keepdims=True))
        pick_b = pick_table.astype(jnp.bfloat16)
        picks.append(pick_table)
        picks_s[s, slots, :] = pick_b
        rows_in.append(product(pick_b, rows_s[digits(s, bits)]).astype(jnp.bfloat16))
        cots.append(product(pick_b, cot_s[digits(s, bits)]))
    arrived = jnp.concatenate(rows_in, 0)
    weight = jnp.concatenate(weights, 0)
    grad_mix = branch_scale * jnp.concatenate(cots, 0)
    gate_up = gate_up_ref[0]
    down = down_ref[0]
    hidden_units = down.shape[0]
    both = product(arrived, gate_up)
    gate_part = both[:, :hidden_units]
    up_part = both[:, hidden_units:]
    sigmoid_gate = jax.nn.sigmoid(gate_part)
    active = (gate_part * sigmoid_gate * up_part).astype(jnp.bfloat16)
    produced = product(active, down).astype(jnp.bfloat16).astype(jnp.float32)
    inner = jnp.sum(grad_mix * produced, 1, keepdims=True)
    sent_out = (weight * produced).astype(jnp.bfloat16)
    grad_out = (weight * grad_mix).astype(jnp.bfloat16)
    grad_active = dot_nt(grad_out, down)
    grad_down = dot_tn(active, grad_out).astype(jnp.bfloat16)
    grad_gate = grad_active * up_part * sigmoid_gate * (1.0 + gate_part * (1.0 - sigmoid_gate))
    grad_up = grad_active * gate_part * sigmoid_gate
    grad_both = jnp.concatenate([grad_gate, grad_up], 1).astype(jnp.bfloat16)
    grad_gate_up = dot_tn(arrived, grad_both).astype(jnp.bfloat16)
    share = grad_down.shape[1] // copies
    tall = hidden_units // copies

    def put(order, mine):
        bit, *later = order
        for r in range(copies):
            spot = 0
            for b in later:
                spot = 2 * spot + ((r >> b) & 1)
            ref = keep_ref.at[0] if (r >> bit) & 1 == mine else send_s.at[step]
            ref[spot, :share, :] = grad_gate_up[r * share : (r + 1) * share]
            for k in range(copies):
                ref[spot, share : share + tall, k * share : (k + 1) * share] = grad_down[
                    k * tall : (k + 1) * tall, r * share : (r + 1) * share
                ]

    for order in {tuple(order): order for order in orders}.values():
        members = [e for e in range(count) if orders[e] == order]
        here = functools.reduce(jnp.logical_or, [step == e for e in members])
        side_mine, _ = side("rep", order[0])
        for mine in range(2):

            @pl.when(here & (side_mine == mine))
            def _(order=order, mine=mine):
                put(order, mine)

    grad_in = dot_nt(grad_both, gate_up).astype(jnp.bfloat16)
    for s in range(sources):
        part = slice(s * CAP, (s + 1) * CAP)
        out_s[s, slots, :] = sent_out[part]
        grad_s[s, slots, :] = grad_in[part]
        inner_s[s, pl.ds(step, 1), :] = jnp.sum(picks[s] * inner[part], 0, keepdims=True)
    for e in range(count):

        @pl.when(step == e)
        def _(e=e):
            unit_copy(e).start()

    @pl.when(step == count - 1)
    def _():
        for table_of, target, lane in ((grad_s, cot_s, grad_lane), (out_s, rows_s, out_lane)):
            for s in range(sources):
                target[digits(s, bits)] = dot_tn(picks_s[s], table_of[s]).astype(jnp.bfloat16)
            lane.start(0)
        for d in range(1, sources):
            inner_copy(d).start()
        for k in range(bits):
            for lane, total in ((grad_lane, grad_ref), (out_lane, out_ref)):
                lane.add(k, total)
                if k + 1 < bits:
                    lane.start(k + 1)
        inner_got[me] = inner_s[me]
        for d in range(1, sources):
            inner_copy(d).wait_recv()
        inner_ref[...] = inner_got[...]
        for d in range(1, sources):
            inner_copy(d).wait_send()
        grad_lane.finish()
        out_lane.finish()
        for e in range(count):
            unit_copy(e).wait()


def experts(rows, cots, ranks, probs, w_gate_up, w_down, copies, orders, near, labels, ep_order):
    sources, count, rows_dev = ranks.shape
    total, model_width = rows.shape
    hidden_units = w_down.shape[1]
    bits = len(labels)
    tall = model_width // copies + hidden_units // copies
    flat = lambda i: (0, 0)
    cube = lambda i: (0, 0, 0)
    once = pl.Buffered(1)
    anywhere = pl.BlockSpec(memory_space=pl.ANY)
    far = count - near
    shape = (2,) * bits + (rows_dev, model_width)
    piece = (copies // 2, tall, model_width)
    return pl.pallas_call(
        functools.partial(
            experts_kernel,
            sources=sources,
            rows_dev=rows_dev,
            count=count,
            copies=copies,
            orders=orders,
            near=near,
            labels=labels,
            ep_order=ep_order,
        ),
        out_shape=(
            jax.ShapeDtypeStruct((rows_dev, model_width), jnp.float32),
            jax.ShapeDtypeStruct((rows_dev, model_width), jnp.float32),
            jax.ShapeDtypeStruct((sources, count, rows_dev), jnp.float32),
            jax.ShapeDtypeStruct((count,) + piece, jnp.bfloat16),
            jax.ShapeDtypeStruct((near,) + piece, jnp.bfloat16),
        )
        + (jax.ShapeDtypeStruct(piece, jnp.bfloat16),) * far,
        grid=(count,),
        in_specs=[
            anywhere,
            anywhere,
            pl.BlockSpec((sources, count, rows_dev), cube, pipeline_mode=once),
            pl.BlockSpec((sources, count, rows_dev), cube, pipeline_mode=once),
            pl.BlockSpec((1, model_width, 2 * hidden_units), lambda i: (i, 0, 0)),
            pl.BlockSpec((1, hidden_units, model_width), lambda i: (i, 0, 0)),
        ],
        out_specs=[
            pl.BlockSpec((rows_dev, model_width), flat, pipeline_mode=once),
            pl.BlockSpec((rows_dev, model_width), flat, pipeline_mode=once),
            pl.BlockSpec((sources, count, rows_dev), cube, pipeline_mode=once),
            pl.BlockSpec((1,) + piece, lambda i: (i, 0, 0, 0)),
            anywhere,
        ]
        + [anywhere] * far,
        scratch_shapes=[
            pltpu.VMEM(shape, jnp.bfloat16),
            pltpu.VMEM(shape, jnp.bfloat16),
            pltpu.VMEM((sources, count * CAP, rows_dev), jnp.bfloat16),
            pltpu.VMEM((sources, count * CAP, model_width), jnp.bfloat16),
            pltpu.VMEM((sources, count * CAP, model_width), jnp.bfloat16),
            pltpu.VMEM((count,) + piece, jnp.bfloat16),
            pltpu.VMEM((sources, count, rows_dev), jnp.float32),
            pltpu.VMEM((sources, count, rows_dev), jnp.float32),
        ]
        + Lane.scratch(bits, (rows_dev, model_width), jnp.bfloat16) * 2
        + [
            pltpu.SemaphoreType.DMA((2,)),
            pltpu.SemaphoreType.DMA((count,)),
            pltpu.SemaphoreType.DMA((near,)),
            pltpu.SemaphoreType.DMA((2, bits)),
            pltpu.SemaphoreType.DMA((2, bits)),
            pltpu.SemaphoreType.DMA((sources - 1,)),
            pltpu.SemaphoreType.DMA((sources - 1,)),
        ],
        compiler_params=pltpu.CompilerParams(
            collective_id=1, has_side_effects=True, vmem_limit_bytes=67 * 1000 * 1000
        ),
        name="experts",
    )(rows.reshape(shape), cots.reshape(shape), ranks, probs, w_gate_up, w_down)


def on_device(
    tokens,
    segments,
    routes,
    attn_gain,
    w_query,
    w_key,
    w_value,
    w_out,
    mlp_gain,
    w_router,
    w_gate_up,
    w_down,
    cotangent,
    *,
    n_ep,
    n_rep,
):
    inputs = tokens[0]
    own_routes = routes[0]
    grad_output = cotangent[0]
    rows_dev, model_width = inputs.shape
    everyone = ("ep", "rep")
    heads = HEADS // n_rep
    head_width = heads * HEAD_DIM
    shared = max(1, n_rep // KV_HEADS)
    query_width = w_query.shape[1]
    key_width = w_key.shape[1]
    experts_all = w_router.shape[1]
    half_dim = HEAD_DIM // 2

    rep_bits = [("rep", b) for b in range(bits_of(n_rep))]
    ep_bits = [("ep", b) for b in range(bits_of(n_ep))]
    labels = ep_bits[::-1] + rep_bits[::-1]
    rep_down, ep_down = (rep_bits[::-1], ep_bits[::-1])
    full_query, full_rest, pack_ids = gather(
        [w_query, jnp.concatenate([w_key, w_value], 1), segments],
        [
            (labels, rep_down + ep_down),
            (labels, rep_down[:-1] + ep_down[:-1] + rep_bits[:1] + ep_bits[:1]),
            (rep_down, rep_down),
        ],
        labels,
    )
    full_query = full_query.reshape(model_width, -1)
    full_rest = full_rest.reshape(model_width, -1)
    pack_ids = pack_ids.reshape(-1)
    rotated_width = query_width + key_width
    input_width = rotated_width + key_width
    joined = after(jnp.concatenate([w_out, w_router], 1), full_query)
    full = lax.all_gather(joined, everyone, axis=0, tiled=True)
    full_out = full[:, :model_width]
    full_router = full[:, model_width:]

    length = pack_ids.shape[0]
    blocks = length // BLOCK
    offset = lax.axis_index("rep") * rows_dev
    doc_start = jnp.sum((pack_ids[None, :] < pack_ids[:, None]).astype(jnp.int32), 1)
    starts = doc_start.reshape(blocks, 1, BLOCK)
    lows = doc_start[::BLOCK] // BLOCK
    pace = jnp.exp(jnp.arange(half_dim, dtype=jnp.float32) * (-math.log(10000.0) / half_dim))

    def rope_tables(first, begins):
        places = first + jnp.arange(begins.shape[0], dtype=jnp.int32)
        angles = (places - begins).astype(jnp.float32)[:, None] * pace[None, :]
        cosine = jnp.cos(angles)
        sine = jnp.sin(angles)
        return (jnp.concatenate([cosine, cosine], 1), jnp.concatenate([-sine, sine], 1))

    own_starts = jnp.sum((pack_ids[None, :] < segments[0][:, None]).astype(jnp.int32), 1)
    own_cosine, own_sine = rope_tables(offset, own_starts)

    normed, factor_one = rms_norm(inputs, attn_gain)
    normed_b = normed.astype(jnp.bfloat16)
    mixed_in = jnp.concatenate([product(normed_b, full_query), product(normed_b, full_rest)], 1)
    turn = mixed_in[:, :rotated_width]
    times = rotated_width // HEAD_DIM
    turned = turn * jnp.tile(own_cosine, (1, times)) + swap_halves(turn) * jnp.tile(
        own_sine, (1, times)
    )
    turned_b = turned.astype(jnp.bfloat16)
    value_b = mixed_in[:, rotated_width:].astype(jnp.bfloat16)
    query_part = turned_b[:, :query_width].reshape(rows_dev, n_rep, head_width)
    key_part = turned_b[:, query_width:].reshape(rows_dev, KV_HEADS, HEAD_DIM)
    value_part = value_b.reshape(rows_dev, KV_HEADS, HEAD_DIM)
    if shared > 1:
        key_part = jnp.repeat(key_part, shared, 1)
        value_part = jnp.repeat(value_part, shared, 1)
    sending = jnp.concatenate([query_part, key_part, value_part], 2).transpose(1, 0, 2)
    head_rows = lax.all_to_all(sending, "rep", split_axis=0, concat_axis=0, tiled=True)
    head_rows = head_rows.reshape(length, head_width + 2 * HEAD_DIM)
    cosine, sine = rope_tables(0, after(doc_start, sending))
    head_rows = after(head_rows, cosine, sine)
    mixed, mixed_out, totals = attend_forward(head_rows, starts, lows, heads)
    mixed_rows = lax.all_to_all(
        mixed.reshape(n_rep, rows_dev, head_width), "rep", split_axis=0, concat_axis=0, tiled=True
    )
    mixed_rows = mixed_rows.transpose(1, 0, 2).reshape(rows_dev, query_width)
    hidden = inputs + branch_scale * product(mixed_rows, full_out)

    normed_two, factor_two = rms_norm(hidden, mlp_gain)
    normed_two_b = normed_two.astype(jnp.bfloat16)
    router_f = full_router.astype(jnp.float32)
    logits = product(normed_two_b, full_router)
    numbers = jnp.arange(experts_all, dtype=jnp.int32)
    onehot = jnp.sum((own_routes[:, :, None] == numbers).astype(jnp.float32), 1)
    chosen = onehot > 0.5
    peak = jnp.max(jnp.where(chosen, logits, far_below), 1, keepdims=True)
    raised = jnp.where(chosen, jnp.exp(jnp.minimum(logits - peak, 0.0)), 0.0)
    probs = raised / jnp.sum(raised, 1, keepdims=True)
    before = (
        lax.broadcasted_iota(jnp.int32, (rows_dev, rows_dev), 0)
        > lax.broadcasted_iota(jnp.int32, (rows_dev, rows_dev), 1)
    ).astype(jnp.bfloat16)
    rank = product(before, onehot.astype(jnp.bfloat16))
    kept = chosen & (rank < CAP)
    rank_sent = jnp.where(kept, rank, -1.0).T
    probs_sent = probs.T
    both_sent = jnp.concatenate(
        [rank_sent.reshape(n_ep, -1, rows_dev), probs_sent.reshape(n_ep, -1, rows_dev)], 1
    )
    both_all = lax.all_to_all(both_sent, "ep", split_axis=0, concat_axis=0, tiled=True)
    ranks = both_all[:, : experts_all // n_ep]
    prob_all = both_all[:, experts_all // n_ep :]
    expert_rows = lax.all_gather(normed_two_b, "ep", axis=0, tiled=True)
    expert_cots = lax.all_gather(grad_output.astype(jnp.bfloat16), "ep", axis=0, tiled=True)
    count = experts_all // n_ep
    near = count * 3 // 4
    kinds = [k % 2 for k in range(near)] + [0] * (count - near)
    leads = [0, len(rep_bits) - 2]
    orders = [
        [leads[kind]] + [b for b in range(len(rep_bits)) if b != leads[kind]] for kind in kinds
    ]
    out_sum, grad_sum, inner_back, grad_keep, came_near, *sent = experts(
        expert_rows,
        expert_cots,
        ranks,
        prob_all,
        w_gate_up,
        w_down,
        n_rep,
        orders,
        near,
        ep_bits[::-1],
        ep_bits,
    )
    rep_orders = [[("rep", b) for b in order] for order in orders]
    early = list(range(0, near, 2))
    early = early[:2]

    def halves(left, right, label, e=None):
        mine, _ = side(*label)
        half = left.shape[-3] // 2

        def total(which):
            parts = []
            for stack in (left, right):
                start = [jnp.int32(0)] * stack.ndim
                start[-3] = (which * half).astype(jnp.int32)
                size = stack.shape[-3:]
                if e is not None:
                    start[0] = jnp.int32(e)
                part = lax.dynamic_slice(
                    stack, start, (1,) * (stack.ndim - 3) + (half,) + size[1:]
                )
                parts.append(part.reshape((half,) + size[1:]).astype(jnp.float32))
            return (parts[0] + parts[1]).astype(jnp.bfloat16)

        return (total(1 - mine), total(mine))

    output = hidden + branch_scale * out_sum
    grad_probs = inner_back.reshape(experts_all, rows_dev).T
    grad_logits = probs * (grad_probs - jnp.sum(grad_probs * probs, -1, keepdims=True))
    normed_two_f = normed_two_b.astype(jnp.float32)
    grad_router = jnp.dot(normed_two_f.T, grad_logits, precision=lax.Precision.HIGHEST)
    grad_normed_two = grad_sum + jnp.dot(
        grad_logits, router_f.T, precision=lax.Precision.HIGHEST
    )
    grad_hidden_norm, grad_mlp_gain = norm_back(grad_normed_two, hidden, factor_two, mlp_gain)
    grad_hidden = grad_output + grad_hidden_norm
    grad_attn = (branch_scale * grad_hidden).astype(jnp.bfloat16)
    grad_out_w = dot_tn(mixed_rows, grad_attn)
    grad_mixed = dot_nt(grad_attn, full_out).astype(jnp.bfloat16)
    grad_heads = lax.all_to_all(
        grad_mixed.reshape(rows_dev, n_rep, head_width).transpose(1, 0, 2),
        "rep",
        split_axis=0,
        concat_axis=0,
        tiled=True,
    ).reshape(length, head_width)
    beside = [swap(after(sent[0], grad_heads), *rep_orders[near][0])]
    second = {}
    for e in early:
        give, own = halves(grad_keep, came_near, rep_orders[e][1], e)
        second[e] = (own, swap(after(give, grad_heads), *rep_orders[e][1]))
        beside.append(second[e][1])
    returning = attend_backward(
        head_rows, grad_heads, mixed_out, totals, starts, lows, cosine, sine, heads
    )
    returning = after(returning, *beside)
    returned = lax.all_to_all(
        returning.reshape(n_rep, rows_dev, head_width + 2 * HEAD_DIM),
        "rep",
        split_axis=0,
        concat_axis=0,
        tiled=True,
    ).transpose(1, 0, 2)
    parts = [grad_keep, came_near]
    steps_of = {e: ((0, e), (1, e), 0) for e in range(near)}

    def put_by(e, own, got, skip):
        steps_of[e] = ((len(parts), 0), (len(parts) + 1, 0), skip)
        parts.extend([own[None], got[None]])

    for k, half in enumerate(sent):
        steps_of[near + k] = ((0, near + k), (len(parts), 0), 0 if k == 0 else -1)
        parts.append((beside[0] if k == 0 else half)[None])
    for e in early[1:]:
        put_by(e, *second[e], 1)
    for e in early[:1]:
        give, own = halves(*second[e], rep_orders[e][2])
        put_by(e, own, swap(after(give, returned), *rep_orders[e][2]), 2)
    units = [
        (e, steps_of[e][:2], rep_orders[e], steps_of[e][2])
        for e in sorted(range(count), key=lambda e: (e < near, e > 1 and e % 2, e))
    ]
    grad_query_rows = returned[:, :, :head_width].reshape(rows_dev, query_width)
    key_back = returned[:, :, head_width : head_width + HEAD_DIM]
    value_back = returned[:, :, head_width + HEAD_DIM :]
    if shared > 1:
        key_back = jnp.sum(
            key_back.reshape(rows_dev, KV_HEADS, shared, HEAD_DIM).astype(jnp.float32), 2
        ).astype(jnp.bfloat16)
        value_back = jnp.sum(
            value_back.reshape(rows_dev, KV_HEADS, shared, HEAD_DIM).astype(jnp.float32), 2
        ).astype(jnp.bfloat16)
    grad_in_rows = jnp.concatenate(
        [
            grad_query_rows,
            key_back.reshape(rows_dev, key_width),
            value_back.reshape(rows_dev, key_width),
        ],
        1,
    )
    grad_w_in = dot_tn(normed_b, grad_in_rows)
    grad_normed = dot_nt(grad_in_rows[:, :query_width], full_query) + dot_nt(
        grad_in_rows[:, query_width:], full_rest
    )
    grad_inputs_norm, grad_attn_gain = norm_back(grad_normed, inputs, factor_one, attn_gain)
    grad_inputs = grad_hidden + grad_inputs_norm
    everything = n_ep * n_rep
    gains = jnp.concatenate(
        [grad_attn_gain.reshape(everything, -1), grad_mlp_gain.reshape(everything, -1)], 1
    )
    shape = (2,) * len(labels)
    grads = [grad.astype(jnp.bfloat16) for grad in (grad_w_in, grad_out_w, grad_router)]
    lanes = [grad.reshape(shape + (-1, grad.shape[1])) for grad in grads]
    lanes.append(gains.reshape(shape + (1, -1)))
    expert_up, expert_down, weights, weights_out, weights_router, gains, _ = reduce_rest(
        parts,
        lanes,
        units,
        labels,
        ep_bits + rep_bits,
        model_width // n_rep,
    )
    gains = gains[0]
    part = model_width // everything
    return (
        output[None],
        grad_inputs[None],
        gains[:part],
        weights[:, :query_width],
        weights[:, query_width:rotated_width],
        weights[:, rotated_width:input_width],
        weights_out,
        gains[part:],
        weights_router,
        expert_up,
        expert_down,
    )


def solution(mesh):
    placed = (
        P("ep", "rep", None),
        P("ep", "rep"),
        P("ep", "rep", None),
        P(),
        P(("ep", "rep"), None),
        P(("ep", "rep"), None),
        P(("ep", "rep"), None),
        P(("ep", "rep"), None),
        P(),
        P(("ep", "rep"), None),
        P("ep", None, None),
        P("ep", None, None),
        P("ep", "rep", None),
    )
    return jax.shard_map(
        functools.partial(on_device, n_ep=mesh.shape["ep"], n_rep=mesh.shape["rep"]),
        mesh=mesh,
        in_specs=placed,
        out_specs=(
            P("ep", "rep", None),
            P("ep", "rep", None),
            P(("ep", "rep")),
            P(("ep", "rep"), None),
            P(("ep", "rep"), None),
            P(("ep", "rep"), None),
            P(("ep", "rep"), None),
            P(("ep", "rep")),
            P(("ep", "rep"), None),
            P("ep", "rep", None),
            P("ep", None, "rep"),
        ),
        check_vma=False,
    )
```

```python
import functools
import math

import jax
import jax.numpy as jnp
from jax import lax
from jax.experimental import pallas as pl
from jax.experimental.pallas import tpu as pltpu
from jax.sharding import PartitionSpec as P

HEADS = 16
KV_HEADS = 8
HEAD_DIM = 64
CAP = 80
BLOCK = 256

epsilon = 1e-06
score_scale = 0.015625
branch_scale = 0.22
far_below = -1e30

NT = (((1,), (1,)), ((), ()))
TN = (((0,), (0,)), ((), ()))


def product(left, right):
    return jnp.dot(left, right, preferred_element_type=jnp.float32)


def dot_nt(left, right):
    return lax.dot_general(left, right, NT, preferred_element_type=jnp.float32)


def dot_tn(left, right):
    return lax.dot_general(left, right, TN, preferred_element_type=jnp.float32)


def rms_norm(values, gain):
    factor = lax.rsqrt(jnp.mean(values * values, -1, keepdims=True) + epsilon)
    return (values * factor * gain, factor)


def norm_back(grad_normed, values, factor, gain):
    scaled = grad_normed * gain
    gain_part = jnp.sum(grad_normed * values * factor, 0)
    inner_sum = jnp.mean(scaled * values, -1, keepdims=True)
    return (factor * scaled - values * (factor * factor * factor) * inner_sum, gain_part)


def swap_halves(values):
    count, width = values.shape
    half_dim = HEAD_DIM // 2
    lane = lax.broadcasted_iota(jnp.int32, values.shape, 1)
    return jnp.where(
        lane % HEAD_DIM < half_dim,
        jnp.roll(values, -half_dim, 1),
        jnp.roll(values, half_dim, 1),
    )


def attend_forward_kernel(
    low_ref, rows_ref, start_ref, mixed_ref, out_ref, total_ref, key_s, value_s, *, heads
):
    step = pl.program_id(0)
    width = heads * HEAD_DIM

    @pl.when(step == 0)
    def _():
        key_s[...] = rows_ref[:, width : width + HEAD_DIM]
        value_s[...] = rows_ref[:, width + HEAD_DIM : width + 2 * HEAD_DIM]

    block_rows = rows_ref[pl.ds(pl.multiple_of(step * BLOCK, BLOCK), BLOCK), :]
    queries = [
        block_rows[:, h * HEAD_DIM : (h + 1) * HEAD_DIM] * jnp.bfloat16(score_scale)
        for h in range(heads)
    ]
    starts = start_ref[0]
    at = step * BLOCK + lax.broadcasted_iota(jnp.int32, (1, BLOCK), 1)

    def one(j, carry):
        rows = pl.ds(pl.multiple_of(j * BLOCK, BLOCK), BLOCK)
        key_block = key_s[rows, :]
        value_block = value_s[rows, :]
        place = j * BLOCK + lax.broadcasted_iota(jnp.int32, (BLOCK, BLOCK), 0)
        allowed = (place >= starts) & (place <= at)
        result = []
        for h in range(heads):
            peak, total, mixed = carry[h]
            scores = jnp.where(allowed, dot_nt(key_block, queries[h]), far_below)
            new_peak = jnp.maximum(peak, jnp.max(scores, 0, keepdims=True))
            fade = jnp.exp(peak - new_peak)
            raised = jnp.exp(scores - new_peak)
            total = fade * total + jnp.sum(raised, 0, keepdims=True)
            mixed = fade * mixed + dot_tn(value_block, raised.astype(jnp.bfloat16))
            result.append((new_peak, total, mixed))
        return tuple(result)

    first = tuple(
        (
            jnp.full((1, BLOCK), far_below, jnp.float32),
            jnp.zeros((1, BLOCK), jnp.float32),
            jnp.zeros((HEAD_DIM, BLOCK), jnp.float32),
        )
        for _ in range(heads)
    )
    done = lax.fori_loop(low_ref[step], step + 1, one, first)
    for h in range(heads):
        peak, total, mixed = done[h]
        mixed = mixed / total
        out_ref[h * HEAD_DIM : (h + 1) * HEAD_DIM, :] = mixed
        total_ref[0, h : h + 1, :] = peak + jnp.log(total)
        mixed_ref[:, h * HEAD_DIM : (h + 1) * HEAD_DIM] = mixed.T.astype(jnp.bfloat16)


def attend_forward(rows, starts, lows, heads):
    length, width = rows.shape
    blocks = length // BLOCK
    whole = lambda i, low: (0, 0)
    return pl.pallas_call(
        functools.partial(attend_forward_kernel, heads=heads),
        out_shape=(
            jax.ShapeDtypeStruct((length, heads * HEAD_DIM), jnp.bfloat16),
            jax.ShapeDtypeStruct((heads * HEAD_DIM, length), jnp.float32),
            jax.ShapeDtypeStruct((blocks, heads, BLOCK), jnp.float32),
        ),
        grid_spec=pltpu.PrefetchScalarGridSpec(
            num_scalar_prefetch=1,
            grid=(blocks,),
            in_specs=[
                pl.BlockSpec((length, width), whole),
                pl.BlockSpec((1, 1, BLOCK), lambda i, low: (i, 0, 0)),
            ],
            out_specs=[
                pl.BlockSpec((BLOCK, heads * HEAD_DIM), lambda i, low: (i, 0)),
                pl.BlockSpec((heads * HEAD_DIM, BLOCK), lambda i, low: (0, i)),
                pl.BlockSpec((1, heads, BLOCK), lambda i, low: (i, 0, 0)),
            ],
            scratch_shapes=[
                pltpu.VMEM((length, HEAD_DIM), jnp.bfloat16),
                pltpu.VMEM((length, HEAD_DIM), jnp.bfloat16),
            ],
        ),
        name="attend_forward",
    )(lows, rows, starts)


def attend_backward_kernel(
    low_ref,
    rows_ref,
    grad_ref,
    out_ref,
    total_ref,
    start_ref,
    cosine_ref,
    sine_ref,
    back_ref,
    key_s,
    value_s,
    grad_query_s,
    grad_key_s,
    grad_value_s,
    *,
    heads,
    blocks,
):
    step = pl.program_id(0)
    width = heads * HEAD_DIM

    @pl.when(step == 0)
    def _():
        key_s[...] = rows_ref[:, width : width + HEAD_DIM]
        value_s[...] = rows_ref[:, width + HEAD_DIM : width + 2 * HEAD_DIM]
        grad_key_s[...] = jnp.zeros_like(grad_key_s)
        grad_value_s[...] = jnp.zeros_like(grad_value_s)

    own = pl.ds(pl.multiple_of(step * BLOCK, BLOCK), BLOCK)
    block_rows = rows_ref[own, :]
    grads_all = grad_ref[...]
    starts = start_ref[0]
    at = step * BLOCK + lax.broadcasted_iota(jnp.int32, (1, BLOCK), 1)
    queries, scaled, grads, inners, totals = [], [], [], [], []
    for h in range(heads):
        span = slice(h * HEAD_DIM, (h + 1) * HEAD_DIM)
        queries.append(block_rows[:, span])
        scaled.append(block_rows[:, span] * jnp.bfloat16(score_scale))
        grads.append(grads_all[:, span])
        turned = grads_all[:, span].astype(jnp.float32).T
        inners.append(jnp.sum(turned * out_ref[span, :], 0, keepdims=True))
        totals.append(total_ref[0, h : h + 1, :])

    def one(j, carry):
        rows = pl.ds(pl.multiple_of(j * BLOCK, BLOCK), BLOCK)
        key_block = key_s[rows, :]
        value_block = value_s[rows, :]
        place = j * BLOCK + lax.broadcasted_iota(jnp.int32, (BLOCK, BLOCK), 0)
        allowed = (place >= starts) & (place <= at)
        result = []
        key_sum = grad_key_s[rows, :]
        value_sum = grad_value_s[rows, :]
        for h in range(heads):
            scores = jnp.where(allowed, dot_nt(key_block, scaled[h]), far_below)
            prob = jnp.exp(scores - totals[h])
            grad_prob = dot_nt(value_block, grads[h])
            grad_scores = (prob * (grad_prob - inners[h]) * score_scale).astype(jnp.bfloat16)
            value_sum = value_sum + product(prob.astype(jnp.bfloat16), grads[h])
            key_sum = key_sum + product(grad_scores, queries[h])
            result.append(carry[h] + dot_tn(grad_scores, key_block))
        grad_key_s[rows, :] = key_sum
        grad_value_s[rows, :] = value_sum
        return tuple(result)

    first = tuple(jnp.zeros((BLOCK, HEAD_DIM), jnp.float32) for _ in range(heads))
    done = lax.fori_loop(low_ref[step], step + 1, one, first)
    for h in range(heads):
        grad_query_s[own, h * HEAD_DIM : (h + 1) * HEAD_DIM] = done[h]

    @pl.when(step == blocks - 1)
    def _():
        def turn(j, carry):
            rows = pl.ds(pl.multiple_of(j * BLOCK, BLOCK), BLOCK)
            cosine = cosine_ref[rows, :]
            sine = sine_ref[rows, :]
            parts = [
                grad_query_s[rows, h * HEAD_DIM : (h + 1) * HEAD_DIM] for h in range(heads)
            ]
            parts.append(grad_key_s[rows, :])
            half = HEAD_DIM // 2
            turned = [
                part * cosine - jnp.concatenate([part[:, half:], part[:, :half]], 1) * sine
                for part in parts
            ]
            turned.append(grad_value_s[rows, :])
            back_ref[rows, :] = jnp.concatenate(turned, 1).astype(jnp.bfloat16)
            return carry

        lax.fori_loop(0, blocks, turn, 0)


def attend_backward(rows, grads, outs, totals, starts, lows, cosine, sine, heads):
    length, width = rows.shape
    blocks = length // BLOCK
    whole = lambda i, low: (0, 0)
    once = pl.Buffered(1)
    return pl.pallas_call(
        functools.partial(attend_backward_kernel, heads=heads, blocks=blocks),
        out_shape=jax.ShapeDtypeStruct((length, width), jnp.bfloat16),
        grid_spec=pltpu.PrefetchScalarGridSpec(
            num_scalar_prefetch=1,
            grid=(blocks,),
            in_specs=[
                pl.BlockSpec((length, width), whole),
                pl.BlockSpec((BLOCK, heads * HEAD_DIM), lambda i, low: (i, 0)),
                pl.BlockSpec((heads * HEAD_DIM, BLOCK), lambda i, low: (0, i)),
                pl.BlockSpec((1, heads, BLOCK), lambda i, low: (i, 0, 0)),
                pl.BlockSpec((1, 1, BLOCK), lambda i, low: (i, 0, 0)),
                pl.BlockSpec((length, HEAD_DIM), whole, pipeline_mode=once),
                pl.BlockSpec((length, HEAD_DIM), whole, pipeline_mode=once),
            ],
            out_specs=pl.BlockSpec((length, width), whole),
            scratch_shapes=[
                pltpu.VMEM((length, HEAD_DIM), jnp.bfloat16),
                pltpu.VMEM((length, HEAD_DIM), jnp.bfloat16),
                pltpu.VMEM((length, heads * HEAD_DIM), jnp.float32),
                pltpu.VMEM((length, HEAD_DIM), jnp.float32),
                pltpu.VMEM((length, HEAD_DIM), jnp.float32),
            ],
        ),
        name="attend_backward",
    )(lows, rows, grads, outs, totals, starts, cosine, sine)


def after(value, *others):
    return lax.optimization_barrier((value, *others))[0]


def bits_of(size):
    return max(size.bit_length() - 1, 0)


def swap(sent, axis, bit):
    size = lax.axis_size(axis)
    return lax.ppermute(sent, axis, [(i, i ^ (1 << bit)) for i in range(size)])


def side(axis, bit):
    index = lax.axis_index(axis)
    mine = (index // (1 << bit)) % 2
    return (mine, index + (1 - 2 * mine) * (1 << bit))


def pick(dim, index):
    return (slice(None),) * dim + (index,)


def digits(number, count):
    return tuple((number // (1 << (count - 1 - k))) % 2 for k in range(count))


def mesh_copy(source, target, sends, gets, axis, partner):
    return pltpu.make_async_remote_copy(
        src_ref=source,
        dst_ref=target,
        send_sem=sends,
        recv_sem=gets,
        device_id={axis: partner},
        device_id_type=pl.DeviceIdType.MESH,
    )


def greet(partners):
    barrier = pltpu.get_barrier_semaphore()
    for axis, partner in partners:
        pl.semaphore_signal(
            barrier, inc=1, device_id={axis: partner}, device_id_type=pl.DeviceIdType.MESH
        )
    pl.semaphore_wait(barrier, len(partners))


class Lane:
    def __init__(self, labels, order, first, refs, sends, gets, rows=None):
        bits = len(labels)
        self.order, self.first, self.sends, self.gets = (order, first, sends, gets)
        self.sums, self.got = (refs[: bits - 1], refs[bits - 1 : 2 * bits - 1])
        self.labels = [list(labels)]
        for label in order:
            self.labels.append([other for other in self.labels[-1] if other != label])
        self.rows = rows

    @staticmethod
    def scratch(bits, tail, dtype):
        shapes = [pltpu.VMEM((2,) * (bits - 1 - k) + tail, dtype) for k in range(bits)]
        return shapes[:-1] + shapes

    def source(self, k):
        return self.first if k == 0 else self.sums[k - 1]

    def copy(self, k):
        axis, bit = self.order[k]
        mine, partner = side(axis, bit)
        dim = self.labels[k].index((axis, bit))
        return mesh_copy(
            self.source(k).at[pick(dim, 1 - mine)],
            self.got[k],
            self.sends.at[k],
            self.gets.at[k],
            axis,
            partner,
        )

    def start(self, k):
        self.copy(k).start()

    def add(self, k, out=None):
        axis, bit = self.order[k]
        mine, _ = side(axis, bit)
        dim = self.labels[k].index((axis, bit))
        left = len(self.order) - 1 - k
        self.copy(k).wait_recv()
        source, got = (self.source(k), self.got[k])
        target = out if left == 0 else self.sums[k]
        height = got.shape[left]
        rows = self.rows or height
        blocks = height // rows

        def body(i, carry):
            at = digits(i // blocks, left)
            own = pl.ds(pl.multiple_of((i % blocks) * rows, rows), rows)
            if blocks == 1:
                own = slice(None)
            here = at[:dim] + (mine,) + at[dim:]
            total = source[here + (own,)].astype(jnp.float32) + got[at + (own,)].astype(
                jnp.float32
            )
            target[at + (own,)] = total.astype(target.dtype)
            return carry

        lax.fori_loop(0, blocks << left, body, 0)

    def finish(self):
        for k in range(len(self.order)):
            self.copy(k).wait_send()


def gather_kernel(*refs, lanes, partners):
    count = len(lanes)
    ins, outs = (refs[:count], refs[count : 2 * count])
    sends, gets = refs[2 * count :]
    greet([(axis, side(axis, bit)[1]) for axis, bit in partners])

    def copy(number, k):
        labels, order = lanes[number]
        region = tuple(
            slice(None) if label in order[:k] else side(*label)[0] for label in labels
        )
        target = outs[number].at[region]
        axis, bit = order[k]
        return mesh_copy(
            ins[number] if k == 0 else target,
            target,
            sends.at[number, k],
            gets.at[number, k],
            axis,
            side(axis, bit)[1],
        )

    most = max(len(order) for _, order in lanes)
    for k in range(most + 1):
        for number, (labels, order) in enumerate(lanes):
            if 0 < k <= len(order):
                copy(number, k - 1).wait_recv()
            if k < len(order):
                copy(number, k).start()
            if k == 0:
                outs[number][tuple(side(*label)[0] for label in labels)] = ins[number][...]
    for number, (_, order) in enumerate(lanes):
        for k in range(len(order)):
            copy(number, k).wait_send()


def gather(arrays, lanes, partners):
    vmem = pl.BlockSpec(memory_space=pltpu.VMEM)
    most = max(len(order) for _, order in lanes)
    return pl.pallas_call(
        functools.partial(gather_kernel, lanes=lanes, partners=partners),
        out_shape=[
            jax.ShapeDtypeStruct((2,) * len(order) + array.shape, array.dtype)
            for array, (_, order) in zip(arrays, lanes)
        ],
        in_specs=[vmem] * len(arrays),
        out_specs=[vmem] * len(arrays),
        scratch_shapes=[
            pltpu.SemaphoreType.DMA((len(arrays), most)),
            pltpu.SemaphoreType.DMA((len(arrays), most)),
        ],
        compiler_params=pltpu.CompilerParams(collective_id=2, has_side_effects=True),
        name="gather",
    )(*arrays)


def reduce_kernel(*refs, units, n_parts, n_lanes, labels, weight_order, share):
    part_refs, refs = (refs[:n_parts], refs[n_parts:])
    lane_ins, (up_ref, down_ref, *refs) = (refs[:n_lanes], refs[n_lanes:])
    lane_outs, (late_ref, *refs) = (refs[:n_lanes], refs[n_lanes:])
    steps = len(units[0][2]) - 1
    sends, keeps, gets = ([], [], [])
    for _ in range(steps):
        sends.append(refs[0])
        keeps.append(refs[1])
        gets.append(refs[2])
        refs = refs[3:]
    bits = len(labels)
    each = 2 * bits - 1
    lane_refs, refs = (refs[: n_lanes * each], refs[n_lanes * each :])
    load_keep, load_came, load_sem, unit_send, unit_get, lane_send, lane_get, late_sem = refs
    lanes = [
        Lane(
            labels,
            weight_order,
            first,
            lane_refs[number * each : (number + 1) * each],
            lane_send.at[number],
            lane_get.at[number],
        )
        for number, first in enumerate(lane_ins)
    ]
    _, spots, tall, width = load_keep.shape
    rows = 32 if tall % 32 == 0 else tall
    blocks = tall // rows

    greet([(axis, side(axis, bit)[1]) for axis, bit in weight_order])

    def lane_start(k):
        for lane in lanes:
            lane.start(k)

    def lane_add(k):
        for lane, out in zip(lanes, lane_outs):
            lane.add(k, out)

    lane_start(0)

    late = [n for n, unit in enumerate(units) if unit[3] < 0]
    half_way = [n for n, unit in enumerate(units) if 0 < unit[3] < steps]
    fresh = [n for n, unit in enumerate(units) if unit[3] == 0]
    done = [n for n, unit in enumerate(units) if unit[3] == steps]
    sequence = half_way + fresh + late + done

    def late_copy(n):
        _, ((_, _), (which, place)), order, _ = units[n]
        axis, bit = order[0]
        return mesh_copy(
            part_refs[which].at[place],
            late_ref.at[late.index(n)],
            late_sem.at[0, late.index(n)],
            late_sem.at[1, late.index(n)],
            axis,
            side(axis, bit)[1],
        )

    def loads(turn):
        n = sequence[turn]
        _, parts, _, skip = units[n]
        slot = turn % 2
        size = spots >> max(skip, 0)
        sources = [part_refs[which].at[place] for which, place in parts]
        if skip < 0:
            sources[1] = late_ref.at[late.index(n)]
        return [
            pltpu.make_async_copy(
                source, buffer.at[slot, pl.ds(0, size)], load_sem.at[slot, number]
            )
            for number, (source, buffer) in enumerate(zip(sources, (load_keep, load_came)))
        ]

    def load(turn):
        if turn < len(units) and units[sequence[turn]][3] >= 0:
            for copy in loads(turn):
                copy.start()

    def unit_copy(unit, order, k):
        axis, bit = order[k + 1]
        return mesh_copy(
            sends[k].at[unit],
            gets[k].at[unit],
            unit_send.at[unit, k],
            unit_get.at[unit, k],
            axis,
            side(axis, bit)[1],
        )

    def unit_add(unit, order, k, left, right):
        mine, _ = side(*order[k + 1])
        half = spots >> (k + 1)

        def fill(target, which):
            def body(i, carry):
                piece = i // blocks
                own = pl.ds(pl.multiple_of((i % blocks) * rows, rows), rows)
                total = left[which * half + piece, own, :].astype(jnp.float32) + right[
                    which * half + piece, own, :
                ].astype(jnp.float32)
                target[unit, piece, own, :] = total.astype(jnp.bfloat16)
                return carry

            lax.fori_loop(0, half * blocks, body, 0)

        fill(sends[k], 1 - mine)
        unit_copy(unit, order, k).start()
        fill(keeps[k], mine)

    def begin_unit(n):
        unit, _, order, skip = units[n]
        turn = sequence.index(n)
        if skip < 0:
            late_copy(n).wait_recv()
            for copy in loads(turn):
                copy.start()
        for copy in loads(turn):
            copy.wait()
        left, right = (load_keep.at[turn % 2], load_came.at[turn % 2])
        if skip < steps:
            unit_add(unit, order, max(skip, 0), left, right)
        else:
            give(unit, left[0].astype(jnp.float32) + right[0].astype(jnp.float32))
        load(turn + 2)

    def next_unit(n, k):
        unit, _, order, _ = units[n]
        unit_copy(unit, order, k - 1).wait_recv()
        unit_add(unit, order, k, keeps[k - 1].at[unit], gets[k - 1].at[unit])

    def end_unit(n):
        unit, _, order, _ = units[n]
        unit_copy(unit, order, steps - 1).wait_recv()
        give(unit, keeps[-1][unit, 0].astype(jnp.float32) + gets[-1][unit, 0].astype(jnp.float32))

    def give(unit, total):
        up_ref[unit] = total[:share]
        pieces = width // share
        rest = tall - share
        for p in range(pieces):
            down_ref[unit, p * rest : (p + 1) * rest, :] = total[
                share:, p * share : (p + 1) * share
            ]

    load(0)
    load(1)
    def late_start():
        for n in late:
            late_copy(n).start()

    def lane_turn(k):
        lane_add(k)
        if k + 1 < bits:
            lane_start(k + 1)

    work = [(begin_unit, n) for n in half_way + fresh[:1]] + [(lane_turn, 0)]
    work += [(begin_unit, n) for n in fresh[1:2]] + [(late_start,)]
    work += [(begin_unit, n) for n in fresh[2:]]
    for k in range(1, steps):
        onward = [n for n in half_way if units[n][3] < k] + fresh
        work += [(next_unit, n, k) for n in onward[:3]]
        if k == 1:
            work += [(lane_turn, 1)] + [(begin_unit, n) for n in late]
        work += [(next_unit, n, k) for n in onward[3:4]]
        work += [(next_unit, n, k) for n in late]
        work += [(next_unit, n, k) for n in onward[4:]]
    work += [(begin_unit, n) for n in done]
    work += [(end_unit, n) for n in half_way + fresh[:3] + late] + [(lane_turn, 2)]
    work += [(end_unit, n) for n in fresh[3:4]] + [(lane_turn, 3)]
    work += [(end_unit, n) for n in fresh[4:]]
    work += [(lane_turn, k) for k in range(4, bits)]
    for job, *arguments in work:
        job(*arguments)
    for unit, _, order, skip in units:
        for k in range(max(skip, 0), steps):
            unit_copy(unit, order, k).wait_send()
    for n in late:
        late_copy(n).wait_send()
    for lane in lanes:
        lane.finish()


def reduce_rest(parts, lanes, units, labels, weight_order, share):
    _, spots, tall, width = parts[0].shape
    count = len(units)
    bits = len(labels)
    steps = len(units[0][2]) - 1
    late = max(1, len([unit for unit in units if unit[3] < 0]))
    anywhere = pl.BlockSpec(memory_space=pl.ANY)
    vmem = pl.BlockSpec(memory_space=pltpu.VMEM)
    scratch = []
    for k in range(steps):
        scratch += [pltpu.VMEM((count, spots >> (k + 1), tall, width), jnp.bfloat16)] * 3
    for lane in lanes:
        scratch += Lane.scratch(bits, lane.shape[bits:], lane.dtype)
    scratch += [
        pltpu.VMEM((2, spots, tall, width), jnp.bfloat16),
        pltpu.VMEM((2, spots, tall, width), jnp.bfloat16),
        pltpu.SemaphoreType.DMA((2, 2)),
        pltpu.SemaphoreType.DMA((count, steps)),
        pltpu.SemaphoreType.DMA((count, steps)),
        pltpu.SemaphoreType.DMA((len(lanes), bits)),
        pltpu.SemaphoreType.DMA((len(lanes), bits)),
        pltpu.SemaphoreType.DMA((2, late)),
    ]
    return pl.pallas_call(
        functools.partial(
            reduce_kernel,
            units=units,
            n_parts=len(parts),
            n_lanes=len(lanes),
            labels=labels,
            weight_order=weight_order,
            share=share,
        ),
        out_shape=(
            jax.ShapeDtypeStruct((count, share, width), jnp.float32),
            jax.ShapeDtypeStruct((count, (tall - share) * (width // share), share), jnp.float32),
        )
        + tuple(jax.ShapeDtypeStruct(lane.shape[bits:], jnp.float32) for lane in lanes)
        + (jax.ShapeDtypeStruct((late, spots, tall, width), jnp.bfloat16),),
        in_specs=[anywhere] * len(parts) + [vmem] * len(lanes),
        out_specs=[vmem] * (2 + len(lanes)) + [anywhere],
        scratch_shapes=scratch,
        compiler_params=pltpu.CompilerParams(
            collective_id=0, has_side_effects=True, vmem_limit_bytes=67 * 1000 * 1000
        ),
        name="reduce_rest",
    )(*parts, *lanes)


def experts_kernel(
    *refs, sources, rows_dev, count, copies, orders, near, labels, ep_order
):
    rows_hbm, cot_hbm, rank_ref, prob_ref, gate_up_ref, down_ref, *refs = refs
    out_ref, grad_ref, inner_ref, keep_ref, came_ref, *refs = refs
    far = count - near
    sent_refs, refs = (refs[:far], refs[far:])
    rows_s, cot_s, picks_s, out_s, grad_s, send_s, inner_s, inner_got, *refs = refs
    bits = len(labels)
    lane_refs, refs = (refs[: 2 * (2 * bits - 1)], refs[2 * (2 * bits - 1) :])
    load_sem, unit_send, unit_get, lane_send, lane_get, inner_send, inner_take = refs
    me = lax.axis_index("ep")
    step = pl.program_id(0)
    grad_lane, out_lane = [
        Lane(
            labels,
            ep_order,
            first,
            lane_refs[number * (2 * bits - 1) : (number + 1) * (2 * bits - 1)],
            lane_send.at[number],
            lane_get.at[number],
            rows=32,
        )
        for number, first in enumerate((cot_s, rows_s))
    ]

    def unit_copy(e):
        bit = orders[e][0]
        if e < near:
            return mesh_copy(
                send_s.at[e],
                came_ref.at[e],
                unit_send.at[e],
                unit_get.at[e],
                "rep",
                side("rep", bit)[1],
            )
        return pltpu.make_async_copy(send_s.at[e], sent_refs[e - near], unit_send.at[e])

    def inner_copy(d):
        peer = (me + d) % sources
        return mesh_copy(
            inner_s.at[peer],
            inner_got.at[me],
            inner_send.at[d - 1],
            inner_take.at[d - 1],
            "ep",
            peer,
        )

    @pl.when(step == 0)
    def _():
        loads = [
            pltpu.make_async_copy(rows_hbm, rows_s, load_sem.at[0]),
            pltpu.make_async_copy(cot_hbm, cot_s, load_sem.at[1]),
        ]
        for copy in loads:
            copy.start()
        partners = [("ep", (me + d) % sources) for d in range(1, sources)]
        for bit in sorted({order[0] for order in orders[:near]}):
            partners.append(("rep", side("rep", bit)[1]))
        greet(partners)
        for copy in loads:
            copy.wait()

    slots = pl.ds(pl.multiple_of(step * CAP, 16), CAP)
    numbers = lax.broadcasted_iota(jnp.int32, (CAP, rows_dev), 0).astype(jnp.float32)
    rows_in, cots, weights, picks = [], [], [], []
    for s in range(sources):
        rank = rank_ref[s, pl.ds(step, 1), :]
        pick_table = jnp.where(rank == numbers, 1.0, 0.0)
        weights.append(jnp.sum(pick_table * prob_ref[s, pl.ds(step, 1), :], 1, keepdims=True))
        pick_b = pick_table.astype(jnp.bfloat16)
        picks.append(pick_table)
        picks_s[s, slots, :] = pick_b
        rows_in.append(product(pick_b, rows_s[digits(s, bits)]).astype(jnp.bfloat16))
        cots.append(product(pick_b, cot_s[digits(s, bits)]))
    arrived = jnp.concatenate(rows_in, 0)
    weight = jnp.concatenate(weights, 0)
    grad_mix = branch_scale * jnp.concatenate(cots, 0)
    gate_up = gate_up_ref[0]
    down = down_ref[0]
    hidden_units = down.shape[0]
    both = product(arrived, gate_up)
    gate_part = both[:, :hidden_units]
    up_part = both[:, hidden_units:]
    sigmoid_gate = jax.nn.sigmoid(gate_part)
    active = (gate_part * sigmoid_gate * up_part).astype(jnp.bfloat16)
    produced = product(active, down).astype(jnp.bfloat16).astype(jnp.float32)
    inner = jnp.sum(grad_mix * produced, 1, keepdims=True)
    sent_out = (weight * produced).astype(jnp.bfloat16)
    grad_out = (weight * grad_mix).astype(jnp.bfloat16)
    grad_active = dot_nt(grad_out, down)
    grad_down = dot_tn(active, grad_out).astype(jnp.bfloat16)
    grad_gate = grad_active * up_part * sigmoid_gate * (1.0 + gate_part * (1.0 - sigmoid_gate))
    grad_up = grad_active * gate_part * sigmoid_gate
    grad_both = jnp.concatenate([grad_gate, grad_up], 1).astype(jnp.bfloat16)
    grad_gate_up = dot_tn(arrived, grad_both).astype(jnp.bfloat16)
    share = grad_down.shape[1] // copies
    tall = hidden_units // copies

    def put(order, mine):
        bit, *later = order
        for r in range(copies):
            spot = 0
            for b in later:
                spot = 2 * spot + ((r >> b) & 1)
            ref = keep_ref.at[0] if (r >> bit) & 1 == mine else send_s.at[step]
            ref[spot, :share, :] = grad_gate_up[r * share : (r + 1) * share]
            for k in range(copies):
                ref[spot, share : share + tall, k * share : (k + 1) * share] = grad_down[
                    k * tall : (k + 1) * tall, r * share : (r + 1) * share
                ]

    for order in {tuple(order): order for order in orders}.values():
        members = [e for e in range(count) if orders[e] == order]
        here = functools.reduce(jnp.logical_or, [step == e for e in members])
        side_mine, _ = side("rep", order[0])
        for mine in range(2):

            @pl.when(here & (side_mine == mine))
            def _(order=order, mine=mine):
                put(order, mine)

    grad_in = dot_nt(grad_both, gate_up).astype(jnp.bfloat16)
    for s in range(sources):
        part = slice(s * CAP, (s + 1) * CAP)
        out_s[s, slots, :] = sent_out[part]
        grad_s[s, slots, :] = grad_in[part]
        inner_s[s, pl.ds(step, 1), :] = jnp.sum(picks[s] * inner[part], 0, keepdims=True)
    for e in range(count):

        @pl.when(step == e)
        def _(e=e):
            unit_copy(e).start()

    @pl.when(step == count - 1)
    def _():
        for table_of, target, lane in ((grad_s, cot_s, grad_lane), (out_s, rows_s, out_lane)):
            for s in range(sources):
                target[digits(s, bits)] = dot_tn(picks_s[s], table_of[s]).astype(jnp.bfloat16)
            lane.start(0)
        for d in range(1, sources):
            inner_copy(d).start()
        for k in range(bits):
            for lane, total in ((grad_lane, grad_ref), (out_lane, out_ref)):
                lane.add(k, total)
                if k + 1 < bits:
                    lane.start(k + 1)
        inner_got[me] = inner_s[me]
        for d in range(1, sources):
            inner_copy(d).wait_recv()
        inner_ref[...] = inner_got[...]
        for d in range(1, sources):
            inner_copy(d).wait_send()
        grad_lane.finish()
        out_lane.finish()
        for e in range(count):
            unit_copy(e).wait()


def experts(rows, cots, ranks, probs, w_gate_up, w_down, copies, orders, near, labels, ep_order):
    sources, count, rows_dev = ranks.shape
    total, model_width = rows.shape
    hidden_units = w_down.shape[1]
    bits = len(labels)
    tall = model_width // copies + hidden_units // copies
    flat = lambda i: (0, 0)
    cube = lambda i: (0, 0, 0)
    once = pl.Buffered(1)
    anywhere = pl.BlockSpec(memory_space=pl.ANY)
    far = count - near
    shape = (2,) * bits + (rows_dev, model_width)
    piece = (copies // 2, tall, model_width)
    return pl.pallas_call(
        functools.partial(
            experts_kernel,
            sources=sources,
            rows_dev=rows_dev,
            count=count,
            copies=copies,
            orders=orders,
            near=near,
            labels=labels,
            ep_order=ep_order,
        ),
        out_shape=(
            jax.ShapeDtypeStruct((rows_dev, model_width), jnp.float32),
            jax.ShapeDtypeStruct((rows_dev, model_width), jnp.float32),
            jax.ShapeDtypeStruct((sources, count, rows_dev), jnp.float32),
            jax.ShapeDtypeStruct((count,) + piece, jnp.bfloat16),
            jax.ShapeDtypeStruct((near,) + piece, jnp.bfloat16),
        )
        + (jax.ShapeDtypeStruct(piece, jnp.bfloat16),) * far,
        grid=(count,),
        in_specs=[
            anywhere,
            anywhere,
            pl.BlockSpec((sources, count, rows_dev), cube, pipeline_mode=once),
            pl.BlockSpec((sources, count, rows_dev), cube, pipeline_mode=once),
            pl.BlockSpec((1, model_width, 2 * hidden_units), lambda i: (i, 0, 0)),
            pl.BlockSpec((1, hidden_units, model_width), lambda i: (i, 0, 0)),
        ],
        out_specs=[
            pl.BlockSpec((rows_dev, model_width), flat, pipeline_mode=once),
            pl.BlockSpec((rows_dev, model_width), flat, pipeline_mode=once),
            pl.BlockSpec((sources, count, rows_dev), cube, pipeline_mode=once),
            pl.BlockSpec((1,) + piece, lambda i: (i, 0, 0, 0)),
            anywhere,
        ]
        + [anywhere] * far,
        scratch_shapes=[
            pltpu.VMEM(shape, jnp.bfloat16),
            pltpu.VMEM(shape, jnp.bfloat16),
            pltpu.VMEM((sources, count * CAP, rows_dev), jnp.bfloat16),
            pltpu.VMEM((sources, count * CAP, model_width), jnp.bfloat16),
            pltpu.VMEM((sources, count * CAP, model_width), jnp.bfloat16),
            pltpu.VMEM((count,) + piece, jnp.bfloat16),
            pltpu.VMEM((sources, count, rows_dev), jnp.float32),
            pltpu.VMEM((sources, count, rows_dev), jnp.float32),
        ]
        + Lane.scratch(bits, (rows_dev, model_width), jnp.bfloat16) * 2
        + [
            pltpu.SemaphoreType.DMA((2,)),
            pltpu.SemaphoreType.DMA((count,)),
            pltpu.SemaphoreType.DMA((near,)),
            pltpu.SemaphoreType.DMA((2, bits)),
            pltpu.SemaphoreType.DMA((2, bits)),
            pltpu.SemaphoreType.DMA((sources - 1,)),
            pltpu.SemaphoreType.DMA((sources - 1,)),
        ],
        compiler_params=pltpu.CompilerParams(
            collective_id=1, has_side_effects=True, vmem_limit_bytes=67 * 1000 * 1000
        ),
        name="experts",
    )(rows.reshape(shape), cots.reshape(shape), ranks, probs, w_gate_up, w_down)


def on_device(
    tokens,
    segments,
    routes,
    attn_gain,
    w_query,
    w_key,
    w_value,
    w_out,
    mlp_gain,
    w_router,
    w_gate_up,
    w_down,
    cotangent,
    *,
    n_ep,
    n_rep,
):
    inputs = tokens[0]
    own_routes = routes[0]
    grad_output = cotangent[0]
    rows_dev, model_width = inputs.shape
    everyone = ("ep", "rep")
    heads = HEADS // n_rep
    head_width = heads * HEAD_DIM
    shared = max(1, n_rep // KV_HEADS)
    query_width = w_query.shape[1]
    key_width = w_key.shape[1]
    experts_all = w_router.shape[1]
    half_dim = HEAD_DIM // 2

    rep_bits = [("rep", b) for b in range(bits_of(n_rep))]
    ep_bits = [("ep", b) for b in range(bits_of(n_ep))]
    labels = ep_bits[::-1] + rep_bits[::-1]
    rep_down, ep_down = (rep_bits[::-1], ep_bits[::-1])
    full_query, full_rest, pack_ids = gather(
        [w_query, jnp.concatenate([w_key, w_value], 1), segments],
        [
            (labels, rep_down + ep_down),
            (labels, rep_down[:-1] + ep_down[:-1] + rep_bits[:1] + ep_bits[:1]),
            (rep_down, rep_down),
        ],
        labels,
    )
    full_query = full_query.reshape(model_width, -1)
    full_rest = full_rest.reshape(model_width, -1)
    pack_ids = pack_ids.reshape(-1)
    rotated_width = query_width + key_width
    input_width = rotated_width + key_width
    joined = after(jnp.concatenate([w_out, w_router], 1), full_query)
    full = lax.all_gather(joined, everyone, axis=0, tiled=True)
    full_out = full[:, :model_width]
    full_router = full[:, model_width:]

    length = pack_ids.shape[0]
    blocks = length // BLOCK
    offset = lax.axis_index("rep") * rows_dev
    doc_start = jnp.sum((pack_ids[None, :] < pack_ids[:, None]).astype(jnp.int32), 1)
    starts = doc_start.reshape(blocks, 1, BLOCK)
    lows = doc_start[::BLOCK] // BLOCK
    pace = jnp.exp(jnp.arange(half_dim, dtype=jnp.float32) * (-math.log(10000.0) / half_dim))

    def rope_tables(first, begins):
        places = first + jnp.arange(begins.shape[0], dtype=jnp.int32)
        angles = (places - begins).astype(jnp.float32)[:, None] * pace[None, :]
        cosine = jnp.cos(angles)
        sine = jnp.sin(angles)
        return (jnp.concatenate([cosine, cosine], 1), jnp.concatenate([-sine, sine], 1))

    own_starts = jnp.sum((pack_ids[None, :] < segments[0][:, None]).astype(jnp.int32), 1)
    own_cosine, own_sine = rope_tables(offset, own_starts)

    normed, factor_one = rms_norm(inputs, attn_gain)
    normed_b = normed.astype(jnp.bfloat16)
    mixed_in = jnp.concatenate([product(normed_b, full_query), product(normed_b, full_rest)], 1)
    turn = mixed_in[:, :rotated_width]
    times = rotated_width // HEAD_DIM
    turned = turn * jnp.tile(own_cosine, (1, times)) + swap_halves(turn) * jnp.tile(
        own_sine, (1, times)
    )
    turned_b = turned.astype(jnp.bfloat16)
    value_b = mixed_in[:, rotated_width:].astype(jnp.bfloat16)
    query_part = turned_b[:, :query_width].reshape(rows_dev, n_rep, head_width)
    key_part = turned_b[:, query_width:].reshape(rows_dev, KV_HEADS, HEAD_DIM)
    value_part = value_b.reshape(rows_dev, KV_HEADS, HEAD_DIM)
    if shared > 1:
        key_part = jnp.repeat(key_part, shared, 1)
        value_part = jnp.repeat(value_part, shared, 1)
    sending = jnp.concatenate([query_part, key_part, value_part], 2).transpose(1, 0, 2)
    head_rows = lax.all_to_all(sending, "rep", split_axis=0, concat_axis=0, tiled=True)
    head_rows = head_rows.reshape(length, head_width + 2 * HEAD_DIM)
    cosine, sine = rope_tables(0, after(doc_start, sending))
    head_rows = after(head_rows, cosine, sine)
    mixed, mixed_out, totals = attend_forward(head_rows, starts, lows, heads)
    mixed_rows = lax.all_to_all(
        mixed.reshape(n_rep, rows_dev, head_width), "rep", split_axis=0, concat_axis=0, tiled=True
    )
    mixed_rows = mixed_rows.transpose(1, 0, 2).reshape(rows_dev, query_width)
    hidden = inputs + branch_scale * product(mixed_rows, full_out)

    normed_two, factor_two = rms_norm(hidden, mlp_gain)
    normed_two_b = normed_two.astype(jnp.bfloat16)
    router_f = full_router.astype(jnp.float32)
    logits = product(normed_two_b, full_router)
    numbers = jnp.arange(experts_all, dtype=jnp.int32)
    onehot = jnp.sum((own_routes[:, :, None] == numbers).astype(jnp.float32), 1)
    chosen = onehot > 0.5
    peak = jnp.max(jnp.where(chosen, logits, far_below), 1, keepdims=True)
    raised = jnp.where(chosen, jnp.exp(jnp.minimum(logits - peak, 0.0)), 0.0)
    probs = raised / jnp.sum(raised, 1, keepdims=True)
    before = (
        lax.broadcasted_iota(jnp.int32, (rows_dev, rows_dev), 0)
        > lax.broadcasted_iota(jnp.int32, (rows_dev, rows_dev), 1)
    ).astype(jnp.bfloat16)
    rank = product(before, onehot.astype(jnp.bfloat16))
    kept = chosen & (rank < CAP)
    rank_sent = jnp.where(kept, rank, -1.0).T
    probs_sent = probs.T
    both_sent = jnp.concatenate(
        [rank_sent.reshape(n_ep, -1, rows_dev), probs_sent.reshape(n_ep, -1, rows_dev)], 1
    )
    both_all = lax.all_to_all(both_sent, "ep", split_axis=0, concat_axis=0, tiled=True)
    ranks = both_all[:, : experts_all // n_ep]
    prob_all = both_all[:, experts_all // n_ep :]
    expert_rows = lax.all_gather(normed_two_b, "ep", axis=0, tiled=True)
    expert_cots = lax.all_gather(grad_output.astype(jnp.bfloat16), "ep", axis=0, tiled=True)
    count = experts_all // n_ep
    near = count * 3 // 4
    kinds = [k % 2 for k in range(near)] + [0] * (count - near)
    leads = [0, len(rep_bits) - 2]
    orders = [
        [leads[kind]] + [b for b in range(len(rep_bits)) if b != leads[kind]] for kind in kinds
    ]
    out_sum, grad_sum, inner_back, grad_keep, came_near, *sent = experts(
        expert_rows,
        expert_cots,
        ranks,
        prob_all,
        w_gate_up,
        w_down,
        n_rep,
        orders,
        near,
        ep_bits[::-1],
        ep_bits,
    )
    rep_orders = [[("rep", b) for b in order] for order in orders]
    early = list(range(0, near, 2))
    early = early[:2]

    def halves(left, right, label, e=None):
        mine, _ = side(*label)
        half = left.shape[-3] // 2

        def total(which):
            parts = []
            for stack in (left, right):
                start = [jnp.int32(0)] * stack.ndim
                start[-3] = (which * half).astype(jnp.int32)
                size = stack.shape[-3:]
                if e is not None:
                    start[0] = jnp.int32(e)
                part = lax.dynamic_slice(
                    stack, start, (1,) * (stack.ndim - 3) + (half,) + size[1:]
                )
                parts.append(part.reshape((half,) + size[1:]).astype(jnp.float32))
            return (parts[0] + parts[1]).astype(jnp.bfloat16)

        return (total(1 - mine), total(mine))

    output = hidden + branch_scale * out_sum
    grad_probs = inner_back.reshape(experts_all, rows_dev).T
    grad_logits = probs * (grad_probs - jnp.sum(grad_probs * probs, -1, keepdims=True))
    normed_two_f = normed_two_b.astype(jnp.float32)
    grad_router = jnp.dot(normed_two_f.T, grad_logits, precision=lax.Precision.HIGHEST)
    grad_normed_two = grad_sum + jnp.dot(
        grad_logits, router_f.T, precision=lax.Precision.HIGHEST
    )
    grad_hidden_norm, grad_mlp_gain = norm_back(grad_normed_two, hidden, factor_two, mlp_gain)
    grad_hidden = grad_output + grad_hidden_norm
    grad_attn = (branch_scale * grad_hidden).astype(jnp.bfloat16)
    grad_out_w = dot_tn(mixed_rows, grad_attn)
    grad_mixed = dot_nt(grad_attn, full_out).astype(jnp.bfloat16)
    grad_heads = lax.all_to_all(
        grad_mixed.reshape(rows_dev, n_rep, head_width).transpose(1, 0, 2),
        "rep",
        split_axis=0,
        concat_axis=0,
        tiled=True,
    ).reshape(length, head_width)
    beside = [swap(after(sent[0], grad_heads), *rep_orders[near][0])]
    second = {}
    for e in early:
        give, own = halves(grad_keep, came_near, rep_orders[e][1], e)
        second[e] = (own, swap(after(give, grad_heads), *rep_orders[e][1]))
        beside.append(second[e][1])
    returning = attend_backward(
        head_rows, grad_heads, mixed_out, totals, starts, lows, cosine, sine, heads
    )
    returning = after(returning, *beside)
    onward, third = ({}, {})
    for e in early[:1]:
        give, third[e] = halves(*second[e], rep_orders[e][2])
        onward[e] = swap(after(give, returning), *rep_orders[e][2])
    returned = lax.all_to_all(
        returning.reshape(n_rep, rows_dev, head_width + 2 * HEAD_DIM),
        "rep",
        split_axis=0,
        concat_axis=0,
        tiled=True,
    ).transpose(1, 0, 2)
    parts = [grad_keep, came_near]
    steps_of = {e: ((0, e), (1, e), 0) for e in range(near)}

    def put_by(e, own, got, skip):
        steps_of[e] = ((len(parts), 0), (len(parts) + 1, 0), skip)
        parts.extend([own[None], got[None]])

    for k, half in enumerate(sent):
        steps_of[near + k] = ((0, near + k), (len(parts), 0), 0 if k == 0 else -1)
        parts.append((beside[0] if k == 0 else half)[None])
    for e in early[1:]:
        put_by(e, *second[e], 1)
    for e in early[:1]:
        own = third[e]
        put_by(e, own, onward[e], 2)
    units = [
        (e, steps_of[e][:2], rep_orders[e], steps_of[e][2])
        for e in sorted(range(count), key=lambda e: (e < near, e > 1 and e % 2, e))
    ]
    grad_query_rows = returned[:, :, :head_width].reshape(rows_dev, query_width)
    key_back = returned[:, :, head_width : head_width + HEAD_DIM]
    value_back = returned[:, :, head_width + HEAD_DIM :]
    if shared > 1:
        key_back = jnp.sum(
            key_back.reshape(rows_dev, KV_HEADS, shared, HEAD_DIM).astype(jnp.float32), 2
        ).astype(jnp.bfloat16)
        value_back = jnp.sum(
            value_back.reshape(rows_dev, KV_HEADS, shared, HEAD_DIM).astype(jnp.float32), 2
        ).astype(jnp.bfloat16)
    grad_in_rows = jnp.concatenate(
        [
            grad_query_rows,
            key_back.reshape(rows_dev, key_width),
            value_back.reshape(rows_dev, key_width),
        ],
        1,
    )
    grad_w_in = dot_tn(normed_b, grad_in_rows)
    grad_normed = dot_nt(grad_in_rows[:, :query_width], full_query) + dot_nt(
        grad_in_rows[:, query_width:], full_rest
    )
    grad_inputs_norm, grad_attn_gain = norm_back(grad_normed, inputs, factor_one, attn_gain)
    grad_inputs = grad_hidden + grad_inputs_norm
    everything = n_ep * n_rep
    gains = jnp.concatenate(
        [grad_attn_gain.reshape(everything, -1), grad_mlp_gain.reshape(everything, -1)], 1
    )
    shape = (2,) * len(labels)
    grads = [grad.astype(jnp.bfloat16) for grad in (grad_w_in, grad_out_w, grad_router)]
    lanes = [grad.reshape(shape + (-1, grad.shape[1])) for grad in grads]
    lanes.append(gains.reshape(shape + (1, -1)))
    expert_up, expert_down, weights, weights_out, weights_router, gains, _ = reduce_rest(
        parts,
        lanes,
        units,
        labels,
        ep_bits + rep_bits,
        model_width // n_rep,
    )
    gains = gains[0]
    part = model_width // everything
    return (
        output[None],
        grad_inputs[None],
        gains[:part],
        weights[:, :query_width],
        weights[:, query_width:rotated_width],
        weights[:, rotated_width:input_width],
        weights_out,
        gains[part:],
        weights_router,
        expert_up,
        expert_down,
    )


def solution(mesh):
    placed = (
        P("ep", "rep", None),
        P("ep", "rep"),
        P("ep", "rep", None),
        P(),
        P(("ep", "rep"), None),
        P(("ep", "rep"), None),
        P(("ep", "rep"), None),
        P(("ep", "rep"), None),
        P(),
        P(("ep", "rep"), None),
        P("ep", None, None),
        P("ep", None, None),
        P("ep", "rep", None),
    )
    return jax.shard_map(
        functools.partial(on_device, n_ep=mesh.shape["ep"], n_rep=mesh.shape["rep"]),
        mesh=mesh,
        in_specs=placed,
        out_specs=(
            P("ep", "rep", None),
            P("ep", "rep", None),
            P(("ep", "rep")),
            P(("ep", "rep"), None),
            P(("ep", "rep"), None),
            P(("ep", "rep"), None),
            P(("ep", "rep"), None),
            P(("ep", "rep")),
            P(("ep", "rep"), None),
            P("ep", "rep", None),
            P("ep", None, "rep"),
        ),
        check_vma=False,
    )
```
